32 devices in a mesh: ctx: 16 (over z, y, core), fsdp: 2 (over x).
Axes of the slice: x: 2, y: 2, z: 4, core: 2. Of those that a mesh axis runs over, the one named last changes fastest.
Arguments:
- tokens: bfloat16 [2, 2048, 768], P('fsdp', 'ctx'), may hold values from -6 to 6
- segments: int32 [2, 2048], P('fsdp', 'ctx'), may hold values from 0 to 7, as said below
- routes: int32 [4096, 2], P(('ctx', 'fsdp')), may hold values from 0 to 7, all different within a row; in each aligned block of 128 rows (0 to 127, 128 to 255, ...) at most 40 rows name the same one
- bucket_table: int32 [2048], replicated, may hold values from 0 to 31, as said below
- attn_gain: bfloat16 [768], P('fsdp'), may hold values from 0.5 to 1.5
- qkv_weight: bfloat16 [768, 2304], P('fsdp'), may hold values from -0.21875 to 0.21875
- out_weight: bfloat16 [768, 768], P('fsdp'), may hold values from -1.25 to 1.25
- bias_table: bfloat16 [32, 12], P('fsdp'), may hold values from -4 to 4
- moe_gain: bfloat16 [768], P('fsdp'), may hold values from 0.5 to 1.5
- router_weight: bfloat16 [768, 8], P('fsdp'), may hold values from -0.15625 to 0.15625
- up_weight: bfloat16 [8, 768, 3072], P('fsdp'), may hold values from -0.21875 to 0.21875
- down_weight: bfloat16 [8, 768, 3072], P('fsdp'), may hold values from -0.21875 to 0.21875
- cotangent: bfloat16 [2, 2048, 768], P('fsdp', 'ctx'), may hold values from -6 to 6
Outputs:
- layer_out: bfloat16 [2, 2048, 768], P('fsdp', 'ctx')
- tokens_grad: bfloat16 [2, 2048, 768], P('fsdp', 'ctx')
- attn_gain_grad: float32 [768], P('fsdp')
- qkv_grad: float32 [768, 2304], P('fsdp', 'ctx')
- out_grad: float32 [768, 768], P('fsdp', 'ctx')
- bias_grad: float32 [32, 12], P('fsdp')
- moe_gain_grad: float32 [768], P('fsdp')
- router_grad: float32 [768, 8], P('fsdp')
- up_grad: float32 [8, 768, 3072], P('fsdp', 'ctx')
- down_grad: float32 [8, 768, 3072], P('fsdp', 'ctx')
The draws below stay inside these ranges and needn't reach their ends.
Inputs may be any that keep to these rules, and one draw needn't show every extreme that they name: `segments`: in the order of positions p, document numbers never fall; they are 0 at position 0 and 7 at position 2047. `bucket_table`: never falls with the distance; 0 at distance 0 and 31 at distance 2048 - 1. `routes`: each row names 2 different experts; among the 128 rows of one device no expert is named more than 40 times.
All inputs are finite; a program needn't handle non-finite values.
Results may differ from the reference program's by a relative error of at most 0.02.
Values may be sent and summed in bfloat16 or wider, within the bound.
No kernel may reach another device: no remote copies, remote signals or barrier semaphores. Data moves between devices by JAX's collectives and lax.ppermute only.
A program may use at most 512 MiB of HBM per device.

```python
import math
from functools import partial
import jax
import jax.numpy as jnp
import numpy as np
from jax import lax

D = 768
HEADS = 12
HEAD_DIM = 64
FF = 3072
EXPERTS = 8
TOP = 2
BUCKETS = 32
DOCS = 8
SEQ_DEV = 1
TOK_SEQ = 128
TOK_DEV = 128
LEN = 2048
SEQS = 2
CAP = 40
N_CTX = 16
N_FSDP = 2


def counted_cuts(key, row_total, cut_total, length):
    draws = jax.random.randint(key, (row_total, cut_total), 0, length - 1)
    marks = 1 + draws * draws // length
    places = jnp.arange(length, dtype=jnp.int32)
    return jnp.sum((marks[:, None, :] <= places[None, :, None]).astype(jnp.int32), axis=2)


def draw_segments(key, part):
    natural = counted_cuts(jax.random.fold_in(key, 11), SEQS, DOCS - 1, LEN)
    blocks_count = LEN // TOK_SEQ
    row_index = jnp.arange(LEN, dtype=jnp.int32)
    half_len = TOK_SEQ // 2
    owner_idx = row_index // TOK_SEQ
    within = row_index % TOK_SEQ
    late_place = (2 * blocks_count - 1 - owner_idx) * half_len + within - half_len
    dealt = jnp.where(within < half_len, owner_idx * half_len + within, late_place)
    return natural[:, dealt].astype(jnp.int32)


def draw_bucket_table(key, part):
    return counted_cuts(jax.random.fold_in(key, 23), 1, BUCKETS - 1, LEN)[0].astype(jnp.int32)


def block_levels(stream_key, shape, shards, least, largest):
    def one(position, shards_of):
        steps = jax.random.uniform(jax.random.fold_in(jax.random.fold_in(stream_key, 6), position), (shards_of,), jnp.float32, least / len(shards), largest / len(shards))
        return jnp.repeat(jnp.exp(steps), shape[position] // shards_of).reshape((-1,) + (1,) * (len(shape) - position - 1))

    gain = one(*shards[0])
    for cut in shards[1:]:
        gain = gain * one(*cut)
    return gain


def deal_out(rng, own, number, rows, count, top, reach, lean):
    sequence = jax.random.permutation(rng, count)
    crowded, usual = load_shares(count, rows * top, reach, lean, True), load_shares(count, rows * top, reach, lean, False)
    places = jnp.arange(count)

    def named(tallies, rotation):
        used = int((tallies > 0).sum())
        fixed = max(1, used // 4)
        passed = fixed + (places - fixed + rotation * (used - fixed)) % max(1, count - fixed)
        return jnp.zeros((count,), jnp.int32).at[sequence[jnp.where(places < fixed, places, passed)]].set(jnp.asarray(tallies, jnp.int32))

    tallies = jnp.where(number % 4 == 0, named(crowded, number // 4), named(usual, number - number // 4 - 1))
    mixed = jax.random.permutation(jax.random.fold_in(own, 3), count)
    source_of, receiver = mixed[0:count // 2 * 2:2], mixed[1:count // 2 * 2:2]
    slack = jnp.minimum(tallies[source_of] - 1, reach - tallies[receiver]) // 2
    slack = jnp.where((source_of == sequence[0]) | (receiver == sequence[0]) | (tallies[receiver] == 0), 0, jnp.maximum(slack, 0))
    passed = jax.random.randint(jax.random.fold_in(own, 4), (count // 2,), 0, 1 << 20) % (slack + 1)
    tallies = tallies.at[source_of].add(-passed).at[receiver].add(passed)
    labels = jnp.searchsorted(jnp.cumsum(tallies), jnp.arange(rows * top), side="right").astype(jnp.int32)
    listing = labels.reshape(top, rows).T
    listing = listing[jax.random.permutation(jax.random.fold_in(own, 1), rows)]
    rotation = jax.random.randint(jax.random.fold_in(own, 2), (rows, 1), 0, top)
    return jnp.take_along_axis(listing, (jnp.arange(top)[None, :] + rotation) % top, axis=1)


def load_shares(number_of, total, limit, lean, full):
    portions = [(1 << 20) // math.isqrt(standing ** lean) + 1 for standing in range(1, number_of + 1)]
    largest = limit if full else min(limit, max(-(-total // number_of), total * portions[0] // sum(portions)))
    least = 1 if total - largest >= number_of - 1 else 0
    given, surplus = [largest] + [least] * (number_of - 1), total - largest - least * (number_of - 1)
    while surplus > 0:
        movable = [i for i in range(1, number_of) if given[i] < largest] or [i for i in range(1, number_of) if given[i] < limit]
        pool, left = sum([portions[i] for i in movable]), surplus
        for i in movable:
            extra = min(limit - given[i], max(1, left * portions[i] // pool), surplus)
            given[i] = given[i] + extra
            surplus = surplus - extra
    return np.array(given)


def gaussian(stream_key, dims, deviation, most, cuts=(), kind=jnp.bfloat16):
    entries = deviation * jax.random.normal(stream_key, dims, jnp.float32)
    if cuts:
        entries = entries * block_levels(stream_key, dims, cuts, -0.22, 0.18)
    return jnp.clip(entries, -most, most).astype(kind)


def setup_inputs(seed: int = 0) -> dict:
    seeds = jax.random.split(jax.random.key(seed), 14)
    tokens = gaussian(seeds[0], (SEQS, LEN, D), 1.0, 6.0, ((0, 2), (1, 16)))
    segments = draw_segments(jax.random.fold_in(seeds[13], 71), 0)
    routes_keys = jax.random.split(jax.random.fold_in(seeds[2], 1), (N_CTX * N_FSDP * TOK_DEV) // TOK_DEV)
    routes_turns = jax.random.permutation(jax.random.fold_in(seeds[2], 3), (N_CTX * N_FSDP * TOK_DEV) // TOK_DEV)
    routes = jax.vmap(lambda own, number: deal_out(jax.random.fold_in(seeds[2], 2), own, number, TOK_DEV, EXPERTS, TOP, CAP, 1))(routes_keys, routes_turns).reshape((N_CTX * N_FSDP * TOK_DEV, TOP))
    bucket_table = draw_bucket_table(jax.random.fold_in(seeds[13], 71), 0)
    attn_gain = jnp.clip(1.0 + 0.1 * jax.random.normal(seeds[4], (D,), jnp.float32), 0.5, 1.5).astype(jnp.bfloat16)
    qkv_weight = gaussian(seeds[5], (D, 3 * D), D ** -0.5, 0.21875, ((0, 2),))
    out_weight = gaussian(seeds[6], (D, D), (D // 32) ** -0.5, 1.25, ((0, 2),))
    bias_table = gaussian(seeds[7], (BUCKETS, HEADS), 1.0, 4.0, ((0, 2),))
    moe_gain = jnp.clip(1.0 + 0.1 * jax.random.normal(seeds[8], (D,), jnp.float32), 0.5, 1.5).astype(jnp.bfloat16)
    router_weight = gaussian(seeds[9], (D, EXPERTS), (2 * D) ** -0.5, 0.15625, ((0, 2),))
    up_weight = gaussian(seeds[10], (EXPERTS, D, FF), D ** -0.5, 0.21875, ((0, 2),))
    down_weight = gaussian(seeds[11], (EXPERTS, D, FF), (FF // 4) ** -0.5, 0.21875, ((0, 2),))
    cotangent = gaussian(seeds[12], (SEQS, LEN, D), 1.0, 6.0, ((0, 2), (1, 16)))
    return dict(tokens=tokens, segments=segments, routes=routes, bucket_table=bucket_table, attn_gain=attn_gain, qkv_weight=qkv_weight, out_weight=out_weight, bias_table=bias_table, moe_gain=moe_gain, router_weight=router_weight, up_weight=up_weight, down_weight=down_weight, cotangent=cotangent)


@jax.custom_vjp
def low(v):
    return lax.optimization_barrier(v.astype(jnp.bfloat16)).astype(jnp.float32)

@jax.custom_vjp
def low_back(v):
    return v

def low_keep(v):
    return (low(v), None)

def low_pass(kept, grad):
    return (grad,)

def back_keep(v):
    return (v, None)

def back_low(kept, grad):
    return (low(grad),)
low.defvjp(low_keep, low_pass)
low_back.defvjp(back_keep, back_low)
LOG2E = 1.4426950408889634
EPS = 1e-06
PRECISION_FULL = lax.Precision.HIGHEST

def normalize(values, weight):
    inv_rms = lax.rsqrt(lax.optimization_barrier(jnp.mean(values * values, axis=-1, keepdims=True)) + EPS)
    return values * inv_rms * weight

def positions():
    row_index = jnp.arange(LEN, dtype=jnp.int32)
    half_len = TOK_SEQ // 2
    owner_idx = row_index // TOK_SEQ
    within = row_index % TOK_SEQ
    late_place = (2 * N_CTX - 1 - owner_idx) * half_len + within - half_len
    return jnp.where(within < half_len, owner_idx * half_len + within, late_place).astype(jnp.int32)

def attend(packed, bias_table, bucket_table):
    queries, key_vecs, values, segment = packed
    places = positions()
    distance = jnp.maximum(places[:, None] - places[None, :], 0).astype(jnp.int32)
    bias_vals = jnp.take(bias_table, bucket_table[distance], axis=0)
    allowed = (segment[:, None] == segment[None, :]) & (places[None, :] <= places[:, None])
    raw_scores = low_back(jnp.einsum('qhd,khd->hqk', queries, key_vecs, precision=PRECISION_FULL) * HEAD_DIM ** (-0.5))
    scores = raw_scores + jnp.transpose(bias_vals, (2, 0, 1))
    scaled = jnp.where(allowed[None], scores * LOG2E, -jnp.inf)
    row_shift = jnp.ceil(lax.optimization_barrier(jnp.max(scaled, axis=-1, keepdims=True)))
    numerator = jnp.exp2(scaled - row_shift)
    totals = lax.optimization_barrier(jnp.sum(numerator, axis=-1))
    weighted = low_back(jnp.einsum('hqk,khd->qhd', low(numerator), values, precision=PRECISION_FULL))
    return weighted / jnp.transpose(totals)[:, :, None]

def expert_block(packed, router_weight, up_weight, down_weight):
    hidden_rows, route_ids = packed
    logits = jnp.dot(hidden_rows, router_weight, precision=PRECISION_FULL)
    chosen = jnp.take_along_axis(logits, route_ids, axis=1)
    gate_vals = jax.nn.softmax(chosen, axis=-1)
    flat_routes = route_ids.reshape(-1)
    flat_hot = (flat_routes[:, None] == jnp.arange(EXPERTS, dtype=jnp.int32)[None, :]).astype(jnp.int32)
    before = jnp.cumsum(flat_hot, axis=0) - flat_hot
    places = (flat_routes * CAP + lax.optimization_barrier(jnp.sum(before * flat_hot, axis=1))).astype(jnp.int32)
    copies = low_back(jnp.repeat(hidden_rows, TOP, axis=0))
    dispatch = jnp.zeros((EXPERTS * CAP, D), hidden_rows.dtype).at[places].set(copies).reshape(EXPERTS, CAP, D)
    upper_vals = low_back(jnp.einsum('ecd,edf->ecf', dispatch, up_weight, precision=PRECISION_FULL))
    active = low(jax.nn.gelu(upper_vals, approximate=False))
    result = low(low_back(jnp.einsum('ecf,edf->ecd', active, down_weight, precision=PRECISION_FULL)))
    picked = result.reshape(EXPERTS * CAP, D)[places].reshape(TOK_DEV, TOP, D)
    return lax.optimization_barrier(jnp.sum(gate_vals[:, :, None] * picked, axis=1))

def reference(tokens, segments, routes, bucket_table, attn_gain, qkv_weight, out_weight, bias_table, moe_gain, router_weight, up_weight, down_weight, cotangent):

    def layer(token_vals, attn_scale, query_key_value_rows, output_values, bias_vals, moe_scale, router_vals, up_vals, down_vals):
        attention_input = low(normalize(token_vals, attn_scale))
        projected_rows = jnp.einsum('hou,ui->hoi', attention_input, query_key_value_rows, precision=PRECISION_FULL)
        queries = low(low_back(projected_rows[..., :D])).reshape(SEQS, LEN, HEADS, HEAD_DIM)
        key_vecs = low(low_back(projected_rows[..., D:2 * D])).reshape(SEQS, LEN, HEADS, HEAD_DIM)
        value_vecs = low(low_back(projected_rows[..., 2 * D:])).reshape(SEQS, LEN, HEADS, HEAD_DIM)
        seq_attend = jax.checkpoint(partial(attend, bias_table=bias_vals, bucket_table=bucket_table))
        context_rows = lax.map(seq_attend, (queries, key_vecs, value_vecs, segments))
        context_rows = low(context_rows.reshape(SEQS, LEN, D))
        attention_output = low_back(jnp.einsum('hou,ui->hoi', context_rows, output_values, precision=PRECISION_FULL))
        residual = token_vals + attention_output
        moe_in = low(normalize(residual, moe_scale))
        blocks = moe_in.reshape(N_FSDP, SEQ_DEV, N_CTX, TOK_SEQ, D).transpose(2, 0, 1, 3, 4).reshape(N_CTX * N_FSDP, TOK_DEV, D)
        route_blocks = routes.reshape(N_CTX * N_FSDP, TOK_DEV, TOP)
        block_fn = jax.checkpoint(partial(expert_block, router_weight=router_vals, up_weight=up_vals, down_weight=down_vals))
        expert_sum = lax.map(block_fn, (blocks, route_blocks))
        expert_sum = expert_sum.reshape(N_CTX, N_FSDP, SEQ_DEV, TOK_SEQ, D).transpose(1, 2, 0, 3, 4).reshape(SEQS, LEN, D)
        return residual + expert_sum
    layer_out, pullback = jax.vjp(layer, tokens.astype(jnp.float32), attn_gain.astype(jnp.float32), qkv_weight.astype(jnp.float32), out_weight.astype(jnp.float32), bias_table.astype(jnp.float32), moe_gain.astype(jnp.float32), router_weight.astype(jnp.float32), up_weight.astype(jnp.float32), down_weight.astype(jnp.float32))
    gradients = pullback(cotangent.astype(jnp.float32))
    return (layer_out.astype(jnp.bfloat16), gradients[0].astype(jnp.bfloat16), gradients[1], gradients[2], gradients[3], gradients[4], gradients[5], gradients[6], gradients[7], gradients[8])
```

```python
import functools

import jax
import jax.numpy as jnp
from jax import lax
from jax.experimental import pallas as pl
from jax.experimental.pallas import tpu as pltpu
from jax.sharding import Mesh, PartitionSpec as P

HEADS = 12
HEAD_DIM = 64
EXPERTS = 8
TOP = 2
BUCKETS = 32
DOCS = 8
CAP = 40
GROUPS = 4
GHEADS = HEADS // GROUPS
GWIDTH = GHEADS * HEAD_DIM
CHUNK = 256

LOG2E = 1.4426950408889634
EPS = 1e-06
LOWEST = -1e30
FULL = lax.Precision.HIGHEST
BF = jnp.bfloat16
F32 = jnp.float32


def normalize(values, weight):
    inv_rms = lax.rsqrt(jnp.mean(values * values, axis=-1, keepdims=True) + EPS)
    return values * inv_rms * weight


def dot(a, b, dims=((1,), (0,))):
    return lax.dot_general(a, b, (dims, ((), ())), preferred_element_type=F32)


def gelu_both(upper, upstream):
    value, pullback = jax.vjp(lambda a: jax.nn.gelu(a, approximate=False), upper)
    return value, pullback(upstream)[0]


def xor_perm(mask, size):
    return [(i, i ^ mask) for i in range(size)]


def bits_of(size):
    bit = size // 2
    while bit:
        yield bit
        bit //= 2


def strip_width(blocks, half):
    need = half * (blocks - 1) + CHUNK + half
    return -(-need // 128) * 128


def strips_kernel(g_ref, out_ref):
    half = out_ref.shape[1]
    row = jnp.broadcast_to(g_ref[0], (half, g_ref.shape[2]))
    out_ref[0] = pltpu.roll(row, 0, 1, stride=1, stride_axis=0)


def make_strips(lines, half):
    count, _, width = lines.shape
    return pl.pallas_call(
        strips_kernel,
        grid=(count,),
        in_specs=[pl.BlockSpec((1, 1, width), lambda i: (i, 0, 0))],
        out_specs=pl.BlockSpec((1, half, width), lambda i: (i, 0, 0)),
        out_shape=jax.ShapeDtypeStruct((count, half, width), F32),
    )(lines)


def order_keys(me, kv_ref, kpos, half):
    members, groups = kv_ref.shape[0], kv_ref.shape[1]
    shards = members * groups
    for block in range(2 * shards):
        owner = block if block < shards else 2 * shards - 1 - block
        late = 0 if block < shards else half
        slot = (owner % members) ^ me
        kpos[block * half : (block + 1) * half, :] = kv_ref[
            slot, owner // members, late : late + half, :
        ]


def tile_terms(block, chunk, half, blocks, start):
    shift = blocks - 1 - (block - (CHUNK // half) * chunk)
    parity = lax.rem(shift, 2)
    lane = pl.multiple_of((shift - parity) * half, 128)
    keys = chunk * CHUNK + lax.broadcasted_iota(jnp.int32, (half, CHUNK), 1)
    rows = block * half + lax.broadcasted_iota(jnp.int32, (half, CHUNK), 0)
    return parity, lane, (keys <= rows) & (keys >= start)


def forward_kernel(half, blocks, info, q_ref, kv_ref, strip_ref, start_ref, o_ref, stat_ref, kpos):
    step = pl.program_id(0)

    @pl.when(step == 0)
    def _():
        order_keys(info[2, 0], kv_ref, kpos, half)

    block, first = info[0, step], info[1, step]
    q = q_ref[...]
    start = start_ref[...]

    def visit(chunk, carry):
        parity, lane, allowed = tile_terms(block, chunk, half, blocks, start)
        rows = pl.ds(pl.multiple_of(chunk * CHUNK, CHUNK), CHUNK)
        out = []
        for n in range(GHEADS):
            peak, total, acc = carry[n]
            cols = slice(n * HEAD_DIM, (n + 1) * HEAD_DIM)
            vcols = slice(GWIDTH + n * HEAD_DIM, GWIDTH + (n + 1) * HEAD_DIM)
            raw = dot(q[:, cols], kpos[rows, cols], ((1,), (1,)))
            t = raw * (HEAD_DIM**-0.5 * LOG2E) + strip_ref[parity * GHEADS + n, :, pl.ds(lane, CHUNK)]
            t = jnp.where(allowed, t, LOWEST)
            new = jnp.maximum(peak, jnp.ceil(jnp.max(t, axis=1, keepdims=True)))
            e = jnp.exp2(t - new)
            fade = jnp.exp2(peak - new)
            total = total * fade + jnp.sum(e, axis=1, keepdims=True)
            acc = acc * fade + dot(e.astype(BF), kpos[rows, vcols])
            out.append((new, total, acc))
        return tuple(out)

    init = tuple(
        (
            jnp.full((half, 1), LOWEST, F32),
            jnp.zeros((half, 1), F32),
            jnp.zeros((half, HEAD_DIM), F32),
        )
        for _ in range(GHEADS)
    )
    done = lax.fori_loop(first, block // (CHUNK // half) + 1, visit, init)
    for n in range(GHEADS):
        peak, total, acc = done[n]
        o_ref[:, n * HEAD_DIM : (n + 1) * HEAD_DIM] = acc / total
        stat_ref[:, n : n + 1] = peak
        stat_ref[:, GHEADS + n : GHEADS + n + 1] = total


def backward_kernel(
    half, blocks, info, q_ref, kv_ref, strip_ref, start_ref, do_ref, o_ref, stat_ref,
    dq_ref, dkv_ref, dline_ref, kpos, dkv, dstrip,
):
    step = pl.program_id(0)
    width = dstrip.shape[2]

    @pl.when(step == 0)
    def _():
        order_keys(info[2, 0], kv_ref, kpos, half)
        dkv[...] = jnp.zeros_like(dkv)
        dstrip[...] = jnp.zeros_like(dstrip)

    block, first = info[0, step], info[1, step]
    q = q_ref[...]
    start = start_ref[...]
    peaks, scaled, corr = [], [], []
    for n in range(GHEADS):
        cols = slice(n * HEAD_DIM, (n + 1) * HEAD_DIM)
        total = stat_ref[:, GHEADS + n : GHEADS + n + 1]
        do = do_ref[:, cols].astype(F32)
        peaks.append(stat_ref[:, n : n + 1])
        scaled.append((do / total).astype(BF))
        corr.append(jnp.sum(do * o_ref[:, cols], axis=1, keepdims=True) / total)

    def visit(chunk, carry):
        parity, lane, allowed = tile_terms(block, chunk, half, blocks, start)
        rows = pl.ds(pl.multiple_of(chunk * CHUNK, CHUNK), CHUNK)
        out = []
        for n in range(GHEADS):
            cols = slice(n * HEAD_DIM, (n + 1) * HEAD_DIM)
            vcols = slice(GWIDTH + n * HEAD_DIM, GWIDTH + (n + 1) * HEAD_DIM)
            strip = parity * GHEADS + n
            raw = dot(q[:, cols], kpos[rows, cols], ((1,), (1,)))
            t = raw * (HEAD_DIM**-0.5 * LOG2E) + strip_ref[strip, :, pl.ds(lane, CHUNK)]
            e = jnp.exp2(jnp.where(allowed, t, LOWEST) - peaks[n])
            dp = dot(scaled[n], kpos[rows, vcols], ((1,), (1,)))
            s = e * (dp - corr[n])
            low = s.astype(BF)
            out.append(carry[n] + dot(low, kpos[rows, cols]))
            dkv[rows, cols] += dot(low, q[:, cols], ((0,), (0,)))
            dkv[rows, vcols] += dot(e.astype(BF), scaled[n], ((0,), (0,)))
            dstrip[strip, :, pl.ds(lane, CHUNK)] += s
        return tuple(out)

    init = tuple(jnp.zeros((half, HEAD_DIM), F32) for _ in range(GHEADS))
    done = lax.fori_loop(first, block // (CHUNK // half) + 1, visit, init)
    for n in range(GHEADS):
        dq_ref[:, n * HEAD_DIM : (n + 1) * HEAD_DIM] = (done[n] * HEAD_DIM**-0.5).astype(BF)

    @pl.when(step == pl.num_programs(0) - 1)
    def _():
        me = info[2, 0]
        members, groups = dkv_ref.shape[0], dkv_ref.shape[1]
        shards = members * groups
        for b in range(2 * shards):
            owner = b if b < shards else 2 * shards - 1 - b
            late = 0 if b < shards else half
            part = dkv[b * half : (b + 1) * half, :]
            lanes = lax.broadcasted_iota(jnp.int32, part.shape, 1)
            part = part * jnp.where(lanes < GWIDTH, HEAD_DIM**-0.5, 1.0)
            dkv_ref[(owner % members) ^ me, owner // members, late : late + half, :] = part.astype(BF)
        for n in range(GHEADS):
            for parity in range(2):
                x = dstrip[parity * GHEADS + n]
                rows = half
                while rows > 8:
                    rows //= 2
                    x = x[:rows] + pltpu.roll(x[rows:], width - rows, 1)
                sub = lax.broadcasted_iota(jnp.int32, x.shape, 0)
                for bit in (4, 2, 1):
                    x = jnp.where((sub & bit) != 0, pltpu.roll(x, width - bit, 1), x)
                line = jnp.sum(x, axis=0, keepdims=True)
                if parity == 0:
                    even = line
                else:
                    dline_ref[n : n + 1, :] = even + pltpu.roll(line, half, 1)


def whole(shape):
    return pl.BlockSpec(shape, lambda i, info: (0,) * len(shape))


def attend(info, q, kv, strips, start, blocks):
    rows = q.shape[0]
    half = strips.shape[1]
    block = lambda width: pl.BlockSpec((half, width), lambda i, info: (i, 0))
    return pl.pallas_call(
        functools.partial(forward_kernel, half, blocks),
        grid_spec=pltpu.PrefetchScalarGridSpec(
            num_scalar_prefetch=1,
            grid=(rows // half,),
            in_specs=[block(GWIDTH), whole(kv.shape), whole(strips.shape), block(1)],
            out_specs=[block(GWIDTH), block(8)],
            scratch_shapes=[pltpu.VMEM((blocks * half, 2 * GWIDTH), BF)],
        ),
        out_shape=[
            jax.ShapeDtypeStruct((rows, GWIDTH), F32),
            jax.ShapeDtypeStruct((rows, 8), F32),
        ],
        compiler_params=pltpu.CompilerParams(vmem_limit_bytes=48 << 20),
        name="attend",
    )(info, q, kv, strips, start)


def attend_back(info, q, kv, strips, start, do, o, stat, blocks):
    rows = q.shape[0]
    half = strips.shape[1]
    width = strips.shape[2]
    block = lambda width: pl.BlockSpec((half, width), lambda i, info: (i, 0))
    return pl.pallas_call(
        functools.partial(backward_kernel, half, blocks),
        grid_spec=pltpu.PrefetchScalarGridSpec(
            num_scalar_prefetch=1,
            grid=(rows // half,),
            in_specs=[
                block(GWIDTH), whole(kv.shape), whole(strips.shape), block(1),
                block(GWIDTH), block(GWIDTH), block(8),
            ],
            out_specs=[block(GWIDTH), whole(kv.shape), whole((GHEADS, width))],
            scratch_shapes=[
                pltpu.VMEM((blocks * half, 2 * GWIDTH), BF),
                pltpu.VMEM((blocks * half, 2 * GWIDTH), F32),
                pltpu.VMEM(strips.shape, F32),
            ],
        ),
        out_shape=[
            jax.ShapeDtypeStruct((rows, GWIDTH), BF),
            jax.ShapeDtypeStruct(kv.shape, BF),
            jax.ShapeDtypeStruct((GHEADS, width), F32),
        ],
        compiler_params=pltpu.CompilerParams(vmem_limit_bytes=56 << 20),
        name="attend_back",
    )(info, q, kv, strips, start, do, o, stat)


def gather_members(x):
    size = lax.axis_size("m")
    held = {0: x[None]}
    for bit in bits_of(size):
        keys = sorted(held)
        sent = jnp.concatenate([held[k] for k in keys]) if len(keys) > 1 else held[keys[0]]
        came = lax.ppermute(sent, "m", xor_perm(bit, size))
        for i, k in enumerate(keys):
            held[k | bit] = came[i : i + 1]
    return jnp.concatenate([held[k] for k in range(size)])


def reduce_members(x):
    size = lax.axis_size("m")
    held = {k: x[k] for k in range(size)}
    bit = 1
    while bit < size:
        keep = [k for k in sorted(held) if not k & bit]
        sent = jnp.stack([held[k | bit] for k in keep]).astype(BF)
        came = lax.ppermute(sent, "m", xor_perm(bit, size))
        held = {k: held[k].astype(F32) + came[i].astype(F32) for i, k in enumerate(keep)}
        bit *= 2
    return held[0]


def halve(x, axis, bit):
    mine = lax.rem(lax.axis_index(axis) // bit, 2)
    keep = lax.dynamic_index_in_dim(x, mine, 0, False)
    send = lax.dynamic_index_in_dim(x, 1 - mine, 0, False)
    came = lax.ppermute(send.astype(BF), axis, xor_perm(bit, lax.axis_size(axis)))
    return keep.astype(F32) + came.astype(F32)


def butterfly(x):
    for axis in ("fsdp", "m", "h"):
        size = lax.axis_size(axis)
        for bit in bits_of(size):
            x = x + lax.ppermute(x, axis, xor_perm(bit, size))
    return x


class Rows:
    def __init__(self):
        self.split = lax.axis_size("fsdp") == 2 and lax.axis_size("m") % 2 == 0
        self.f = lax.axis_index("fsdp")
        self.core = lax.rem(lax.axis_index("m"), 2)

    def gather(self, w):
        if not self.split:
            return lax.all_gather(w, "fsdp", axis=0, tiled=True)
        half = w.shape[0] // 2
        part = lax.dynamic_slice_in_dim(w, self.core * half, half, 0)
        first = lax.ppermute(part, "fsdp", xor_perm(1, 2))
        second = lax.ppermute(first, "m", xor_perm(1, lax.axis_size("m")))
        return jnp.concatenate([w, first, second])

    def into(self, x):
        if not self.split:
            return x
        half = x.shape[-1] // 2
        low, high = x[..., :half], x[..., half:]
        own = jnp.where(self.f == 0, low, high)
        other = jnp.where(self.f == 0, high, low)
        a, b = other[..., : half // 2], other[..., half // 2 :]
        return jnp.concatenate(
            [own, jnp.where(self.core == 0, a, b), jnp.where(self.core == 0, b, a)], axis=-1
        )

    def back(self, y):
        if not self.split:
            return y
        half = y.shape[-1] // 2
        own, first, second = y[..., :half], y[..., half : half + half // 2], y[..., half + half // 2 :]
        other = jnp.concatenate(
            [jnp.where(self.core == 0, first, second), jnp.where(self.core == 0, second, first)], axis=-1
        )
        return jnp.concatenate(
            [jnp.where(self.f == 0, own, other), jnp.where(self.f == 0, other, own)], axis=-1
        )


def per_device(
    tokens, segments, routes, bucket_table, attn_gain, qkv_weight, out_weight, bias_table,
    moe_gain, router_weight, up_weight, down_weight, cotangent,
):
    tok, width = tokens.shape[1], tokens.shape[2]
    half = tok // 2
    h, m, f = lax.axis_index("h"), lax.axis_index("m"), lax.axis_index("fsdp")
    members, n_fsdp = lax.axis_size("m"), lax.axis_size("fsdp")
    shards = GROUPS * members
    blocks = 2 * shards
    length = shards * tok
    here = EXPERTS // n_fsdp
    spread = here > 1
    ffn = up_weight.shape[2]
    rows_f = width // n_fsdp
    order = Rows()

    qkv_full = order.gather(qkv_weight)
    out_full = order.gather(out_weight)
    pad = jnp.zeros((1, rows_f), BF)
    bias_flat = bias_table.reshape(1, -1)
    bias_rows = -(-bias_flat.shape[1] // rows_f)
    bias_flat = jnp.pad(bias_flat, ((0, 0), (0, bias_rows * rows_f - bias_flat.shape[1])))
    small = jnp.concatenate(
        [attn_gain[None], moe_gain[None], router_weight.T, bias_flat.reshape(bias_rows, rows_f)]
        + [pad] * (16 - 10 - bias_rows)
    )
    small = lax.all_gather(small, "fsdp", axis=0)
    attn_scale = small[:, 0].reshape(width).astype(F32)
    moe_scale = small[:, 1].reshape(width).astype(F32)
    router_t = jnp.transpose(small[:, 2:10], (1, 0, 2)).reshape(EXPERTS, width)
    bias_full = small[:, 10 : 10 + bias_rows].reshape(n_fsdp, -1)[:, : bias_table.size]
    bias_full = bias_full.reshape(BUCKETS, HEADS)

    seg_all = lax.all_to_all(
        jnp.broadcast_to(segments, (shards, tok)), ("h", "m"), 0, 0, tiled=True
    )
    docs = jnp.arange(DOCS, dtype=jnp.int32)
    starts = jnp.sum((seg_all[None] < docs[:, None, None]).astype(jnp.int32), axis=(1, 2))
    seg_q = lax.dynamic_index_in_dim(seg_all.reshape(GROUPS, members, tok), m, 1, False).reshape(-1)
    start_q = jnp.sum(jnp.where(seg_q[:, None] == docs, starts, 0), axis=1)
    owner = jnp.arange(GROUPS, dtype=jnp.int32) * members + m
    block_q = jnp.stack([owner, blocks - 1 - owner], axis=1).reshape(-1)
    first_q = jnp.min(start_q.reshape(2 * GROUPS, half), axis=1) // CHUNK
    info = jnp.stack([block_q, first_q, jnp.full_like(block_q, m)])
    start_col = start_q[:, None]

    wide = strip_width(blocks, half)
    top = half * (blocks - 1)
    line = jnp.concatenate(
        [
            bucket_table[: top + 1][::-1],
            jnp.full((wide - length,), -1, jnp.int32),
            bucket_table[top + 1 :][::-1],
        ]
    )
    hot = (line[None] == jnp.arange(BUCKETS, dtype=jnp.int32)[:, None]).astype(BF)
    bias_mine = lax.dynamic_slice_in_dim(bias_full, h * GHEADS, GHEADS, 1)
    lines = dot(bias_mine, hot, ((0,), (0,))) * LOG2E
    lines = jnp.concatenate([lines, jnp.roll(lines, -half, axis=1)])[:, None]
    strips = make_strips(lines, half)

    hot_routes = (routes.reshape(-1)[:, None] == jnp.arange(EXPERTS)[None]).astype(F32)
    earlier = jnp.arange(tok * TOP)
    earlier = (earlier[None, :] < earlier[:, None]).astype(BF)
    before = dot(earlier, hot_routes.astype(BF))
    slot = jnp.sum(before * hot_routes, axis=1).astype(jnp.int32).reshape(tok, TOP)
    target = (routes % here) * n_fsdp + routes // here
    place = target * CAP + slot
    slots = jnp.arange(EXPERTS * CAP, dtype=jnp.int32)
    pick = [slots[:, None] == place[None, :, k] for k in range(TOP)]
    pick_any = (pick[0] | pick[1]).astype(BF)
    exchange = ("h", "fsdp") if spread else ("fsdp",)

    def deal(rows):
        send = rows.reshape(EXPERTS, CAP, rows.shape[-1])
        return lax.all_to_all(send, exchange, 0, 0, tiled=True).reshape(rows.shape)

    dy_slots = deal(dot(pick_any, cotangent[0]).astype(BF))

    x = tokens[0].astype(F32)
    attn_in = normalize(x, attn_scale).astype(BF)
    proj = dot(order.into(attn_in), qkv_full).astype(BF)
    proj = jnp.transpose(proj.reshape(tok, 3, GROUPS, GWIDTH), (2, 0, 1, 3)).reshape(GROUPS, tok, 3 * GWIDTH)
    proj = lax.all_to_all(proj, "h", 0, 0, tiled=True)
    q = proj[..., :GWIDTH].reshape(GROUPS * tok, GWIDTH)
    kv = gather_members(proj[..., GWIDTH:])
    o_pre, stat = attend(info, q, kv, strips, start_col, blocks)
    context = lax.all_to_all(o_pre.astype(BF).reshape(GROUPS, tok, GWIDTH), "h", 0, 0, tiled=True)
    context = jnp.transpose(context, (1, 0, 2)).reshape(tok, width)
    residual = x + dot(order.into(context), out_full)

    moe_in = normalize(residual, moe_scale).astype(BF)
    logits = dot(moe_in, router_t, ((1,), (1,)))
    route_hot = hot_routes.reshape(tok, TOP, EXPERTS)
    chosen = jnp.sum(logits[:, None, :] * route_hot, axis=-1)
    gates = jax.nn.softmax(chosen, axis=-1)
    gate_slots = sum(
        jnp.sum(jnp.where(pick[k], gates[None, :, k], 0.0), axis=1, keepdims=True) for k in range(TOP)
    )
    high = lax.reduce_precision(gate_slots, 8, 7)
    mid = lax.reduce_precision(gate_slots - high, 8, 7)
    low = gate_slots - high - mid
    extra = jnp.concatenate([high, mid, low, jnp.zeros((slots.shape[0], 125), F32)], axis=1)
    rows_out = jnp.concatenate([dot(pick_any, moe_in).astype(BF), extra.astype(BF)], axis=1)

    came = deal(rows_out)
    rows_in = came[:, :width]
    gate_in = jnp.sum(came[:, width : width + 3].astype(F32), axis=1, keepdims=True)
    mine = h if spread else 0
    up = lax.dynamic_index_in_dim(up_weight, mine, 0, False)
    down = lax.dynamic_index_in_dim(down_weight, mine, 0, False)
    slot_grad = (gate_in * dy_slots.astype(F32)).astype(BF)
    upper = dot(rows_in, up)
    active_grad = dot(slot_grad, down)
    active, upper_grad = gelu_both(upper, active_grad)
    active, upper_grad = active.astype(BF), upper_grad.astype(BF)
    expert_out = dot(active, down, ((1,), (1,))).astype(BF)
    dispatch_grad = dot(upper_grad, up, ((1,), (1,))).astype(BF)
    back = deal(jnp.concatenate([expert_out, dispatch_grad], axis=1))
    result, input_grad = back[:, :width], back[:, width:]

    def members_first(rows):
        if not spread:
            return rows
        cut = rows.reshape(rows.shape[0], GROUPS, members, width // shards)
        return jnp.transpose(cut, (0, 2, 1, 3)).reshape(rows.shape)

    up_term = dot(members_first(rows_in), upper_grad, ((0,), (0,))).astype(BF)
    down_term = dot(members_first(slot_grad), active, ((0,), (0,))).astype(BF)
    terms = jnp.concatenate([up_term, down_term], axis=1)
    terms = lax.psum_scatter(terms, "m" if spread else ("h", "m"), scatter_dimension=0, tiled=True)
    terms = terms.reshape(here, width // shards, 2 * ffn)
    if spread:
        terms = lax.all_to_all(terms, "h", 0, 0, tiled=True)
    up_grad, down_grad = terms[..., :ffn].astype(F32), terms[..., ffn:].astype(F32)

    dy = cotangent[0].astype(F32)
    picked = [dot(pick[k].astype(BF), result, ((0,), (0,))) for k in range(TOP)]
    layer_out = residual + gates[:, :1] * picked[0] + gates[:, 1:] * picked[1]
    gate_grad = jnp.stack([jnp.sum(dy * p, axis=1) for p in picked], axis=1)
    chosen_grad = gates * (gate_grad - jnp.sum(gates * gate_grad, axis=1, keepdims=True))
    logit_grad = jnp.sum(chosen_grad[:, :, None] * route_hot, axis=1)
    router_grad = lax.dot_general(
        logit_grad, moe_in.astype(F32), (((0,), (0,)), ((), ())), precision=FULL
    )
    moe_in_grad = lax.dot_general(
        logit_grad, router_t.astype(F32), (((1,), (0,)), ((), ())), precision=FULL
    )
    moe_in_grad = moe_in_grad + dot(pick_any, input_grad, ((0,), (0,)))
    norm_grad, moe_gain_grad = jax.vjp(normalize, residual, moe_scale)[1](moe_in_grad)
    resid_grad = dy + norm_grad
    attn_grad = resid_grad.astype(BF)

    out_term = dot(attn_grad, context, ((0,), (0,))).astype(BF)
    out_term = lax.psum_scatter(out_term, ("h", "m"), scatter_dimension=0, tiled=True)
    out_term = lax.psum_scatter(out_term.T, "fsdp", scatter_dimension=0, tiled=True)
    out_grad = out_term.astype(F32)
    do = order.back(dot(attn_grad, out_full, ((1,), (1,)))).astype(BF)
    do = jnp.transpose(do.reshape(tok, GROUPS, GWIDTH), (1, 0, 2))
    do = lax.all_to_all(do, "h", 0, 0, tiled=True).reshape(GROUPS * tok, GWIDTH)

    dq, dkv, dline = attend_back(info, q, kv, strips, start_col, do, o_pre, stat, blocks)
    dkv = reduce_members(dkv).astype(BF)
    dproj = jnp.concatenate([dq.reshape(GROUPS, tok, GWIDTH), dkv], axis=2)
    bias_mine = lax.dot_general(
        hot.astype(F32), dline, (((1,), (1,)), ((), ())), precision=FULL
    )

    ain = lax.all_gather(attn_in, "h", axis=0).reshape(GROUPS * tok, width)
    flat = dproj.reshape(GROUPS * tok, 3 * GWIDTH)
    term = dot(flat, ain, ((0,), (0,)))
    unit = GWIDTH // members
    term = term.reshape(3, members, unit, width)
    for bit in bits_of(members):
        cut = jnp.transpose(term.reshape(3, 2, -1, unit, width), (1, 0, 2, 3, 4))
        term = halve(cut, "m", bit)
    for bit in bits_of(n_fsdp):
        cut = jnp.stack(jnp.split(term, 2, axis=-1))
        term = halve(cut, "fsdp", bit)
    term = term.reshape(3, unit, rows_f).astype(BF)
    me = h * members + m
    parts = []
    for r in range(3):
        source = [((3 * d + r) % shards, d) for d in range(shards)]
        target_of = [0] * shards
        for s, d in source:
            target_of[s] = (3 * d + r) // shards
        which = jnp.sum(jnp.where(jnp.arange(shards) == me, jnp.asarray(target_of), 0))
        send = lax.dynamic_index_in_dim(term, which, 0, False)
        parts.append(lax.ppermute(send, ("h", "m"), source))
    qkv_grad = jnp.concatenate(parts).astype(F32).T

    dproj = lax.all_to_all(dproj, "h", 0, 0, tiled=True)
    dproj = jnp.transpose(dproj.reshape(GROUPS, tok, 3, GWIDTH), (1, 2, 0, 3)).reshape(tok, 3 * width)
    attn_in_grad = order.back(dot(dproj, qkv_full, ((1,), (1,))))
    token_grad, attn_gain_grad = jax.vjp(normalize, x, attn_scale)[1](attn_in_grad)
    tokens_grad = (resid_grad + token_grad).astype(BF)

    bias_own = lax.dynamic_update_slice_in_dim(jnp.zeros((BUCKETS, HEADS), F32), bias_mine, h * GHEADS, 1)
    pack = jnp.concatenate(
        [router_grad, attn_gain_grad[None], moe_gain_grad[None]]
        + [jnp.pad(bias_own.reshape(1, -1), ((0, 0), (0, width - bias_own.size)))]
    )
    pack = butterfly(pack)
    mine_f = lax.dynamic_slice_in_dim(pack[:10], f * rows_f, rows_f, 1)
    bias_grad = pack[10, : bias_own.size].reshape(BUCKETS, HEADS)
    bias_grad = lax.dynamic_slice_in_dim(bias_grad, f * (BUCKETS // n_fsdp), BUCKETS // n_fsdp, 0)
    return (
        layer_out.astype(BF)[None],
        tokens_grad[None],
        mine_f[8],
        qkv_grad,
        out_grad,
        bias_grad,
        mine_f[9],
        mine_f[:8].T,
        up_grad,
        down_grad,
    )


def solution(mesh):
    n_ctx, n_fsdp = mesh.shape["ctx"], mesh.shape["fsdp"]
    cut = Mesh(mesh.devices.reshape(GROUPS, n_ctx // GROUPS, n_fsdp), ("h", "m", "fsdp"))
    ctx = ("h", "m")
    return jax.shard_map(
        per_device,
        mesh=cut,
        in_specs=(
            P("fsdp", ctx, None),
            P("fsdp", ctx),
            P(("h", "m", "fsdp"), None),
            P(),
            P("fsdp"),
            P("fsdp", None),
            P("fsdp", None),
            P("fsdp", None),
            P("fsdp"),
            P("fsdp", None),
            P("fsdp", None, None),
            P("fsdp", None, None),
            P("fsdp", ctx, None),
        ),
        out_specs=(
            P("fsdp", ctx, None),
            P("fsdp", ctx, None),
            P("fsdp"),
            P("fsdp", ctx),
            P("fsdp", ctx),
            P("fsdp", None),
            P("fsdp"),
            P("fsdp", None),
            P("fsdp", ctx, None),
            P("fsdp", ctx, None),
        ),
        check_vma=False,
    )
```

```python
import functools

import jax
import jax.numpy as jnp
from jax import lax
from jax.experimental import pallas as pl
from jax.experimental.pallas import tpu as pltpu
from jax.sharding import Mesh, PartitionSpec as P

HEADS = 12
HEAD_DIM = 64
EXPERTS = 8
TOP = 2
BUCKETS = 32
DOCS = 8
CAP = 40
GROUPS = 4
GHEADS = HEADS // GROUPS
GWIDTH = GHEADS * HEAD_DIM
CHUNK = 256

LOG2E = 1.4426950408889634
EPS = 1e-06
LOWEST = -1e30
FULL = lax.Precision.HIGHEST
BF = jnp.bfloat16
F32 = jnp.float32
MEMBERS = ("r", "core")
CTX = ("h", "r", "core")


def normalize(values, weight):
    inv_rms = lax.rsqrt(jnp.mean(values * values, axis=-1, keepdims=True) + EPS)
    return values * inv_rms * weight


def dot(a, b, dims=((1,), (0,))):
    return lax.dot_general(a, b, (dims, ((), ())), preferred_element_type=F32)


def exact_dot(a, b, dims):
    return lax.dot_general(a, b, (dims, ((), ())), precision=FULL)


def xor_perm(mask, size):
    return [(i, i ^ mask) for i in range(size)]


def bits_of(size):
    bit = size // 2
    while bit:
        yield bit
        bit //= 2


def strip_width(blocks, half):
    need = half * (blocks - 1) + CHUNK + half
    return -(-need // 128) * 128


def strips_kernel(g_ref, out_ref):
    half = out_ref.shape[1] // GHEADS
    rolled = [
        pltpu.roll(
            jnp.broadcast_to(g_ref[n : n + 1, :], (half, g_ref.shape[1])), 0, 1, stride=1, stride_axis=0
        )
        for n in range(GHEADS)
    ]
    out_ref[...] = jnp.concatenate(rolled).T


def make_strips(lines, half):
    return pl.pallas_call(
        strips_kernel,
        out_shape=jax.ShapeDtypeStruct((lines.shape[1], GHEADS * half), F32),
        cost_estimate=pl.CostEstimate(flops=3 * 10**9, bytes_accessed=2 * 10**6, transcendentals=0),
        name="strips",
    )(lines)


def own_blocks(size, half):
    a = lax.broadcasted_iota(jnp.int32, (size, size), 0) // half
    b = lax.broadcasted_iota(jnp.int32, (size, size), 1) // half
    return a == b


def spread_rows(x, same):
    return jnp.where(same, jnp.concatenate([x] * GHEADS), 0.0)


def fold_rows(x, same, half):
    y = jnp.where(same, x, 0.0).T
    return sum(y[n * half : (n + 1) * half] for n in range(GHEADS))


def group_of(slot, h):
    return lax.rem(h + GROUPS - slot, GROUPS)


def place_of(slot, early, me, h, members, blocks):
    owner = group_of(slot, h) * members + me
    return owner if early else blocks - 1 - owner


def bounds(block, chunk, half, blocks, start):
    top = (blocks - 1 - (block - (CHUNK // half) * chunk)) * half
    lane = lax.broadcasted_iota(jnp.int32, (1, GHEADS * half), 1)
    last = block * half + lax.rem(lane, half) - chunk * CHUNK
    return pl.multiple_of(top, half), last, start - chunk * CHUNK


def forward_kernel(half, blocks, members, pos, q_ref, *refs):
    kvs, refs = refs[:members], refs[members:]
    strip_ref, o_ref, low_ref, stat_ref, k_out, v_out, kt_out, k_ref, v_ref, kt_ref, vt, sems = refs
    size = GHEADS * half
    me, h = pos[0], pos[1]
    tok = 2 * half
    same = own_blocks(size, half)
    key = lax.broadcasted_iota(jnp.int32, (CHUNK, size), 0)
    per = CHUNK // half

    @pl.loop(0, GROUPS)
    def _(slot):
        for j in range(members):
            for early in (True, False):
                block = place_of(slot, early, jnp.bitwise_xor(me, j), h, members, blocks)
                at = pl.ds(pl.multiple_of(lax.rem(block, per) * half, half), half)
                rows = kvs[j][slot, 0 if early else half : half if early else tok, :]
                k_ref[block // per, at, :] = rows[:, :GWIDTH]
                v_ref[block // per, at, :] = rows[:, GWIDTH:]

    @pl.loop(0, blocks // per)
    def _(chunk):
        kt_ref[chunk] = k_ref[chunk].astype(F32).T.astype(BF)
        vt[chunk] = v_ref[chunk].astype(F32).T.astype(BF)

    copies = [
        pltpu.make_async_copy(src, dst, sems.at[i])
        for i, (src, dst) in enumerate(((k_ref, k_out), (v_ref, v_out), (kt_ref, kt_out)))
    ]
    for copy in copies:
        copy.start()

    docs = jnp.concatenate([kv[a, tok : tok + 1, :tok].astype(F32) for kv in kvs for a in range(GROUPS)])
    begins = [jnp.sum(jnp.where(docs < s, 1.0, 0.0)) for s in range(1, DOCS)]

    @pl.loop(0, q_ref.shape[0] // half)
    def _(i):
        slot, late = i // 2, lax.rem(i, 2)
        owner = group_of(slot, h) * members + me
        block = jnp.where(late == 0, owner, blocks - 1 - owner)
        at = pl.ds(pl.multiple_of(i * half, half), half)
        qt = spread_rows(q_ref[at, :].astype(F32), same).T.astype(BF)
        doc = kvs[0][slot, tok : tok + 1, :tok].astype(F32)
        doc = jnp.where(late == 0, doc[:, :half], doc[:, half:])
        begin = jnp.zeros((1, half), F32)
        for s in range(1, DOCS):
            begin = jnp.where(doc == s, begins[s - 1], begin)
        first = jnp.min(begin).astype(jnp.int32) // CHUNK
        begin = jnp.concatenate([begin] * GHEADS, axis=1)
        start = begin.astype(jnp.int32)

        def visit(chunk, carry):
            peak, total, acc = carry
            top, last, begin = bounds(block, chunk, half, blocks, start)
            t = dot(k_ref[chunk], qt) * (HEAD_DIM**-0.5 * LOG2E) + strip_ref[pl.ds(top, CHUNK), :]
            t = jnp.where((key <= last) & (key >= begin), t, LOWEST)
            new = jnp.maximum(peak, jnp.ceil(jnp.max(t, axis=0, keepdims=True)))
            e = jnp.exp2(t - new)
            fade = jnp.exp2(peak - new)
            total = total * fade + jnp.sum(e, axis=0, keepdims=True)
            acc = acc * fade + dot(vt[chunk], e.astype(BF))
            return new, total, acc

        init = (
            jnp.full((1, size), LOWEST, F32),
            jnp.zeros((1, size), F32),
            jnp.zeros((GWIDTH, size), F32),
        )
        peak, total, acc = lax.fori_loop(first, block // per + 1, visit, init)
        out = fold_rows(acc / total, same, half)
        o_ref[at, :] = out
        low_ref[group_of(slot, h), pl.ds(pl.multiple_of(late * half, half), half), :] = out.astype(BF)
        stat_ref[i, 0:1, :] = peak
        stat_ref[i, 1:2, :] = total
        stat_ref[i, 2:3, :] = begin

    for copy in copies:
        copy.wait()


def backward_kernel(half, blocks, members, pos, q_ref, strip_ref, do_ref, o_ref, stat_ref, *refs):
    (k_in, v_in, kt_in, dq_ref), refs = refs[:4], refs[4:]
    dkvs, refs = refs[:members], refs[members:]
    dline_ref, k_ref, v_ref, kt_ref, dk, dv, dstrip, sems = refs
    size = GHEADS * half
    me, h = pos[0], pos[1]
    width = dstrip.shape[0]
    per = CHUNK // half
    copies = [
        pltpu.make_async_copy(src, dst, sems.at[i])
        for i, (src, dst) in enumerate(((k_in, k_ref), (v_in, v_ref), (kt_in, kt_ref)))
    ]
    for copy in copies:
        copy.start()
    same = own_blocks(size, half)
    key = lax.broadcasted_iota(jnp.int32, (CHUNK, size), 0)

    @pl.loop(0, blocks // per)
    def _(chunk):
        dk[chunk] = jnp.zeros(dk.shape[1:], F32)
        dv[chunk] = jnp.zeros(dv.shape[1:], F32)

    @pl.loop(0, width // 128)
    def _(j):
        dstrip[pl.ds(pl.multiple_of(j * 128, 128), 128), :] = jnp.zeros((128, size), F32)

    for copy in copies:
        copy.wait()

    @pl.loop(0, q_ref.shape[0] // half)
    def _(i):
        slot, late = i // 2, lax.rem(i, 2)
        owner = group_of(slot, h) * members + me
        block = jnp.where(late == 0, owner, blocks - 1 - owner)
        at = pl.ds(pl.multiple_of(i * half, half), half)
        peak, total, start = (stat_ref[i, n : n + 1, :] for n in range(3))
        first = jnp.min(start).astype(jnp.int32) // CHUNK
        start = start.astype(jnp.int32)
        qs = spread_rows(q_ref[at, :].astype(F32), same)
        qt, qs = qs.T.astype(BF), qs.astype(BF)
        do = do_ref[group_of(slot, h), pl.ds(pl.multiple_of(late * half, half), half), :].astype(F32)
        corr = jnp.sum(spread_rows(do * o_ref[at, :], same).T, axis=0, keepdims=True) / total
        gt = spread_rows(do, same).T / total
        gs = gt.T.astype(BF)
        gt = gt.astype(BF)

        def visit(chunk, dq):
            top, last, begin = bounds(block, chunk, half, blocks, start)
            t = dot(k_ref[chunk], qt) * (HEAD_DIM**-0.5 * LOG2E) + strip_ref[pl.ds(top, CHUNK), :]
            t = jnp.where((key <= last) & (key >= begin), t - peak, LOWEST)
            e = jnp.exp2(t)
            s = e * (dot(v_ref[chunk], gt) - corr)
            low = s.astype(BF)
            dk[chunk] += dot(low, qs)
            dv[chunk] += dot(e.astype(BF), gs)
            dstrip[pl.ds(top, CHUNK), :] += s
            return dq + dot(kt_ref[chunk], low)

        dq = lax.fori_loop(first, block // per + 1, visit, jnp.zeros((GWIDTH, size), F32))
        dq_ref[at, :] = (fold_rows(dq, same, half) * HEAD_DIM**-0.5).astype(BF)

    @pl.loop(0, GROUPS)
    def _(slot):
        for j in range(members):
            for early in (True, False):
                block = place_of(slot, early, jnp.bitwise_xor(me, j), h, members, blocks)
                at = pl.ds(pl.multiple_of(lax.rem(block, per) * half, half), half)
                part = jnp.concatenate(
                    [dk[block // per, at, :] * HEAD_DIM**-0.5, dv[block // per, at, :]], axis=1
                )
                dkvs[j][slot, 0 if early else half : half if early else 2 * half, :] = part.astype(BF)

    lines = dstrip[...].T
    for n in range(GHEADS):
        x = lines[n * half : (n + 1) * half]
        rows = half
        while rows > 8:
            rows //= 2
            x = x[:rows] + pltpu.roll(x[rows:], width - rows, 1)
        sub = lax.broadcasted_iota(jnp.int32, x.shape, 0)
        for bit in (4, 2, 1):
            x = jnp.where((sub & bit) != 0, pltpu.roll(x, width - bit, 1), x)
        dline_ref[n : n + 1, :] = jnp.sum(x, axis=0, keepdims=True)


VMEM_SPEC = pl.BlockSpec(memory_space=pltpu.VMEM)
SMEM_SPEC = pl.BlockSpec(memory_space=pltpu.SMEM)
HBM_SPEC = pl.BlockSpec(memory_space=pltpu.HBM)


def key_shapes(blocks, half):
    chunks = blocks * half // CHUNK
    return ((chunks, CHUNK, GWIDTH), (chunks, CHUNK, GWIDTH), (chunks, GWIDTH, CHUNK))


def attend(pos, q, kvs, strips, blocks):
    rows = q.shape[0]
    half = strips.shape[1] // GHEADS
    shapes = key_shapes(blocks, half)
    return pl.pallas_call(
        functools.partial(forward_kernel, half, blocks, len(kvs)),
        in_specs=[SMEM_SPEC] + [VMEM_SPEC] * (2 + len(kvs)),
        out_specs=[VMEM_SPEC] * 3 + [HBM_SPEC] * 3,
        scratch_shapes=[pltpu.VMEM(s, BF) for s in shapes + shapes[2:]] + [pltpu.SemaphoreType.DMA((3,))],
        out_shape=[
            jax.ShapeDtypeStruct((rows, GWIDTH), F32),
            jax.ShapeDtypeStruct((GROUPS, rows // GROUPS, GWIDTH), BF),
            jax.ShapeDtypeStruct((rows // half, 8, GHEADS * half), F32),
        ]
        + [jax.ShapeDtypeStruct(s, BF) for s in shapes],
        compiler_params=pltpu.CompilerParams(vmem_limit_bytes=40 << 20),
        cost_estimate=pl.CostEstimate(flops=10**10, bytes_accessed=10**7, transcendentals=10**6),
        name="attend",
    )(pos, q, *kvs, strips)


def attend_back(pos, q, keys, strips, do, o, stat, members, blocks):
    rows = q.shape[0]
    half = strips.shape[1] // GHEADS
    shapes = key_shapes(blocks, half)
    kv = jax.ShapeDtypeStruct((GROUPS, 2 * half, 2 * GWIDTH), BF)
    return pl.pallas_call(
        functools.partial(backward_kernel, half, blocks, members),
        in_specs=[SMEM_SPEC] + [VMEM_SPEC] * 5 + [HBM_SPEC] * 3,
        out_specs=[VMEM_SPEC] * (2 + members),
        scratch_shapes=[pltpu.VMEM(s, BF) for s in shapes]
        + [pltpu.VMEM(s, F32) for s in shapes[:2]]
        + [pltpu.VMEM(strips.shape, F32), pltpu.SemaphoreType.DMA((3,))],
        out_shape=[jax.ShapeDtypeStruct((rows, GWIDTH), BF)]
        + [kv] * members
        + [jax.ShapeDtypeStruct((GHEADS, strips.shape[0]), F32)],
        compiler_params=pltpu.CompilerParams(vmem_limit_bytes=48 << 20),
        cost_estimate=pl.CostEstimate(flops=15 * 10**9, bytes_accessed=10**7, transcendentals=10**6),
        name="attend_back",
    )(pos, q, strips, do, o, stat, *keys)


FBLOCK = 768


def three_parts(x):
    high = x.astype(BF).astype(F32)
    mid = (x - high).astype(BF).astype(F32)
    low = x - high - mid
    lane = lax.broadcasted_iota(jnp.int32, (x.shape[0], 128), 1)
    return jnp.where(lane == 0, high, jnp.where(lane == 1, mid, jnp.where(lane == 2, low, 0.0))).astype(BF)


def expert_kernel(
    cuts, info, came_ref, dy_ref, up_ref, down_ref, out_ref, back_ref, act_ref, lhs_ref,
    grad, out_acc, back_acc,
):
    step = pl.program_id(0)
    width = dy_ref.shape[1]

    @pl.when(step == 0)
    def _():
        gate = jnp.sum(came_ref[:, width:].astype(F32), axis=1, keepdims=True)
        grad[...] = (gate * dy_ref[...].astype(F32)).astype(BF)
        out_acc[...] = jnp.zeros_like(out_acc)
        back_acc[...] = jnp.zeros_like(back_acc)
        outer, inner = cuts
        unit = width // (outer * inner)
        for n, value in enumerate((came_ref[:, :width], grad[...])):
            turned = value.astype(F32).T.astype(BF)
            if outer == 1:
                lhs_ref[n] = turned
                continue
            for b in range(inner):
                slot = jnp.bitwise_xor(info[1], b)
                first = (slot & 1) * (inner // 2) + slot // 2
                for a in range(outer):
                    dest = lax.rem(a + outer - info[0], outer)
                    row = pl.multiple_of((first * outer + dest) * unit, 16)
                    lhs_ref[n, pl.ds(row, unit), :] = turned[(a * inner + b) * unit : (a * inner + b + 1) * unit]

    up, down = up_ref[0], down_ref[0]
    upper = dot(came_ref[:, :width], up)
    active_grad = dot(grad[...], down)
    cdf = 0.5 + 0.5 * lax.erf(upper * 0.7071067811865476)
    active = (upper * cdf).astype(BF)
    upper_grad = (active_grad * (cdf + upper * (0.3989422804014327 * jnp.exp(-0.5 * upper * upper)))).astype(BF)
    act_ref[0] = upper_grad
    act_ref[1] = active
    back_acc[...] += dot(upper_grad, up, ((1,), (1,)))
    out_acc[...] += dot(active, down, ((1,), (1,)))

    @pl.when(step == pl.num_programs(0) - 1)
    def _():
        out = out_acc[...].astype(BF)
        out_ref[...] = out
        back_ref[:, :width] = back_acc[...].astype(BF)
        gate_grad = jnp.sum(dy_ref[...].astype(F32) * out.astype(F32), axis=1, keepdims=True)
        back_ref[:, width:] = three_parts(gate_grad)


def expert(info, came, dy, up, down, cuts):
    rows, width = dy.shape
    ffn = up.shape[2]
    whole = lambda *shape: pl.BlockSpec(shape, lambda j, info: (0,) * len(shape))
    weight = pl.BlockSpec((1, width, FBLOCK), lambda j, info: (info[0], 0, j))
    return pl.pallas_call(
        functools.partial(expert_kernel, cuts),
        grid_spec=pltpu.PrefetchScalarGridSpec(
            num_scalar_prefetch=1,
            grid=(ffn // FBLOCK,),
            in_specs=[whole(*came.shape), whole(rows, width), weight, weight],
            out_specs=[
                whole(rows, width),
                whole(*came.shape),
                pl.BlockSpec((2, rows, FBLOCK), lambda j, info: (0, 0, j)),
                whole(2, width, rows),
            ],
            scratch_shapes=[
                pltpu.VMEM((rows, width), BF),
                pltpu.VMEM((rows, width), F32),
                pltpu.VMEM((rows, width), F32),
            ],
        ),
        out_shape=[
            jax.ShapeDtypeStruct((rows, width), BF),
            jax.ShapeDtypeStruct(came.shape, BF),
            jax.ShapeDtypeStruct((2, rows, ffn), BF),
            jax.ShapeDtypeStruct((2, width, rows), BF),
        ],
        compiler_params=pltpu.CompilerParams(vmem_limit_bytes=48 << 20),
        cost_estimate=pl.CostEstimate(flops=11 * 10**9, bytes_accessed=2 * 10**7, transcendentals=10**6),
        name="expert",
    )(info, came, dy, up, down)


def weight_kernel(lhs_ref, act_ref, keep_ref, pass_ref, send_ref):
    rows = keep_ref.shape[0]
    keep_ref[...] = dot(lhs_ref[0, :rows, :], act_ref[0]).astype(BF)
    pass_ref[...] = dot(lhs_ref[0, rows : 2 * rows, :], act_ref[0]).astype(BF)
    send_ref[...] = dot(lhs_ref[0, 2 * rows :, :], act_ref[0]).astype(BF)


def weight_terms(lhs, act, which):
    _, width, rows = lhs.shape
    ffn = act.shape[2]
    cuts = (width // 4, width // 4, width // 2)
    return pl.pallas_call(
        weight_kernel,
        grid=(ffn // FBLOCK,),
        in_specs=[
            pl.BlockSpec((1, width, rows), lambda j: (which, 0, 0)),
            pl.BlockSpec((1, rows, FBLOCK), lambda j: (which, 0, j)),
        ],
        out_specs=[pl.BlockSpec((c, FBLOCK), lambda j: (0, j)) for c in cuts],
        out_shape=[jax.ShapeDtypeStruct((c, ffn), BF) for c in cuts],
        compiler_params=pltpu.CompilerParams(vmem_limit_bytes=32 << 20),
        cost_estimate=pl.CostEstimate(flops=35 * 10**8, bytes_accessed=10**7, transcendentals=0),
        name="weight_terms",
    )(lhs, act)


def together(*values):
    return lax.optimization_barrier(values)


def turn(shift):
    return [(i, (i + shift) % GROUPS) for i in range(GROUPS)]


def gather_groups(x):
    came = {k: lax.ppermute(x, "h", turn(k)) for k in (2, 1, 3)}
    return jnp.stack([x] + [came[k] for k in range(1, GROUPS)])


def gather_members(x):
    size = lax.axis_size(MEMBERS)
    held = {0: x}
    for bit in bits_of(size):
        for k in sorted(held):
            held[k | bit] = lax.ppermute(held[k], MEMBERS, xor_perm(bit, size))
    return [held[k] for k in range(size)]


def part_of(x, mine):
    low, high = jnp.split(x, 2, axis=-1)
    return jnp.where(mine == 0, low, high), jnp.where(mine == 0, high, low)


def swap(x, axis, bit):
    return lax.ppermute(x, axis, xor_perm(bit, lax.axis_size(axis))).astype(F32)


def two_parts(x):
    high = lax.reduce_precision(x, 8, 7)
    return jnp.concatenate([high, x - high]).astype(BF)


def from_fsdp(part):
    if lax.axis_size("fsdp") != 2:
        return lax.all_gather(part, "fsdp", axis=0)
    came = lax.ppermute(part, "fsdp", xor_perm(1, 2))
    return jnp.where(lax.axis_index("fsdp") == 0, jnp.stack([part, came]), jnp.stack([came, part]))


def swap_groups(x):
    return lax.all_to_all(x, "h", 0, 0, tiled=True)


def per_device(
    tokens, segments, routes, bucket_table, attn_gain, qkv_weight, out_weight, bias_table,
    moe_gain, router_weight, up_weight, down_weight, cotangent,
):
    tok, width = tokens.shape[1], tokens.shape[2]
    half = tok // 2
    h, m, f = lax.axis_index("h"), lax.axis_index(MEMBERS), lax.axis_index("fsdp")
    core = lax.axis_index("core")
    members, n_fsdp = lax.axis_size(MEMBERS), lax.axis_size("fsdp")
    shards = GROUPS * members
    blocks = 2 * shards
    length = shards * tok
    here = EXPERTS // n_fsdp
    spread = here > 1
    ffn = up_weight.shape[2]
    rows_f = width // n_fsdp
    rows_c = width // shards
    pos = jnp.stack([m, h]).astype(jnp.int32)

    extra = jnp.pad(segments.astype(BF), ((0, 7), (0, width - tok)))
    mixed = gather_groups(jnp.concatenate([tokens[0], extra]))

    bias_flat = bias_table.reshape(1, -1)
    bias_rows = -(-bias_flat.shape[1] // rows_f)
    bias_flat = jnp.pad(bias_flat, ((0, 0), (0, bias_rows * rows_f - bias_flat.shape[1])))
    small = jnp.concatenate(
        [attn_gain[None], moe_gain[None], router_weight.T, bias_flat.reshape(bias_rows, rows_f)]
        + [jnp.zeros((16 - 10 - bias_rows, rows_f), BF)]
    )
    small = from_fsdp(small)
    attn_scale = small[:, 0].reshape(width).astype(F32)
    moe_scale = small[:, 1].reshape(width).astype(F32)
    router_t = jnp.transpose(small[:, 2:10], (1, 0, 2)).reshape(EXPERTS, width)
    bias_full = small[:, 10 : 10 + bias_rows].reshape(n_fsdp, -1)[:, : bias_table.size]
    bias_full = bias_full.reshape(BUCKETS, HEADS)
    cut = [
        lax.dynamic_slice_in_dim(qkv_weight, n * width + h * GWIDTH, GWIDTH, 1) for n in range(3)
    ]
    qkv_heads = from_fsdp(jnp.concatenate(cut, axis=1)).reshape(width, 3 * GWIDTH)
    out_full = from_fsdp(together(out_weight, qkv_heads)[0]).reshape(width, width)

    wide = strip_width(blocks, half)
    top = half * (blocks - 1)
    line = jnp.concatenate(
        [
            bucket_table[: top + 1][::-1],
            jnp.full((wide - length,), -1, jnp.int32),
            bucket_table[top + 1 :][::-1],
        ]
    )
    hot = (line[None] == jnp.arange(BUCKETS, dtype=jnp.int32)[:, None]).astype(BF)
    bias_mine = lax.dynamic_slice_in_dim(bias_full, h * GHEADS, GHEADS, 1)
    strips = make_strips(dot(bias_mine, hot, ((0,), (0,))) * LOG2E, half)

    hot_routes = (routes.reshape(-1)[:, None] == jnp.arange(EXPERTS)[None]).astype(F32)
    earlier = jnp.arange(tok * TOP)
    earlier = (earlier[None, :] < earlier[:, None]).astype(BF)
    before = dot(earlier, hot_routes.astype(BF))
    slot = jnp.sum(before * hot_routes, axis=1).astype(jnp.int32).reshape(tok, TOP)
    target = (routes % here) * n_fsdp + routes // here
    place = target * CAP + slot
    slots = jnp.arange(EXPERTS * CAP, dtype=jnp.int32)
    pick = [slots[:, None] == place[None, :, k] for k in range(TOP)]
    pick_any = (pick[0] | pick[1]).astype(BF)
    exchange = ("h", "fsdp") if spread else ("fsdp",)

    def deal(rows):
        send = rows.reshape(EXPERTS, CAP, rows.shape[-1])
        return lax.all_to_all(send, exchange, 0, 0, tiled=True).reshape(rows.shape)

    mixed, strips = together(mixed, strips)
    ain = normalize(mixed[:, :tok].astype(F32), attn_scale).astype(BF).reshape(GROUPS * tok, width)
    proj = dot(ain, qkv_heads).astype(BF)
    q = proj[:, :GWIDTH]
    kv = proj[:, GWIDTH:].reshape(GROUPS, tok, 2 * GWIDTH)
    kvs = gather_members(jnp.concatenate([kv, mixed[:, tok:, : 2 * GWIDTH]], axis=1))
    dy_send = together(dot(pick_any, cotangent[0]).astype(BF), mixed)[0]
    q, dy_slots = together(q, deal(dy_send))
    o_pre, o_low, stat, *keys = attend(pos, q, kvs, strips, blocks)
    context = swap_groups(o_low)
    context = jnp.transpose(context, (1, 0, 2)).reshape(tok, width)
    x = tokens[0].astype(F32)
    residual = x + dot(context, out_full)

    moe_in = normalize(residual, moe_scale).astype(BF)
    logits = dot(moe_in, router_t, ((1,), (1,)))
    route_hot = hot_routes.reshape(tok, TOP, EXPERTS)
    chosen = jnp.sum(logits[:, None, :] * route_hot, axis=-1)
    gates = jax.nn.softmax(chosen, axis=-1)
    gate_slots = sum(
        jnp.sum(jnp.where(pick[k], gates[None, :, k], 0.0), axis=1, keepdims=True) for k in range(TOP)
    )
    high = lax.reduce_precision(gate_slots, 8, 7)
    mid = lax.reduce_precision(gate_slots - high, 8, 7)
    low = gate_slots - high - mid
    lane = jnp.arange(128)[None]
    extra = jnp.where(lane == 0, high, jnp.where(lane == 1, mid, jnp.where(lane == 2, low, 0.0)))
    rows_out = jnp.concatenate([dot(pick_any, moe_in), extra], axis=1).astype(BF)

    came = deal(rows_out)
    cuts = (GROUPS, members) if spread else (1, 1)
    info = jnp.stack([h if spread else jnp.zeros_like(h), m]).astype(jnp.int32)
    expert_out, back, act, lhs = expert(info, came, dy_slots, up_weight, down_weight, cuts)
    back = deal(back)

    terms = [weight_terms(lhs, act, n) for n in range(2)]
    staged = spread and members == 4
    if staged:
        terms = [(keep, passed, swap(send, "core", 1)) for keep, passed, send in terms]

    dy = cotangent[0].astype(F32)
    gate_grad = jnp.stack(
        [jnp.sum(dot(pick[k].astype(BF), back[:, width:], ((0,), (0,))), axis=1) for k in range(TOP)], axis=1
    )
    chosen_grad = gates * (gate_grad - jnp.sum(gates * gate_grad, axis=1, keepdims=True))
    logit_grad = jnp.sum(chosen_grad[:, :, None] * route_hot, axis=1)
    moe_in_grad = exact_dot(logit_grad, router_t.astype(F32), ((1,), (0,)))
    moe_in_grad = moe_in_grad + dot(pick_any, back[:, :width], ((0,), (0,)))
    norm_grad, moe_gain_grad = jax.vjp(normalize, residual, moe_scale)[1](moe_in_grad)
    resid_grad = dy + norm_grad
    attn_grad = resid_grad.astype(BF)
    router_grad = exact_dot(logit_grad, moe_in.astype(F32), ((0,), (0,)))

    do = dot(attn_grad, out_full, ((1,), (1,))).astype(BF)
    do = jnp.transpose(do.reshape(tok, GROUPS, GWIDTH), (1, 0, 2))
    do, terms = together(do, terms)
    do = swap_groups(do)
    out_term = dot(attn_grad, context, ((0,), (0,))).reshape(shards // 2, 2, rows_c, width)
    out_send = lax.dynamic_index_in_dim(out_term, 1 - core, 1, False).astype(BF)
    do, out_came = together(do, swap(out_send, "core", 1))
    out_term = lax.dynamic_index_in_dim(out_term, core, 1, False) + out_came
    for bit in bits_of(n_fsdp):
        out_term, out_send = part_of(out_term, (f // bit) % 2)
        out_term = out_term + swap(out_send.astype(BF), "fsdp", bit)
    dq, *dkvs, dline = attend_back(pos, q, keys, strips, do, o_pre, stat, members, blocks)
    dkvs[0], out_term = together(dkvs[0], out_term)
    bias_mine = exact_dot(hot.astype(F32), dline, ((1,), (1,)))
    held = dict(enumerate(dkvs))
    for k in range(1, members, 2):
        held[k - 1] = held[k - 1].astype(F32) + swap(held.pop(k), "core", 1)
    if staged:
        first = [(passed.astype(F32) + came[came.shape[0] // 2 :]).astype(BF) for _, passed, came in terms]
        first[0] = swap(first[0], "r", 1)
        held[2], first[0] = together(held[2], first[0])
    bit = 2
    while bit < members:
        for k in [k for k in sorted(held) if k & bit]:
            held[k - bit] = held[k - bit] + swap(held.pop(k).astype(BF), "r", bit // 2)
        bit *= 2
    dkv = held[0].astype(BF).reshape(GROUPS * tok, 2 * GWIDTH)
    if staged:
        first[1], dkv = together(first[1], dkv)
        first[1] = swap(first[1], "r", 1)
    dproj = jnp.concatenate([dq, dkv], axis=1)

    def to_shards(term, came):
        keep, _, from_core = term
        total = (keep.astype(F32) + from_core[: keep.shape[0]] + came).astype(BF)
        total = total.reshape(GROUPS, rows_c, ffn)
        return [total[0]] + [lax.ppermute(total[k], "h", turn(k)) for k in range(1, GROUPS)]

    def in_order(came):
        came = jnp.stack(came)
        return jnp.concatenate(
            [lax.dynamic_index_in_dim(came, group_of(s, h), 0) for s in range(GROUPS)]
        ).astype(F32)

    result = deal(together(expert_out, do)[0])
    back_ain = dot(dproj, qkv_heads, ((1,), (1,)))
    back_low = back_ain.astype(BF).reshape(GROUPS, tok, width)
    if staged:
        up_came = to_shards(terms[0], first[0])
        back_low, up_came, result = together(back_low, up_came, result)

    mid = lax.ppermute(back_low[2], "h", turn(-1))
    side = lax.ppermute(back_low[3], "h", turn(1)).astype(F32)
    mid = (back_low[1].astype(F32) + mid.astype(F32)).astype(BF)
    mid = lax.ppermute(mid, "h", turn(-1)).astype(F32)
    attn_in_grad = back_ain[:tok] + side + mid
    token_grad = jax.vjp(lambda v: normalize(v, attn_scale), x)[1](attn_in_grad)[0]
    tokens_grad = (resid_grad + token_grad).astype(BF)

    picked = [dot(pick[k].astype(BF), result, ((0,), (0,))) for k in range(TOP)]
    layer_out = residual + gates[:, :1] * picked[0] + gates[:, 1:] * picked[1]

    attn_gain_grad = jnp.sum(back_ain * ain.astype(F32), axis=0) / attn_scale
    bias_own = lax.dynamic_update_slice_in_dim(jnp.zeros((BUCKETS, HEADS), F32), bias_mine, h * GHEADS, 1)
    bias_own = jnp.pad(bias_own.reshape(n_fsdp, -1), ((0, 0), (0, rows_f - bias_own.size // n_fsdp)))
    pack = jnp.concatenate(
        [router_grad, attn_gain_grad[None], moe_gain_grad[None], bias_own.reshape(1, width)]
        + [jnp.zeros((5, width), F32)]
    )
    small_rows = pack.shape[0]

    def swap_both(send, pack, axis, bit):
        sent = jnp.concatenate([send.reshape(-1, send.shape[-1]).astype(BF), two_parts(pack)])
        came = swap(sent, axis, bit)
        return came[: -2 * small_rows].reshape(send.shape), came[-2 * small_rows : -small_rows] + came[-small_rows:]

    unit = GWIDTH // members
    term = dot(dproj, ain, ((0,), (0,))).reshape(3, members // 2, 2, unit, width)
    came, pack_came = swap_both(lax.dynamic_index_in_dim(term, 1 - core, 2, False), pack, "core", 1)
    term = (lax.dynamic_index_in_dim(term, core, 2, False) + came).reshape(-1, width)
    pack = pack + pack_came
    for bit in bits_of(n_fsdp):
        term, send = part_of(term, (f // bit) % 2)
        pack, pack_send = part_of(pack, (f // bit) % 2)
        came, pack_came = swap_both(send, pack_send, "fsdp", bit)
        term, pack = term + came, pack + pack_came
    term = jnp.concatenate(
        [term.reshape(3, members // 2, unit, rows_f).swapaxes(0, 1).reshape(members // 2, -1, rows_f)]
        + [out_term.reshape(GROUPS, members // 2, rows_c, rows_f).swapaxes(0, 1).reshape(members // 2, -1, rows_f)],
        axis=1,
    )
    for bit in bits_of(members // 2):
        mine = (lax.axis_index("r") // bit) % 2
        term = term.reshape((2, -1) + term.shape[1:])
        came, pack_came = swap_both(lax.dynamic_index_in_dim(term, 1 - mine, 0, False), pack, "r", bit)
        term = lax.dynamic_index_in_dim(term, mine, 0, False) + came
        pack = pack + pack_came
    term = term[0]
    out_term = term[3 * unit :].reshape(GROUPS, rows_c, rows_f)
    term = term[: 3 * unit].astype(BF).reshape(3, unit, rows_f)
    out_sum, pack_sum = lax.dynamic_index_in_dim(out_term, h, 0, False), pack
    for k in (2, 1, 3):
        piece = lax.dynamic_index_in_dim(out_term, lax.rem(h + k, GROUPS), 0, False)
        came = lax.ppermute(jnp.concatenate([piece.astype(BF), two_parts(pack)]), "h", turn(k)).astype(F32)
        out_sum = out_sum + came[:rows_c]
        pack_sum = pack_sum + came[rows_c : rows_c + small_rows] + came[rows_c + small_rows :]
    at = h * members + m
    parts = []
    for r in range(3):
        pairs = [((3 * d + r) % shards, d) for d in range(shards)]
        entry = [0] * shards
        for s, d in pairs:
            entry[s] = (3 * d + r) // shards
        which = jnp.sum(jnp.where(jnp.arange(shards) == at, jnp.asarray(entry), 0))
        parts.append(lax.ppermute(lax.dynamic_index_in_dim(term, which, 0, False), CTX, pairs))
    qkv_grad = jnp.concatenate(parts).astype(F32).T

    if staged:
        grads = [in_order(up_came), in_order(to_shards(terms[1], first[1]))]
    else:
        grads = [
            lax.psum_scatter(jnp.concatenate(term), CTX, scatter_dimension=0, tiled=True)[None].astype(F32)
            for term in terms
        ]
    return (
        layer_out.astype(BF)[None],
        tokens_grad[None],
        pack_sum[8],
        qkv_grad,
        out_sum.T,
        pack_sum[10, : bias_table.size].reshape(BUCKETS // n_fsdp, HEADS),
        pack_sum[9],
        pack_sum[:8].T,
        grads[0],
        grads[1],
    )


def solution(mesh):
    n_ctx, n_fsdp = mesh.shape["ctx"], mesh.shape["fsdp"]
    cut = mesh.devices.reshape(GROUPS, n_ctx // (2 * GROUPS), 2, n_fsdp)
    row = P("fsdp", CTX, None)
    return jax.shard_map(
        per_device,
        mesh=Mesh(cut, CTX + ("fsdp",)),
        in_specs=(
            row,
            P("fsdp", CTX),
            P(CTX + ("fsdp",), None),
            P(),
            P("fsdp"),
            P("fsdp", None),
            P("fsdp", None),
            P("fsdp", None),
            P("fsdp"),
            P("fsdp", None),
            P("fsdp", None, None),
            P("fsdp", None, None),
            row,
        ),
        out_specs=(
            row,
            row,
            P("fsdp"),
            P("fsdp", CTX),
            P("fsdp", CTX),
            P("fsdp", None),
            P("fsdp"),
            P("fsdp", None),
            row,
            row,
        ),
        check_vma=False,
    )
```

```python
import functools

import jax
import jax.numpy as jnp
from jax import lax
from jax.experimental import pallas as pl
from jax.experimental.pallas import tpu as pltpu
from jax.sharding import Mesh, PartitionSpec as P

HEADS = 12
HEAD_DIM = 64
EXPERTS = 8
TOP = 2
BUCKETS = 32
DOCS = 8
CAP = 40
GROUPS = 4
GHEADS = HEADS // GROUPS
GWIDTH = GHEADS * HEAD_DIM
CHUNK = 256

LOG2E = 1.4426950408889634
EPS = 1e-06
LOWEST = -1e30
FULL = lax.Precision.HIGHEST
BF = jnp.bfloat16
F32 = jnp.float32
MEMBERS = ("r", "core")
CTX = ("h", "r", "core")


def normalize(values, weight):
    inv_rms = lax.rsqrt(jnp.mean(values * values, axis=-1, keepdims=True) + EPS)
    return values * inv_rms * weight


def dot(a, b, dims=((1,), (0,))):
    return lax.dot_general(a, b, (dims, ((), ())), preferred_element_type=F32)


def exact_dot(a, b, dims):
    return lax.dot_general(a, b, (dims, ((), ())), precision=FULL)


def xor_perm(mask, size):
    return [(i, i ^ mask) for i in range(size)]


def bits_of(size):
    bit = size // 2
    while bit:
        yield bit
        bit //= 2


def strip_width(blocks, half):
    need = half * (blocks - 1) + CHUNK + half
    return -(-need // 128) * 128


def strips_kernel(g_ref, out_ref):
    half = out_ref.shape[1] // GHEADS
    rolled = [
        pltpu.roll(
            jnp.broadcast_to(g_ref[n : n + 1, :], (half, g_ref.shape[1])), 0, 1, stride=1, stride_axis=0
        )
        for n in range(GHEADS)
    ]
    out_ref[...] = jnp.concatenate(rolled).T


def make_strips(lines, half):
    return pl.pallas_call(
        strips_kernel,
        out_specs=pl.BlockSpec((lines.shape[1], GHEADS * half), lambda: (0, 0)),
        out_shape=pltpu.HBM((lines.shape[1], GHEADS * half), F32),
        cost_estimate=pl.CostEstimate(flops=10**5, bytes_accessed=10**4, transcendentals=0),
        name="strips",
    )(lines)


def own_blocks(size, half):
    a = lax.broadcasted_iota(jnp.int32, (size, size), 0) // half
    b = lax.broadcasted_iota(jnp.int32, (size, size), 1) // half
    return a == b


def spread_rows(x, same):
    return jnp.where(same, jnp.concatenate([x] * GHEADS), 0.0)


def fold_rows(x, same, half):
    y = jnp.where(same, x, 0.0).T
    return sum(y[n * half : (n + 1) * half] for n in range(GHEADS))


def own_columns(x, half):
    return jnp.concatenate(
        [x[n * HEAD_DIM : (n + 1) * HEAD_DIM, n * half : (n + 1) * half] for n in range(GHEADS)]
    )


def spread_columns(x, same):
    return jnp.where(same, jnp.concatenate([x] * GHEADS, axis=1), 0.0)


def group_of(slot, h):
    return lax.rem(h + GROUPS - slot, GROUPS)


def place_of(slot, early, me, h, members, blocks):
    owner = group_of(slot, h) * members + me
    return owner if early else blocks - 1 - owner


def bounds(block, chunk, half, blocks, start):
    top = (blocks - 1 - (block - (CHUNK // half) * chunk)) * half
    lane = lax.broadcasted_iota(jnp.int32, (1, GHEADS * half), 1)
    last = block * half + lax.rem(lane, half) - chunk * CHUNK
    return pl.multiple_of(top, half), last, start - chunk * CHUNK


def forward_kernel(half, blocks, members, pos, q_ref, *refs):
    kvs, refs = refs[:members], refs[members:]
    strip_in, o_ref, *lows, stat_ref, k_out, v_out, kt_out, k_ref, v_ref, kt_ref, vt, strip_ref, sems, strip_sem = refs
    loads = start_copies([(strip_in, strip_ref)], strip_sem)
    size = GHEADS * half
    me, h = pos[0], pos[1]
    tok = 2 * half
    same = own_blocks(size, half)
    key = lax.broadcasted_iota(jnp.int32, (CHUNK, size), 0)
    per = CHUNK // half

    @pl.loop(0, GROUPS)
    def _(slot):
        for j in range(members):
            for early in (True, False):
                block = place_of(slot, early, jnp.bitwise_xor(me, j), h, members, blocks)
                at = pl.ds(pl.multiple_of(lax.rem(block, per) * half, half), half)
                rows = kvs[j][slot, 0 if early else half : half if early else tok, :]
                k_ref[block // per, at, :] = rows[:, :GWIDTH]
                v_ref[block // per, at, :] = rows[:, GWIDTH:]

    @pl.loop(0, blocks // per)
    def _(chunk):
        kt_ref[chunk] = k_ref[chunk].astype(F32).T.astype(BF)
        vt[chunk] = v_ref[chunk].astype(F32).T.astype(BF)

    copies = start_copies([(k_ref, k_out), (v_ref, v_out), (kt_ref, kt_out)], sems)
    docs = jnp.concatenate([kv[a, tok : tok + 1, :tok].astype(F32) for kv in kvs for a in range(GROUPS)])
    begins = [jnp.sum(jnp.where(docs < s, 1.0, 0.0)) for s in range(1, DOCS)]
    for load in loads:
        load.wait()

    @pl.loop(0, q_ref.shape[0] // half)
    def _(i):
        slot, late = i // 2, lax.rem(i, 2)
        owner = group_of(slot, h) * members + me
        block = jnp.where(late == 0, owner, blocks - 1 - owner)
        at = pl.ds(pl.multiple_of(i * half, half), half)
        qt = spread_rows(q_ref[at, :GWIDTH].astype(F32), same).T.astype(BF)
        doc = kvs[0][slot, tok : tok + 1, :tok].astype(F32)
        doc = jnp.where(late == 0, doc[:, :half], doc[:, half:])
        begin = jnp.zeros((1, half), F32)
        for s in range(1, DOCS):
            begin = jnp.where(doc == s, begins[s - 1], begin)
        first = jnp.min(begin).astype(jnp.int32) // CHUNK
        begin = jnp.concatenate([begin] * GHEADS, axis=1)
        start = begin.astype(jnp.int32)

        def visit(chunk, carry):
            peak, total, acc = carry
            top, last, begin = bounds(block, chunk, half, blocks, start)
            t = dot(k_ref[chunk], qt) * (HEAD_DIM**-0.5 * LOG2E) + strip_ref[pl.ds(top, CHUNK), :]
            t = jnp.where((key <= last) & (key >= begin), t, LOWEST)
            new = jnp.maximum(peak, jnp.ceil(jnp.max(t, axis=0, keepdims=True)))
            e = jnp.exp2(t - new)
            fade = jnp.exp2(peak - new)
            total = total * fade + jnp.sum(e, axis=0, keepdims=True)
            acc = acc * fade + dot(vt[chunk], e.astype(BF))
            return new, total, acc

        init = (
            jnp.full((1, size), LOWEST, F32),
            jnp.zeros((1, size), F32),
            jnp.zeros((GWIDTH, size), F32),
        )
        peak, total, acc = lax.fori_loop(first, block // per + 1, visit, init)
        out = own_columns(acc / total, half)
        o_ref[i] = out
        low = out.astype(BF)
        for n in range(GROUPS):
            for part in range(2):

                @pl.when(i == 2 * n + part)
                def _():
                    lows[n][:, part * half : (part + 1) * half] = low

        stat_ref[i, 0:1, :] = peak
        stat_ref[i, 1:2, :] = total
        stat_ref[i, 2:3, :] = begin

    for copy in copies:
        copy.wait()


def backward_kernel(half, blocks, members, pos, *refs):
    dos, refs = refs[:GROUPS], refs[GROUPS:]
    inputs, (dq_ref, *refs) = refs[:7], refs[7:]
    dkvs, refs = refs[:members], refs[members:]
    dline_ref, *held, dk, dv, dstrip, do_ref, sems = refs
    q_ref, strip_ref, o_ref, stat_ref, k_ref, v_ref, kt_ref = held
    size = GHEADS * half
    me, h = pos[0], pos[1]
    width = dstrip.shape[0]
    per = CHUNK // half
    copies = start_copies(list(zip(inputs, held)), sems)
    same = own_blocks(size, half)
    key = lax.broadcasted_iota(jnp.int32, (CHUNK, size), 0)

    @pl.loop(0, blocks // per)
    def _(chunk):
        dk[chunk] = jnp.zeros(dk.shape[1:], F32)
        dv[chunk] = jnp.zeros(dv.shape[1:], F32)

    @pl.loop(0, width // 128)
    def _(j):
        dstrip[pl.ds(pl.multiple_of(j * 128, 128), 128), :] = jnp.zeros((128, size), F32)

    for n in range(GROUPS):
        do_ref[n] = dos[n][...].astype(F32)
    for copy in copies:
        copy.wait()

    @pl.loop(0, q_ref.shape[0] // half)
    def _(i):
        slot, late = i // 2, lax.rem(i, 2)
        owner = group_of(slot, h) * members + me
        block = jnp.where(late == 0, owner, blocks - 1 - owner)
        at = pl.ds(pl.multiple_of(i * half, half), half)
        peak, total, start = (stat_ref[i, n : n + 1, :] for n in range(3))
        first = jnp.min(start).astype(jnp.int32) // CHUNK
        start = start.astype(jnp.int32)
        qs = spread_rows(q_ref[at, :GWIDTH].astype(F32), same)
        qt, qs = qs.T.astype(BF), qs.astype(BF)
        do = do_ref[slot]
        do = jnp.where(late == 0, do[:, :half], do[:, half:])
        corr = jnp.sum(spread_columns(do * o_ref[i], same), axis=0, keepdims=True) / total
        gt = spread_columns(do, same) / total
        gs = gt.T.astype(BF)
        gt = gt.astype(BF)

        def visit(chunk, dq):
            top, last, begin = bounds(block, chunk, half, blocks, start)
            t = dot(k_ref[chunk], qt) * (HEAD_DIM**-0.5 * LOG2E) + strip_ref[pl.ds(top, CHUNK), :]
            t = jnp.where((key <= last) & (key >= begin), t - peak, LOWEST)
            e = jnp.exp2(t)
            s = e * (dot(v_ref[chunk], gt) - corr)
            low = s.astype(BF)
            dk[chunk] += dot(low, qs)
            dv[chunk] += dot(e.astype(BF), gs)
            dstrip[pl.ds(top, CHUNK), :] += s
            return dq + dot(kt_ref[chunk], low)

        dq = lax.fori_loop(first, block // per + 1, visit, jnp.zeros((GWIDTH, size), F32))
        dq_ref[at, :] = (fold_rows(dq, same, half) * HEAD_DIM**-0.5).astype(BF)

    @pl.loop(0, GROUPS)
    def _(slot):
        for j in range(members):
            for early in (True, False):
                block = place_of(slot, early, jnp.bitwise_xor(me, j), h, members, blocks)
                at = pl.ds(pl.multiple_of(lax.rem(block, per) * half, half), half)
                part = jnp.concatenate(
                    [dk[block // per, at, :] * HEAD_DIM**-0.5, dv[block // per, at, :]], axis=1
                )
                dkvs[j][slot, 0 if early else half : half if early else 2 * half, :] = part.astype(BF)

    lines = dstrip[...].T
    for n in range(GHEADS):
        x = lines[n * half : (n + 1) * half]
        rows = half
        while rows > 8:
            rows //= 2
            x = x[:rows] + pltpu.roll(x[rows:], width - rows, 1)
        sub = lax.broadcasted_iota(jnp.int32, x.shape, 0)
        for bit in (4, 2, 1):
            x = jnp.where((sub & bit) != 0, pltpu.roll(x, width - bit, 1), x)
        dline_ref[n : n + 1, :] = jnp.sum(x, axis=0, keepdims=True)


VMEM_SPEC = pl.BlockSpec(memory_space=pltpu.VMEM)
SMEM_SPEC = pl.BlockSpec(memory_space=pltpu.SMEM)
HBM_SPEC = pl.BlockSpec(memory_space=pltpu.HBM)


def in_hbm(*values):
    return [pltpu.with_memory_space_constraint(v, pltpu.HBM) for v in values]


def all_of(x):
    return pl.BlockSpec(x.shape, lambda: (0,) * len(x.shape))


def start_copies(pairs, sems):
    copies = [pltpu.make_async_copy(src, dst, sems.at[i]) for i, (src, dst) in enumerate(pairs)]
    for copy in copies:
        copy.start()
    return copies


def key_shapes(blocks, half):
    chunks = blocks * half // CHUNK
    return ((chunks, CHUNK, GWIDTH), (chunks, CHUNK, GWIDTH), (chunks, GWIDTH, CHUNK))


def attend(pos, q, kvs, strips, blocks):
    rows = q.shape[0]
    half = strips.shape[1] // GHEADS
    shapes = key_shapes(blocks, half)
    o_shape, stat_shape = (rows // half, GWIDTH, half), (rows // half, 8, GHEADS * half)
    return pl.pallas_call(
        functools.partial(forward_kernel, half, blocks, len(kvs)),
        in_specs=[SMEM_SPEC] + [VMEM_SPEC] * (1 + len(kvs)) + [HBM_SPEC],
        out_specs=[all_of(jax.ShapeDtypeStruct(o_shape, F32))]
        + [VMEM_SPEC] * GROUPS
        + [all_of(jax.ShapeDtypeStruct(stat_shape, F32))]
        + [HBM_SPEC] * 3,
        scratch_shapes=[pltpu.VMEM(s, BF) for s in shapes + shapes[2:]]
        + [pltpu.VMEM(strips.shape, F32), pltpu.SemaphoreType.DMA((3,)), pltpu.SemaphoreType.DMA((1,))],
        out_shape=[pltpu.HBM(o_shape, F32)]
        + [jax.ShapeDtypeStruct((GWIDTH, 2 * half), BF)] * GROUPS
        + [pltpu.HBM(stat_shape, F32)]
        + [pltpu.HBM(s, BF) for s in shapes],
        compiler_params=pltpu.CompilerParams(vmem_limit_bytes=32 << 20),
        cost_estimate=pl.CostEstimate(flops=10**5, bytes_accessed=10**4, transcendentals=0),
        name="attend",
    )(pos, q, *kvs, *in_hbm(strips))


def attend_back(pos, q, keys, strips, dos, o, stat, members, blocks):
    rows = q.shape[0]
    half = strips.shape[1] // GHEADS
    shapes = key_shapes(blocks, half)
    kv = jax.ShapeDtypeStruct((GROUPS, 2 * half, 2 * GWIDTH), BF)
    inputs = in_hbm(q, strips, o, stat, *keys)
    return pl.pallas_call(
        functools.partial(backward_kernel, half, blocks, members),
        in_specs=[SMEM_SPEC] + [VMEM_SPEC] * GROUPS + [HBM_SPEC] * len(inputs),
        out_specs=[VMEM_SPEC] * (1 + members) + [pl.BlockSpec((GHEADS, strips.shape[0]), lambda: (0, 0))],
        scratch_shapes=[pltpu.VMEM(x.shape, x.dtype) for x in inputs]
        + [pltpu.VMEM(s, F32) for s in shapes[:2]]
        + [
            pltpu.VMEM(strips.shape, F32),
            pltpu.VMEM((GROUPS, GWIDTH, 2 * half), F32),
            pltpu.SemaphoreType.DMA((len(inputs),)),
        ],
        out_shape=[jax.ShapeDtypeStruct((rows, GWIDTH), BF)]
        + [kv] * members
        + [pltpu.HBM((GHEADS, strips.shape[0]), F32)],
        compiler_params=pltpu.CompilerParams(vmem_limit_bytes=40 << 20),
        cost_estimate=pl.CostEstimate(flops=10**5, bytes_accessed=10**4, transcendentals=0),
        name="attend_back",
    )(pos, *dos, *inputs)


FBLOCK = 768
PIECES = 8


def three_parts(x):
    high = x.astype(BF).astype(F32)
    mid = (x - high).astype(BF).astype(F32)
    low = x - high - mid
    lane = lax.broadcasted_iota(jnp.int32, (x.shape[0], 128), 1)
    return jnp.where(lane == 0, high, jnp.where(lane == 1, mid, jnp.where(lane == 2, low, 0.0))).astype(BF)


def gather_rows(refs):
    return jnp.concatenate([r[...].astype(F32) for r in refs])


def router_kernel(
    pos, x_ref, out_ref, scale_ref, router_ref, routes_ref, place_ref, *refs
):
    lows, refs = refs[:GROUPS], refs[GROUPS:]
    pieces, (context_ref, resid_ref, moe_ref, gates_ref) = refs[:PIECES], refs[PIECES:]
    tok, width = x_ref.shape
    for k in range(GROUPS):
        row = pl.multiple_of(lax.rem(pos[1] + k, GROUPS) * GWIDTH, GWIDTH)
        context_ref[pl.ds(row, GWIDTH), :] = lows[k][...]
    context = context_ref[...].astype(F32).T.astype(BF)
    resid = x_ref[...].astype(F32) + dot(context, out_ref[...])
    resid_ref[...] = resid
    inv = lax.rsqrt(jnp.mean(resid * resid, axis=1, keepdims=True) + EPS)
    moe_in = (resid * inv * scale_ref[...]).astype(BF)
    moe_ref[...] = moe_in
    logits = dot(moe_in, router_ref[...], ((1,), (1,)))
    lane = lax.broadcasted_iota(jnp.int32, logits.shape, 1)
    chosen = [
        jnp.sum(jnp.where(routes_ref[:, k : k + 1] == lane, logits, 0.0), axis=1, keepdims=True)
        for k in range(TOP)
    ]
    most = jnp.maximum(chosen[0], chosen[1])
    powers = [jnp.exp(c - most) for c in chosen]
    gates = [p / (powers[0] + powers[1]) for p in powers]
    slot = lax.broadcasted_iota(jnp.int32, (EXPERTS * CAP, tok), 0)
    pick = [(place_ref[k : k + 1, :] == slot) for k in range(TOP)]
    rows = dot((pick[0] | pick[1]).astype(BF), moe_in)
    extra = sum(dot(pick[k].astype(BF), three_parts(gates[k])) for k in range(TOP))
    for p in range(PIECES):
        pieces[p][:, :width] = rows[p * CAP : (p + 1) * CAP].astype(BF)
        pieces[p][:, width:] = extra[p * CAP : (p + 1) * CAP].astype(BF)
    for k in range(TOP):
        gates_ref[:, k : k + 1] = gates[k]


def router(pos, x, out_full, scale, router_t, routes, places, lows):
    tok, width = x.shape
    kept = [pltpu.HBM(*s) for s in (((width, tok), BF), ((tok, width), F32), ((tok, width), BF), ((tok, TOP), F32))]
    x, out_full = in_hbm(x, out_full)
    return pl.pallas_call(
        router_kernel,
        in_specs=[SMEM_SPEC, all_of(x), all_of(out_full)] + [VMEM_SPEC] * (4 + GROUPS),
        out_specs=[VMEM_SPEC] * PIECES + [all_of(s.inner_aval) for s in kept],
        out_shape=[jax.ShapeDtypeStruct((CAP, width + 128), BF)] * PIECES + kept,
        compiler_params=pltpu.CompilerParams(vmem_limit_bytes=16 << 20),
        cost_estimate=pl.CostEstimate(flops=10**5, bytes_accessed=10**4, transcendentals=0),
        name="router",
    )(pos, x, out_full, scale, router_t, routes, places, *lows)


def expert_kernel(groups, n_fsdp, info, dy_ref, up_ref, down_ref, *refs):
    cames, refs = refs[:PIECES], refs[PIECES:]
    out_refs, (back_ref, act_ref, rows_ref, grad_in, out_acc, back_acc) = refs[:n_fsdp], refs[n_fsdp:]
    step = pl.program_id(0)
    width = grad_in.shape[1]
    h, f = info[0], info[1]
    source = [
        lax.rem(h + groups - p // n_fsdp, groups) * n_fsdp + jnp.bitwise_xor(f, p % n_fsdp) for p in range(PIECES)
    ]

    @pl.when(step == 0)
    def _():
        came = gather_rows(cames)
        gate = jnp.sum(came[:, width:], axis=1, keepdims=True)
        dy = jnp.concatenate([dy_ref[s].astype(F32) for s in source])
        grad_in[...] = dy
        rows_ref[0] = came[:, :width].astype(BF)
        rows_ref[1] = (gate * dy).astype(BF)
        out_acc[...] = jnp.zeros_like(out_acc)
        back_acc[...] = jnp.zeros_like(back_acc)

    up, down = up_ref[0], down_ref[0]
    upper = dot(rows_ref[0], up)
    active_grad = dot(rows_ref[1], down)
    cdf = 0.5 + 0.5 * lax.erf(upper * 0.7071067811865476)
    active = (upper * cdf).astype(BF)
    slope = cdf + upper * (0.3989422804014327 * jnp.exp(-0.5 * upper * upper))
    upper_grad = (active_grad * slope).astype(BF)
    act_ref[0] = upper_grad
    act_ref[1] = active
    back_acc[...] += dot(upper_grad, up, ((1,), (1,)))
    out_acc[...] += dot(active, down, ((1,), (1,)))

    @pl.when(step == pl.num_programs(0) - 1)
    def _():
        out = out_acc[...].astype(BF).astype(F32)
        gate_grad = three_parts(jnp.sum(grad_in[...] * out, axis=1, keepdims=True)).astype(F32)
        for p in range(PIECES):
            rows = slice(p * CAP, (p + 1) * CAP)
            out_refs[p % n_fsdp][lax.rem(h + groups - p // n_fsdp, groups)] = out[rows].astype(BF)
            back_ref[source[p], :, :width] = back_acc[rows, :].astype(BF)
            back_ref[source[p], :, width:] = gate_grad[rows].astype(BF)


def expert(info, cames, dy, up, down, groups, n_fsdp):
    width, ffn = up.shape[1], up.shape[2]
    rows = EXPERTS * CAP
    whole = lambda *shape: pl.BlockSpec(shape, lambda j, info: (0,) * len(shape))
    weight = pl.BlockSpec((1, width, FBLOCK), lambda j, info: (info[0], 0, j))
    return pl.pallas_call(
        functools.partial(expert_kernel, groups, n_fsdp),
        grid_spec=pltpu.PrefetchScalarGridSpec(
            num_scalar_prefetch=1,
            grid=(ffn // FBLOCK,),
            in_specs=[whole(PIECES, CAP, width), weight, weight] + [whole(CAP, width + 128)] * PIECES,
            out_specs=[whole(groups, CAP, width)] * n_fsdp
            + [
                whole(PIECES, CAP, width + 128),
                pl.BlockSpec((2, rows, FBLOCK), lambda j, info: (0, 0, j)),
                whole(2, rows, width),
            ],
            scratch_shapes=[pltpu.VMEM((rows, width), F32)] * 3,
        ),
        out_shape=[pltpu.HBM((groups, CAP, width), BF)] * n_fsdp
        + [
            jax.ShapeDtypeStruct((PIECES, CAP, width + 128), BF),
            pltpu.HBM((2, rows, ffn), BF),
            pltpu.HBM((2, rows, width), BF),
        ],
        compiler_params=pltpu.CompilerParams(vmem_limit_bytes=32 << 20),
        cost_estimate=pl.CostEstimate(flops=10**5, bytes_accessed=10**4, transcendentals=0),
        name="expert",
    )(info, dy, *in_hbm(up, down), *cames)


def weight_kernel(count, members, side, turned_by, pos, *refs):
    rows, acts, (keep_ref, pass_ref, turned, lhs) = refs[:count], refs[count : 2 * count], refs[2 * count :]
    half = keep_ref.shape[0]

    @pl.when(pl.program_id(0) == 0)
    def _():
        for n in range(count):
            turned[...] = rows[n][0].astype(F32).T.astype(BF)
            if side is not None:
                lhs[n] = turned[side * 2 * half : (side + 1) * 2 * half, :]
                continue
            unit = 2 * half // (GROUPS * members // 2)
            for r in range(members // 2):
                member = jnp.bitwise_xor(pos[0], 2 * r)
                for k in range(GROUPS):
                    row = pl.multiple_of((lax.rem(turned_by * pos[1] + k, GROUPS) * members + member) * unit, 16)
                    at = (r * GROUPS + k) * unit
                    lhs[n, at : at + unit, :] = turned[pl.ds(row, unit), :]

    keep_ref[...] = sum(dot(lhs[n, :half, :], acts[n][0]) for n in range(count)).astype(BF)
    pass_ref[...] = sum(dot(lhs[n, half:, :], acts[n][0]) for n in range(count)).astype(BF)


def weight_terms(pos, rows, acts, which, members, side=None):
    _, count, width = rows[0].shape
    ffn = acts[0].shape[2]
    half = pl.BlockSpec((width // 4, FBLOCK), lambda j: (0, j))
    return pl.pallas_call(
        functools.partial(weight_kernel, len(rows), members, side, which),
        grid=(ffn // FBLOCK,),
        in_specs=[SMEM_SPEC]
        + [pl.BlockSpec((1, count, width), lambda j: (which, 0, 0))] * len(rows)
        + [pl.BlockSpec((1, count, FBLOCK), lambda j: (which, 0, j))] * len(rows),
        out_specs=[half, half],
        out_shape=[pltpu.HBM((width // 4, ffn), BF)] * 2,
        scratch_shapes=[pltpu.VMEM((width, count), BF), pltpu.VMEM((len(rows), width // 2, count), BF)],
        compiler_params=pltpu.CompilerParams(vmem_limit_bytes=20 << 20),
        cost_estimate=pl.CostEstimate(flops=10**5, bytes_accessed=10**4, transcendentals=0),
        name="weight_terms",
    )(pos, *rows, *in_hbm(*acts))


def add_kernel(riders, a_ref, b_ref, *refs):
    rides, out = refs[:riders], refs[riders]
    rows, width = a_ref.shape[0] // GROUPS, out.shape[2]
    blocks = a_ref.shape[1] // width
    for k in range(GROUPS):
        for c in range(blocks):
            at = (slice(k * rows, (k + 1) * rows), slice(c * width, (c + 1) * width))
            out[k, c * rows : (c + 1) * rows, :] = (a_ref[at].astype(F32) + b_ref[at].astype(F32)).astype(BF)
        if riders:
            ride = jnp.concatenate([r[k].astype(F32) for r in rides])
            out[k, blocks * rows :, :] = ride.astype(BF)


def add_groups(a, b, width, rides=()):
    rows, cols = a.shape
    count = rows // GROUPS * cols // width + sum(r.shape[1] for r in rides)
    return pl.pallas_call(
        functools.partial(add_kernel, len(rides)),
        in_specs=[all_of(a)] * 2 + [all_of(r) for r in rides],
        out_specs=pl.BlockSpec((GROUPS, count, width), lambda: (0, 0, 0)),
        out_shape=pltpu.HBM((GROUPS, count, width), BF),
        compiler_params=pltpu.CompilerParams(vmem_limit_bytes=16 << 20),
        cost_estimate=pl.CostEstimate(flops=10**5, bytes_accessed=10**4, transcendentals=0),
        name="add_groups",
    )(*in_hbm(a, b, *rides))


def sum_kernel(a_ref, b_ref, *outs):
    rows = outs[0].shape[0]
    for k, out in enumerate(outs):
        at = slice(k * rows, (k + 1) * rows)
        out[...] = (a_ref[at, :].astype(F32) + b_ref[at, :].astype(F32)).astype(BF)


def sum_pieces(a, b):
    rows, cols = a.shape
    return pl.pallas_call(
        sum_kernel,
        in_specs=[all_of(a)] * 2,
        out_specs=[pl.BlockSpec((rows // GROUPS, cols), lambda: (0, 0))] * GROUPS,
        out_shape=[jax.ShapeDtypeStruct((rows // GROUPS, cols), BF)] * GROUPS,
        compiler_params=pltpu.CompilerParams(vmem_limit_bytes=16 << 20),
        cost_estimate=pl.CostEstimate(flops=10**5, bytes_accessed=10**4, transcendentals=0),
        name="sum_pieces",
    )(*in_hbm(a, b))


def order_kernel(pos, *refs):
    for k in range(GROUPS):
        refs[-1][group_of(k, pos[1])] = refs[k][...].astype(F32)


def in_order(pos, parts):
    shape = (GROUPS,) + parts[0].shape
    return pl.pallas_call(
        order_kernel,
        in_specs=[SMEM_SPEC] + [all_of(p) for p in parts],
        out_specs=pl.BlockSpec(shape, lambda: (0, 0, 0)),
        out_shape=jax.ShapeDtypeStruct(shape, F32),
        compiler_params=pltpu.CompilerParams(vmem_limit_bytes=16 << 20),
        cost_estimate=pl.CostEstimate(flops=10**5, bytes_accessed=10**4, transcendentals=0),
        name="in_order",
    )(pos, *parts)


def wide_kernel(blocks, x_ref, out_ref):
    rows, width = out_ref.shape[1], out_ref.shape[2] // blocks
    for k in range(GROUPS):
        for c in range(blocks):
            out_ref[k, :, c * width : (c + 1) * width] = x_ref[k, c * rows : (c + 1) * rows, :].astype(F32)


def to_wide(x, rows, cols):
    width = x.shape[2]
    return pl.pallas_call(
        functools.partial(wide_kernel, cols // width),
        in_specs=[all_of(x)],
        out_specs=pl.BlockSpec((GROUPS, rows, cols), lambda: (0, 0, 0)),
        out_shape=jax.ShapeDtypeStruct((GROUPS, rows, cols), F32),
        compiler_params=pltpu.CompilerParams(vmem_limit_bytes=16 << 20),
        cost_estimate=pl.CostEstimate(flops=10**5, bytes_accessed=10**4, transcendentals=0),
        name="to_wide",
    )(x)


def turn_kernel(
    info, place_ref, routes_ref, gates_ref, resid_ref, moe_ref, dy_ref, router_ref, scale_ref,
    out_ref, context_ref, back_ref, *refs,
):
    dos, (resid_grad_ref, mine_ref, other_ref, send_ref, router_grad_ref, gain_ref, term) = refs[:GROUPS], refs[GROUPS:]
    tok, width = resid_ref.shape
    back = back_ref[...]
    slots = back.shape[0]
    iota = lax.broadcasted_iota(jnp.int32, (tok, slots), 1)
    pick = [place_ref[:, k : k + 1] == iota for k in range(TOP)]
    gates = [gates_ref[:, k : k + 1] for k in range(TOP)]
    gate_grad = [jnp.sum(dot(p.astype(BF), back[:, width:]), axis=1, keepdims=True) for p in pick]
    mean = gates[0] * gate_grad[0] + gates[1] * gate_grad[1]
    lane = lax.broadcasted_iota(jnp.int32, (tok, 128), 1)
    logit_grad = sum(
        jnp.where(routes_ref[:, k : k + 1] == lane, gates[k] * (gate_grad[k] - mean), 0.0) for k in range(TOP)
    )
    grad = dot((pick[0] | pick[1]).astype(BF), back[:, :width])
    for e in range(EXPERTS):
        grad = grad + logit_grad[:, e : e + 1] * router_ref[e : e + 1, :].astype(F32)
    resid = resid_ref[...]
    inv = lax.rsqrt(jnp.mean(resid * resid, axis=1, keepdims=True) + EPS)
    gain_ref[...] = jnp.sum(grad * (resid * inv), axis=0, keepdims=True)
    scaled = grad * scale_ref[...]
    along = jnp.mean(scaled * resid, axis=1, keepdims=True)
    resid_grad = dy_ref[...].astype(F32) + inv * scaled - resid * (inv * inv * inv * along)
    resid_grad_ref[...] = resid_grad
    low = resid_grad.astype(BF)
    term[:, :tok] = dot(out_ref[...], low, ((1,), (1,)))
    for k in range(GROUPS):
        row = pl.multiple_of(lax.rem(info[0] + k, GROUPS) * GWIDTH, GWIDTH)
        dos[k][...] = term[pl.ds(row, GWIDTH), :tok].astype(BF)
    router_grad_ref[...] = lax.dot_general(
        logit_grad.T[:EXPERTS], moe_ref[...].astype(F32), (((1,), (0,)), ((), ())),
        precision=FULL, preferred_element_type=F32,
    )
    term[...] = dot(low.astype(F32).T.astype(BF), context_ref[...].astype(F32).T.astype(BF))
    rows, cols = mine_ref.shape[1:]
    core, top = info[1], info[2]
    mine = pl.ds(pl.multiple_of(top * cols, 128), cols)
    other = pl.ds(pl.multiple_of((1 - top) * cols, 128), cols)
    for g in range(mine_ref.shape[0]):
        keep = pl.ds(pl.multiple_of((2 * g + core) * rows, 8), rows)
        send = pl.ds(pl.multiple_of((2 * g + 1 - core) * rows, 8), rows)
        mine_ref[g] = term[keep, mine]
        other_ref[g] = term[keep, other]
        send_ref[0, g] = term[send, mine].astype(BF)
        send_ref[1, g] = term[send, other].astype(BF)


def turn_back(info, back, place, routes, gates, resid, moe_in, dy, router, scale, out_full, context, shards):
    tok, width = resid.shape
    rows = width // shards
    part = (shards // 2, rows, width // 2)
    gates, resid, moe_in, dy, out_full, context = in_hbm(gates, resid, moe_in, dy, out_full, context)
    inputs = (place, routes, gates, resid, moe_in, dy, router, scale, out_full, context, back)
    kept = [((tok, width), F32), (part, F32), (part, F32), ((2,) + part, BF), ((EXPERTS, width), F32), ((1, width), F32)]
    kept = [pltpu.HBM(*s) for s in kept]
    return pl.pallas_call(
        turn_kernel,
        in_specs=[SMEM_SPEC] + [all_of(x) for x in inputs],
        out_specs=[VMEM_SPEC] * GROUPS + [all_of(s.inner_aval) for s in kept],
        scratch_shapes=[pltpu.VMEM((width, width), F32)],
        out_shape=[jax.ShapeDtypeStruct((GWIDTH, tok), BF)] * GROUPS + kept,
        compiler_params=pltpu.CompilerParams(vmem_limit_bytes=24 << 20),
        cost_estimate=pl.CostEstimate(flops=10**5, bytes_accessed=10**4, transcendentals=0),
        name="turn_back",
    )(info, *inputs)


def pair_kernel(a_ref, b_ref, c_ref, d_ref, keep_ref, send_ref):
    keep_ref[...] = a_ref[...].astype(F32) + b_ref[...].astype(F32)
    send_ref[...] = (c_ref[...].astype(F32) + d_ref[...].astype(F32)).astype(BF)


def add_pairs(a, b, c, d):
    return pl.pallas_call(
        pair_kernel,
        in_specs=[VMEM_SPEC] * 4,
        out_specs=[VMEM_SPEC] * 2,
        out_shape=[jax.ShapeDtypeStruct(a.shape, F32), jax.ShapeDtypeStruct(a.shape, BF)],
        cost_estimate=pl.CostEstimate(flops=10**5, bytes_accessed=10**4, transcendentals=0),
        compiler_params=pltpu.CompilerParams(vmem_limit_bytes=8 << 20),
        name="add_pairs",
    )(a, b, c, d)


SMALL = 16


def input_kernel(
    members, buckets_here, info, dq_ref, keep_ref, came_ref, ain_ref, weight_ref, scale_ref, router_ref,
    gain_ref, line_ref, dline_ref, own_ref, one_ref, two_ref, three_ref, term_ref, sent_ref, pack_ref, dproj, term,
):
    h, core = info[0], info[1]
    width = ain_ref.shape[1]
    tok = own_ref.shape[0]
    dproj[:, :GWIDTH] = dq_ref[...].astype(F32)
    for k in range(GROUPS):
        dkv = keep_ref[k] if came_ref is None else keep_ref[k] + came_ref[k].astype(F32)
        dproj[k * tok : (k + 1) * tok, GWIDTH:] = dkv.astype(BF).astype(F32)
    low = dproj[...].astype(BF)
    ain = ain_ref[...]
    back = dot(low, weight_ref[...], ((1,), (1,)))
    own_ref[...] = back[:tok]
    for k, ref in enumerate((one_ref, two_ref, three_ref)):
        ref[...] = back[(k + 1) * tok : (k + 2) * tok].astype(BF)
    pack_ref[0:EXPERTS, :] = router_ref[...]
    pack_ref[EXPERTS : EXPERTS + 1, :] = jnp.sum(back * ain.astype(F32), axis=0, keepdims=True) / scale_ref[...]
    pack_ref[EXPERTS + 1 : EXPERTS + 2, :] = gain_ref[...]
    col = lax.broadcasted_iota(jnp.int32, (BUCKETS, width), 1)
    cols_f = width * buckets_here // BUCKETS
    within = lax.rem(col, cols_f) - h * buckets_here
    held = jnp.where((within >= 0) & (within < buckets_here), col // cols_f * buckets_here + within, -1)
    held = held == lax.broadcasted_iota(jnp.int32, (BUCKETS, width), 0)
    bucket = line_ref[...] == lax.broadcasted_iota(jnp.int32, (BUCKETS, line_ref.shape[1]), 0)
    for n in range(GHEADS):
        sums = jnp.sum(jnp.where(bucket, dline_ref[n : n + 1, :], 0.0), axis=1, keepdims=True)
        row = EXPERTS + 2 + n
        pack_ref[row : row + 1, :] = jnp.sum(jnp.where(held, sums, 0.0), axis=0, keepdims=True)
    rest = EXPERTS + 2 + GHEADS
    pack_ref[rest:, :] = jnp.zeros((SMALL - rest, width), F32)
    term[...] = dot(dproj[...].T.astype(BF), ain)
    unit = GWIDTH // members
    for t in range(3):
        for r in range(members // 2):
            at = slice((t * (members // 2) + r) * unit, (t * (members // 2) + r + 1) * unit)
            first = (t * members + 2 * r) * unit
            term_ref[at, :] = term[pl.ds(pl.multiple_of(first + core * unit, 8), unit), :]
            sent_ref[at, :] = term[pl.ds(pl.multiple_of(first + (1 - core) * unit, 8), unit), :].astype(BF)
    pack = pack_ref[...]
    high = pack.astype(BF)
    rows = term_ref.shape[0]
    sent_ref[rows : rows + SMALL, :] = high
    sent_ref[rows + SMALL :, :] = (pack - high.astype(F32)).astype(BF)


def input_back(info, members, buckets_here, dq, keep, came, ain, weight, scale, router_grad, gain_grad, line, dline):
    count, width = ain.shape
    tok = count // GROUPS
    rows = 3 * GWIDTH // 2
    ain, weight = in_hbm(ain, weight)
    inputs = [dq, keep] + ([] if came is None else [came]) + [ain, weight, scale, router_grad, gain_grad, line, dline]
    body = functools.partial(input_kernel, members, buckets_here)
    if came is None:
        body = lambda info, dq, keep, *refs: input_kernel(members, buckets_here, info, dq, keep, None, *refs)
    return pl.pallas_call(
        body,
        in_specs=[SMEM_SPEC] + [all_of(x) for x in inputs],
        out_specs=[VMEM_SPEC] * 7,
        out_shape=[jax.ShapeDtypeStruct((tok, width), F32)]
        + [jax.ShapeDtypeStruct((tok, width), BF)] * 3
        + [
            jax.ShapeDtypeStruct((rows, width), F32),
            jax.ShapeDtypeStruct((rows + 2 * SMALL, width), BF),
            jax.ShapeDtypeStruct((SMALL, width), F32),
        ],
        scratch_shapes=[pltpu.VMEM((count, 3 * GWIDTH), F32), pltpu.VMEM((3 * GWIDTH, width), F32)],
        compiler_params=pltpu.CompilerParams(vmem_limit_bytes=24 << 20),
        cost_estimate=pl.CostEstimate(flops=10**5, bytes_accessed=10**4, transcendentals=0),
        name="input_back",
    )(info, *inputs)


def together(*values):
    return lax.optimization_barrier(values)


def turn(shift):
    return [(i, (i + shift) % GROUPS) for i in range(GROUPS)]


def gather_groups(x):
    came = {k: lax.ppermute(x, "h", turn(k)) for k in (2, 1, 3)}
    return jnp.stack([x] + [came[k] for k in range(1, GROUPS)])


def gather_members(x):
    size = lax.axis_size(MEMBERS)
    held = {0: x}
    for bit in bits_of(size):
        for k in sorted(held):
            held[k | bit] = lax.ppermute(held[k], MEMBERS, xor_perm(bit, size))
    return [held[k] for k in range(size)]


def part_of(x, mine):
    low, high = jnp.split(x, 2, axis=-1)
    return jnp.where(mine == 0, low, high), jnp.where(mine == 0, high, low)


def swap(x, axis, bit):
    return lax.ppermute(x, axis, xor_perm(bit, lax.axis_size(axis)))


def two_parts(x):
    high = lax.reduce_precision(x, 8, 7)
    return jnp.concatenate([high, x - high]).astype(BF)


def from_fsdp(part):
    if lax.axis_size("fsdp") != 2:
        return lax.all_gather(part, "fsdp", axis=0)
    came = lax.ppermute(part, "fsdp", xor_perm(1, 2))
    return jnp.where(lax.axis_index("fsdp") == 0, jnp.stack([part, came]), jnp.stack([came, part]))


def swap_groups(x):
    return lax.all_to_all(x, "h", 0, 0, tiled=True)


def group_pieces(pieces, sign):
    came = {k: lax.ppermute(pieces[k], "h", turn(sign * k)) for k in (2, 1, 3)}
    return [pieces[0]] + [came[k] for k in range(1, GROUPS)]


def deal(pieces, spread, sign):
    n_fsdp = lax.axis_size("fsdp")
    out = [pieces[0]] + [None] * (len(pieces) - 1)
    for p in (5, 4, 3, 7, 2, 6, 1):
        k, j = divmod(p, n_fsdp)
        if spread:
            pairs = [
                (g * n_fsdp + i, (g + sign * k) % GROUPS * n_fsdp + (i ^ j))
                for g in range(GROUPS)
                for i in range(n_fsdp)
            ]
            out[p] = lax.ppermute(pieces[p], ("h", "fsdp"), pairs)
        else:
            out[p] = lax.ppermute(pieces[p], "fsdp", xor_perm(j, n_fsdp))
    return out


def per_device(
    tokens, segments, routes, bucket_table, attn_gain, qkv_weight, out_weight, bias_table,
    moe_gain, router_weight, up_weight, down_weight, cotangent,
):
    tok, width = tokens.shape[1], tokens.shape[2]
    half = tok // 2
    h, m, f = lax.axis_index("h"), lax.axis_index(MEMBERS), lax.axis_index("fsdp")
    core = lax.axis_index("core")
    members, n_fsdp = lax.axis_size(MEMBERS), lax.axis_size("fsdp")
    shards = GROUPS * members
    blocks = 2 * shards
    length = shards * tok
    here = EXPERTS // n_fsdp
    spread = here > 1
    ffn = up_weight.shape[2]
    rows_f = width // n_fsdp
    rows_c = width // shards
    pos = jnp.stack([m, h]).astype(jnp.int32)

    extra = jnp.pad(segments.astype(BF), ((0, 7), (0, width - tok)))
    mixed = gather_groups(jnp.concatenate([tokens[0], extra]))

    bias_flat = bias_table.reshape(1, -1)
    bias_rows = -(-bias_flat.shape[1] // rows_f)
    bias_flat = jnp.pad(bias_flat, ((0, 0), (0, bias_rows * rows_f - bias_flat.shape[1])))
    small = jnp.concatenate(
        [attn_gain[None], moe_gain[None], router_weight.T, bias_flat.reshape(bias_rows, rows_f)]
        + [jnp.zeros((16 - 10 - bias_rows, rows_f), BF)]
    )
    small = from_fsdp(small)
    attn_scale = small[:, 0].reshape(width).astype(F32)
    moe_scale = small[:, 1].reshape(width).astype(F32)
    router_t = jnp.transpose(small[:, 2:10], (1, 0, 2)).reshape(EXPERTS, width)
    bias_full = small[:, 10 : 10 + bias_rows].reshape(n_fsdp, -1)[:, : bias_table.size]
    bias_full = bias_full.reshape(BUCKETS, HEADS)
    cut = [
        lax.dynamic_slice_in_dim(qkv_weight, n * width + h * GWIDTH, GWIDTH, 1) for n in range(3)
    ]
    qkv_heads = from_fsdp(jnp.concatenate(cut, axis=1)).reshape(width, 3 * GWIDTH)
    out_full = from_fsdp(together(out_weight, qkv_heads)[0]).reshape(width, width)

    wide = strip_width(blocks, half)
    top = half * (blocks - 1)
    line = jnp.concatenate(
        [
            bucket_table[: top + 1][::-1],
            jnp.full((wide - length,), -1, jnp.int32),
            bucket_table[top + 1 :][::-1],
        ]
    )
    hot = (line[None] == jnp.arange(BUCKETS, dtype=jnp.int32)[:, None]).astype(BF)
    bias_mine = lax.dynamic_slice_in_dim(bias_full, h * GHEADS, GHEADS, 1)
    strips = make_strips(dot(bias_mine, hot, ((0,), (0,))) * LOG2E, half)

    hot_routes = (routes.reshape(-1)[:, None] == jnp.arange(EXPERTS)[None]).astype(F32)
    earlier = jnp.arange(tok * TOP)
    earlier = (earlier[None, :] < earlier[:, None]).astype(BF)
    before = dot(earlier, hot_routes.astype(BF))
    slot = jnp.sum(before * hot_routes, axis=1).astype(jnp.int32).reshape(tok, TOP)
    group = routes % here
    natural = (group * n_fsdp + routes // here) * CAP + slot
    away = lax.rem(group - h + GROUPS, GROUPS) if spread else group
    place = (away * n_fsdp + jnp.bitwise_xor(routes // here, f)) * CAP + slot
    slots = jnp.arange(EXPERTS * CAP, dtype=jnp.int32)
    pick = [slots[:, None] == natural[None, :, k] for k in range(TOP)]
    exchange = ("h", "fsdp") if spread else ("fsdp",)

    def exchange_rows(rows):
        return lax.all_to_all(rows, exchange, 0, 0, tiled=True)

    mixed, strips = together(mixed, strips)
    ain = normalize(mixed[:, :tok].astype(F32), attn_scale).astype(BF).reshape(GROUPS * tok, width)
    proj = dot(ain, qkv_heads).astype(BF)
    kv = proj[:, GWIDTH:].reshape(GROUPS, tok, 2 * GWIDTH)
    kvs = gather_members(jnp.concatenate([kv, mixed[:, tok:, : 2 * GWIDTH]], axis=1))
    dy_send = dot((pick[0] | pick[1]).astype(BF), cotangent[0]).astype(BF).reshape(PIECES, CAP, width)
    dy_send = together(dy_send, qkv_heads)[0]
    kvs[0], dy_slots = together(kvs[0], exchange_rows(dy_send))
    o_pre, *rest = attend(pos, proj, kvs, strips, blocks)
    lows, stat, keys = rest[:GROUPS], rest[GROUPS], rest[GROUPS + 1 :]
    *pieces, context, residual, moe_in, gates = router(
        pos, tokens[0], out_full, moe_scale[None], router_t, routes, place.T, group_pieces(lows, -1)
    )

    came = deal(pieces, spread, 1)
    info = jnp.stack([h if spread else jnp.zeros_like(h), f]).astype(jnp.int32)
    *outs, back, act, rows = expert(
        info, came, dy_slots, up_weight, down_weight, GROUPS if spread else 1, n_fsdp
    )
    back = exchange_rows(back).reshape(EXPERTS * CAP, -1)

    staged = spread and members == 4
    if staged:
        rows, acts = [rows, swap(rows, "core", 1)], [act, swap(act, "core", 1)]
        terms = [weight_terms(pos, rows, acts, n, members) for n in range(2)]
        back, terms = together(back, terms)
    else:
        terms = [weight_terms(pos, [rows], [act], n, members, side) for n in range(2) for side in range(2)]

    top_bit = n_fsdp // 2
    info = jnp.stack([h, core, (f // top_bit) % 2]).astype(jnp.int32)
    *dos, resid_grad, out_mine, out_other, out_send, router_grad, moe_gain_grad = turn_back(
        info, back, natural, routes, gates, residual, moe_in, cotangent[0], router_t,
        moe_scale[None], out_full, context, shards,
    )
    dos = group_pieces(dos, 1)
    out_came = swap(out_send, "core", 1)
    out_far = (out_other + out_came[1].astype(F32)).astype(BF)
    outs = [outs[0]] + [lax.ppermute(outs[j], "fsdp", xor_perm(j, n_fsdp)) for j in range(1, n_fsdp)]
    dos[0], out_far = together(dos[0], out_far)
    out_far = swap(out_far, "fsdp", top_bit)
    dq, *dkvs, dline = attend_back(pos, proj, keys, strips, dos, o_pre, stat, members, blocks)
    dkvs[1], out_far, outs = together(dkvs[1], out_far, outs)
    cames = [swap(dkvs[k], "core", 1) for k in range(1, members, 2)]
    sends = []
    if members == 4:
        keep, send = add_pairs(dkvs[0], cames[0], dkvs[2], cames[1])
        if staged:
            sends = [swap(terms[0][1], "r", 1)]
            send, sends[0] = together(send, sends[0])
        came = swap(send, "r", 1)
    else:
        held = {k: dkvs[k].astype(F32) + cames[k // 2].astype(F32) for k in range(0, members, 2)}
        bit = 2
        while bit < members:
            for k in [k for k in sorted(held) if k & bit]:
                held[k - bit] = held[k - bit] + swap(held.pop(k).astype(BF), "r", bit // 2).astype(F32)
            bit *= 2
        keep, came = held[0], None
    if staged:
        sends.append(swap(terms[1][1], "r", 1))
        up_send, came = together(add_groups(terms[0][0], sends[0], width, outs), came)
        up_came = swap_groups(up_send)

    own_back, back_1, back_2, back_3, term, sent, pack = input_back(
        jnp.stack([h, core]).astype(jnp.int32), members, BUCKETS // n_fsdp, dq, keep, came, ain, qkv_heads,
        attn_scale[None], router_grad, moe_gain_grad, line[None], dline,
    )

    def swap_both(send, pack, axis, bit):
        sent = jnp.concatenate([send.reshape(-1, send.shape[-1]).astype(BF), two_parts(pack)])
        return split_rows(swap(sent, axis, bit).astype(F32), send.shape)

    def split_rows(came, shape):
        return came[: -2 * SMALL].reshape(shape), came[-2 * SMALL : -SMALL] + came[-SMALL:]

    unit = GWIDTH // members
    came, pack_came = split_rows(swap(sent, "core", 1).astype(F32), term.shape)
    term, pack = term + came, pack + pack_came
    out_term = out_mine + out_came[0].astype(F32) + out_far.astype(F32)
    for bit in list(bits_of(n_fsdp))[1:]:
        out_term, out_send = part_of(out_term, (f // bit) % 2)
        out_term = out_term + swap(out_send.astype(BF), "fsdp", bit).astype(F32)
    for bit in bits_of(n_fsdp):
        term, send = part_of(term, (f // bit) % 2)
        pack, pack_send = part_of(pack, (f // bit) % 2)
        came, pack_came = swap_both(send, pack_send, "fsdp", bit)
        term, pack = term + came, pack + pack_came
    term = jnp.concatenate(
        [term.reshape(3, members // 2, unit, rows_f).swapaxes(0, 1).reshape(members // 2, -1, rows_f)]
        + [out_term.reshape(GROUPS, members // 2, rows_c, rows_f).swapaxes(0, 1).reshape(members // 2, -1, rows_f)],
        axis=1,
    )
    if staged:
        term, up_came = together(term, up_came)
    if staged:
        back_2, back_3, term = together(back_2, back_3, term)
    mid = lax.ppermute(back_2, "h", turn(-1))
    side = lax.ppermute(back_3, "h", turn(1)).astype(F32)
    mid = (back_1.astype(F32) + mid.astype(F32)).astype(BF)
    mid = lax.ppermute(mid, "h", turn(-1)).astype(F32)
    attn_in_grad = own_back + side + mid
    x = tokens[0].astype(F32)
    token_grad = jax.vjp(lambda v: normalize(v, attn_scale), x)[1](attn_in_grad)[0]
    tokens_grad = (resid_grad + token_grad).astype(BF)

    for bit in bits_of(members // 2):
        mine = (lax.axis_index("r") // bit) % 2
        term = term.reshape((2, -1) + term.shape[1:])
        came, pack_came = swap_both(lax.dynamic_index_in_dim(term, 1 - mine, 0, False), pack, "r", bit)
        term = lax.dynamic_index_in_dim(term, mine, 0, False) + came
        pack = pack + pack_came
    term = term[0]
    out_term = term[3 * unit :].reshape(GROUPS, rows_c, rows_f)
    term = term[: 3 * unit].astype(BF).reshape(3, unit, rows_f)
    out_sum, pack_sum = lax.dynamic_index_in_dim(out_term, h, 0, False), pack
    for k in (2, 1, 3):
        piece = lax.dynamic_index_in_dim(out_term, lax.rem(h + k, GROUPS), 0, False)
        came = lax.ppermute(jnp.concatenate([piece.astype(BF), two_parts(pack)]), "h", turn(k)).astype(F32)
        out_sum = out_sum + came[:rows_c]
        pack_sum = pack_sum + came[rows_c : rows_c + SMALL] + came[rows_c + SMALL :]
    at = h * members + m
    parts = []
    for r in range(3):
        pairs = [((3 * d + r) % shards, d) for d in range(shards)]
        third = pow(3, -1, shards)
        which = (3 * lax.rem((at + shards - r) * third, shards) + r) // shards
        parts.append(lax.ppermute(lax.dynamic_index_in_dim(term, which, 0, False), CTX, pairs))
    if staged:
        sends[1], parts, pack_sum = together(sends[1], parts, pack_sum)
        down_came = group_pieces(sum_pieces(terms[1][0], sends[1]), 1)
        grads = [to_wide(up_came, rows_c, ffn), in_order(pos, down_came)]
        home = up_came[:, rows_c * ffn // width :].reshape(EXPERTS * CAP, width)
    else:
        terms = [jnp.concatenate(terms[n] + terms[n + 1]) for n in (0, 2)]
        grads = [
            lax.psum_scatter(term, CTX, scatter_dimension=0, tiled=True)[None].astype(F32) for term in terms
        ]
        home = jnp.concatenate([o.reshape(-1, width) for o in outs])
    qkv_grad = jnp.concatenate(parts).astype(F32).T

    place = (group * n_fsdp + jnp.bitwise_xor(routes // here, f)) * CAP + slot
    layer_out = residual
    for k in range(TOP):
        row = (slots[:, None] == place[None, :, k]).astype(BF)
        layer_out = layer_out + gates[:, k : k + 1] * dot(row, home, ((0,), (0,)))
    bias_grad = pack_sum[EXPERTS + 2 : EXPERTS + 2 + GHEADS, : GROUPS * BUCKETS // n_fsdp]
    bias_grad = bias_grad.reshape(GHEADS, GROUPS, BUCKETS // n_fsdp).transpose(2, 1, 0).reshape(-1, HEADS)
    return (
        layer_out.astype(BF)[None],
        tokens_grad[None],
        pack_sum[8],
        qkv_grad,
        out_sum.T,
        bias_grad,
        pack_sum[9],
        pack_sum[:8].T,
        grads[0],
        grads[1],
    )


def solution(mesh):
    n_ctx, n_fsdp = mesh.shape["ctx"], mesh.shape["fsdp"]
    cut = mesh.devices.reshape(GROUPS, n_ctx // (2 * GROUPS), 2, n_fsdp)
    row = P("fsdp", CTX, None)
    return jax.shard_map(
        per_device,
        mesh=Mesh(cut, CTX + ("fsdp",)),
        in_specs=(
            row,
            P("fsdp", CTX),
            P(CTX + ("fsdp",), None),
            P(),
            P("fsdp"),
            P("fsdp", None),
            P("fsdp", None),
            P("fsdp", None),
            P("fsdp"),
            P("fsdp", None),
            P("fsdp", None, None),
            P("fsdp", None, None),
            row,
        ),
        out_specs=(
            row,
            row,
            P("fsdp"),
            P("fsdp", CTX),
            P("fsdp", CTX),
            P("fsdp", None),
            P("fsdp"),
            P("fsdp", None),
            row,
            row,
        ),
        check_vma=False,
    )
```

```python
import functools

import jax
import jax.numpy as jnp
from jax import lax
from jax.experimental import pallas as pl
from jax.experimental.pallas import tpu as pltpu
from jax.sharding import Mesh, PartitionSpec as P

HEADS = 12
HEAD_DIM = 64
EXPERTS = 8
TOP = 2
BUCKETS = 32
DOCS = 8
CAP = 40
GROUPS = 4
GHEADS = HEADS // GROUPS
GWIDTH = GHEADS * HEAD_DIM
CHUNK = 256

LOG2E = 1.4426950408889634
EPS = 1e-06
LOWEST = -1e30
FULL = lax.Precision.HIGHEST
BF = jnp.bfloat16
F32 = jnp.float32
MEMBERS = ("r", "core")
CTX = ("h", "r", "core")


def normalize(values, weight):
    inv_rms = lax.rsqrt(jnp.mean(values * values, axis=-1, keepdims=True) + EPS)
    return values * inv_rms * weight


def dot(a, b, dims=((1,), (0,))):
    return lax.dot_general(a, b, (dims, ((), ())), preferred_element_type=F32)


def exact_dot(a, b, dims):
    return lax.dot_general(a, b, (dims, ((), ())), precision=FULL)


def xor_perm(mask, size):
    return [(i, i ^ mask) for i in range(size)]


def bits_of(size):
    bit = size // 2
    while bit:
        yield bit
        bit //= 2


def strip_width(blocks, half):
    need = half * (blocks - 1) + CHUNK + half
    return -(-need // 128) * 128


def strips_kernel(g_ref, out_ref):
    half = out_ref.shape[1] // GHEADS
    rolled = [
        pltpu.roll(
            jnp.broadcast_to(g_ref[n : n + 1, :], (half, g_ref.shape[1])), 0, 1, stride=1, stride_axis=0
        )
        for n in range(GHEADS)
    ]
    out_ref[...] = jnp.concatenate(rolled).T


def make_strips(lines, half):
    return pl.pallas_call(
        strips_kernel,
        out_specs=pl.BlockSpec((lines.shape[1], GHEADS * half), lambda: (0, 0)),
        out_shape=pltpu.HBM((lines.shape[1], GHEADS * half), F32),
        cost_estimate=pl.CostEstimate(flops=10**5, bytes_accessed=10**4, transcendentals=0),
        name="strips",
    )(lines)


def own_blocks(size, half):
    a = lax.broadcasted_iota(jnp.int32, (size, size), 0) // half
    b = lax.broadcasted_iota(jnp.int32, (size, size), 1) // half
    return a == b


def spread_rows(x, same):
    return jnp.where(same, jnp.concatenate([x] * GHEADS), 0.0)


def fold_rows(x, same, half):
    y = jnp.where(same, x, 0.0).T
    return sum(y[n * half : (n + 1) * half] for n in range(GHEADS))


def own_columns(x, half):
    return jnp.concatenate(
        [x[n * HEAD_DIM : (n + 1) * HEAD_DIM, n * half : (n + 1) * half] for n in range(GHEADS)]
    )


def spread_columns(x, same):
    return jnp.where(same, jnp.concatenate([x] * GHEADS, axis=1), 0.0)


def group_of(slot, h):
    return lax.rem(h + GROUPS - slot, GROUPS)


def place_of(slot, early, me, h, members, blocks):
    owner = group_of(slot, h) * members + me
    return owner if early else blocks - 1 - owner


def bounds(block, chunk, half, blocks, start):
    top = (blocks - 1 - (block - (CHUNK // half) * chunk)) * half
    lane = lax.broadcasted_iota(jnp.int32, (1, GHEADS * half), 1)
    last = block * half + lax.rem(lane, half) - chunk * CHUNK
    return pl.multiple_of(top, half), last, start - chunk * CHUNK


def forward_kernel(half, blocks, members, pos, q_ref, *refs):
    kvs, refs = refs[:members], refs[members:]
    strip_in, o_ref, *lows, stat_ref, k_out, v_out, kt_out, k_ref, v_ref, kt_ref, vt, strip_ref, sems, strip_sem = refs
    loads = start_copies([(strip_in, strip_ref)], strip_sem)
    size = GHEADS * half
    me, h = pos[0], pos[1]
    tok = 2 * half
    same = own_blocks(size, half)
    key = lax.broadcasted_iota(jnp.int32, (CHUNK, size), 0)
    per = CHUNK // half

    @pl.loop(0, GROUPS)
    def _(slot):
        for j in range(members):
            for early in (True, False):
                block = place_of(slot, early, jnp.bitwise_xor(me, j), h, members, blocks)
                at = pl.ds(pl.multiple_of(lax.rem(block, per) * half, half), half)
                rows = kvs[j][slot, 0 if early else half : half if early else tok, :]
                k_ref[block // per, at, :] = rows[:, :GWIDTH]
                v_ref[block // per, at, :] = rows[:, GWIDTH:]

    @pl.loop(0, blocks // per)
    def _(chunk):
        kt_ref[chunk] = k_ref[chunk].astype(F32).T.astype(BF)
        vt[chunk] = v_ref[chunk].astype(F32).T.astype(BF)

    copies = start_copies([(k_ref, k_out), (v_ref, v_out), (kt_ref, kt_out)], sems)
    docs = jnp.concatenate([kv[a, tok : tok + 1, :tok].astype(F32) for kv in kvs for a in range(GROUPS)])
    begins = [jnp.sum(jnp.where(docs < s, 1.0, 0.0)) for s in range(1, DOCS)]
    for load in loads:
        load.wait()

    @pl.loop(0, q_ref.shape[0] // half)
    def _(i):
        slot, late = i // 2, lax.rem(i, 2)
        owner = group_of(slot, h) * members + me
        block = jnp.where(late == 0, owner, blocks - 1 - owner)
        at = pl.ds(pl.multiple_of(i * half, half), half)
        qt = spread_rows(q_ref[at, :GWIDTH].astype(F32), same).T.astype(BF)
        doc = kvs[0][slot, tok : tok + 1, :tok].astype(F32)
        doc = jnp.where(late == 0, doc[:, :half], doc[:, half:])
        begin = jnp.zeros((1, half), F32)
        for s in range(1, DOCS):
            begin = jnp.where(doc == s, begins[s - 1], begin)
        first = jnp.min(begin).astype(jnp.int32) // CHUNK
        begin = jnp.concatenate([begin] * GHEADS, axis=1)
        start = begin.astype(jnp.int32)

        def visit(chunk, carry):
            peak, total, acc = carry
            top, last, begin = bounds(block, chunk, half, blocks, start)
            t = dot(k_ref[chunk], qt) * (HEAD_DIM**-0.5 * LOG2E) + strip_ref[pl.ds(top, CHUNK), :]
            t = jnp.where((key <= last) & (key >= begin), t, LOWEST)
            new = jnp.maximum(peak, jnp.ceil(jnp.max(t, axis=0, keepdims=True)))
            e = jnp.exp2(t - new)
            fade = jnp.exp2(peak - new)
            total = total * fade + jnp.sum(e, axis=0, keepdims=True)
            acc = acc * fade + dot(vt[chunk], e.astype(BF))
            return new, total, acc

        init = (
            jnp.full((1, size), LOWEST, F32),
            jnp.zeros((1, size), F32),
            jnp.zeros((GWIDTH, size), F32),
        )
        peak, total, acc = lax.fori_loop(first, block // per + 1, visit, init)
        out = own_columns(acc / total, half)
        o_ref[i] = out
        low = out.astype(BF)
        for n in range(GROUPS):
            for part in range(2):

                @pl.when(i == 2 * n + part)
                def _():
                    lows[n][:, part * half : (part + 1) * half] = low

        stat_ref[i, 0:1, :] = peak
        stat_ref[i, 1:2, :] = total
        stat_ref[i, 2:3, :] = begin

    for copy in copies:
        copy.wait()


def backward_kernel(half, blocks, members, pos, *refs):
    dos, refs = refs[:GROUPS], refs[GROUPS:]
    inputs, (dq_ref, *refs) = refs[:7], refs[7:]
    dkvs, refs = refs[:members], refs[members:]
    dline_ref, *held, dk, dv, dstrip, do_ref, sems = refs
    q_ref, strip_ref, o_ref, stat_ref, k_ref, v_ref, kt_ref = held
    size = GHEADS * half
    me, h = pos[0], pos[1]
    width = dstrip.shape[0]
    per = CHUNK // half
    copies = start_copies(list(zip(inputs, held)), sems)
    same = own_blocks(size, half)
    key = lax.broadcasted_iota(jnp.int32, (CHUNK, size), 0)

    @pl.loop(0, blocks // per)
    def _(chunk):
        dk[chunk] = jnp.zeros(dk.shape[1:], F32)
        dv[chunk] = jnp.zeros(dv.shape[1:], F32)

    @pl.loop(0, width // 128)
    def _(j):
        dstrip[pl.ds(pl.multiple_of(j * 128, 128), 128), :] = jnp.zeros((128, size), F32)

    for n in range(GROUPS):
        do_ref[n] = dos[n][...].astype(F32)
    for copy in copies:
        copy.wait()

    @pl.loop(0, q_ref.shape[0] // half)
    def _(i):
        slot, late = i // 2, lax.rem(i, 2)
        owner = group_of(slot, h) * members + me
        block = jnp.where(late == 0, owner, blocks - 1 - owner)
        at = pl.ds(pl.multiple_of(i * half, half), half)
        peak, total, start = (stat_ref[i, n : n + 1, :] for n in range(3))
        first = jnp.min(start).astype(jnp.int32) // CHUNK
        start = start.astype(jnp.int32)
        qs = spread_rows(q_ref[at, :GWIDTH].astype(F32), same)
        qt, qs = qs.T.astype(BF), qs.astype(BF)
        do = do_ref[slot]
        do = jnp.where(late == 0, do[:, :half], do[:, half:])
        corr = jnp.sum(spread_columns(do * o_ref[i], same), axis=0, keepdims=True) / total
        gt = spread_columns(do, same) / total
        gs = gt.T.astype(BF)
        gt = gt.astype(BF)

        def visit(chunk, dq):
            top, last, begin = bounds(block, chunk, half, blocks, start)
            t = dot(k_ref[chunk], qt) * (HEAD_DIM**-0.5 * LOG2E) + strip_ref[pl.ds(top, CHUNK), :]
            t = jnp.where((key <= last) & (key >= begin), t - peak, LOWEST)
            e = jnp.exp2(t)
            s = e * (dot(v_ref[chunk], gt) - corr)
            low = s.astype(BF)
            dk[chunk] += dot(low, qs)
            dv[chunk] += dot(e.astype(BF), gs)
            dstrip[pl.ds(top, CHUNK), :] += s
            return dq + dot(kt_ref[chunk], low)

        dq = lax.fori_loop(first, block // per + 1, visit, jnp.zeros((GWIDTH, size), F32))
        dq_ref[at, :] = (fold_rows(dq, same, half) * HEAD_DIM**-0.5).astype(BF)

    @pl.loop(0, GROUPS)
    def _(slot):
        for j in range(members):
            for early in (True, False):
                block = place_of(slot, early, jnp.bitwise_xor(me, j), h, members, blocks)
                at = pl.ds(pl.multiple_of(lax.rem(block, per) * half, half), half)
                part = jnp.concatenate(
                    [dk[block // per, at, :] * HEAD_DIM**-0.5, dv[block // per, at, :]], axis=1
                )
                dkvs[j][slot, 0 if early else half : half if early else 2 * half, :] = part.astype(BF)

    lines = dstrip[...].T
    for n in range(GHEADS):
        x = lines[n * half : (n + 1) * half]
        rows = half
        while rows > 8:
            rows //= 2
            x = x[:rows] + pltpu.roll(x[rows:], width - rows, 1)
        sub = lax.broadcasted_iota(jnp.int32, x.shape, 0)
        for bit in (4, 2, 1):
            x = jnp.where((sub & bit) != 0, pltpu.roll(x, width - bit, 1), x)
        dline_ref[n : n + 1, :] = jnp.sum(x, axis=0, keepdims=True)


VMEM_SPEC = pl.BlockSpec(memory_space=pltpu.VMEM)
SMEM_SPEC = pl.BlockSpec(memory_space=pltpu.SMEM)
HBM_SPEC = pl.BlockSpec(memory_space=pltpu.HBM)


def in_hbm(*values):
    return [pltpu.with_memory_space_constraint(v, pltpu.HBM) for v in values]


def all_of(x):
    return pl.BlockSpec(x.shape, lambda: (0,) * len(x.shape))


def start_copies(pairs, sems):
    copies = [pltpu.make_async_copy(src, dst, sems.at[i]) for i, (src, dst) in enumerate(pairs)]
    for copy in copies:
        copy.start()
    return copies


def key_shapes(blocks, half):
    chunks = blocks * half // CHUNK
    return ((chunks, CHUNK, GWIDTH), (chunks, CHUNK, GWIDTH), (chunks, GWIDTH, CHUNK))


def attend(pos, q, kvs, strips, blocks):
    rows = q.shape[0]
    half = strips.shape[1] // GHEADS
    shapes = key_shapes(blocks, half)
    o_shape, stat_shape = (rows // half, GWIDTH, half), (rows // half, 8, GHEADS * half)
    return pl.pallas_call(
        functools.partial(forward_kernel, half, blocks, len(kvs)),
        in_specs=[SMEM_SPEC] + [VMEM_SPEC] * (1 + len(kvs)) + [HBM_SPEC],
        out_specs=[all_of(jax.ShapeDtypeStruct(o_shape, F32))]
        + [VMEM_SPEC] * GROUPS
        + [all_of(jax.ShapeDtypeStruct(stat_shape, F32))]
        + [HBM_SPEC] * 3,
        scratch_shapes=[pltpu.VMEM(s, BF) for s in shapes + shapes[2:]]
        + [pltpu.VMEM(strips.shape, F32), pltpu.SemaphoreType.DMA((3,)), pltpu.SemaphoreType.DMA((1,))],
        out_shape=[pltpu.HBM(o_shape, F32)]
        + [jax.ShapeDtypeStruct((GWIDTH, 2 * half), BF)] * GROUPS
        + [pltpu.HBM(stat_shape, F32)]
        + [pltpu.HBM(s, BF) for s in shapes],
        compiler_params=pltpu.CompilerParams(vmem_limit_bytes=32 << 20),
        cost_estimate=pl.CostEstimate(flops=10**5, bytes_accessed=10**4, transcendentals=0),
        name="attend",
    )(pos, q, *kvs, *in_hbm(strips))


def attend_back(pos, q, keys, strips, dos, o, stat, members, blocks):
    rows = q.shape[0]
    half = strips.shape[1] // GHEADS
    shapes = key_shapes(blocks, half)
    kv = jax.ShapeDtypeStruct((GROUPS, 2 * half, 2 * GWIDTH), BF)
    inputs = in_hbm(q, strips, o, stat, *keys)
    return pl.pallas_call(
        functools.partial(backward_kernel, half, blocks, members),
        in_specs=[SMEM_SPEC] + [VMEM_SPEC] * GROUPS + [HBM_SPEC] * len(inputs),
        out_specs=[VMEM_SPEC] * (1 + members) + [pl.BlockSpec((GHEADS, strips.shape[0]), lambda: (0, 0))],
        scratch_shapes=[pltpu.VMEM(x.shape, x.dtype) for x in inputs]
        + [pltpu.VMEM(s, F32) for s in shapes[:2]]
        + [
            pltpu.VMEM(strips.shape, F32),
            pltpu.VMEM((GROUPS, GWIDTH, 2 * half), F32),
            pltpu.SemaphoreType.DMA((len(inputs),)),
        ],
        out_shape=[jax.ShapeDtypeStruct((rows, GWIDTH), BF)]
        + [kv] * members
        + [pltpu.HBM((GHEADS, strips.shape[0]), F32)],
        compiler_params=pltpu.CompilerParams(vmem_limit_bytes=40 << 20),
        cost_estimate=pl.CostEstimate(flops=10**5, bytes_accessed=10**4, transcendentals=0),
        name="attend_back",
    )(pos, *dos, *inputs)


FBLOCK = 768
PIECES = 8


def three_parts(x):
    high = x.astype(BF).astype(F32)
    mid = (x - high).astype(BF).astype(F32)
    low = x - high - mid
    lane = lax.broadcasted_iota(jnp.int32, (x.shape[0], 128), 1)
    return jnp.where(lane == 0, high, jnp.where(lane == 1, mid, jnp.where(lane == 2, low, 0.0))).astype(BF)


def gather_rows(refs):
    return jnp.concatenate([r[...].astype(F32) for r in refs])


def router_kernel(
    pos, x_ref, out_ref, scale_ref, router_ref, routes_ref, place_ref, *refs
):
    lows, refs = refs[:GROUPS], refs[GROUPS:]
    pieces, (context_ref, resid_ref, moe_ref, gates_ref) = refs[:PIECES], refs[PIECES:]
    tok, width = x_ref.shape
    for k in range(GROUPS):
        row = pl.multiple_of(lax.rem(pos[1] + k, GROUPS) * GWIDTH, GWIDTH)
        context_ref[pl.ds(row, GWIDTH), :] = lows[k][...]
    context = context_ref[...].astype(F32).T.astype(BF)
    resid = x_ref[...].astype(F32) + dot(context, out_ref[...])
    resid_ref[...] = resid
    inv = lax.rsqrt(jnp.mean(resid * resid, axis=1, keepdims=True) + EPS)
    moe_in = (resid * inv * scale_ref[...]).astype(BF)
    moe_ref[...] = moe_in
    logits = dot(moe_in, router_ref[...], ((1,), (1,)))
    lane = lax.broadcasted_iota(jnp.int32, logits.shape, 1)
    chosen = [
        jnp.sum(jnp.where(routes_ref[:, k : k + 1] == lane, logits, 0.0), axis=1, keepdims=True)
        for k in range(TOP)
    ]
    most = jnp.maximum(chosen[0], chosen[1])
    powers = [jnp.exp(c - most) for c in chosen]
    gates = [p / (powers[0] + powers[1]) for p in powers]
    slot = lax.broadcasted_iota(jnp.int32, (EXPERTS * CAP, tok), 0)
    pick = [(place_ref[k : k + 1, :] == slot) for k in range(TOP)]
    rows = dot((pick[0] | pick[1]).astype(BF), moe_in)
    extra = sum(dot(pick[k].astype(BF), three_parts(gates[k])) for k in range(TOP))
    for p in range(PIECES):
        pieces[p][:, :width] = rows[p * CAP : (p + 1) * CAP].astype(BF)
        pieces[p][:, width:] = extra[p * CAP : (p + 1) * CAP].astype(BF)
    for k in range(TOP):
        gates_ref[:, k : k + 1] = gates[k]


def router(pos, x, out_full, scale, router_t, routes, places, lows):
    tok, width = x.shape
    kept = [pltpu.HBM(*s) for s in (((width, tok), BF), ((tok, width), F32), ((tok, width), BF), ((tok, TOP), F32))]
    x, out_full = in_hbm(x, out_full)
    return pl.pallas_call(
        router_kernel,
        in_specs=[SMEM_SPEC, all_of(x), all_of(out_full)] + [VMEM_SPEC] * (4 + GROUPS),
        out_specs=[VMEM_SPEC] * PIECES + [all_of(s.inner_aval) for s in kept],
        out_shape=[jax.ShapeDtypeStruct((CAP, width + 128), BF)] * PIECES + kept,
        compiler_params=pltpu.CompilerParams(vmem_limit_bytes=16 << 20),
        cost_estimate=pl.CostEstimate(flops=10**5, bytes_accessed=10**4, transcendentals=0),
        name="router",
    )(pos, x, out_full, scale, router_t, routes, places, *lows)


def expert_kernel(groups, n_fsdp, info, dy_ref, up_ref, down_ref, *refs):
    cames, refs = refs[:PIECES], refs[PIECES:]
    out_refs, (back_ref, act_ref, rows_ref, grad_in, out_acc, back_acc) = refs[:n_fsdp], refs[n_fsdp:]
    step = pl.program_id(0)
    width = grad_in.shape[1]
    h, f = info[0], info[1]
    source = [
        lax.rem(h + groups - p // n_fsdp, groups) * n_fsdp + jnp.bitwise_xor(f, p % n_fsdp) for p in range(PIECES)
    ]

    @pl.when(step == 0)
    def _():
        came = gather_rows(cames)
        gate = jnp.sum(came[:, width:], axis=1, keepdims=True)
        dy = jnp.concatenate([dy_ref[s].astype(F32) for s in source])
        grad_in[...] = dy
        rows_ref[0] = came[:, :width].astype(BF)
        rows_ref[1] = (gate * dy).astype(BF)
        out_acc[...] = jnp.zeros_like(out_acc)
        back_acc[...] = jnp.zeros_like(back_acc)

    up, down = up_ref[0], down_ref[0]
    upper = dot(rows_ref[0], up)
    active_grad = dot(rows_ref[1], down)
    cdf = 0.5 + 0.5 * lax.erf(upper * 0.7071067811865476)
    active = (upper * cdf).astype(BF)
    slope = cdf + upper * (0.3989422804014327 * jnp.exp(-0.5 * upper * upper))
    upper_grad = (active_grad * slope).astype(BF)
    act_ref[0] = upper_grad
    act_ref[1] = active
    back_acc[...] += dot(upper_grad, up, ((1,), (1,)))
    out_acc[...] += dot(active, down, ((1,), (1,)))

    @pl.when(step == pl.num_programs(0) - 1)
    def _():
        out = out_acc[...].astype(BF).astype(F32)
        gate_grad = three_parts(jnp.sum(grad_in[...] * out, axis=1, keepdims=True)).astype(F32)
        for p in range(PIECES):
            rows = slice(p * CAP, (p + 1) * CAP)
            out_refs[p % n_fsdp][(groups - p // n_fsdp) % groups] = out[rows].astype(BF)
            back_ref[source[p], :, :width] = back_acc[rows, :].astype(BF)
            back_ref[source[p], :, width:] = gate_grad[rows].astype(BF)


def expert(info, cames, dy, up, down, groups, n_fsdp):
    width, ffn = up.shape[1], up.shape[2]
    rows = EXPERTS * CAP
    whole = lambda *shape: pl.BlockSpec(shape, lambda j, info: (0,) * len(shape))
    weight = pl.BlockSpec((1, width, FBLOCK), lambda j, info: (info[0], 0, j))
    return pl.pallas_call(
        functools.partial(expert_kernel, groups, n_fsdp),
        grid_spec=pltpu.PrefetchScalarGridSpec(
            num_scalar_prefetch=1,
            grid=(ffn // FBLOCK,),
            in_specs=[whole(PIECES, CAP, width), weight, weight] + [whole(CAP, width + 128)] * PIECES,
            out_specs=[whole(groups, CAP, width)] * n_fsdp
            + [
                whole(PIECES, CAP, width + 128),
                pl.BlockSpec((2, rows, FBLOCK), lambda j, info: (0, 0, j)),
                whole(2, rows, width),
            ],
            scratch_shapes=[pltpu.VMEM((rows, width), F32)] * 3,
        ),
        out_shape=[pltpu.HBM((groups, CAP, width), BF)] * n_fsdp
        + [
            jax.ShapeDtypeStruct((PIECES, CAP, width + 128), BF),
            pltpu.HBM((2, rows, ffn), BF),
            pltpu.HBM((2, rows, width), BF),
        ],
        compiler_params=pltpu.CompilerParams(vmem_limit_bytes=32 << 20),
        cost_estimate=pl.CostEstimate(flops=10**5, bytes_accessed=10**4, transcendentals=0),
        name="expert",
    )(info, dy, *in_hbm(up, down), *cames)


def weight_kernel(count, members, side, pos, *refs):
    rows, acts, (keep_ref, pass_ref, turned, lhs) = refs[:count], refs[count : 2 * count], refs[2 * count :]
    half = keep_ref.shape[0]

    @pl.when(pl.program_id(0) == 0)
    def _():
        for n in range(count):
            turned[...] = rows[n][0].astype(F32).T.astype(BF)
            if side is not None:
                lhs[n] = turned[side * 2 * half : (side + 1) * 2 * half, :]
                continue
            unit = 2 * half // (GROUPS * members // 2)
            for r in range(members // 2):
                member = jnp.bitwise_xor(pos[0], 2 * r)
                for k in range(GROUPS):
                    row = pl.multiple_of((lax.rem(pos[1] + k, GROUPS) * members + member) * unit, 16)
                    at = (r * GROUPS + k) * unit
                    lhs[n, at : at + unit, :] = turned[pl.ds(row, unit), :]

    keep_ref[...] = sum(dot(lhs[n, :half, :], acts[n][0]) for n in range(count)).astype(BF)
    pass_ref[...] = sum(dot(lhs[n, half:, :], acts[n][0]) for n in range(count)).astype(BF)


def weight_terms(pos, rows, acts, which, members, side=None):
    _, count, width = rows[0].shape
    ffn = acts[0].shape[2]
    half = pl.BlockSpec((width // 4, FBLOCK), lambda j: (0, j))
    return pl.pallas_call(
        functools.partial(weight_kernel, len(rows), members, side),
        grid=(ffn // FBLOCK,),
        in_specs=[SMEM_SPEC]
        + [pl.BlockSpec((1, count, width), lambda j: (which, 0, 0))] * len(rows)
        + [pl.BlockSpec((1, count, FBLOCK), lambda j: (which, 0, j))] * len(rows),
        out_specs=[half, half],
        out_shape=[pltpu.HBM((width // 4, ffn), BF)] * 2,
        scratch_shapes=[pltpu.VMEM((width, count), BF), pltpu.VMEM((len(rows), width // 2, count), BF)],
        compiler_params=pltpu.CompilerParams(vmem_limit_bytes=20 << 20),
        cost_estimate=pl.CostEstimate(flops=10**5, bytes_accessed=10**4, transcendentals=0),
        name="weight_terms",
    )(pos, *rows, *in_hbm(*acts))


def add_kernel(riders, a_ref, b_ref, *refs):
    rides, outs = refs[:riders], refs[riders:]
    rows, width = a_ref.shape[0] // GROUPS, outs[0].shape[1]
    blocks = a_ref.shape[1] // width
    for k, out in enumerate(outs):
        for c in range(blocks):
            at = (slice(k * rows, (k + 1) * rows), slice(c * width, (c + 1) * width))
            out[c * rows : (c + 1) * rows, :] = (a_ref[at].astype(F32) + b_ref[at].astype(F32)).astype(BF)
        if riders:
            ride = jnp.concatenate([r[k].astype(F32) for r in rides])
            out[blocks * rows :, :] = ride.astype(BF)


def add_groups(a, b, width, rides=()):
    rows, cols = a.shape
    count = rows // GROUPS * cols // width + sum(r.shape[1] for r in rides)
    return pl.pallas_call(
        functools.partial(add_kernel, len(rides)),
        in_specs=[all_of(a)] * 2 + [all_of(r) for r in rides],
        out_specs=[pl.BlockSpec((count, width), lambda: (0, 0))] * GROUPS,
        out_shape=[jax.ShapeDtypeStruct((count, width), BF)] * GROUPS,
        compiler_params=pltpu.CompilerParams(vmem_limit_bytes=16 << 20),
        cost_estimate=pl.CostEstimate(flops=10**5, bytes_accessed=10**4, transcendentals=0),
        name="add_groups",
    )(*in_hbm(a, b, *rides))


def order_kernel(blocks, pos, *refs):
    out_ref = refs[-1]
    rows, width = out_ref.shape[1], out_ref.shape[2] // blocks
    for k in range(GROUPS):
        group = group_of(k, pos[1])
        for c in range(blocks):
            out_ref[group, :, c * width : (c + 1) * width] = refs[k][c * rows : (c + 1) * rows, :].astype(F32)


def in_order(pos, parts, rows, cols):
    width = parts[0].shape[1]
    return pl.pallas_call(
        functools.partial(order_kernel, cols // width),
        in_specs=[SMEM_SPEC] + [all_of(p) for p in parts],
        out_specs=pl.BlockSpec((GROUPS, rows, cols), lambda: (0, 0, 0)),
        out_shape=jax.ShapeDtypeStruct((GROUPS, rows, cols), F32),
        compiler_params=pltpu.CompilerParams(vmem_limit_bytes=16 << 20),
        cost_estimate=pl.CostEstimate(flops=10**5, bytes_accessed=10**4, transcendentals=0),
        name="in_order",
    )(pos, *parts)


def turn_kernel(
    info, place_ref, routes_ref, gates_ref, resid_ref, moe_ref, dy_ref, router_ref, scale_ref,
    out_ref, context_ref, back_ref, *refs,
):
    dos, (resid_grad_ref, mine_ref, other_ref, send_ref, router_grad_ref, gain_ref, term) = refs[:GROUPS], refs[GROUPS:]
    tok, width = resid_ref.shape
    back = back_ref[...]
    slots = back.shape[0]
    iota = lax.broadcasted_iota(jnp.int32, (tok, slots), 1)
    pick = [place_ref[:, k : k + 1] == iota for k in range(TOP)]
    gates = [gates_ref[:, k : k + 1] for k in range(TOP)]
    gate_grad = [jnp.sum(dot(p.astype(BF), back[:, width:]), axis=1, keepdims=True) for p in pick]
    mean = gates[0] * gate_grad[0] + gates[1] * gate_grad[1]
    lane = lax.broadcasted_iota(jnp.int32, (tok, 128), 1)
    logit_grad = sum(
        jnp.where(routes_ref[:, k : k + 1] == lane, gates[k] * (gate_grad[k] - mean), 0.0) for k in range(TOP)
    )
    grad = dot((pick[0] | pick[1]).astype(BF), back[:, :width])
    for e in range(EXPERTS):
        grad = grad + logit_grad[:, e : e + 1] * router_ref[e : e + 1, :].astype(F32)
    resid = resid_ref[...]
    inv = lax.rsqrt(jnp.mean(resid * resid, axis=1, keepdims=True) + EPS)
    gain_ref[...] = jnp.sum(grad * (resid * inv), axis=0, keepdims=True)
    scaled = grad * scale_ref[...]
    along = jnp.mean(scaled * resid, axis=1, keepdims=True)
    resid_grad = dy_ref[...].astype(F32) + inv * scaled - resid * (inv * inv * inv * along)
    resid_grad_ref[...] = resid_grad
    low = resid_grad.astype(BF)
    term[:, :tok] = dot(out_ref[...], low, ((1,), (1,)))
    for k in range(GROUPS):
        row = pl.multiple_of(lax.rem(info[0] + k, GROUPS) * GWIDTH, GWIDTH)
        dos[k][...] = term[pl.ds(row, GWIDTH), :tok].astype(BF)
    router_grad_ref[...] = lax.dot_general(
        logit_grad.T[:EXPERTS], moe_ref[...].astype(F32), (((1,), (0,)), ((), ())),
        precision=FULL, preferred_element_type=F32,
    )
    term[...] = dot(low.astype(F32).T.astype(BF), context_ref[...].astype(F32).T.astype(BF))
    rows, cols = mine_ref.shape[1:]
    core, top = info[1], info[2]
    mine = pl.ds(pl.multiple_of(top * cols, 128), cols)
    other = pl.ds(pl.multiple_of((1 - top) * cols, 128), cols)
    for g in range(mine_ref.shape[0]):
        keep = pl.ds(pl.multiple_of((2 * g + core) * rows, 8), rows)
        send = pl.ds(pl.multiple_of((2 * g + 1 - core) * rows, 8), rows)
        mine_ref[g] = term[keep, mine]
        other_ref[g] = term[keep, other]
        send_ref[0, g] = term[send, mine].astype(BF)
        send_ref[1, g] = term[send, other].astype(BF)


def turn_back(info, back, place, routes, gates, resid, moe_in, dy, router, scale, out_full, context, shards):
    tok, width = resid.shape
    rows = width // shards
    part = (shards // 2, rows, width // 2)
    gates, resid, moe_in, dy, out_full, context = in_hbm(gates, resid, moe_in, dy, out_full, context)
    inputs = (place, routes, gates, resid, moe_in, dy, router, scale, out_full, context, back)
    kept = [((tok, width), F32), (part, F32), (part, F32), ((2,) + part, BF), ((EXPERTS, width), F32), ((1, width), F32)]
    kept = [pltpu.HBM(*s) for s in kept]
    return pl.pallas_call(
        turn_kernel,
        in_specs=[SMEM_SPEC] + [all_of(x) for x in inputs],
        out_specs=[VMEM_SPEC] * GROUPS + [all_of(s.inner_aval) for s in kept],
        scratch_shapes=[pltpu.VMEM((width, width), F32)],
        out_shape=[jax.ShapeDtypeStruct((GWIDTH, tok), BF)] * GROUPS + kept,
        compiler_params=pltpu.CompilerParams(vmem_limit_bytes=24 << 20),
        cost_estimate=pl.CostEstimate(flops=10**5, bytes_accessed=10**4, transcendentals=0),
        name="turn_back",
    )(info, *inputs)


def pair_kernel(a_ref, b_ref, c_ref, d_ref, keep_ref, send_ref):
    keep_ref[...] = a_ref[...].astype(F32) + b_ref[...].astype(F32)
    send_ref[...] = (c_ref[...].astype(F32) + d_ref[...].astype(F32)).astype(BF)


def add_pairs(a, b, c, d):
    return pl.pallas_call(
        pair_kernel,
        in_specs=[VMEM_SPEC] * 4,
        out_specs=[VMEM_SPEC] * 2,
        out_shape=[jax.ShapeDtypeStruct(a.shape, F32), jax.ShapeDtypeStruct(a.shape, BF)],
        cost_estimate=pl.CostEstimate(flops=10**5, bytes_accessed=10**4, transcendentals=0),
        compiler_params=pltpu.CompilerParams(vmem_limit_bytes=8 << 20),
        name="add_pairs",
    )(a, b, c, d)


SMALL = 16


def input_kernel(
    members, buckets_here, info, dq_ref, keep_ref, came_ref, ain_ref, weight_ref, scale_ref, router_ref,
    gain_ref, line_ref, dline_ref, own_ref, one_ref, two_ref, three_ref, term_ref, sent_ref, pack_ref, dproj, term,
):
    h, core = info[0], info[1]
    width = ain_ref.shape[1]
    tok = own_ref.shape[0]
    dproj[:, :GWIDTH] = dq_ref[...].astype(F32)
    for k in range(GROUPS):
        dkv = keep_ref[k] if came_ref is None else keep_ref[k] + came_ref[k].astype(F32)
        dproj[k * tok : (k + 1) * tok, GWIDTH:] = dkv.astype(BF).astype(F32)
    low = dproj[...].astype(BF)
    ain = ain_ref[...]
    back = dot(low, weight_ref[...], ((1,), (1,)))
    own_ref[...] = back[:tok]
    for k, ref in enumerate((one_ref, two_ref, three_ref)):
        ref[...] = back[(k + 1) * tok : (k + 2) * tok].astype(BF)
    pack_ref[0:EXPERTS, :] = router_ref[...]
    pack_ref[EXPERTS : EXPERTS + 1, :] = jnp.sum(back * ain.astype(F32), axis=0, keepdims=True) / scale_ref[...]
    pack_ref[EXPERTS + 1 : EXPERTS + 2, :] = gain_ref[...]
    col = lax.broadcasted_iota(jnp.int32, (BUCKETS, width), 1)
    cols_f = width * buckets_here // BUCKETS
    within = lax.rem(col, cols_f) - h * buckets_here
    held = jnp.where((within >= 0) & (within < buckets_here), col // cols_f * buckets_here + within, -1)
    held = held == lax.broadcasted_iota(jnp.int32, (BUCKETS, width), 0)
    bucket = line_ref[...] == lax.broadcasted_iota(jnp.int32, (BUCKETS, line_ref.shape[1]), 0)
    for n in range(GHEADS):
        sums = jnp.sum(jnp.where(bucket, dline_ref[n : n + 1, :], 0.0), axis=1, keepdims=True)
        row = EXPERTS + 2 + n
        pack_ref[row : row + 1, :] = jnp.sum(jnp.where(held, sums, 0.0), axis=0, keepdims=True)
    rest = EXPERTS + 2 + GHEADS
    pack_ref[rest:, :] = jnp.zeros((SMALL - rest, width), F32)
    term[...] = dot(dproj[...].T.astype(BF), ain)
    unit = GWIDTH // members
    for t in range(3):
        for r in range(members // 2):
            at = slice((t * (members // 2) + r) * unit, (t * (members // 2) + r + 1) * unit)
            first = (t * members + 2 * r) * unit
            term_ref[at, :] = term[pl.ds(pl.multiple_of(first + core * unit, 8), unit), :]
            sent_ref[at, :] = term[pl.ds(pl.multiple_of(first + (1 - core) * unit, 8), unit), :].astype(BF)
    pack = pack_ref[...]
    high = pack.astype(BF)
    rows = term_ref.shape[0]
    sent_ref[rows : rows + SMALL, :] = high
    sent_ref[rows + SMALL :, :] = (pack - high.astype(F32)).astype(BF)


def input_back(info, members, buckets_here, dq, keep, came, ain, weight, scale, router_grad, gain_grad, line, dline):
    count, width = ain.shape
    tok = count // GROUPS
    rows = 3 * GWIDTH // 2
    ain, weight = in_hbm(ain, weight)
    inputs = [dq, keep] + ([] if came is None else [came]) + [ain, weight, scale, router_grad, gain_grad, line, dline]
    body = functools.partial(input_kernel, members, buckets_here)
    if came is None:
        body = lambda info, dq, keep, *refs: input_kernel(members, buckets_here, info, dq, keep, None, *refs)
    return pl.pallas_call(
        body,
        in_specs=[SMEM_SPEC] + [all_of(x) for x in inputs],
        out_specs=[VMEM_SPEC] * 7,
        out_shape=[jax.ShapeDtypeStruct((tok, width), F32)]
        + [jax.ShapeDtypeStruct((tok, width), BF)] * 3
        + [
            jax.ShapeDtypeStruct((rows, width), F32),
            jax.ShapeDtypeStruct((rows + 2 * SMALL, width), BF),
            jax.ShapeDtypeStruct((SMALL, width), F32),
        ],
        scratch_shapes=[pltpu.VMEM((count, 3 * GWIDTH), F32), pltpu.VMEM((3 * GWIDTH, width), F32)],
        compiler_params=pltpu.CompilerParams(vmem_limit_bytes=24 << 20),
        cost_estimate=pl.CostEstimate(flops=10**5, bytes_accessed=10**4, transcendentals=0),
        name="input_back",
    )(info, *inputs)


def together(*values):
    return lax.optimization_barrier(values)


def turn(shift):
    return [(i, (i + shift) % GROUPS) for i in range(GROUPS)]


def gather_groups(x):
    came = {k: lax.ppermute(x, "h", turn(k)) for k in (2, 1, 3)}
    return jnp.stack([x] + [came[k] for k in range(1, GROUPS)])


def gather_members(x):
    size = lax.axis_size(MEMBERS)
    held = {0: x}
    for bit in bits_of(size):
        for k in sorted(held):
            held[k | bit] = lax.ppermute(held[k], MEMBERS, xor_perm(bit, size))
    return [held[k] for k in range(size)]


def part_of(x, mine):
    low, high = jnp.split(x, 2, axis=-1)
    return jnp.where(mine == 0, low, high), jnp.where(mine == 0, high, low)


def swap(x, axis, bit):
    return lax.ppermute(x, axis, xor_perm(bit, lax.axis_size(axis)))


def two_parts(x):
    high = lax.reduce_precision(x, 8, 7)
    return jnp.concatenate([high, x - high]).astype(BF)


def from_fsdp(part):
    if lax.axis_size("fsdp") != 2:
        return lax.all_gather(part, "fsdp", axis=0)
    came = lax.ppermute(part, "fsdp", xor_perm(1, 2))
    return jnp.where(lax.axis_index("fsdp") == 0, jnp.stack([part, came]), jnp.stack([came, part]))


def group_pieces(pieces, sign):
    came = {k: lax.ppermute(pieces[k], "h", turn(sign * k)) for k in (2, 1, 3)}
    return [pieces[0]] + [came[k] for k in range(1, GROUPS)]


def deal(pieces, spread, sign):
    n_fsdp = lax.axis_size("fsdp")
    out = [pieces[0]] + [None] * (len(pieces) - 1)
    for p in (5, 4, 3, 7, 2, 6, 1):
        k, j = divmod(p, n_fsdp)
        if spread:
            pairs = [
                (g * n_fsdp + i, (g + sign * k) % GROUPS * n_fsdp + (i ^ j))
                for g in range(GROUPS)
                for i in range(n_fsdp)
            ]
            out[p] = lax.ppermute(pieces[p], ("h", "fsdp"), pairs)
        else:
            out[p] = lax.ppermute(pieces[p], "fsdp", xor_perm(j, n_fsdp))
    return out


def per_device(
    tokens, segments, routes, bucket_table, attn_gain, qkv_weight, out_weight, bias_table,
    moe_gain, router_weight, up_weight, down_weight, cotangent,
):
    tok, width = tokens.shape[1], tokens.shape[2]
    half = tok // 2
    h, m, f = lax.axis_index("h"), lax.axis_index(MEMBERS), lax.axis_index("fsdp")
    core = lax.axis_index("core")
    members, n_fsdp = lax.axis_size(MEMBERS), lax.axis_size("fsdp")
    shards = GROUPS * members
    blocks = 2 * shards
    length = shards * tok
    here = EXPERTS // n_fsdp
    spread = here > 1
    ffn = up_weight.shape[2]
    rows_f = width // n_fsdp
    rows_c = width // shards
    pos = jnp.stack([m, h]).astype(jnp.int32)

    extra = jnp.pad(segments.astype(BF), ((0, 7), (0, width - tok)))
    mixed = gather_groups(jnp.concatenate([tokens[0], extra]))

    bias_flat = bias_table.reshape(1, -1)
    bias_rows = -(-bias_flat.shape[1] // rows_f)
    bias_flat = jnp.pad(bias_flat, ((0, 0), (0, bias_rows * rows_f - bias_flat.shape[1])))
    small = jnp.concatenate(
        [attn_gain[None], moe_gain[None], router_weight.T, bias_flat.reshape(bias_rows, rows_f)]
        + [jnp.zeros((16 - 10 - bias_rows, rows_f), BF)]
    )
    small = from_fsdp(small)
    attn_scale = small[:, 0].reshape(width).astype(F32)
    moe_scale = small[:, 1].reshape(width).astype(F32)
    router_t = jnp.transpose(small[:, 2:10], (1, 0, 2)).reshape(EXPERTS, width)
    bias_full = small[:, 10 : 10 + bias_rows].reshape(n_fsdp, -1)[:, : bias_table.size]
    bias_full = bias_full.reshape(BUCKETS, HEADS)
    cut = [
        lax.dynamic_slice_in_dim(qkv_weight, n * width + h * GWIDTH, GWIDTH, 1) for n in range(3)
    ]
    qkv_heads = from_fsdp(jnp.concatenate(cut, axis=1)).reshape(width, 3 * GWIDTH)
    out_full = from_fsdp(together(out_weight, qkv_heads)[0]).reshape(width, width)

    wide = strip_width(blocks, half)
    top = half * (blocks - 1)
    line = jnp.concatenate(
        [
            bucket_table[: top + 1][::-1],
            jnp.full((wide - length,), -1, jnp.int32),
            bucket_table[top + 1 :][::-1],
        ]
    )
    hot = (line[None] == jnp.arange(BUCKETS, dtype=jnp.int32)[:, None]).astype(BF)
    bias_mine = lax.dynamic_slice_in_dim(bias_full, h * GHEADS, GHEADS, 1)
    strips = make_strips(dot(bias_mine, hot, ((0,), (0,))) * LOG2E, half)

    hot_routes = (routes.reshape(-1)[:, None] == jnp.arange(EXPERTS)[None]).astype(F32)
    earlier = jnp.arange(tok * TOP)
    earlier = (earlier[None, :] < earlier[:, None]).astype(BF)
    before = dot(earlier, hot_routes.astype(BF))
    slot = jnp.sum(before * hot_routes, axis=1).astype(jnp.int32).reshape(tok, TOP)
    group = routes % here
    natural = (group * n_fsdp + routes // here) * CAP + slot
    away = lax.rem(group - h + GROUPS, GROUPS) if spread else group
    place = (away * n_fsdp + jnp.bitwise_xor(routes // here, f)) * CAP + slot
    slots = jnp.arange(EXPERTS * CAP, dtype=jnp.int32)
    pick = [slots[:, None] == natural[None, :, k] for k in range(TOP)]
    exchange = ("h", "fsdp") if spread else ("fsdp",)

    def exchange_rows(rows):
        return lax.all_to_all(rows, exchange, 0, 0, tiled=True)

    mixed, strips = together(mixed, strips)
    ain = normalize(mixed[:, :tok].astype(F32), attn_scale).astype(BF).reshape(GROUPS * tok, width)
    proj = dot(ain, qkv_heads).astype(BF)
    kv = proj[:, GWIDTH:].reshape(GROUPS, tok, 2 * GWIDTH)
    kvs = gather_members(jnp.concatenate([kv, mixed[:, tok:, : 2 * GWIDTH]], axis=1))
    dy_send = dot((pick[0] | pick[1]).astype(BF), cotangent[0]).astype(BF).reshape(PIECES, CAP, width)
    dy_slots = exchange_rows(together(dy_send, proj)[0])
    o_pre, *rest = attend(pos, proj, kvs, strips, blocks)
    lows, stat, keys = rest[:GROUPS], rest[GROUPS], rest[GROUPS + 1 :]
    lows[1], dy_slots = together(lows[1], dy_slots)
    *pieces, context, residual, moe_in, gates = router(
        pos, tokens[0], out_full, moe_scale[None], router_t, routes, place.T, group_pieces(lows, -1)
    )

    came = deal(pieces, spread, 1)
    info = jnp.stack([h if spread else jnp.zeros_like(h), f]).astype(jnp.int32)
    *outs, back, act, rows = expert(
        info, came, dy_slots, up_weight, down_weight, GROUPS if spread else 1, n_fsdp
    )
    back = exchange_rows(back).reshape(EXPERTS * CAP, -1)

    staged = spread and members == 4
    if staged:
        rows, acts = [rows, swap(rows, "core", 1)], [act, swap(act, "core", 1)]
        terms = [weight_terms(pos, rows, acts, n, members) for n in range(2)]
        back, terms = together(back, terms)
    else:
        terms = [weight_terms(pos, [rows], [act], n, members, side) for n in range(2) for side in range(2)]

    top_bit = n_fsdp // 2
    info = jnp.stack([h, core, (f // top_bit) % 2]).astype(jnp.int32)
    *dos, resid_grad, out_mine, out_other, out_send, router_grad, moe_gain_grad = turn_back(
        info, back, natural, routes, gates, residual, moe_in, cotangent[0], router_t,
        moe_scale[None], out_full, context, shards,
    )
    dos = group_pieces(dos, 1)
    out_came = swap(out_send, "core", 1)
    out_far = (out_other + out_came[1].astype(F32)).astype(BF)
    outs = [outs[0]] + [lax.ppermute(outs[j], "fsdp", xor_perm(j, n_fsdp)) for j in range(1, n_fsdp)]
    dos[0], out_far = together(dos[0], out_far)
    out_far = swap(out_far, "fsdp", top_bit)
    dq, *dkvs, dline = attend_back(pos, proj, keys, strips, dos, o_pre, stat, members, blocks)
    dkvs[1], out_far, outs = together(dkvs[1], out_far, outs)
    cames = [swap(dkvs[k], "core", 1) for k in range(1, members, 2)]
    sends = []
    if members == 4:
        keep, send = add_pairs(dkvs[0], cames[0], dkvs[2], cames[1])
        if staged:
            sends = [swap(terms[0][1], "r", 1)]
            send, sends[0] = together(send, sends[0])
        came = swap(send, "r", 1)
    else:
        held = {k: dkvs[k].astype(F32) + cames[k // 2].astype(F32) for k in range(0, members, 2)}
        bit = 2
        while bit < members:
            for k in [k for k in sorted(held) if k & bit]:
                held[k - bit] = held[k - bit] + swap(held.pop(k).astype(BF), "r", bit // 2).astype(F32)
            bit *= 2
        keep, came = held[0], None
    if staged:
        up_came = group_pieces(add_groups(terms[0][0], sends[0], width, outs), 1)
        sends.append(swap(together(terms[1][1], came)[0], "r", 1))
        came, up_came[2] = together(came, up_came[2])

    own_back, back_1, back_2, back_3, term, sent, pack = input_back(
        jnp.stack([h, core]).astype(jnp.int32), members, BUCKETS // n_fsdp, dq, keep, came, ain, qkv_heads,
        attn_scale[None], router_grad, moe_gain_grad, line[None], dline,
    )

    def swap_both(send, pack, axis, bit):
        sent = jnp.concatenate([send.reshape(-1, send.shape[-1]).astype(BF), two_parts(pack)])
        return split_rows(swap(sent, axis, bit).astype(F32), send.shape)

    def split_rows(came, shape):
        return came[: -2 * SMALL].reshape(shape), came[-2 * SMALL : -SMALL] + came[-SMALL:]

    unit = GWIDTH // members
    came, pack_came = split_rows(swap(sent, "core", 1).astype(F32), term.shape)
    term, pack = term + came, pack + pack_came
    out_term = out_mine + out_came[0].astype(F32) + out_far.astype(F32)
    for bit in list(bits_of(n_fsdp))[1:]:
        out_term, out_send = part_of(out_term, (f // bit) % 2)
        out_term = out_term + swap(out_send.astype(BF), "fsdp", bit).astype(F32)
    for bit in bits_of(n_fsdp):
        term, send = part_of(term, (f // bit) % 2)
        pack, pack_send = part_of(pack, (f // bit) % 2)
        came, pack_came = swap_both(send, pack_send, "fsdp", bit)
        term, pack = term + came, pack + pack_came
    term = jnp.concatenate(
        [term.reshape(3, members // 2, unit, rows_f).swapaxes(0, 1).reshape(members // 2, -1, rows_f)]
        + [out_term.reshape(GROUPS, members // 2, rows_c, rows_f).swapaxes(0, 1).reshape(members // 2, -1, rows_f)],
        axis=1,
    )
    if staged:
        term, sends[1], up_came = together(term, sends[1], up_came)
    for bit in bits_of(members // 2):
        mine = (lax.axis_index("r") // bit) % 2
        term = term.reshape((2, -1) + term.shape[1:])
        came, pack_came = swap_both(lax.dynamic_index_in_dim(term, 1 - mine, 0, False), pack, "r", bit)
        term = lax.dynamic_index_in_dim(term, mine, 0, False) + came
        pack = pack + pack_came
    term = term[0]
    if staged:
        back_2, back_3, up_came = together(back_2, back_3, up_came)
    mid = lax.ppermute(back_2, "h", turn(-1))
    side = lax.ppermute(back_3, "h", turn(1)).astype(F32)
    mid = (back_1.astype(F32) + mid.astype(F32)).astype(BF)
    mid = lax.ppermute(mid, "h", turn(-1)).astype(F32)
    attn_in_grad = own_back + side + mid
    x = tokens[0].astype(F32)
    token_grad = jax.vjp(lambda v: normalize(v, attn_scale), x)[1](attn_in_grad)[0]
    tokens_grad = (resid_grad + token_grad).astype(BF)

    out_term = term[3 * unit :].reshape(GROUPS, rows_c, rows_f)
    term = term[: 3 * unit].astype(BF).reshape(3, unit, rows_f)
    if staged:
        down_came = group_pieces(add_groups(terms[1][0], sends[1], width), 1)
    out_sum, pack_sum = lax.dynamic_index_in_dim(out_term, h, 0, False), pack
    for k in (2, 1, 3):
        piece = lax.dynamic_index_in_dim(out_term, lax.rem(h + k, GROUPS), 0, False)
        came = lax.ppermute(jnp.concatenate([piece.astype(BF), two_parts(pack)]), "h", turn(k)).astype(F32)
        out_sum = out_sum + came[:rows_c]
        pack_sum = pack_sum + came[rows_c : rows_c + SMALL] + came[rows_c + SMALL :]
    at = h * members + m
    parts = []
    for r in range(3):
        pairs = [((3 * d + r) % shards, d) for d in range(shards)]
        third = pow(3, -1, shards)
        which = (3 * lax.rem((at + shards - r) * third, shards) + r) // shards
        parts.append(lax.ppermute(lax.dynamic_index_in_dim(term, which, 0, False), CTX, pairs))
    if staged:
        up_came, parts = together(up_came, parts)
        grads = [in_order(pos, part, rows_c, ffn) for part in (up_came, down_came)]
        home = jnp.concatenate([part[rows_c * ffn // width :] for part in up_came])
    else:
        terms = [jnp.concatenate(terms[n] + terms[n + 1]) for n in (0, 2)]
        grads = [
            lax.psum_scatter(term, CTX, scatter_dimension=0, tiled=True)[None].astype(F32) for term in terms
        ]
        home = jnp.concatenate([o.reshape(-1, width) for o in outs])
    qkv_grad = jnp.concatenate(parts).astype(F32).T

    away = lax.rem(h - group + GROUPS, GROUPS) if spread else group
    place = (away * n_fsdp + jnp.bitwise_xor(routes // here, f)) * CAP + slot
    layer_out = residual
    for k in range(TOP):
        row = (slots[:, None] == place[None, :, k]).astype(BF)
        layer_out = layer_out + gates[:, k : k + 1] * dot(row, home, ((0,), (0,)))
    bias_grad = pack_sum[EXPERTS + 2 : EXPERTS + 2 + GHEADS, : GROUPS * BUCKETS // n_fsdp]
    bias_grad = bias_grad.reshape(GHEADS, GROUPS, BUCKETS // n_fsdp).transpose(2, 1, 0).reshape(-1, HEADS)
    return (
        layer_out.astype(BF)[None],
        tokens_grad[None],
        pack_sum[8],
        qkv_grad,
        out_sum.T,
        bias_grad,
        pack_sum[9],
        pack_sum[:8].T,
        grads[0],
        grads[1],
    )


def solution(mesh):
    n_ctx, n_fsdp = mesh.shape["ctx"], mesh.shape["fsdp"]
    cut = mesh.devices.reshape(GROUPS, n_ctx // (2 * GROUPS), 2, n_fsdp)
    row = P("fsdp", CTX, None)
    return jax.shard_map(
        per_device,
        mesh=Mesh(cut, CTX + ("fsdp",)),
        in_specs=(
            row,
            P("fsdp", CTX),
            P(CTX + ("fsdp",), None),
            P(),
            P("fsdp"),
            P("fsdp", None),
            P("fsdp", None),
            P("fsdp", None),
            P("fsdp"),
            P("fsdp", None),
            P("fsdp", None, None),
            P("fsdp", None, None),
            row,
        ),
        out_specs=(
            row,
            row,
            P("fsdp"),
            P("fsdp", CTX),
            P("fsdp", CTX),
            P("fsdp", None),
            P("fsdp"),
            P("fsdp", None),
            row,
            row,
        ),
        check_vma=False,
    )
```

```python
import functools

import jax
import jax.numpy as jnp
from jax import lax
from jax.experimental import pallas as pl
from jax.experimental.pallas import tpu as pltpu
from jax.sharding import Mesh, PartitionSpec as P

HEADS = 12
HEAD_DIM = 64
EXPERTS = 8
TOP = 2
BUCKETS = 32
DOCS = 8
CAP = 40
GROUPS = 4
GHEADS = HEADS // GROUPS
GWIDTH = GHEADS * HEAD_DIM
CHUNK = 256

LOG2E = 1.4426950408889634
EPS = 1e-06
LOWEST = -1e30
FULL = lax.Precision.HIGHEST
BF = jnp.bfloat16
F32 = jnp.float32
MEMBERS = ("r", "core")
CTX = ("h", "r", "core")


def normalize(values, weight):
    inv_rms = lax.rsqrt(jnp.mean(values * values, axis=-1, keepdims=True) + EPS)
    return values * inv_rms * weight


def dot(a, b, dims=((1,), (0,))):
    return lax.dot_general(a, b, (dims, ((), ())), preferred_element_type=F32)


def exact_dot(a, b, dims):
    return lax.dot_general(a, b, (dims, ((), ())), precision=FULL)


def xor_perm(mask, size):
    return [(i, i ^ mask) for i in range(size)]


def bits_of(size):
    bit = size // 2
    while bit:
        yield bit
        bit //= 2


def strip_width(blocks, half):
    need = half * (blocks - 1) + CHUNK + half
    return -(-need // 128) * 128


def strips_kernel(g_ref, out_ref):
    half = out_ref.shape[1] // GHEADS
    rolled = [
        pltpu.roll(
            jnp.broadcast_to(g_ref[n : n + 1, :], (half, g_ref.shape[1])), 0, 1, stride=1, stride_axis=0
        )
        for n in range(GHEADS)
    ]
    out_ref[...] = jnp.concatenate(rolled).T


def make_strips(lines, half):
    return pl.pallas_call(
        strips_kernel,
        out_specs=pl.BlockSpec((lines.shape[1], GHEADS * half), lambda: (0, 0)),
        out_shape=pltpu.HBM((lines.shape[1], GHEADS * half), F32),
        cost_estimate=pl.CostEstimate(flops=10**5, bytes_accessed=10**4, transcendentals=0),
        name="strips",
    )(lines)


def own_blocks(size, half):
    a = lax.broadcasted_iota(jnp.int32, (size, size), 0) // half
    b = lax.broadcasted_iota(jnp.int32, (size, size), 1) // half
    return a == b


def spread_rows(x, same):
    return jnp.where(same, jnp.concatenate([x] * GHEADS), 0.0)


def identity(size):
    a, b = (lax.broadcasted_iota(jnp.int32, (size, size), n) for n in range(2))
    return jnp.where(a == b, 1.0, 0.0).astype(BF)


def own_columns(x, half):
    return jnp.concatenate(
        [x[n * HEAD_DIM : (n + 1) * HEAD_DIM, n * half : (n + 1) * half] for n in range(GHEADS)]
    )


def fold_rows(x, same, half):
    y = jnp.where(same, x, 0.0).T
    return sum(y[n * half : (n + 1) * half] for n in range(GHEADS))


def spread_columns(x, same):
    return jnp.where(same, jnp.concatenate([x] * GHEADS, axis=1), 0.0)


def group_of(slot, h):
    return lax.rem(h + GROUPS - slot, GROUPS)


def place_of(slot, early, me, h, members, blocks):
    owner = group_of(slot, h) * members + me
    return owner if early else blocks - 1 - owner


def bounds(block, chunk, half, blocks, start):
    top = (blocks - 1 - (block - (CHUNK // half) * chunk)) * half
    lane = lax.broadcasted_iota(jnp.int32, (1, GHEADS * half), 1)
    last = block * half + lax.rem(lane, half) - chunk * CHUNK
    return pl.multiple_of(top, half), last, start - chunk * CHUNK


def forward_kernel(half, blocks, members, pos, q_ref, *refs):
    kvs, refs = refs[:members], refs[members:]
    strip_in, o_ref, *lows, stat_ref, k_out, v_out, kt_out, k_ref, v_ref, kt_ref, vt, strip_ref, low, sems, strip_sem = refs
    loads = start_copies([(strip_in, strip_ref)], strip_sem)
    size = GHEADS * half
    me, h = pos[0], pos[1]
    tok = 2 * half
    same = own_blocks(size, half)
    key = lax.broadcasted_iota(jnp.int32, (CHUNK, size), 0)
    per = CHUNK // half

    @pl.loop(0, GROUPS)
    def _(slot):
        for j in range(members):
            for early in (True, False):
                block = place_of(slot, early, jnp.bitwise_xor(me, j), h, members, blocks)
                at = pl.ds(pl.multiple_of(lax.rem(block, per) * half, half), half)
                rows = kvs[j][slot, 0 if early else half : half if early else tok, :]
                k_ref[block // per, at, :] = rows[:, :GWIDTH]
                v_ref[block // per, at, :] = rows[:, GWIDTH:]

    eye = identity(GWIDTH)

    @pl.loop(0, blocks // per, unroll=4)
    def _(chunk):
        kt_ref[chunk] = dot(eye, k_ref[chunk], ((1,), (1,))).astype(BF)
        vt[chunk] = dot(eye, v_ref[chunk], ((1,), (1,))).astype(BF)

    copies = start_copies([(k_ref, k_out), (v_ref, v_out), (kt_ref, kt_out)], sems)
    docs = jnp.concatenate([kv[a, tok : tok + 1, :tok].astype(F32) for kv in kvs for a in range(GROUPS)])
    begins = [jnp.sum(jnp.where(docs < s, 1.0, 0.0)) for s in range(1, DOCS)]
    for load in loads:
        load.wait()

    def prepare(slot, late):
        owner = group_of(slot, h) * members + me
        block = owner if late == 0 else blocks - 1 - owner
        at = pl.ds(pl.multiple_of(slot * tok + late * half, half), half)
        qs = spread_rows(q_ref[at, :GWIDTH].astype(F32), same).astype(BF)
        qt = dot(eye, qs, ((1,), (1,))).astype(BF)
        doc = kvs[0][slot, tok : tok + 1, :tok].astype(F32)[:, late * half : (late + 1) * half]
        begin = jnp.zeros((1, half), F32)
        for s in range(1, DOCS):
            begin = jnp.where(doc == s, begins[s - 1], begin)
        first = jnp.min(begin).astype(jnp.int32) // CHUNK
        begin = jnp.concatenate([begin] * GHEADS, axis=1)
        return block, first, block // per, begin, qt

    def advance(state, step, carry):
        block, first, final, begin, qt = state
        peak, total, acc = carry
        chunk = jnp.minimum(first + step, final)
        top, last, begin = bounds(block, chunk, half, blocks, begin.astype(jnp.int32))
        last = jnp.where(first + step <= final, last, -1)
        t = dot(k_ref[chunk], qt) * (HEAD_DIM**-0.5 * LOG2E) + strip_ref[pl.ds(top, CHUNK), :]
        t = jnp.where((key <= last) & (key >= begin), t, LOWEST)
        new = jnp.maximum(peak, jnp.ceil(jnp.max(t, axis=0, keepdims=True)))
        e = jnp.exp2(t - new)
        fade = jnp.exp2(peak - new)
        total = total * fade + jnp.sum(e, axis=0, keepdims=True)
        acc = acc * fade + dot(vt[chunk], e.astype(BF))
        return new, total, acc

    init = (
        jnp.full((1, size), LOWEST, F32),
        jnp.zeros((1, size), F32),
        jnp.zeros((GWIDTH, size), F32),
    )

    def pair_of(pair, late):
        slots = [group_of(2 * pair + n, h) for n in range(2)]
        states = [prepare(slot, late) for slot in slots]
        steps = functools.reduce(jnp.maximum, [s[2] - s[1] + 1 for s in states])
        done = lax.fori_loop(
            0, steps, lambda i, c: tuple(advance(s, i, x) for s, x in zip(states, c)), (init,) * 2
        )
        for slot, state, (peak, total, acc) in zip(slots, states, done):
            out = own_columns(acc / total, half)
            o_ref[2 * slot + late] = out
            low[slot, :, late * half : (late + 1) * half] = out.astype(BF)
            stat_ref[2 * slot + late, 0:1, :] = peak
            stat_ref[2 * slot + late, 1:2, :] = total
            stat_ref[2 * slot + late, 2:3, :] = state[3]

    @pl.loop(0, GROUPS // 2)
    def _(pair):
        pair_of(pair, 0)
        pair_of(pair, 1)

    for n in range(GROUPS):
        lows[n][...] = low[n]
    for copy in copies:
        copy.wait()


def backward_kernel(half, blocks, members, pos, *refs):
    dos, refs = refs[:GROUPS], refs[GROUPS:]
    inputs, (dq_ref, *refs) = refs[:7], refs[7:]
    dkvs, refs = refs[:members], refs[members:]
    dline_ref, *held, dk, dv, dstrip, do_ref, sems = refs
    q_ref, strip_ref, o_ref, stat_ref, k_ref, v_ref, kt_ref = held
    size = GHEADS * half
    me, h = pos[0], pos[1]
    width = dstrip.shape[0]
    per = CHUNK // half
    copies = start_copies(list(zip(inputs, held)), sems)
    same = own_blocks(size, half)
    key = lax.broadcasted_iota(jnp.int32, (CHUNK, size), 0)

    @pl.loop(0, blocks // per)
    def _(chunk):
        dk[chunk] = jnp.zeros(dk.shape[1:], F32)
        dv[chunk] = jnp.zeros(dv.shape[1:], F32)

    @pl.loop(0, width // 128)
    def _(j):
        dstrip[pl.ds(pl.multiple_of(j * 128, 128), 128), :] = jnp.zeros((128, size), F32)

    for n in range(GROUPS):
        do_ref[n] = dos[n][...].astype(F32)
    for copy in copies:
        copy.wait()

    def prepare(slot, late):
        i = 2 * slot + late
        owner = group_of(slot, h) * members + me
        block = owner if late == 0 else blocks - 1 - owner
        at = pl.ds(pl.multiple_of(slot * 2 * half + late * half, half), half)
        peak, total, start = (stat_ref[i, n : n + 1, :] for n in range(3))
        first = jnp.min(start).astype(jnp.int32) // CHUNK
        qs = spread_rows(q_ref[at, :GWIDTH].astype(F32), same)
        qt, qs = qs.T.astype(BF), qs.astype(BF)
        do = do_ref[slot][:, late * half : (late + 1) * half]
        corr = jnp.sum(spread_columns(do * o_ref[i], same), axis=0, keepdims=True) / total
        gt = spread_columns(do, same) / total
        gs = gt.T.astype(BF)
        return block, first, block // per, start.astype(jnp.int32), peak, corr, qt, qs, gt.astype(BF), gs, at

    def scores(state, step):
        block, first, final, start, peak, corr, qt, _, gt = state[:9]
        chunk = jnp.minimum(first + step, final)
        top, last, begin = bounds(block, chunk, half, blocks, start)
        last = jnp.where(first + step <= final, last, -1)
        t = dot(k_ref[chunk], qt) * (HEAD_DIM**-0.5 * LOG2E) + strip_ref[pl.ds(top, CHUNK), :]
        t = jnp.where((key <= last) & (key >= begin), t - peak, LOWEST)
        e = jnp.exp2(t)
        return chunk, top, e.astype(BF), e * (dot(v_ref[chunk], gt) - corr)

    def pair_of(pair, late):
        states = [prepare(group_of(2 * pair + n, h), late) for n in range(2)]

        def visit(step, carry):
            found = [scores(s, step) for s in states]
            out = []
            for (chunk, top, e, s), state, dq in zip(found, states, carry):
                low = s.astype(BF)
                dk[chunk] += dot(low, state[7])
                dv[chunk] += dot(e, state[9])
                dstrip[pl.ds(top, CHUNK), :] += s
                out.append(dq + dot(kt_ref[chunk], low))
            return tuple(out)

        steps = functools.reduce(jnp.maximum, [s[2] - s[1] + 1 for s in states])
        done = lax.fori_loop(0, steps, visit, (jnp.zeros((GWIDTH, size), F32),) * 2)
        for state, dq in zip(states, done):
            dq_ref[state[10], :] = (fold_rows(dq, same, half) * HEAD_DIM**-0.5).astype(BF)

    @pl.loop(0, GROUPS // 2)
    def _(pair):
        pair_of(pair, 0)
        pair_of(pair, 1)

    @pl.loop(0, GROUPS)
    def _(slot):
        for j in range(members):
            for early in (True, False):
                block = place_of(slot, early, jnp.bitwise_xor(me, j), h, members, blocks)
                at = pl.ds(pl.multiple_of(lax.rem(block, per) * half, half), half)
                part = jnp.concatenate(
                    [dk[block // per, at, :] * HEAD_DIM**-0.5, dv[block // per, at, :]], axis=1
                )
                dkvs[j][slot, 0 if early else half : half if early else 2 * half, :] = part.astype(BF)

    lines = dstrip[...].T
    for n in range(GHEADS):
        x = lines[n * half : (n + 1) * half]
        rows = half
        while rows > 8:
            rows //= 2
            x = x[:rows] + pltpu.roll(x[rows:], width - rows, 1)
        sub = lax.broadcasted_iota(jnp.int32, x.shape, 0)
        for bit in (4, 2, 1):
            x = jnp.where((sub & bit) != 0, pltpu.roll(x, width - bit, 1), x)
        dline_ref[n : n + 1, :] = jnp.sum(x, axis=0, keepdims=True)


VMEM_SPEC = pl.BlockSpec(memory_space=pltpu.VMEM)
SMEM_SPEC = pl.BlockSpec(memory_space=pltpu.SMEM)
HBM_SPEC = pl.BlockSpec(memory_space=pltpu.HBM)


def in_hbm(*values):
    return [pltpu.with_memory_space_constraint(v, pltpu.HBM) for v in values]


def all_of(x):
    return pl.BlockSpec(x.shape, lambda: (0,) * len(x.shape))


def start_copies(pairs, sems):
    copies = [pltpu.make_async_copy(src, dst, sems.at[i]) for i, (src, dst) in enumerate(pairs)]
    for copy in copies:
        copy.start()
    return copies


def key_shapes(blocks, half):
    chunks = blocks * half // CHUNK
    return ((chunks, CHUNK, GWIDTH), (chunks, CHUNK, GWIDTH), (chunks, GWIDTH, CHUNK))


def attend(pos, q, kvs, strips, blocks):
    rows = q.shape[0]
    half = strips.shape[1] // GHEADS
    shapes = key_shapes(blocks, half)
    o_shape, stat_shape = (rows // half, GWIDTH, half), (rows // half, 8, GHEADS * half)
    return pl.pallas_call(
        functools.partial(forward_kernel, half, blocks, len(kvs)),
        in_specs=[SMEM_SPEC] + [VMEM_SPEC] * (1 + len(kvs)) + [HBM_SPEC],
        out_specs=[all_of(jax.ShapeDtypeStruct(o_shape, F32))]
        + [VMEM_SPEC] * GROUPS
        + [all_of(jax.ShapeDtypeStruct(stat_shape, F32))]
        + [HBM_SPEC] * 3,
        scratch_shapes=[pltpu.VMEM(s, BF) for s in shapes + shapes[2:]]
        + [
            pltpu.VMEM(strips.shape, F32),
            pltpu.VMEM((GROUPS, GWIDTH, 2 * half), BF),
            pltpu.SemaphoreType.DMA((3,)),
            pltpu.SemaphoreType.DMA((1,)),
        ],
        out_shape=[pltpu.HBM(o_shape, F32)]
        + [jax.ShapeDtypeStruct((GWIDTH, 2 * half), BF)] * GROUPS
        + [pltpu.HBM(stat_shape, F32)]
        + [pltpu.HBM(s, BF) for s in shapes],
        compiler_params=pltpu.CompilerParams(vmem_limit_bytes=32 << 20),
        cost_estimate=pl.CostEstimate(flops=10**5, bytes_accessed=10**4, transcendentals=0),
        name="attend",
    )(pos, q, *kvs, *in_hbm(strips))


def attend_back(pos, q, keys, strips, dos, o, stat, members, blocks):
    rows = q.shape[0]
    half = strips.shape[1] // GHEADS
    shapes = key_shapes(blocks, half)
    kv = jax.ShapeDtypeStruct((GROUPS, 2 * half, 2 * GWIDTH), BF)
    inputs = in_hbm(q, strips, o, stat, *keys)
    return pl.pallas_call(
        functools.partial(backward_kernel, half, blocks, members),
        in_specs=[SMEM_SPEC] + [VMEM_SPEC] * GROUPS + [HBM_SPEC] * len(inputs),
        out_specs=[VMEM_SPEC] * (1 + members) + [pl.BlockSpec((GHEADS, strips.shape[0]), lambda: (0, 0))],
        scratch_shapes=[pltpu.VMEM(x.shape, x.dtype) for x in inputs]
        + [pltpu.VMEM(s, F32) for s in shapes[:2]]
        + [
            pltpu.VMEM(strips.shape, F32),
            pltpu.VMEM((GROUPS, GWIDTH, 2 * half), F32),
            pltpu.SemaphoreType.DMA((len(inputs),)),
        ],
        out_shape=[jax.ShapeDtypeStruct((rows, GWIDTH), BF)]
        + [kv] * members
        + [pltpu.HBM((GHEADS, strips.shape[0]), F32)],
        compiler_params=pltpu.CompilerParams(vmem_limit_bytes=40 << 20),
        cost_estimate=pl.CostEstimate(flops=10**5, bytes_accessed=10**4, transcendentals=0),
        name="attend_back",
    )(pos, *dos, *inputs)


FBLOCK = 768
PIECES = 8


def three_parts(x):
    high = x.astype(BF).astype(F32)
    mid = (x - high).astype(BF).astype(F32)
    low = x - high - mid
    lane = lax.broadcasted_iota(jnp.int32, (x.shape[0], 128), 1)
    return jnp.where(lane == 0, high, jnp.where(lane == 1, mid, jnp.where(lane == 2, low, 0.0))).astype(BF)


def gather_rows(refs):
    return jnp.concatenate([r[...].astype(F32) for r in refs])


def router_kernel(
    pos, x_ref, out_ref, scale_ref, router_ref, routes_ref, place_ref, *refs
):
    lows, refs = refs[:GROUPS], refs[GROUPS:]
    pieces, (context_ref, resid_ref, moe_ref, gates_ref) = refs[:PIECES], refs[PIECES:]
    tok, width = x_ref.shape
    for k in range(GROUPS):
        row = pl.multiple_of(lax.rem(pos[1] + k, GROUPS) * GWIDTH, GWIDTH)
        context_ref[pl.ds(row, GWIDTH), :] = lows[k][...]
    context = context_ref[...].astype(F32).T.astype(BF)
    resid = x_ref[...].astype(F32) + dot(context, out_ref[...])
    resid_ref[...] = resid
    inv = lax.rsqrt(jnp.mean(resid * resid, axis=1, keepdims=True) + EPS)
    moe_in = (resid * inv * scale_ref[...]).astype(BF)
    moe_ref[...] = moe_in
    logits = dot(moe_in, router_ref[...], ((1,), (1,)))
    lane = lax.broadcasted_iota(jnp.int32, logits.shape, 1)
    chosen = [
        jnp.sum(jnp.where(routes_ref[:, k : k + 1] == lane, logits, 0.0), axis=1, keepdims=True)
        for k in range(TOP)
    ]
    most = jnp.maximum(chosen[0], chosen[1])
    powers = [jnp.exp(c - most) for c in chosen]
    gates = [p / (powers[0] + powers[1]) for p in powers]
    slot = lax.broadcasted_iota(jnp.int32, (EXPERTS * CAP, tok), 0)
    pick = [(place_ref[k : k + 1, :] == slot) for k in range(TOP)]
    rows = dot((pick[0] | pick[1]).astype(BF), moe_in)
    extra = sum(dot(pick[k].astype(BF), three_parts(gates[k])) for k in range(TOP))
    for p in range(PIECES):
        pieces[p][:, :width] = rows[p * CAP : (p + 1) * CAP].astype(BF)
        pieces[p][:, width:] = extra[p * CAP : (p + 1) * CAP].astype(BF)
    for k in range(TOP):
        gates_ref[:, k : k + 1] = gates[k]


def router(pos, x, out_full, scale, router_t, routes, places, lows):
    tok, width = x.shape
    kept = [pltpu.HBM(*s) for s in (((width, tok), BF), ((tok, width), F32), ((tok, width), BF), ((tok, TOP), F32))]
    x, out_full = in_hbm(x, out_full)
    return pl.pallas_call(
        router_kernel,
        in_specs=[SMEM_SPEC, all_of(x), all_of(out_full)] + [VMEM_SPEC] * (4 + GROUPS),
        out_specs=[VMEM_SPEC] * PIECES + [all_of(s.inner_aval) for s in kept],
        out_shape=[jax.ShapeDtypeStruct((CAP, width + 128), BF)] * PIECES + kept,
        compiler_params=pltpu.CompilerParams(vmem_limit_bytes=16 << 20),
        cost_estimate=pl.CostEstimate(flops=10**5, bytes_accessed=10**4, transcendentals=0),
        name="router",
    )(pos, x, out_full, scale, router_t, routes, places, *lows)


def expert_kernel(groups, n_fsdp, info, dy_ref, up_ref, down_ref, *refs):
    cames, refs = refs[:PIECES], refs[PIECES:]
    out_refs, (back_ref, act_ref, rows_ref, grad_in, out_acc, back_acc) = refs[:n_fsdp], refs[n_fsdp:]
    step = pl.program_id(0)
    width = grad_in.shape[1]
    h, f = info[0], info[1]
    source = [
        lax.rem(h + groups - p // n_fsdp, groups) * n_fsdp + jnp.bitwise_xor(f, p % n_fsdp) for p in range(PIECES)
    ]

    @pl.when(step == 0)
    def _():
        came = gather_rows(cames)
        gate = jnp.sum(came[:, width:], axis=1, keepdims=True)
        dy = jnp.concatenate([dy_ref[s].astype(F32) for s in source])
        grad_in[...] = dy
        rows_ref[0] = came[:, :width].astype(BF)
        rows_ref[1] = (gate * dy).astype(BF)
        out_acc[...] = jnp.zeros_like(out_acc)
        back_acc[...] = jnp.zeros_like(back_acc)

    up, down = up_ref[0], down_ref[0]
    upper = dot(rows_ref[0], up)
    active_grad = dot(rows_ref[1], down)
    cdf = 0.5 + 0.5 * lax.erf(upper * 0.7071067811865476)
    active = (upper * cdf).astype(BF)
    slope = cdf + upper * (0.3989422804014327 * jnp.exp(-0.5 * upper * upper))
    upper_grad = (active_grad * slope).astype(BF)
    act_ref[0] = upper_grad
    act_ref[1] = active
    back_acc[...] += dot(upper_grad, up, ((1,), (1,)))
    out_acc[...] += dot(active, down, ((1,), (1,)))

    @pl.when(step == pl.num_programs(0) - 1)
    def _():
        out = out_acc[...].astype(BF).astype(F32)
        gate_grad = three_parts(jnp.sum(grad_in[...] * out, axis=1, keepdims=True)).astype(F32)
        for p in range(PIECES):
            rows = slice(p * CAP, (p + 1) * CAP)
            out_refs[p % n_fsdp][(groups - p // n_fsdp) % groups] = out[rows].astype(BF)
            back_ref[source[p], :, :width] = back_acc[rows, :].astype(BF)
            back_ref[source[p], :, width:] = gate_grad[rows].astype(BF)


def expert(info, cames, dy, up, down, groups, n_fsdp):
    width, ffn = up.shape[1], up.shape[2]
    rows = EXPERTS * CAP
    whole = lambda *shape: pl.BlockSpec(shape, lambda j, info: (0,) * len(shape))
    weight = pl.BlockSpec((1, width, FBLOCK), lambda j, info: (info[0], 0, j))
    return pl.pallas_call(
        functools.partial(expert_kernel, groups, n_fsdp),
        grid_spec=pltpu.PrefetchScalarGridSpec(
            num_scalar_prefetch=1,
            grid=(ffn // FBLOCK,),
            in_specs=[whole(PIECES, CAP, width), weight, weight] + [whole(CAP, width + 128)] * PIECES,
            out_specs=[whole(groups, CAP, width)] * n_fsdp
            + [
                whole(PIECES, CAP, width + 128),
                pl.BlockSpec((2, rows, FBLOCK), lambda j, info: (0, 0, j)),
                whole(2, rows, width),
            ],
            scratch_shapes=[pltpu.VMEM((rows, width), F32)] * 3,
        ),
        out_shape=[pltpu.HBM((groups, CAP, width), BF)] * n_fsdp
        + [
            jax.ShapeDtypeStruct((PIECES, CAP, width + 128), BF),
            pltpu.HBM((2, rows, ffn), BF),
            pltpu.HBM((2, rows, width), BF),
        ],
        compiler_params=pltpu.CompilerParams(vmem_limit_bytes=32 << 20),
        cost_estimate=pl.CostEstimate(flops=10**5, bytes_accessed=10**4, transcendentals=0),
        name="expert",
    )(info, dy, *in_hbm(up, down), *cames)


def weight_kernel(count, members, side, pos, *refs):
    rows, acts, (keep_ref, pass_ref, turned, lhs) = refs[:count], refs[count : 2 * count], refs[2 * count :]
    half = keep_ref.shape[0]

    @pl.when(pl.program_id(0) == 0)
    def _():
        for n in range(count):
            turned[...] = rows[n][0].astype(F32).T.astype(BF)
            if side is not None:
                lhs[n] = turned[side * 2 * half : (side + 1) * 2 * half, :]
                continue
            unit = 2 * half // (GROUPS * members // 2)
            for r in range(members // 2):
                member = jnp.bitwise_xor(pos[0], 2 * r)
                for k in range(GROUPS):
                    row = pl.multiple_of((lax.rem(pos[1] + k, GROUPS) * members + member) * unit, 16)
                    at = (r * GROUPS + k) * unit
                    lhs[n, at : at + unit, :] = turned[pl.ds(row, unit), :]

    keep_ref[...] = sum(dot(lhs[n, :half, :], acts[n][0]) for n in range(count)).astype(BF)
    pass_ref[...] = sum(dot(lhs[n, half:, :], acts[n][0]) for n in range(count)).astype(BF)


def weight_terms(pos, rows, acts, which, members, side=None):
    _, count, width = rows[0].shape
    ffn = acts[0].shape[2]
    half = pl.BlockSpec((width // 4, FBLOCK), lambda j: (0, j))
    return pl.pallas_call(
        functools.partial(weight_kernel, len(rows), members, side),
        grid=(ffn // FBLOCK,),
        in_specs=[SMEM_SPEC]
        + [pl.BlockSpec((1, count, width), lambda j: (which, 0, 0))] * len(rows)
        + [pl.BlockSpec((1, count, FBLOCK), lambda j: (which, 0, j))] * len(rows),
        out_specs=[half, half],
        out_shape=[pltpu.HBM((width // 4, ffn), BF)] * 2,
        scratch_shapes=[pltpu.VMEM((width, count), BF), pltpu.VMEM((len(rows), width // 2, count), BF)],
        compiler_params=pltpu.CompilerParams(vmem_limit_bytes=20 << 20),
        cost_estimate=pl.CostEstimate(flops=10**5, bytes_accessed=10**4, transcendentals=0),
        name="weight_terms",
    )(pos, *rows, *in_hbm(*acts))


def add_kernel(riders, a_ref, b_ref, *refs):
    rides, outs = refs[:riders], refs[riders:]
    rows, width = a_ref.shape[0] // GROUPS, outs[0].shape[1]
    blocks = a_ref.shape[1] // width
    for k, out in enumerate(outs):
        for c in range(blocks):
            at = (slice(k * rows, (k + 1) * rows), slice(c * width, (c + 1) * width))
            out[c * rows : (c + 1) * rows, :] = (a_ref[at].astype(F32) + b_ref[at].astype(F32)).astype(BF)
        if riders:
            ride = jnp.concatenate([r[k].astype(F32) for r in rides])
            out[blocks * rows :, :] = ride.astype(BF)


def add_groups(a, b, width, rides=()):
    rows, cols = a.shape
    count = rows // GROUPS * cols // width + sum(r.shape[1] for r in rides)
    return pl.pallas_call(
        functools.partial(add_kernel, len(rides)),
        in_specs=[all_of(a)] * 2 + [all_of(r) for r in rides],
        out_specs=[pl.BlockSpec((count, width), lambda: (0, 0))] * GROUPS,
        out_shape=[jax.ShapeDtypeStruct((count, width), BF)] * GROUPS,
        compiler_params=pltpu.CompilerParams(vmem_limit_bytes=16 << 20),
        cost_estimate=pl.CostEstimate(flops=10**5, bytes_accessed=10**4, transcendentals=0),
        name="add_groups",
    )(*in_hbm(a, b, *rides))


def order_kernel(blocks, pos, *refs):
    out_ref = refs[-1]
    rows, width = out_ref.shape[1], out_ref.shape[2] // blocks
    for k in range(GROUPS):
        group = group_of(k, pos[1])
        for c in range(blocks):
            out_ref[group, :, c * width : (c + 1) * width] = refs[k][c * rows : (c + 1) * rows, :].astype(F32)


def in_order(pos, parts, rows, cols):
    width = parts[0].shape[1]
    return pl.pallas_call(
        functools.partial(order_kernel, cols // width),
        in_specs=[SMEM_SPEC] + [all_of(p) for p in parts],
        out_specs=pl.BlockSpec((GROUPS, rows, cols), lambda: (0, 0, 0)),
        out_shape=jax.ShapeDtypeStruct((GROUPS, rows, cols), F32),
        compiler_params=pltpu.CompilerParams(vmem_limit_bytes=16 << 20),
        cost_estimate=pl.CostEstimate(flops=10**5, bytes_accessed=10**4, transcendentals=0),
        name="in_order",
    )(pos, *parts)


def turn_kernel(
    info, place_ref, routes_ref, gates_ref, resid_ref, moe_ref, dy_ref, router_ref, scale_ref,
    out_ref, context_ref, back_ref, *refs,
):
    dos, (resid_grad_ref, mine_ref, other_ref, send_ref, router_grad_ref, gain_ref, term) = refs[:GROUPS], refs[GROUPS:]
    tok, width = resid_ref.shape
    back = back_ref[...]
    slots = back.shape[0]
    iota = lax.broadcasted_iota(jnp.int32, (tok, slots), 1)
    pick = [place_ref[:, k : k + 1] == iota for k in range(TOP)]
    gates = [gates_ref[:, k : k + 1] for k in range(TOP)]
    gate_grad = [jnp.sum(dot(p.astype(BF), back[:, width:]), axis=1, keepdims=True) for p in pick]
    mean = gates[0] * gate_grad[0] + gates[1] * gate_grad[1]
    lane = lax.broadcasted_iota(jnp.int32, (tok, 128), 1)
    logit_grad = sum(
        jnp.where(routes_ref[:, k : k + 1] == lane, gates[k] * (gate_grad[k] - mean), 0.0) for k in range(TOP)
    )
    grad = dot((pick[0] | pick[1]).astype(BF), back[:, :width])
    for e in range(EXPERTS):
        grad = grad + logit_grad[:, e : e + 1] * router_ref[e : e + 1, :].astype(F32)
    resid = resid_ref[...]
    inv = lax.rsqrt(jnp.mean(resid * resid, axis=1, keepdims=True) + EPS)
    gain_ref[...] = jnp.sum(grad * (resid * inv), axis=0, keepdims=True)
    scaled = grad * scale_ref[...]
    along = jnp.mean(scaled * resid, axis=1, keepdims=True)
    resid_grad = dy_ref[...].astype(F32) + inv * scaled - resid * (inv * inv * inv * along)
    resid_grad_ref[...] = resid_grad
    low = resid_grad.astype(BF)
    term[:, :tok] = dot(out_ref[...], low, ((1,), (1,)))
    for k in range(GROUPS):
        row = pl.multiple_of(lax.rem(info[0] + k, GROUPS) * GWIDTH, GWIDTH)
        dos[k][...] = term[pl.ds(row, GWIDTH), :tok].astype(BF)
    router_grad_ref[...] = lax.dot_general(
        logit_grad.T[:EXPERTS], moe_ref[...].astype(F32), (((1,), (0,)), ((), ())),
        precision=FULL, preferred_element_type=F32,
    )
    term[...] = dot(low.astype(F32).T.astype(BF), context_ref[...].astype(F32).T.astype(BF))
    rows, cols = mine_ref.shape[1:]
    core, top = info[1], info[2]
    mine = pl.ds(pl.multiple_of(top * cols, 128), cols)
    other = pl.ds(pl.multiple_of((1 - top) * cols, 128), cols)
    for g in range(mine_ref.shape[0]):
        keep = pl.ds(pl.multiple_of((2 * g + core) * rows, 8), rows)
        send = pl.ds(pl.multiple_of((2 * g + 1 - core) * rows, 8), rows)
        mine_ref[g] = term[keep, mine]
        other_ref[g] = term[keep, other]
        send_ref[0, g] = term[send, mine].astype(BF)
        send_ref[1, g] = term[send, other].astype(BF)


def turn_back(info, back, place, routes, gates, resid, moe_in, dy, router, scale, out_full, context, shards):
    tok, width = resid.shape
    rows = width // shards
    part = (shards // 2, rows, width // 2)
    gates, resid, moe_in, dy, out_full, context = in_hbm(gates, resid, moe_in, dy, out_full, context)
    inputs = (place, routes, gates, resid, moe_in, dy, router, scale, out_full, context, back)
    kept = [((tok, width), F32), (part, F32), (part, F32), ((2,) + part, BF), ((EXPERTS, width), F32), ((1, width), F32)]
    kept = [pltpu.HBM(*s) for s in kept]
    return pl.pallas_call(
        turn_kernel,
        in_specs=[SMEM_SPEC] + [all_of(x) for x in inputs],
        out_specs=[VMEM_SPEC] * GROUPS + [all_of(s.inner_aval) for s in kept],
        scratch_shapes=[pltpu.VMEM((width, width), F32)],
        out_shape=[jax.ShapeDtypeStruct((GWIDTH, tok), BF)] * GROUPS + kept,
        compiler_params=pltpu.CompilerParams(vmem_limit_bytes=24 << 20),
        cost_estimate=pl.CostEstimate(flops=10**5, bytes_accessed=10**4, transcendentals=0),
        name="turn_back",
    )(info, *inputs)


def pair_kernel(a_ref, b_ref, c_ref, d_ref, keep_ref, send_ref):
    keep_ref[...] = a_ref[...].astype(F32) + b_ref[...].astype(F32)
    send_ref[...] = (c_ref[...].astype(F32) + d_ref[...].astype(F32)).astype(BF)


def add_pairs(a, b, c, d):
    return pl.pallas_call(
        pair_kernel,
        in_specs=[VMEM_SPEC] * 4,
        out_specs=[VMEM_SPEC] * 2,
        out_shape=[jax.ShapeDtypeStruct(a.shape, F32), jax.ShapeDtypeStruct(a.shape, BF)],
        cost_estimate=pl.CostEstimate(flops=10**5, bytes_accessed=10**4, transcendentals=0),
        compiler_params=pltpu.CompilerParams(vmem_limit_bytes=8 << 20),
        name="add_pairs",
    )(a, b, c, d)


SMALL = 16


def input_kernel(
    members, buckets_here, info, dq_ref, keep_ref, came_ref, ain_ref, weight_ref, scale_ref, router_ref,
    gain_ref, line_ref, dline_ref, own_ref, one_ref, two_ref, three_ref, term_ref, sent_ref, pack_ref, dproj, term,
):
    h, core = info[0], info[1]
    width = ain_ref.shape[1]
    tok = own_ref.shape[0]
    dproj[:, :GWIDTH] = dq_ref[...].astype(F32)
    for k in range(GROUPS):
        dkv = keep_ref[k] if came_ref is None else keep_ref[k] + came_ref[k].astype(F32)
        dproj[k * tok : (k + 1) * tok, GWIDTH:] = dkv.astype(BF).astype(F32)
    low = dproj[...].astype(BF)
    ain = ain_ref[...]
    back = dot(low, weight_ref[...], ((1,), (1,)))
    own_ref[...] = back[:tok]
    for k, ref in enumerate((one_ref, two_ref, three_ref)):
        ref[...] = back[(k + 1) * tok : (k + 2) * tok].astype(BF)
    pack_ref[0:EXPERTS, :] = router_ref[...]
    pack_ref[EXPERTS : EXPERTS + 1, :] = jnp.sum(back * ain.astype(F32), axis=0, keepdims=True) / scale_ref[...]
    pack_ref[EXPERTS + 1 : EXPERTS + 2, :] = gain_ref[...]
    col = lax.broadcasted_iota(jnp.int32, (BUCKETS, width), 1)
    cols_f = width * buckets_here // BUCKETS
    within = lax.rem(col, cols_f) - h * buckets_here
    held = jnp.where((within >= 0) & (within < buckets_here), col // cols_f * buckets_here + within, -1)
    held = held == lax.broadcasted_iota(jnp.int32, (BUCKETS, width), 0)
    bucket = line_ref[...] == lax.broadcasted_iota(jnp.int32, (BUCKETS, line_ref.shape[1]), 0)
    for n in range(GHEADS):
        sums = jnp.sum(jnp.where(bucket, dline_ref[n : n + 1, :], 0.0), axis=1, keepdims=True)
        row = EXPERTS + 2 + n
        pack_ref[row : row + 1, :] = jnp.sum(jnp.where(held, sums, 0.0), axis=0, keepdims=True)
    rest = EXPERTS + 2 + GHEADS
    pack_ref[rest:, :] = jnp.zeros((SMALL - rest, width), F32)
    term[...] = dot(dproj[...].T.astype(BF), ain)
    unit = GWIDTH // members
    for t in range(3):
        for r in range(members // 2):
            at = slice((t * (members // 2) + r) * unit, (t * (members // 2) + r + 1) * unit)
            first = (t * members + 2 * r) * unit
            term_ref[at, :] = term[pl.ds(pl.multiple_of(first + core * unit, 8), unit), :]
            sent_ref[at, :] = term[pl.ds(pl.multiple_of(first + (1 - core) * unit, 8), unit), :].astype(BF)
    pack = pack_ref[...]
    high = pack.astype(BF)
    rows = term_ref.shape[0]
    sent_ref[rows : rows + SMALL, :] = high
    sent_ref[rows + SMALL :, :] = (pack - high.astype(F32)).astype(BF)


def input_back(info, members, buckets_here, dq, keep, came, ain, weight, scale, router_grad, gain_grad, line, dline):
    count, width = ain.shape
    tok = count // GROUPS
    rows = 3 * GWIDTH // 2
    ain, weight = in_hbm(ain, weight)
    inputs = [dq, keep] + ([] if came is None else [came]) + [ain, weight, scale, router_grad, gain_grad, line, dline]
    body = functools.partial(input_kernel, members, buckets_here)
    if came is None:
        body = lambda info, dq, keep, *refs: input_kernel(members, buckets_here, info, dq, keep, None, *refs)
    return pl.pallas_call(
        body,
        in_specs=[SMEM_SPEC] + [all_of(x) for x in inputs],
        out_specs=[VMEM_SPEC] * 7,
        out_shape=[jax.ShapeDtypeStruct((tok, width), F32)]
        + [jax.ShapeDtypeStruct((tok, width), BF)] * 3
        + [
            jax.ShapeDtypeStruct((rows, width), F32),
            jax.ShapeDtypeStruct((rows + 2 * SMALL, width), BF),
            jax.ShapeDtypeStruct((SMALL, width), F32),
        ],
        scratch_shapes=[pltpu.VMEM((count, 3 * GWIDTH), F32), pltpu.VMEM((3 * GWIDTH, width), F32)],
        compiler_params=pltpu.CompilerParams(vmem_limit_bytes=24 << 20),
        cost_estimate=pl.CostEstimate(flops=10**5, bytes_accessed=10**4, transcendentals=0),
        name="input_back",
    )(info, *inputs)


def together(*values):
    return lax.optimization_barrier(values)


def turn(shift):
    return [(i, (i + shift) % GROUPS) for i in range(GROUPS)]


def gather_groups(x):
    came = {k: lax.ppermute(x, "h", turn(k)) for k in (2, 1, 3)}
    return jnp.stack([x] + [came[k] for k in range(1, GROUPS)])


def gather_members(x):
    size = lax.axis_size(MEMBERS)
    held = {0: x}
    for bit in bits_of(size):
        for k in sorted(held):
            held[k | bit] = lax.ppermute(held[k], MEMBERS, xor_perm(bit, size))
    return [held[k] for k in range(size)]


def part_of(x, mine):
    low, high = jnp.split(x, 2, axis=-1)
    return jnp.where(mine == 0, low, high), jnp.where(mine == 0, high, low)


def swap(x, axis, bit):
    return lax.ppermute(x, axis, xor_perm(bit, lax.axis_size(axis)))


def two_parts(x):
    high = lax.reduce_precision(x, 8, 7)
    return jnp.concatenate([high, x - high]).astype(BF)


def from_fsdp(part):
    if lax.axis_size("fsdp") != 2:
        return lax.all_gather(part, "fsdp", axis=0)
    came = lax.ppermute(part, "fsdp", xor_perm(1, 2))
    return jnp.where(lax.axis_index("fsdp") == 0, jnp.stack([part, came]), jnp.stack([came, part]))


def group_pieces(pieces, sign):
    came = {k: lax.ppermute(pieces[k], "h", turn(sign * k)) for k in (2, 1, 3)}
    return [pieces[0]] + [came[k] for k in range(1, GROUPS)]


def deal(pieces, spread, sign):
    n_fsdp = lax.axis_size("fsdp")
    out = [pieces[0]] + [None] * (len(pieces) - 1)
    for p in (5, 4, 3, 7, 2, 6, 1):
        k, j = divmod(p, n_fsdp)
        if spread:
            pairs = [
                (g * n_fsdp + i, (g + sign * k) % GROUPS * n_fsdp + (i ^ j))
                for g in range(GROUPS)
                for i in range(n_fsdp)
            ]
            out[p] = lax.ppermute(pieces[p], ("h", "fsdp"), pairs)
        else:
            out[p] = lax.ppermute(pieces[p], "fsdp", xor_perm(j, n_fsdp))
    return out


def per_device(
    tokens, segments, routes, bucket_table, attn_gain, qkv_weight, out_weight, bias_table,
    moe_gain, router_weight, up_weight, down_weight, cotangent,
):
    tok, width = tokens.shape[1], tokens.shape[2]
    half = tok // 2
    h, m, f = lax.axis_index("h"), lax.axis_index(MEMBERS), lax.axis_index("fsdp")
    core = lax.axis_index("core")
    members, n_fsdp = lax.axis_size(MEMBERS), lax.axis_size("fsdp")
    shards = GROUPS * members
    blocks = 2 * shards
    length = shards * tok
    here = EXPERTS // n_fsdp
    spread = here > 1
    ffn = up_weight.shape[2]
    rows_f = width // n_fsdp
    rows_c = width // shards
    pos = jnp.stack([m, h]).astype(jnp.int32)

    extra = jnp.pad(segments.astype(BF), ((0, 7), (0, width - tok)))
    mixed = gather_groups(jnp.concatenate([tokens[0], extra]))

    bias_flat = bias_table.reshape(1, -1)
    bias_rows = -(-bias_flat.shape[1] // rows_f)
    bias_flat = jnp.pad(bias_flat, ((0, 0), (0, bias_rows * rows_f - bias_flat.shape[1])))
    small = jnp.concatenate(
        [attn_gain[None], moe_gain[None], router_weight.T, bias_flat.reshape(bias_rows, rows_f)]
        + [jnp.zeros((16 - 10 - bias_rows, rows_f), BF)]
    )
    small = from_fsdp(small)
    attn_scale = small[:, 0].reshape(width).astype(F32)
    moe_scale = small[:, 1].reshape(width).astype(F32)
    router_t = jnp.transpose(small[:, 2:10], (1, 0, 2)).reshape(EXPERTS, width)
    bias_full = small[:, 10 : 10 + bias_rows].reshape(n_fsdp, -1)[:, : bias_table.size]
    bias_full = bias_full.reshape(BUCKETS, HEADS)
    cut = [
        lax.dynamic_slice_in_dim(qkv_weight, n * width + h * GWIDTH, GWIDTH, 1) for n in range(3)
    ]
    qkv_heads = from_fsdp(jnp.concatenate(cut, axis=1)).reshape(width, 3 * GWIDTH)
    out_full = from_fsdp(together(out_weight, qkv_heads)[0]).reshape(width, width)

    wide = strip_width(blocks, half)
    top = half * (blocks - 1)
    line = jnp.concatenate(
        [
            bucket_table[: top + 1][::-1],
            jnp.full((wide - length,), -1, jnp.int32),
            bucket_table[top + 1 :][::-1],
        ]
    )
    hot = (line[None] == jnp.arange(BUCKETS, dtype=jnp.int32)[:, None]).astype(BF)
    bias_mine = lax.dynamic_slice_in_dim(bias_full, h * GHEADS, GHEADS, 1)
    strips = make_strips(dot(bias_mine, hot, ((0,), (0,))) * LOG2E, half)

    hot_routes = (routes.reshape(-1)[:, None] == jnp.arange(EXPERTS)[None]).astype(F32)
    earlier = jnp.arange(tok * TOP)
    earlier = (earlier[None, :] < earlier[:, None]).astype(BF)
    before = dot(earlier, hot_routes.astype(BF))
    slot = jnp.sum(before * hot_routes, axis=1).astype(jnp.int32).reshape(tok, TOP)
    group = routes % here
    natural = (group * n_fsdp + routes // here) * CAP + slot
    away = lax.rem(group - h + GROUPS, GROUPS) if spread else group
    place = (away * n_fsdp + jnp.bitwise_xor(routes // here, f)) * CAP + slot
    slots = jnp.arange(EXPERTS * CAP, dtype=jnp.int32)
    pick = [slots[:, None] == natural[None, :, k] for k in range(TOP)]
    exchange = ("h", "fsdp") if spread else ("fsdp",)

    def exchange_rows(rows):
        return lax.all_to_all(rows, exchange, 0, 0, tiled=True)

    mixed, strips = together(mixed, strips)
    ain = normalize(mixed[:, :tok].astype(F32), attn_scale).astype(BF).reshape(GROUPS * tok, width)
    proj = dot(ain, qkv_heads).astype(BF)
    kv = proj[:, GWIDTH:].reshape(GROUPS, tok, 2 * GWIDTH)
    kvs = gather_members(jnp.concatenate([kv, mixed[:, tok:, : 2 * GWIDTH]], axis=1))
    dy_send = dot((pick[0] | pick[1]).astype(BF), cotangent[0]).astype(BF).reshape(PIECES, CAP, width)
    dy_slots = exchange_rows(together(dy_send, proj)[0])
    o_pre, *rest = attend(pos, proj, kvs, strips, blocks)
    lows, stat, keys = rest[:GROUPS], rest[GROUPS], rest[GROUPS + 1 :]
    lows[1], dy_slots = together(lows[1], dy_slots)
    *pieces, context, residual, moe_in, gates = router(
        pos, tokens[0], out_full, moe_scale[None], router_t, routes, place.T, group_pieces(lows, -1)
    )

    came = deal(pieces, spread, 1)
    info = jnp.stack([h if spread else jnp.zeros_like(h), f]).astype(jnp.int32)
    *outs, back, act, rows = expert(
        info, came, dy_slots, up_weight, down_weight, GROUPS if spread else 1, n_fsdp
    )
    back = exchange_rows(back).reshape(EXPERTS * CAP, -1)

    staged = spread and members == 4
    if staged:
        rows, acts = [rows, swap(rows, "core", 1)], [act, swap(act, "core", 1)]
        terms = [weight_terms(pos, rows, acts, n, members) for n in range(2)]
        back, terms = together(back, terms)
    else:
        terms = [weight_terms(pos, [rows], [act], n, members, side) for n in range(2) for side in range(2)]

    top_bit = n_fsdp // 2
    info = jnp.stack([h, core, (f // top_bit) % 2]).astype(jnp.int32)
    *dos, resid_grad, out_mine, out_other, out_send, router_grad, moe_gain_grad = turn_back(
        info, back, natural, routes, gates, residual, moe_in, cotangent[0], router_t,
        moe_scale[None], out_full, context, shards,
    )
    dos = group_pieces(dos, 1)
    out_came = swap(out_send, "core", 1)
    out_far = (out_other + out_came[1].astype(F32)).astype(BF)
    outs = [outs[0]] + [lax.ppermute(outs[j], "fsdp", xor_perm(j, n_fsdp)) for j in range(1, n_fsdp)]
    dos[0], out_far = together(dos[0], out_far)
    out_far = swap(out_far, "fsdp", top_bit)
    dq, *dkvs, dline = attend_back(pos, proj, keys, strips, dos, o_pre, stat, members, blocks)
    dkvs[1], out_far, outs = together(dkvs[1], out_far, outs)
    cames = [swap(dkvs[k], "core", 1) for k in range(1, members, 2)]
    sends = []
    if members == 4:
        keep, send = add_pairs(dkvs[0], cames[0], dkvs[2], cames[1])
        if staged:
            sends = [swap(terms[0][1], "r", 1)]
            send, sends[0] = together(send, sends[0])
        came = swap(send, "r", 1)
    else:
        held = {k: dkvs[k].astype(F32) + cames[k // 2].astype(F32) for k in range(0, members, 2)}
        bit = 2
        while bit < members:
            for k in [k for k in sorted(held) if k & bit]:
                held[k - bit] = held[k - bit] + swap(held.pop(k).astype(BF), "r", bit // 2).astype(F32)
            bit *= 2
        keep, came = held[0], None
    if staged:
        up_came = group_pieces(add_groups(terms[0][0], sends[0], width, outs), 1)
        sends.append(swap(together(terms[1][1], came)[0], "r", 1))
        came, up_came[2] = together(came, up_came[2])

    own_back, back_1, back_2, back_3, term, sent, pack = input_back(
        jnp.stack([h, core]).astype(jnp.int32), members, BUCKETS // n_fsdp, dq, keep, came, ain, qkv_heads,
        attn_scale[None], router_grad, moe_gain_grad, line[None], dline,
    )

    def swap_both(send, pack, axis, bit):
        sent = jnp.concatenate([send.reshape(-1, send.shape[-1]).astype(BF), two_parts(pack)])
        return split_rows(swap(sent, axis, bit).astype(F32), send.shape)

    def split_rows(came, shape):
        return came[: -2 * SMALL].reshape(shape), came[-2 * SMALL : -SMALL] + came[-SMALL:]

    unit = GWIDTH // members
    came, pack_came = split_rows(swap(sent, "core", 1).astype(F32), term.shape)
    term, pack = term + came, pack + pack_came
    out_term = out_mine + out_came[0].astype(F32) + out_far.astype(F32)
    for bit in list(bits_of(n_fsdp))[1:]:
        out_term, out_send = part_of(out_term, (f // bit) % 2)
        out_term = out_term + swap(out_send.astype(BF), "fsdp", bit).astype(F32)
    for bit in bits_of(n_fsdp):
        term, send = part_of(term, (f // bit) % 2)
        pack, pack_send = part_of(pack, (f // bit) % 2)
        came, pack_came = swap_both(send, pack_send, "fsdp", bit)
        term, pack = term + came, pack + pack_came
    term = jnp.concatenate(
        [term.reshape(3, members // 2, unit, rows_f).swapaxes(0, 1).reshape(members // 2, -1, rows_f)]
        + [out_term.reshape(GROUPS, members // 2, rows_c, rows_f).swapaxes(0, 1).reshape(members // 2, -1, rows_f)],
        axis=1,
    )
    if staged:
        term, sends[1], up_came = together(term, sends[1], up_came)
    for bit in bits_of(members // 2):
        mine = (lax.axis_index("r") // bit) % 2
        term = term.reshape((2, -1) + term.shape[1:])
        came, pack_came = swap_both(lax.dynamic_index_in_dim(term, 1 - mine, 0, False), pack, "r", bit)
        term = lax.dynamic_index_in_dim(term, mine, 0, False) + came
        pack = pack + pack_came
    term = term[0]
    if staged:
        back_2, back_3, up_came = together(back_2, back_3, up_came)
    mid = lax.ppermute(back_2, "h", turn(-1))
    side = lax.ppermute(back_3, "h", turn(1)).astype(F32)
    mid = (back_1.astype(F32) + mid.astype(F32)).astype(BF)
    mid = lax.ppermute(mid, "h", turn(-1)).astype(F32)
    attn_in_grad = own_back + side + mid
    x = tokens[0].astype(F32)
    token_grad = jax.vjp(lambda v: normalize(v, attn_scale), x)[1](attn_in_grad)[0]
    tokens_grad = (resid_grad + token_grad).astype(BF)

    out_term = term[3 * unit :].reshape(GROUPS, rows_c, rows_f)
    term = term[: 3 * unit].astype(BF).reshape(3, unit, rows_f)
    if staged:
        down_came = group_pieces(add_groups(terms[1][0], sends[1], width), 1)
    out_sum, pack_sum = lax.dynamic_index_in_dim(out_term, h, 0, False), pack
    for k in (2, 1, 3):
        piece = lax.dynamic_index_in_dim(out_term, lax.rem(h + k, GROUPS), 0, False)
        came = lax.ppermute(jnp.concatenate([piece.astype(BF), two_parts(pack)]), "h", turn(k)).astype(F32)
        out_sum = out_sum + came[:rows_c]
        pack_sum = pack_sum + came[rows_c : rows_c + SMALL] + came[rows_c + SMALL :]
    at = h * members + m
    parts = []
    for r in range(3):
        pairs = [((3 * d + r) % shards, d) for d in range(shards)]
        third = pow(3, -1, shards)
        which = (3 * lax.rem((at + shards - r) * third, shards) + r) // shards
        parts.append(lax.ppermute(lax.dynamic_index_in_dim(term, which, 0, False), CTX, pairs))
    if staged:
        up_came, parts = together(up_came, parts)
        grads = [in_order(pos, part, rows_c, ffn) for part in (up_came, down_came)]
        home = jnp.concatenate([part[rows_c * ffn // width :] for part in up_came])
    else:
        terms = [jnp.concatenate(terms[n] + terms[n + 1]) for n in (0, 2)]
        grads = [
            lax.psum_scatter(term, CTX, scatter_dimension=0, tiled=True)[None].astype(F32) for term in terms
        ]
        home = jnp.concatenate([o.reshape(-1, width) for o in outs])
    qkv_grad = jnp.concatenate(parts).astype(F32).T

    away = lax.rem(h - group + GROUPS, GROUPS) if spread else group
    place = (away * n_fsdp + jnp.bitwise_xor(routes // here, f)) * CAP + slot
    layer_out = residual
    for k in range(TOP):
        row = (slots[:, None] == place[None, :, k]).astype(BF)
        layer_out = layer_out + gates[:, k : k + 1] * dot(row, home, ((0,), (0,)))
    bias_grad = pack_sum[EXPERTS + 2 : EXPERTS + 2 + GHEADS, : GROUPS * BUCKETS // n_fsdp]
    bias_grad = bias_grad.reshape(GHEADS, GROUPS, BUCKETS // n_fsdp).transpose(2, 1, 0).reshape(-1, HEADS)
    return (
        layer_out.astype(BF)[None],
        tokens_grad[None],
        pack_sum[8],
        qkv_grad,
        out_sum.T,
        bias_grad,
        pack_sum[9],
        pack_sum[:8].T,
        grads[0],
        grads[1],
    )


def solution(mesh):
    n_ctx, n_fsdp = mesh.shape["ctx"], mesh.shape["fsdp"]
    cut = mesh.devices.reshape(GROUPS, n_ctx // (2 * GROUPS), 2, n_fsdp)
    row = P("fsdp", CTX, None)
    return jax.shard_map(
        per_device,
        mesh=Mesh(cut, CTX + ("fsdp",)),
        in_specs=(
            row,
            P("fsdp", CTX),
            P(CTX + ("fsdp",), None),
            P(),
            P("fsdp"),
            P("fsdp", None),
            P("fsdp", None),
            P("fsdp", None),
            P("fsdp"),
            P("fsdp", None),
            P("fsdp", None, None),
            P("fsdp", None, None),
            row,
        ),
        out_specs=(
            row,
            row,
            P("fsdp"),
            P("fsdp", CTX),
            P("fsdp", CTX),
            P("fsdp", None),
            P("fsdp"),
            P("fsdp", None),
            row,
            row,
        ),
        check_vma=False,
    )
```

```python
import functools

import jax
import jax.numpy as jnp
from jax import lax
from jax.experimental import pallas as pl
from jax.experimental.pallas import tpu as pltpu
from jax.sharding import Mesh, PartitionSpec as P

HEADS = 12
HEAD_DIM = 64
EXPERTS = 8
TOP = 2
BUCKETS = 32
DOCS = 8
CAP = 40
GROUPS = 4
GHEADS = HEADS // GROUPS
GWIDTH = GHEADS * HEAD_DIM
CHUNK = 256

LOG2E = 1.4426950408889634
EPS = 1e-06
LOWEST = -1e30
FULL = lax.Precision.HIGHEST
BF = jnp.bfloat16
F32 = jnp.float32
MEMBERS = ("r", "core")
CTX = ("h", "r", "core")


def normalize(values, weight):
    inv_rms = lax.rsqrt(jnp.mean(values * values, axis=-1, keepdims=True) + EPS)
    return values * inv_rms * weight


def dot(a, b, dims=((1,), (0,))):
    return lax.dot_general(a, b, (dims, ((), ())), preferred_element_type=F32)


def exact_dot(a, b, dims):
    return lax.dot_general(a, b, (dims, ((), ())), precision=FULL)


def xor_perm(mask, size):
    return [(i, i ^ mask) for i in range(size)]


def bits_of(size):
    bit = size // 2
    while bit:
        yield bit
        bit //= 2


def strip_width(blocks, half):
    need = half * (blocks - 1) + CHUNK + half
    return -(-need // 128) * 128


def strips_kernel(g_ref, out_ref):
    half = out_ref.shape[1] // GHEADS
    rolled = [
        pltpu.roll(
            jnp.broadcast_to(g_ref[n : n + 1, :], (half, g_ref.shape[1])), 0, 1, stride=1, stride_axis=0
        )
        for n in range(GHEADS)
    ]
    out_ref[...] = jnp.concatenate(rolled).T


def make_strips(lines, half):
    return pl.pallas_call(
        strips_kernel,
        out_specs=pl.BlockSpec((lines.shape[1], GHEADS * half), lambda: (0, 0)),
        out_shape=pltpu.HBM((lines.shape[1], GHEADS * half), F32),
        cost_estimate=pl.CostEstimate(flops=10**5, bytes_accessed=10**4, transcendentals=0),
        name="strips",
    )(lines)


def own_blocks(size, half):
    a = lax.broadcasted_iota(jnp.int32, (size, size), 0) // half
    b = lax.broadcasted_iota(jnp.int32, (size, size), 1) // half
    return a == b


def spread_rows(x, same):
    return jnp.where(same, jnp.concatenate([x] * GHEADS), 0.0)


def identity(size):
    a, b = (lax.broadcasted_iota(jnp.int32, (size, size), n) for n in range(2))
    return jnp.where(a == b, 1.0, 0.0).astype(BF)


def own_columns(x, half):
    return jnp.concatenate(
        [x[n * HEAD_DIM : (n + 1) * HEAD_DIM, n * half : (n + 1) * half] for n in range(GHEADS)]
    )


def fold_rows(x, same, half):
    y = jnp.where(same, x, 0.0).T
    return sum(y[n * half : (n + 1) * half] for n in range(GHEADS))


def spread_columns(x, same):
    return jnp.where(same, jnp.concatenate([x] * GHEADS, axis=1), 0.0)


def group_of(slot, h):
    return lax.rem(h + GROUPS - slot, GROUPS)


def place_of(slot, early, me, h, members, blocks):
    owner = group_of(slot, h) * members + me
    return owner if early else blocks - 1 - owner


def bounds(block, chunk, half, blocks, start):
    top = (blocks - 1 - (block - (CHUNK // half) * chunk)) * half
    lane = lax.broadcasted_iota(jnp.int32, (1, GHEADS * half), 1)
    last = block * half + lax.rem(lane, half) - chunk * CHUNK
    return pl.multiple_of(top, half), last, start - chunk * CHUNK


def forward_kernel(half, blocks, members, pos, q_ref, *refs):
    kvs, refs = refs[:members], refs[members:]
    strip_in, o_ref, *lows, stat_ref, k_out, v_out, kt_out, k_ref, v_ref, kt_ref, vt, strip_ref, low, sems, strip_sem = refs
    loads = start_copies([(strip_in, strip_ref)], strip_sem)
    size = GHEADS * half
    me, h = pos[0], pos[1]
    tok = 2 * half
    same = own_blocks(size, half)
    key = lax.broadcasted_iota(jnp.int32, (CHUNK, size), 0)
    per = CHUNK // half

    @pl.loop(0, GROUPS)
    def _(slot):
        for j in range(members):
            for early in (True, False):
                block = place_of(slot, early, jnp.bitwise_xor(me, j), h, members, blocks)
                at = pl.ds(pl.multiple_of(lax.rem(block, per) * half, half), half)
                rows = kvs[j][slot, 0 if early else half : half if early else tok, :]
                k_ref[block // per, at, :] = rows[:, :GWIDTH]
                v_ref[block // per, at, :] = rows[:, GWIDTH:]

    eye = identity(GWIDTH)

    @pl.loop(0, blocks // per, unroll=4)
    def _(chunk):
        kt_ref[chunk] = dot(eye, k_ref[chunk], ((1,), (1,))).astype(BF)
        vt[chunk] = dot(eye, v_ref[chunk], ((1,), (1,))).astype(BF)

    copies = start_copies([(k_ref, k_out), (v_ref, v_out), (kt_ref, kt_out)], sems)
    docs = jnp.concatenate([kv[a, tok : tok + 1, :tok].astype(F32) for kv in kvs for a in range(GROUPS)])
    begins = [jnp.sum(jnp.where(docs < s, 1.0, 0.0)) for s in range(1, DOCS)]
    for load in loads:
        load.wait()

    def prepare(slot, late):
        owner = group_of(slot, h) * members + me
        block = owner if late == 0 else blocks - 1 - owner
        at = pl.ds(pl.multiple_of(slot * tok + late * half, half), half)
        qs = spread_rows(q_ref[at, :GWIDTH].astype(F32), same).astype(BF)
        qt = dot(eye, qs, ((1,), (1,))).astype(BF)
        doc = kvs[0][slot, tok : tok + 1, :tok].astype(F32)[:, late * half : (late + 1) * half]
        begin = jnp.zeros((1, half), F32)
        for s in range(1, DOCS):
            begin = jnp.where(doc == s, begins[s - 1], begin)
        first = jnp.min(begin).astype(jnp.int32) // CHUNK
        begin = jnp.concatenate([begin] * GHEADS, axis=1)
        return block, first, block // per, begin, qt

    def advance(state, step, carry):
        block, first, final, begin, qt = state
        peak, total, acc = carry
        chunk = jnp.minimum(first + step, final)
        top, last, begin = bounds(block, chunk, half, blocks, begin.astype(jnp.int32))
        last = jnp.where(first + step <= final, last, -1)
        t = dot(k_ref[chunk], qt) * (HEAD_DIM**-0.5 * LOG2E) + strip_ref[pl.ds(top, CHUNK), :]
        t = jnp.where((key <= last) & (key >= begin), t, LOWEST)
        new = jnp.maximum(peak, jnp.ceil(jnp.max(t, axis=0, keepdims=True)))
        e = jnp.exp2(t - new)
        fade = jnp.exp2(peak - new)
        total = total * fade + jnp.sum(e, axis=0, keepdims=True)
        acc = acc * fade + dot(vt[chunk], e.astype(BF))
        return new, total, acc

    init = (
        jnp.full((1, size), LOWEST, F32),
        jnp.zeros((1, size), F32),
        jnp.zeros((GWIDTH, size), F32),
    )

    def pair_of(pair, late):
        slots = [group_of(2 * pair + n, h) for n in range(2)]
        states = [prepare(slot, late) for slot in slots]
        steps = functools.reduce(jnp.maximum, [s[2] - s[1] + 1 for s in states])
        done = lax.fori_loop(
            0, steps, lambda i, c: tuple(advance(s, i, x) for s, x in zip(states, c)), (init,) * 2
        )
        for slot, state, (peak, total, acc) in zip(slots, states, done):
            out = own_columns(acc / total, half)
            o_ref[2 * slot + late] = out
            low[slot, :, late * half : (late + 1) * half] = out.astype(BF)
            stat_ref[2 * slot + late, 0:1, :] = peak
            stat_ref[2 * slot + late, 1:2, :] = total
            stat_ref[2 * slot + late, 2:3, :] = state[3]

    @pl.loop(0, GROUPS // 2)
    def _(pair):
        pair_of(pair, 0)
        pair_of(pair, 1)

    for n in range(GROUPS):
        lows[n][...] = low[n]
    for copy in copies:
        copy.wait()


def backward_kernel(half, blocks, members, pos, *refs):
    dos, refs = refs[:GROUPS], refs[GROUPS:]
    inputs, (dq_ref, *refs) = refs[:7], refs[7:]
    dkvs, refs = refs[:members], refs[members:]
    dline_ref, *held, dk, dv, dstrip, do_ref, sems = refs
    q_ref, strip_ref, o_ref, stat_ref, k_ref, v_ref, kt_ref = held
    size = GHEADS * half
    me, h = pos[0], pos[1]
    width = dstrip.shape[0]
    per = CHUNK // half
    copies = start_copies(list(zip(inputs, held)), sems)
    same = own_blocks(size, half)
    key = lax.broadcasted_iota(jnp.int32, (CHUNK, size), 0)

    @pl.loop(0, blocks // per)
    def _(chunk):
        dk[chunk] = jnp.zeros(dk.shape[1:], F32)
        dv[chunk] = jnp.zeros(dv.shape[1:], F32)

    @pl.loop(0, width // 128)
    def _(j):
        dstrip[pl.ds(pl.multiple_of(j * 128, 128), 128), :] = jnp.zeros((128, size), F32)

    for n in range(GROUPS):
        do_ref[n] = dos[n][...].astype(F32)
    for copy in copies:
        copy.wait()

    def prepare(slot, late):
        i = 2 * slot + late
        owner = group_of(slot, h) * members + me
        block = owner if late == 0 else blocks - 1 - owner
        at = pl.ds(pl.multiple_of(slot * 2 * half + late * half, half), half)
        peak, total, start = (stat_ref[i, n : n + 1, :] for n in range(3))
        first = jnp.min(start).astype(jnp.int32) // CHUNK
        qs = spread_rows(q_ref[at, :GWIDTH].astype(F32), same)
        qt, qs = qs.T.astype(BF), qs.astype(BF)
        do = do_ref[slot][:, late * half : (late + 1) * half]
        corr = jnp.sum(spread_columns(do * o_ref[i], same), axis=0, keepdims=True) / total
        gt = spread_columns(do, same) / total
        gs = gt.T.astype(BF)
        return block, first, block // per, start.astype(jnp.int32), peak, corr, qt, qs, gt.astype(BF), gs, at

    def scores(state, step):
        block, first, final, start, peak, corr, qt, _, gt = state[:9]
        chunk = jnp.minimum(first + step, final)
        top, last, begin = bounds(block, chunk, half, blocks, start)
        last = jnp.where(first + step <= final, last, -1)
        t = dot(k_ref[chunk], qt) * (HEAD_DIM**-0.5 * LOG2E) + strip_ref[pl.ds(top, CHUNK), :]
        t = jnp.where((key <= last) & (key >= begin), t - peak, LOWEST)
        e = jnp.exp2(t)
        return chunk, top, e.astype(BF), e * (dot(v_ref[chunk], gt) - corr)

    def pair_of(pair, late):
        states = [prepare(group_of(2 * pair + n, h), late) for n in range(2)]

        def visit(step, carry):
            found = [scores(s, step) for s in states]
            out = []
            for (chunk, top, e, s), state, dq in zip(found, states, carry):
                low = s.astype(BF)
                dk[chunk] += dot(low, state[7])
                dv[chunk] += dot(e, state[9])
                dstrip[pl.ds(top, CHUNK), :] += s
                out.append(dq + dot(kt_ref[chunk], low))
            return tuple(out)

        steps = functools.reduce(jnp.maximum, [s[2] - s[1] + 1 for s in states])
        done = lax.fori_loop(0, steps, visit, (jnp.zeros((GWIDTH, size), F32),) * 2)
        for state, dq in zip(states, done):
            dq_ref[state[10], :] = (fold_rows(dq, same, half) * HEAD_DIM**-0.5).astype(BF)

    @pl.loop(0, GROUPS // 2)
    def _(pair):
        pair_of(pair, 0)
        pair_of(pair, 1)

    @pl.loop(0, GROUPS)
    def _(slot):
        for j in range(members):
            for early in (True, False):
                block = place_of(slot, early, jnp.bitwise_xor(me, j), h, members, blocks)
                at = pl.ds(pl.multiple_of(lax.rem(block, per) * half, half), half)
                part = jnp.concatenate(
                    [dk[block // per, at, :] * HEAD_DIM**-0.5, dv[block // per, at, :]], axis=1
                )
                dkvs[j][slot, 0 if early else half : half if early else 2 * half, :] = part.astype(BF)

    lines = dstrip[...].T
    for n in range(GHEADS):
        x = lines[n * half : (n + 1) * half]
        rows = half
        while rows > 8:
            rows //= 2
            x = x[:rows] + pltpu.roll(x[rows:], width - rows, 1)
        sub = lax.broadcasted_iota(jnp.int32, x.shape, 0)
        for bit in (4, 2, 1):
            x = jnp.where((sub & bit) != 0, pltpu.roll(x, width - bit, 1), x)
        dline_ref[n : n + 1, :] = jnp.sum(x, axis=0, keepdims=True)


VMEM_SPEC = pl.BlockSpec(memory_space=pltpu.VMEM)
SMEM_SPEC = pl.BlockSpec(memory_space=pltpu.SMEM)
HBM_SPEC = pl.BlockSpec(memory_space=pltpu.HBM)


def in_hbm(*values):
    return [pltpu.with_memory_space_constraint(v, pltpu.HBM) for v in values]


def all_of(x):
    return pl.BlockSpec(x.shape, lambda: (0,) * len(x.shape))


def start_copies(pairs, sems):
    copies = [pltpu.make_async_copy(src, dst, sems.at[i]) for i, (src, dst) in enumerate(pairs)]
    for copy in copies:
        copy.start()
    return copies


def key_shapes(blocks, half):
    chunks = blocks * half // CHUNK
    return ((chunks, CHUNK, GWIDTH), (chunks, CHUNK, GWIDTH), (chunks, GWIDTH, CHUNK))


def attend(pos, q, kvs, strips, blocks):
    rows = q.shape[0]
    half = strips.shape[1] // GHEADS
    shapes = key_shapes(blocks, half)
    o_shape, stat_shape = (rows // half, GWIDTH, half), (rows // half, 8, GHEADS * half)
    return pl.pallas_call(
        functools.partial(forward_kernel, half, blocks, len(kvs)),
        in_specs=[SMEM_SPEC] + [VMEM_SPEC] * (1 + len(kvs)) + [HBM_SPEC],
        out_specs=[all_of(jax.ShapeDtypeStruct(o_shape, F32))]
        + [VMEM_SPEC] * GROUPS
        + [all_of(jax.ShapeDtypeStruct(stat_shape, F32))]
        + [HBM_SPEC] * 3,
        scratch_shapes=[pltpu.VMEM(s, BF) for s in shapes + shapes[2:]]
        + [
            pltpu.VMEM(strips.shape, F32),
            pltpu.VMEM((GROUPS, GWIDTH, 2 * half), BF),
            pltpu.SemaphoreType.DMA((3,)),
            pltpu.SemaphoreType.DMA((1,)),
        ],
        out_shape=[pltpu.HBM(o_shape, F32)]
        + [jax.ShapeDtypeStruct((GWIDTH, 2 * half), BF)] * GROUPS
        + [pltpu.HBM(stat_shape, F32)]
        + [pltpu.HBM(s, BF) for s in shapes],
        compiler_params=pltpu.CompilerParams(vmem_limit_bytes=32 << 20),
        cost_estimate=pl.CostEstimate(flops=10**5, bytes_accessed=10**4, transcendentals=0),
        name="attend",
    )(pos, q, *kvs, *in_hbm(strips))


def attend_back(pos, q, keys, strips, dos, o, stat, members, blocks):
    rows = q.shape[0]
    half = strips.shape[1] // GHEADS
    shapes = key_shapes(blocks, half)
    kv = jax.ShapeDtypeStruct((GROUPS, 2 * half, 2 * GWIDTH), BF)
    inputs = in_hbm(q, strips, o, stat, *keys)
    return pl.pallas_call(
        functools.partial(backward_kernel, half, blocks, members),
        in_specs=[SMEM_SPEC] + [VMEM_SPEC] * GROUPS + [HBM_SPEC] * len(inputs),
        out_specs=[VMEM_SPEC] * (1 + members) + [pl.BlockSpec((GHEADS, strips.shape[0]), lambda: (0, 0))],
        scratch_shapes=[pltpu.VMEM(x.shape, x.dtype) for x in inputs]
        + [pltpu.VMEM(s, F32) for s in shapes[:2]]
        + [
            pltpu.VMEM(strips.shape, F32),
            pltpu.VMEM((GROUPS, GWIDTH, 2 * half), F32),
            pltpu.SemaphoreType.DMA((len(inputs),)),
        ],
        out_shape=[jax.ShapeDtypeStruct((rows, GWIDTH), BF)]
        + [kv] * members
        + [pltpu.HBM((GHEADS, strips.shape[0]), F32)],
        compiler_params=pltpu.CompilerParams(vmem_limit_bytes=40 << 20),
        cost_estimate=pl.CostEstimate(flops=10**5, bytes_accessed=10**4, transcendentals=0),
        name="attend_back",
    )(pos, *dos, *inputs)


FBLOCK = 768
PIECES = 8


def three_parts(x):
    high = x.astype(BF).astype(F32)
    mid = (x - high).astype(BF).astype(F32)
    low = x - high - mid
    lane = lax.broadcasted_iota(jnp.int32, (x.shape[0], 128), 1)
    return jnp.where(lane == 0, high, jnp.where(lane == 1, mid, jnp.where(lane == 2, low, 0.0))).astype(BF)


def gather_rows(refs):
    return jnp.concatenate([r[...].astype(F32) for r in refs])


def router_kernel(
    pos, x_ref, out_ref, scale_ref, router_ref, routes_ref, place_ref, *refs
):
    lows, refs = refs[:GROUPS], refs[GROUPS:]
    pieces, (context_ref, resid_ref, moe_ref, gates_ref) = refs[:PIECES], refs[PIECES:]
    tok, width = x_ref.shape
    for k in range(GROUPS):
        row = pl.multiple_of(lax.rem(pos[1] + k, GROUPS) * GWIDTH, GWIDTH)
        context_ref[pl.ds(row, GWIDTH), :] = lows[k][...]
    context = context_ref[...].astype(F32).T.astype(BF)
    resid = x_ref[...].astype(F32) + dot(context, out_ref[...])
    resid_ref[...] = resid
    inv = lax.rsqrt(jnp.mean(resid * resid, axis=1, keepdims=True) + EPS)
    moe_in = (resid * inv * scale_ref[...]).astype(BF)
    moe_ref[...] = moe_in
    logits = dot(moe_in, router_ref[...], ((1,), (1,)))
    lane = lax.broadcasted_iota(jnp.int32, logits.shape, 1)
    chosen = [
        jnp.sum(jnp.where(routes_ref[:, k : k + 1] == lane, logits, 0.0), axis=1, keepdims=True)
        for k in range(TOP)
    ]
    most = jnp.maximum(chosen[0], chosen[1])
    powers = [jnp.exp(c - most) for c in chosen]
    gates = [p / (powers[0] + powers[1]) for p in powers]
    slot = lax.broadcasted_iota(jnp.int32, (EXPERTS * CAP, tok), 0)
    pick = [(place_ref[k : k + 1, :] == slot) for k in range(TOP)]
    rows = dot((pick[0] | pick[1]).astype(BF), moe_in)
    extra = sum(dot(pick[k].astype(BF), three_parts(gates[k])) for k in range(TOP))
    for p in range(PIECES):
        pieces[p][:, :width] = rows[p * CAP : (p + 1) * CAP].astype(BF)
        pieces[p][:, width:] = extra[p * CAP : (p + 1) * CAP].astype(BF)
    for k in range(TOP):
        gates_ref[:, k : k + 1] = gates[k]


def router(pos, x, out_full, scale, router_t, routes, places, lows):
    tok, width = x.shape
    kept = [pltpu.HBM(*s) for s in (((width, tok), BF), ((tok, width), F32), ((tok, width), BF), ((tok, TOP), F32))]
    x, out_full = in_hbm(x, out_full)
    return pl.pallas_call(
        router_kernel,
        in_specs=[SMEM_SPEC, all_of(x), all_of(out_full)] + [VMEM_SPEC] * (4 + GROUPS),
        out_specs=[VMEM_SPEC] * PIECES + [all_of(s.inner_aval) for s in kept],
        out_shape=[jax.ShapeDtypeStruct((CAP, width + 128), BF)] * PIECES + kept,
        compiler_params=pltpu.CompilerParams(vmem_limit_bytes=16 << 20),
        cost_estimate=pl.CostEstimate(flops=10**5, bytes_accessed=10**4, transcendentals=0),
        name="router",
    )(pos, x, out_full, scale, router_t, routes, places, *lows)


def expert_kernel(groups, n_fsdp, info, dy_ref, up_ref, down_ref, *refs):
    cames, refs = refs[:PIECES], refs[PIECES:]
    out_refs, (back_ref, act_ref, rows_ref, grad_in, out_acc, back_acc) = refs[:n_fsdp], refs[n_fsdp:]
    step = pl.program_id(0)
    width = grad_in.shape[1]
    h, f = info[0], info[1]
    source = [
        lax.rem(h + groups - p // n_fsdp, groups) * n_fsdp + jnp.bitwise_xor(f, p % n_fsdp) for p in range(PIECES)
    ]

    @pl.when(step == 0)
    def _():
        came = gather_rows(cames)
        gate = jnp.sum(came[:, width:], axis=1, keepdims=True)
        dy = jnp.concatenate([dy_ref[s].astype(F32) for s in source])
        grad_in[...] = dy
        rows_ref[0] = came[:, :width].astype(BF)
        rows_ref[1] = (gate * dy).astype(BF)
        out_acc[...] = jnp.zeros_like(out_acc)
        back_acc[...] = jnp.zeros_like(back_acc)

    up, down = up_ref[0], down_ref[0]
    upper = dot(rows_ref[0], up)
    active_grad = dot(rows_ref[1], down)
    cdf = 0.5 + 0.5 * lax.erf(upper * 0.7071067811865476)
    active = (upper * cdf).astype(BF)
    slope = cdf + upper * (0.3989422804014327 * jnp.exp(-0.5 * upper * upper))
    upper_grad = (active_grad * slope).astype(BF)
    act_ref[0] = upper_grad
    act_ref[1] = active
    back_acc[...] += dot(upper_grad, up, ((1,), (1,)))
    out_acc[...] += dot(active, down, ((1,), (1,)))

    @pl.when(step == pl.num_programs(0) - 1)
    def _():
        out = out_acc[...].astype(BF).astype(F32)
        gate_grad = three_parts(jnp.sum(grad_in[...] * out, axis=1, keepdims=True)).astype(F32)
        for p in range(PIECES):
            rows = slice(p * CAP, (p + 1) * CAP)
            out_refs[p % n_fsdp][(groups - p // n_fsdp) % groups] = out[rows].astype(BF)
            back_ref[source[p], :, :width] = back_acc[rows, :].astype(BF)
            back_ref[source[p], :, width:] = gate_grad[rows].astype(BF)


def expert(info, cames, dy, up, down, groups, n_fsdp):
    width, ffn = up.shape[1], up.shape[2]
    rows = EXPERTS * CAP
    whole = lambda *shape: pl.BlockSpec(shape, lambda j, info: (0,) * len(shape))
    weight = pl.BlockSpec((1, width, FBLOCK), lambda j, info: (info[0], 0, j))
    return pl.pallas_call(
        functools.partial(expert_kernel, groups, n_fsdp),
        grid_spec=pltpu.PrefetchScalarGridSpec(
            num_scalar_prefetch=1,
            grid=(ffn // FBLOCK,),
            in_specs=[whole(PIECES, CAP, width), weight, weight] + [whole(CAP, width + 128)] * PIECES,
            out_specs=[whole(groups, CAP, width)] * n_fsdp
            + [
                whole(PIECES, CAP, width + 128),
                pl.BlockSpec((2, rows, FBLOCK), lambda j, info: (0, 0, j)),
                whole(2, rows, width),
            ],
            scratch_shapes=[pltpu.VMEM((rows, width), F32)] * 3,
        ),
        out_shape=[pltpu.HBM((groups, CAP, width), BF)] * n_fsdp
        + [
            jax.ShapeDtypeStruct((PIECES, CAP, width + 128), BF),
            pltpu.HBM((2, rows, ffn), BF),
            pltpu.HBM((2, rows, width), BF),
        ],
        compiler_params=pltpu.CompilerParams(vmem_limit_bytes=32 << 20),
        cost_estimate=pl.CostEstimate(flops=10**5, bytes_accessed=10**4, transcendentals=0),
        name="expert",
    )(info, dy, *in_hbm(up, down), *cames)


def weight_kernel(count, members, side, pos, *refs):
    rows, acts, (keep_ref, pass_ref, turned, lhs) = refs[:count], refs[count : 2 * count], refs[2 * count :]
    half = keep_ref.shape[0]

    @pl.when(pl.program_id(0) == 0)
    def _():
        for n in range(count):
            turned[...] = rows[n][0].astype(F32).T.astype(BF)
            if side is not None:
                lhs[n] = turned[side * 2 * half : (side + 1) * 2 * half, :]
                continue
            unit = 2 * half // (GROUPS * members // 2)
            for r in range(members // 2):
                member = jnp.bitwise_xor(pos[0], 2 * r)
                for k in range(GROUPS):
                    row = pl.multiple_of((lax.rem(pos[1] + k, GROUPS) * members + member) * unit, 16)
                    at = (r * GROUPS + k) * unit
                    lhs[n, at : at + unit, :] = turned[pl.ds(row, unit), :]

    keep_ref[...] = sum(dot(lhs[n, :half, :], acts[n][0]) for n in range(count)).astype(BF)
    pass_ref[...] = sum(dot(lhs[n, half:, :], acts[n][0]) for n in range(count)).astype(BF)


def weight_terms(pos, rows, acts, which, members, side=None):
    _, count, width = rows[0].shape
    ffn = acts[0].shape[2]
    half = pl.BlockSpec((width // 4, FBLOCK), lambda j: (0, j))
    return pl.pallas_call(
        functools.partial(weight_kernel, len(rows), members, side),
        grid=(ffn // FBLOCK,),
        in_specs=[SMEM_SPEC]
        + [pl.BlockSpec((1, count, width), lambda j: (which, 0, 0))] * len(rows)
        + [pl.BlockSpec((1, count, FBLOCK), lambda j: (which, 0, j))] * len(rows),
        out_specs=[half, half],
        out_shape=[pltpu.HBM((width // 4, ffn), BF)] * 2,
        scratch_shapes=[pltpu.VMEM((width, count), BF), pltpu.VMEM((len(rows), width // 2, count), BF)],
        compiler_params=pltpu.CompilerParams(vmem_limit_bytes=20 << 20),
        cost_estimate=pl.CostEstimate(flops=10**5, bytes_accessed=10**4, transcendentals=0),
        name="weight_terms",
    )(pos, *rows, *in_hbm(*acts))


def add_kernel(riders, a_ref, b_ref, *refs):
    rides, outs = refs[:riders], refs[riders:]
    rows, width = a_ref.shape[0] // GROUPS, outs[0].shape[1]
    blocks = a_ref.shape[1] // width
    for k, out in enumerate(outs):
        for c in range(blocks):
            at = (slice(k * rows, (k + 1) * rows), slice(c * width, (c + 1) * width))
            out[c * rows : (c + 1) * rows, :] = (a_ref[at].astype(F32) + b_ref[at].astype(F32)).astype(BF)
        if riders:
            ride = jnp.concatenate([r[k].astype(F32) for r in rides])
            out[blocks * rows :, :] = ride.astype(BF)


def add_groups(a, b, width, rides=()):
    rows, cols = a.shape
    count = rows // GROUPS * cols // width + sum(r.shape[1] for r in rides)
    return pl.pallas_call(
        functools.partial(add_kernel, len(rides)),
        in_specs=[all_of(a)] * 2 + [all_of(r) for r in rides],
        out_specs=[pl.BlockSpec((count, width), lambda: (0, 0))] * GROUPS,
        out_shape=[jax.ShapeDtypeStruct((count, width), BF)] * GROUPS,
        compiler_params=pltpu.CompilerParams(vmem_limit_bytes=16 << 20),
        cost_estimate=pl.CostEstimate(flops=10**5, bytes_accessed=10**4, transcendentals=0),
        name="add_groups",
    )(*in_hbm(a, b, *rides))


def order_kernel(blocks, pos, *refs):
    out_ref = refs[-1]
    rows, width = out_ref.shape[1], out_ref.shape[2] // blocks
    for k in range(GROUPS):
        group = group_of(k, pos[1])
        for c in range(blocks):
            out_ref[group, :, c * width : (c + 1) * width] = refs[k][c * rows : (c + 1) * rows, :].astype(F32)


def in_order(pos, parts, rows, cols):
    width = parts[0].shape[1]
    return pl.pallas_call(
        functools.partial(order_kernel, cols // width),
        in_specs=[SMEM_SPEC] + [all_of(p) for p in parts],
        out_specs=pl.BlockSpec((GROUPS, rows, cols), lambda: (0, 0, 0)),
        out_shape=jax.ShapeDtypeStruct((GROUPS, rows, cols), F32),
        compiler_params=pltpu.CompilerParams(vmem_limit_bytes=16 << 20),
        cost_estimate=pl.CostEstimate(flops=10**5, bytes_accessed=10**4, transcendentals=0),
        name="in_order",
    )(pos, *parts)


def turn_kernel(
    info, place_ref, routes_ref, gates_ref, resid_ref, moe_ref, dy_ref, router_ref, scale_ref,
    out_ref, context_ref, back_ref, *refs,
):
    dos, (resid_grad_ref, mine_ref, other_ref, send_ref, router_grad_ref, gain_ref, term) = refs[:GROUPS], refs[GROUPS:]
    tok, width = resid_ref.shape
    back = back_ref[...]
    slots = back.shape[0]
    iota = lax.broadcasted_iota(jnp.int32, (tok, slots), 1)
    pick = [place_ref[:, k : k + 1] == iota for k in range(TOP)]
    gates = [gates_ref[:, k : k + 1] for k in range(TOP)]
    gate_grad = [jnp.sum(dot(p.astype(BF), back[:, width:]), axis=1, keepdims=True) for p in pick]
    mean = gates[0] * gate_grad[0] + gates[1] * gate_grad[1]
    lane = lax.broadcasted_iota(jnp.int32, (tok, 128), 1)
    logit_grad = sum(
        jnp.where(routes_ref[:, k : k + 1] == lane, gates[k] * (gate_grad[k] - mean), 0.0) for k in range(TOP)
    )
    grad = dot((pick[0] | pick[1]).astype(BF), back[:, :width])
    for e in range(EXPERTS):
        grad = grad + logit_grad[:, e : e + 1] * router_ref[e : e + 1, :].astype(F32)
    resid = resid_ref[...]
    inv = lax.rsqrt(jnp.mean(resid * resid, axis=1, keepdims=True) + EPS)
    gain_ref[...] = jnp.sum(grad * (resid * inv), axis=0, keepdims=True)
    scaled = grad * scale_ref[...]
    along = jnp.mean(scaled * resid, axis=1, keepdims=True)
    resid_grad = dy_ref[...].astype(F32) + inv * scaled - resid * (inv * inv * inv * along)
    resid_grad_ref[...] = resid_grad
    low = resid_grad.astype(BF)
    term[:, :tok] = dot(out_ref[...], low, ((1,), (1,)))
    for k in range(GROUPS):
        row = pl.multiple_of(lax.rem(info[0] + k, GROUPS) * GWIDTH, GWIDTH)
        dos[k][...] = term[pl.ds(row, GWIDTH), :tok].astype(BF)
    router_grad_ref[...] = lax.dot_general(
        logit_grad.T[:EXPERTS], moe_ref[...].astype(F32), (((1,), (0,)), ((), ())),
        precision=FULL, preferred_element_type=F32,
    )
    term[...] = dot(low.astype(F32).T.astype(BF), context_ref[...].astype(F32).T.astype(BF))
    rows, cols = mine_ref.shape[1:]
    core, top = info[1], info[2]
    mine = pl.ds(pl.multiple_of(top * cols, 128), cols)
    other = pl.ds(pl.multiple_of((1 - top) * cols, 128), cols)
    for g in range(mine_ref.shape[0]):
        keep = pl.ds(pl.multiple_of((2 * g + core) * rows, 8), rows)
        send = pl.ds(pl.multiple_of((2 * g + 1 - core) * rows, 8), rows)
        mine_ref[g] = term[keep, mine]
        other_ref[g] = term[keep, other]
        send_ref[0, g] = term[send, mine].astype(BF)
        send_ref[1, g] = term[send, other].astype(BF)


def turn_back(info, back, place, routes, gates, resid, moe_in, dy, router, scale, out_full, context, shards):
    tok, width = resid.shape
    rows = width // shards
    part = (shards // 2, rows, width // 2)
    gates, resid, moe_in, dy, out_full, context = in_hbm(gates, resid, moe_in, dy, out_full, context)
    inputs = (place, routes, gates, resid, moe_in, dy, router, scale, out_full, context, back)
    kept = [((tok, width), F32), (part, F32), (part, F32), ((2,) + part, BF), ((EXPERTS, width), F32), ((1, width), F32)]
    kept = [pltpu.HBM(*s) for s in kept]
    return pl.pallas_call(
        turn_kernel,
        in_specs=[SMEM_SPEC] + [all_of(x) for x in inputs],
        out_specs=[VMEM_SPEC] * GROUPS + [all_of(s.inner_aval) for s in kept],
        scratch_shapes=[pltpu.VMEM((width, width), F32)],
        out_shape=[jax.ShapeDtypeStruct((GWIDTH, tok), BF)] * GROUPS + kept,
        compiler_params=pltpu.CompilerParams(vmem_limit_bytes=24 << 20),
        cost_estimate=pl.CostEstimate(flops=10**5, bytes_accessed=10**4, transcendentals=0),
        name="turn_back",
    )(info, *inputs)


def pair_kernel(a_ref, b_ref, c_ref, d_ref, keep_ref, send_ref):
    keep_ref[...] = a_ref[...].astype(F32) + b_ref[...].astype(F32)
    send_ref[...] = (c_ref[...].astype(F32) + d_ref[...].astype(F32)).astype(BF)


def add_pairs(a, b, c, d):
    return pl.pallas_call(
        pair_kernel,
        in_specs=[VMEM_SPEC] * 4,
        out_specs=[VMEM_SPEC] * 2,
        out_shape=[jax.ShapeDtypeStruct(a.shape, F32), jax.ShapeDtypeStruct(a.shape, BF)],
        cost_estimate=pl.CostEstimate(flops=10**5, bytes_accessed=10**4, transcendentals=0),
        compiler_params=pltpu.CompilerParams(vmem_limit_bytes=8 << 20),
        name="add_pairs",
    )(a, b, c, d)


SMALL = 16


def input_kernel(
    members, buckets_here, info, dq_ref, keep_ref, came_ref, ain_ref, weight_ref, scale_ref, router_ref,
    gain_ref, line_ref, dline_ref, own_ref, one_ref, two_ref, three_ref, term_ref, sent_ref, pack_ref, dproj, term,
):
    h, core = info[0], info[1]
    width = ain_ref.shape[1]
    tok = own_ref.shape[0]
    dproj[:, :GWIDTH] = dq_ref[...].astype(F32)
    for k in range(GROUPS):
        dkv = keep_ref[k] if came_ref is None else keep_ref[k] + came_ref[k].astype(F32)
        dproj[k * tok : (k + 1) * tok, GWIDTH:] = dkv.astype(BF).astype(F32)
    low = dproj[...].astype(BF)
    ain = ain_ref[...]
    back = dot(low, weight_ref[...], ((1,), (1,)))
    own_ref[...] = back[:tok]
    for k, ref in enumerate((one_ref, two_ref, three_ref)):
        ref[...] = back[(k + 1) * tok : (k + 2) * tok].astype(BF)
    pack_ref[0:EXPERTS, :] = router_ref[...]
    pack_ref[EXPERTS : EXPERTS + 1, :] = jnp.sum(back * ain.astype(F32), axis=0, keepdims=True) / scale_ref[...]
    pack_ref[EXPERTS + 1 : EXPERTS + 2, :] = gain_ref[...]
    col = lax.broadcasted_iota(jnp.int32, (BUCKETS, width), 1)
    cols_f = width * buckets_here // BUCKETS
    within = lax.rem(col, cols_f) - h * buckets_here
    held = jnp.where((within >= 0) & (within < buckets_here), col // cols_f * buckets_here + within, -1)
    held = held == lax.broadcasted_iota(jnp.int32, (BUCKETS, width), 0)
    bucket = line_ref[...] == lax.broadcasted_iota(jnp.int32, (BUCKETS, line_ref.shape[1]), 0)
    for n in range(GHEADS):
        sums = jnp.sum(jnp.where(bucket, dline_ref[n : n + 1, :], 0.0), axis=1, keepdims=True)
        row = EXPERTS + 2 + n
        pack_ref[row : row + 1, :] = jnp.sum(jnp.where(held, sums, 0.0), axis=0, keepdims=True)
    rest = EXPERTS + 2 + GHEADS
    pack_ref[rest:, :] = jnp.zeros((SMALL - rest, width), F32)
    term[...] = dot(dproj[...].T.astype(BF), ain)
    unit = GWIDTH // members
    for t in range(3):
        for r in range(members // 2):
            at = slice((t * (members // 2) + r) * unit, (t * (members // 2) + r + 1) * unit)
            first = (t * members + 2 * r) * unit
            term_ref[at, :] = term[pl.ds(pl.multiple_of(first + core * unit, 8), unit), :]
            sent_ref[at, :] = term[pl.ds(pl.multiple_of(first + (1 - core) * unit, 8), unit), :].astype(BF)
    pack = pack_ref[...]
    high = pack.astype(BF)
    rows = term_ref.shape[0]
    sent_ref[rows : rows + SMALL, :] = high
    sent_ref[rows + SMALL :, :] = (pack - high.astype(F32)).astype(BF)


def input_back(info, members, buckets_here, dq, keep, came, ain, weight, scale, router_grad, gain_grad, line, dline):
    count, width = ain.shape
    tok = count // GROUPS
    rows = 3 * GWIDTH // 2
    ain, weight = in_hbm(ain, weight)
    inputs = [dq, keep] + ([] if came is None else [came]) + [ain, weight, scale, router_grad, gain_grad, line, dline]
    body = functools.partial(input_kernel, members, buckets_here)
    if came is None:
        body = lambda info, dq, keep, *refs: input_kernel(members, buckets_here, info, dq, keep, None, *refs)
    return pl.pallas_call(
        body,
        in_specs=[SMEM_SPEC] + [all_of(x) for x in inputs],
        out_specs=[VMEM_SPEC] * 7,
        out_shape=[jax.ShapeDtypeStruct((tok, width), F32)]
        + [jax.ShapeDtypeStruct((tok, width), BF)] * 3
        + [
            jax.ShapeDtypeStruct((rows, width), F32),
            jax.ShapeDtypeStruct((rows + 2 * SMALL, width), BF),
            jax.ShapeDtypeStruct((SMALL, width), F32),
        ],
        scratch_shapes=[pltpu.VMEM((count, 3 * GWIDTH), F32), pltpu.VMEM((3 * GWIDTH, width), F32)],
        compiler_params=pltpu.CompilerParams(vmem_limit_bytes=24 << 20),
        cost_estimate=pl.CostEstimate(flops=10**5, bytes_accessed=10**4, transcendentals=0),
        name="input_back",
    )(info, *inputs)


def together(*values):
    return lax.optimization_barrier(values)


def turn(shift):
    return [(i, (i + shift) % GROUPS) for i in range(GROUPS)]


def gather_groups(x):
    came = {k: lax.ppermute(x, "h", turn(k)) for k in (2, 1, 3)}
    return jnp.stack([x] + [came[k] for k in range(1, GROUPS)])


def gather_members(x):
    size = lax.axis_size(MEMBERS)
    held = {0: x}
    for bit in bits_of(size):
        for k in sorted(held):
            held[k | bit] = lax.ppermute(held[k], MEMBERS, xor_perm(bit, size))
    return [held[k] for k in range(size)]


def part_of(x, mine):
    low, high = jnp.split(x, 2, axis=-1)
    return jnp.where(mine == 0, low, high), jnp.where(mine == 0, high, low)


def swap(x, axis, bit):
    return lax.ppermute(x, axis, xor_perm(bit, lax.axis_size(axis)))


def two_parts(x):
    high = lax.reduce_precision(x, 8, 7)
    return jnp.concatenate([high, x - high]).astype(BF)


def from_fsdp(part):
    if lax.axis_size("fsdp") != 2:
        return lax.all_gather(part, "fsdp", axis=0)
    came = lax.ppermute(part, "fsdp", xor_perm(1, 2))
    return jnp.where(lax.axis_index("fsdp") == 0, jnp.stack([part, came]), jnp.stack([came, part]))


def group_pieces(pieces, sign):
    came = {k: lax.ppermute(pieces[k], "h", turn(sign * k)) for k in (2, 1, 3)}
    return [pieces[0]] + [came[k] for k in range(1, GROUPS)]


def deal(pieces, spread, sign):
    n_fsdp = lax.axis_size("fsdp")
    out = [pieces[0]] + [None] * (len(pieces) - 1)
    for p in (5, 4, 3, 7, 2, 6, 1):
        k, j = divmod(p, n_fsdp)
        if spread:
            pairs = [
                (g * n_fsdp + i, (g + sign * k) % GROUPS * n_fsdp + (i ^ j))
                for g in range(GROUPS)
                for i in range(n_fsdp)
            ]
            out[p] = lax.ppermute(pieces[p], ("h", "fsdp"), pairs)
        else:
            out[p] = lax.ppermute(pieces[p], "fsdp", xor_perm(j, n_fsdp))
    return out


def per_device(
    tokens, segments, routes, bucket_table, attn_gain, qkv_weight, out_weight, bias_table,
    moe_gain, router_weight, up_weight, down_weight, cotangent,
):
    tok, width = tokens.shape[1], tokens.shape[2]
    half = tok // 2
    h, m, f = lax.axis_index("h"), lax.axis_index(MEMBERS), lax.axis_index("fsdp")
    core = lax.axis_index("core")
    members, n_fsdp = lax.axis_size(MEMBERS), lax.axis_size("fsdp")
    shards = GROUPS * members
    blocks = 2 * shards
    length = shards * tok
    here = EXPERTS // n_fsdp
    spread = here > 1
    ffn = up_weight.shape[2]
    rows_f = width // n_fsdp
    rows_c = width // shards
    pos = jnp.stack([m, h]).astype(jnp.int32)

    extra = jnp.pad(segments.astype(BF), ((0, 7), (0, width - tok)))
    mixed = gather_groups(jnp.concatenate([tokens[0], extra]))

    bias_flat = bias_table.reshape(1, -1)
    bias_rows = -(-bias_flat.shape[1] // rows_f)
    bias_flat = jnp.pad(bias_flat, ((0, 0), (0, bias_rows * rows_f - bias_flat.shape[1])))
    small = jnp.concatenate(
        [attn_gain[None], moe_gain[None], router_weight.T, bias_flat.reshape(bias_rows, rows_f)]
        + [jnp.zeros((16 - 10 - bias_rows, rows_f), BF)]
    )
    small = from_fsdp(small)
    attn_scale = small[:, 0].reshape(width).astype(F32)
    moe_scale = small[:, 1].reshape(width).astype(F32)
    router_t = jnp.transpose(small[:, 2:10], (1, 0, 2)).reshape(EXPERTS, width)
    bias_full = small[:, 10 : 10 + bias_rows].reshape(n_fsdp, -1)[:, : bias_table.size]
    bias_full = bias_full.reshape(BUCKETS, HEADS)
    cut = [
        lax.dynamic_slice_in_dim(qkv_weight, n * width + h * GWIDTH, GWIDTH, 1) for n in range(3)
    ]
    qkv_heads = from_fsdp(jnp.concatenate(cut, axis=1)).reshape(width, 3 * GWIDTH)
    out_full = from_fsdp(together(out_weight, qkv_heads)[0]).reshape(width, width)

    wide = strip_width(blocks, half)
    top = half * (blocks - 1)
    line = jnp.concatenate(
        [
            bucket_table[: top + 1][::-1],
            jnp.full((wide - length,), -1, jnp.int32),
            bucket_table[top + 1 :][::-1],
        ]
    )
    hot = (line[None] == jnp.arange(BUCKETS, dtype=jnp.int32)[:, None]).astype(BF)
    bias_mine = lax.dynamic_slice_in_dim(bias_full, h * GHEADS, GHEADS, 1)
    strips = make_strips(dot(bias_mine, hot, ((0,), (0,))) * LOG2E, half)

    hot_routes = (routes.reshape(-1)[:, None] == jnp.arange(EXPERTS)[None]).astype(F32)
    earlier = jnp.arange(tok * TOP)
    earlier = (earlier[None, :] < earlier[:, None]).astype(BF)
    before = dot(earlier, hot_routes.astype(BF))
    slot = jnp.sum(before * hot_routes, axis=1).astype(jnp.int32).reshape(tok, TOP)
    group = routes % here
    natural = (group * n_fsdp + routes // here) * CAP + slot
    away = lax.rem(group - h + GROUPS, GROUPS) if spread else group
    place = (away * n_fsdp + jnp.bitwise_xor(routes // here, f)) * CAP + slot
    slots = jnp.arange(EXPERTS * CAP, dtype=jnp.int32)
    pick = [slots[:, None] == natural[None, :, k] for k in range(TOP)]
    exchange = ("h", "fsdp") if spread else ("fsdp",)

    def exchange_rows(rows):
        return lax.all_to_all(rows, exchange, 0, 0, tiled=True)

    mixed, strips = together(mixed, strips)
    ain = normalize(mixed[:, :tok].astype(F32), attn_scale).astype(BF).reshape(GROUPS * tok, width)
    proj = dot(ain, qkv_heads).astype(BF)
    kv = proj[:, GWIDTH:].reshape(GROUPS, tok, 2 * GWIDTH)
    kvs = gather_members(jnp.concatenate([kv, mixed[:, tok:, : 2 * GWIDTH]], axis=1))
    dy_send = dot((pick[0] | pick[1]).astype(BF), cotangent[0]).astype(BF).reshape(PIECES, CAP, width)
    dy_slots = exchange_rows(together(dy_send, proj)[0])
    o_pre, *rest = attend(pos, proj, kvs, strips, blocks)
    lows, stat, keys = rest[:GROUPS], rest[GROUPS], rest[GROUPS + 1 :]
    lows[1], dy_slots = together(lows[1], dy_slots)
    *pieces, context, residual, moe_in, gates = router(
        pos, tokens[0], out_full, moe_scale[None], router_t, routes, place.T, group_pieces(lows, -1)
    )

    came = deal(pieces, spread, 1)
    info = jnp.stack([h if spread else jnp.zeros_like(h), f]).astype(jnp.int32)
    *outs, back, act, rows = expert(
        info, came, dy_slots, up_weight, down_weight, GROUPS if spread else 1, n_fsdp
    )
    back = exchange_rows(back).reshape(EXPERTS * CAP, -1)

    staged = spread and members == 4
    if staged:
        rows, acts = [rows, swap(rows, "core", 1)], [act, swap(act, "core", 1)]
        terms = [weight_terms(pos, rows, acts, n, members) for n in range(2)]
        back, terms = together(back, terms)
    else:
        terms = [weight_terms(pos, [rows], [act], n, members, side) for n in range(2) for side in range(2)]

    top_bit = n_fsdp // 2
    info = jnp.stack([h, core, (f // top_bit) % 2]).astype(jnp.int32)
    *dos, resid_grad, out_mine, out_other, out_send, router_grad, moe_gain_grad = turn_back(
        info, back, natural, routes, gates, residual, moe_in, cotangent[0], router_t,
        moe_scale[None], out_full, context, shards,
    )
    dos = group_pieces(dos, 1)
    out_came = swap(out_send, "core", 1)
    out_far = (out_other + out_came[1].astype(F32)).astype(BF)
    outs = [outs[0]] + [lax.ppermute(outs[j], "fsdp", xor_perm(j, n_fsdp)) for j in range(1, n_fsdp)]
    dos[0], out_far = together(dos[0], out_far)
    out_far = swap(out_far, "fsdp", top_bit)
    dq, *dkvs, dline = attend_back(pos, proj, keys, strips, dos, o_pre, stat, members, blocks)
    dkvs[1], out_far, outs = together(dkvs[1], out_far, outs)
    cames = [swap(dkvs[k], "core", 1) for k in range(1, members, 2)]
    sends = []
    if members == 4:
        keep, send = add_pairs(dkvs[0], cames[0], dkvs[2], cames[1])
        if staged:
            sends = [swap(terms[0][1], "r", 1)]
            send, sends[0] = together(send, sends[0])
        came = swap(send, "r", 1)
    else:
        held = {k: dkvs[k].astype(F32) + cames[k // 2].astype(F32) for k in range(0, members, 2)}
        bit = 2
        while bit < members:
            for k in [k for k in sorted(held) if k & bit]:
                held[k - bit] = held[k - bit] + swap(held.pop(k).astype(BF), "r", bit // 2).astype(F32)
            bit *= 2
        keep, came = held[0], None
    if staged:
        up_came = group_pieces(add_groups(terms[0][0], sends[0], width, outs), 1)
        sends.append(swap(together(terms[1][1], came)[0], "r", 1))
        came, up_came[1] = together(came, up_came[1])

    own_back, back_1, back_2, back_3, term, sent, pack = input_back(
        jnp.stack([h, core]).astype(jnp.int32), members, BUCKETS // n_fsdp, dq, keep, came, ain, qkv_heads,
        attn_scale[None], router_grad, moe_gain_grad, line[None], dline,
    )

    def swap_both(send, pack, axis, bit):
        sent = jnp.concatenate([send.reshape(-1, send.shape[-1]).astype(BF), two_parts(pack)])
        return split_rows(swap(sent, axis, bit).astype(F32), send.shape)

    def split_rows(came, shape):
        return came[: -2 * SMALL].reshape(shape), came[-2 * SMALL : -SMALL] + came[-SMALL:]

    unit = GWIDTH // members
    came, pack_came = split_rows(swap(sent, "core", 1).astype(F32), term.shape)
    term, pack = term + came, pack + pack_came
    out_term = out_mine + out_came[0].astype(F32) + out_far.astype(F32)
    for bit in list(bits_of(n_fsdp))[1:]:
        out_term, out_send = part_of(out_term, (f // bit) % 2)
        out_term = out_term + swap(out_send.astype(BF), "fsdp", bit).astype(F32)
    for bit in bits_of(n_fsdp):
        term, send = part_of(term, (f // bit) % 2)
        pack, pack_send = part_of(pack, (f // bit) % 2)
        came, pack_came = swap_both(send, pack_send, "fsdp", bit)
        term, pack = term + came, pack + pack_came
    term = jnp.concatenate(
        [term.reshape(3, members // 2, unit, rows_f).swapaxes(0, 1).reshape(members // 2, -1, rows_f)]
        + [out_term.reshape(GROUPS, members // 2, rows_c, rows_f).swapaxes(0, 1).reshape(members // 2, -1, rows_f)],
        axis=1,
    )
    if staged:
        term, sends[1], up_came = together(term, sends[1], up_came)
    for bit in bits_of(members // 2):
        mine = (lax.axis_index("r") // bit) % 2
        term = term.reshape((2, -1) + term.shape[1:])
        came, pack_came = swap_both(lax.dynamic_index_in_dim(term, 1 - mine, 0, False), pack, "r", bit)
        term = lax.dynamic_index_in_dim(term, mine, 0, False) + came
        pack = pack + pack_came
    term = term[0]
    if staged:
        back_2, up_came = together(back_2, up_came)
        back_3, term = together(back_3, term)
    mid = lax.ppermute(back_2, "h", turn(-1))
    side = lax.ppermute(back_3, "h", turn(1)).astype(F32)
    mid = (back_1.astype(F32) + mid.astype(F32)).astype(BF)
    mid = lax.ppermute(mid, "h", turn(-1)).astype(F32)
    attn_in_grad = own_back + side + mid
    x = tokens[0].astype(F32)
    token_grad = jax.vjp(lambda v: normalize(v, attn_scale), x)[1](attn_in_grad)[0]
    tokens_grad = (resid_grad + token_grad).astype(BF)

    out_term = term[3 * unit :].reshape(GROUPS, rows_c, rows_f)
    term = term[: 3 * unit].astype(BF).reshape(3, unit, rows_f)
    if staged:
        down_came = group_pieces(add_groups(terms[1][0], sends[1], width), 1)
    out_sum, pack_sum = lax.dynamic_index_in_dim(out_term, h, 0, False), pack
    for k in (2, 1, 3):
        piece = lax.dynamic_index_in_dim(out_term, lax.rem(h + k, GROUPS), 0, False)
        came = lax.ppermute(jnp.concatenate([piece.astype(BF), two_parts(pack)]), "h", turn(k)).astype(F32)
        out_sum = out_sum + came[:rows_c]
        pack_sum = pack_sum + came[rows_c : rows_c + SMALL] + came[rows_c + SMALL :]
    at = h * members + m
    parts = []
    for r in range(3):
        pairs = [((3 * d + r) % shards, d) for d in range(shards)]
        third = pow(3, -1, shards)
        which = (3 * lax.rem((at + shards - r) * third, shards) + r) // shards
        parts.append(lax.ppermute(lax.dynamic_index_in_dim(term, which, 0, False), CTX, pairs))
    if staged:
        up_came, parts = together(up_came, parts)
        grads = [in_order(pos, part, rows_c, ffn) for part in (up_came, down_came)]
        home = jnp.concatenate([part[rows_c * ffn // width :] for part in up_came])
    else:
        terms = [jnp.concatenate(terms[n] + terms[n + 1]) for n in (0, 2)]
        grads = [
            lax.psum_scatter(term, CTX, scatter_dimension=0, tiled=True)[None].astype(F32) for term in terms
        ]
        home = jnp.concatenate([o.reshape(-1, width) for o in outs])
    qkv_grad = jnp.concatenate(parts).astype(F32).T

    away = lax.rem(h - group + GROUPS, GROUPS) if spread else group
    place = (away * n_fsdp + jnp.bitwise_xor(routes // here, f)) * CAP + slot
    layer_out = residual
    for k in range(TOP):
        row = (slots[:, None] == place[None, :, k]).astype(BF)
        layer_out = layer_out + gates[:, k : k + 1] * dot(row, home, ((0,), (0,)))
    bias_grad = pack_sum[EXPERTS + 2 : EXPERTS + 2 + GHEADS, : GROUPS * BUCKETS // n_fsdp]
    bias_grad = bias_grad.reshape(GHEADS, GROUPS, BUCKETS // n_fsdp).transpose(2, 1, 0).reshape(-1, HEADS)
    return (
        layer_out.astype(BF)[None],
        tokens_grad[None],
        pack_sum[8],
        qkv_grad,
        out_sum.T,
        bias_grad,
        pack_sum[9],
        pack_sum[:8].T,
        grads[0],
        grads[1],
    )


def solution(mesh):
    n_ctx, n_fsdp = mesh.shape["ctx"], mesh.shape["fsdp"]
    cut = mesh.devices.reshape(GROUPS, n_ctx // (2 * GROUPS), 2, n_fsdp)
    row = P("fsdp", CTX, None)
    return jax.shard_map(
        per_device,
        mesh=Mesh(cut, CTX + ("fsdp",)),
        in_specs=(
            row,
            P("fsdp", CTX),
            P(CTX + ("fsdp",), None),
            P(),
            P("fsdp"),
            P("fsdp", None),
            P("fsdp", None),
            P("fsdp", None),
            P("fsdp"),
            P("fsdp", None),
            P("fsdp", None, None),
            P("fsdp", None, None),
            row,
        ),
        out_specs=(
            row,
            row,
            P("fsdp"),
            P("fsdp", CTX),
            P("fsdp", CTX),
            P("fsdp", None),
            P("fsdp"),
            P("fsdp", None),
            row,
            row,
        ),
        check_vma=False,
    )
```

```python
import functools

import jax
import jax.numpy as jnp
from jax import lax
from jax.experimental import pallas as pl
from jax.experimental.pallas import tpu as pltpu
from jax.sharding import Mesh, PartitionSpec as P

HEADS = 12
HEAD_DIM = 64
EXPERTS = 8
TOP = 2
BUCKETS = 32
DOCS = 8
CAP = 40
GROUPS = 4
GHEADS = HEADS // GROUPS
GWIDTH = GHEADS * HEAD_DIM
CHUNK = 256

LOG2E = 1.4426950408889634
EPS = 1e-06
LOWEST = -1e30
FULL = lax.Precision.HIGHEST
BF = jnp.bfloat16
F32 = jnp.float32
MEMBERS = ("r", "core")
CTX = ("h", "r", "core")


def normalize(values, weight):
    inv_rms = lax.rsqrt(jnp.mean(values * values, axis=-1, keepdims=True) + EPS)
    return values * inv_rms * weight


def dot(a, b, dims=((1,), (0,))):
    return lax.dot_general(a, b, (dims, ((), ())), preferred_element_type=F32)


def exact_dot(a, b, dims):
    return lax.dot_general(a, b, (dims, ((), ())), precision=FULL)


def xor_perm(mask, size):
    return [(i, i ^ mask) for i in range(size)]


def bits_of(size):
    bit = size // 2
    while bit:
        yield bit
        bit //= 2


def strip_width(blocks, half):
    need = half * (blocks - 1) + CHUNK + half
    return -(-need // 128) * 128


def strips_kernel(g_ref, out_ref):
    half = out_ref.shape[1] // GHEADS
    rolled = [
        pltpu.roll(
            jnp.broadcast_to(g_ref[n : n + 1, :], (half, g_ref.shape[1])), 0, 1, stride=1, stride_axis=0
        )
        for n in range(GHEADS)
    ]
    out_ref[...] = jnp.concatenate(rolled).T


def make_strips(lines, half):
    return pl.pallas_call(
        strips_kernel,
        out_specs=pl.BlockSpec((lines.shape[1], GHEADS * half), lambda: (0, 0)),
        out_shape=pltpu.HBM((lines.shape[1], GHEADS * half), F32),
        cost_estimate=pl.CostEstimate(flops=10**5, bytes_accessed=10**4, transcendentals=0),
        name="strips",
    )(lines)


def own_blocks(size, half):
    a = lax.broadcasted_iota(jnp.int32, (size, size), 0) // half
    b = lax.broadcasted_iota(jnp.int32, (size, size), 1) // half
    return a == b


def spread_rows(x, same):
    return jnp.where(same, jnp.concatenate([x] * GHEADS), 0.0)


def identity(size):
    a, b = (lax.broadcasted_iota(jnp.int32, (size, size), n) for n in range(2))
    return jnp.where(a == b, 1.0, 0.0).astype(BF)


def own_columns(x, half):
    return jnp.concatenate(
        [x[n * HEAD_DIM : (n + 1) * HEAD_DIM, n * half : (n + 1) * half] for n in range(GHEADS)]
    )


def fold_rows(x, same, half):
    y = jnp.where(same, x, 0.0).T
    return sum(y[n * half : (n + 1) * half] for n in range(GHEADS))


def spread_columns(x, same):
    return jnp.where(same, jnp.concatenate([x] * GHEADS, axis=1), 0.0)


def group_of(slot, h):
    return lax.rem(h + GROUPS - slot, GROUPS)


def place_of(slot, early, me, h, members, blocks):
    owner = group_of(slot, h) * members + me
    return owner if early else blocks - 1 - owner


def bounds(block, chunk, half, blocks, start):
    top = (blocks - 1 - (block - (CHUNK // half) * chunk)) * half
    lane = lax.broadcasted_iota(jnp.int32, (1, GHEADS * half), 1)
    last = block * half + lax.rem(lane, half) - chunk * CHUNK
    return pl.multiple_of(top, half), last, start - chunk * CHUNK


def forward_kernel(half, blocks, members, pos, q_ref, *refs):
    kvs, refs = refs[:members], refs[members:]
    strip_in, o_ref, *lows, stat_ref, k_out, v_out, kt_out, k_ref, v_ref, kt_ref, vt, strip_ref, low, sems, strip_sem = refs
    loads = start_copies([(strip_in, strip_ref)], strip_sem)
    size = GHEADS * half
    me, h = pos[0], pos[1]
    tok = 2 * half
    same = own_blocks(size, half)
    key = lax.broadcasted_iota(jnp.int32, (CHUNK, size), 0)
    per = CHUNK // half

    @pl.loop(0, GROUPS, unroll=2)
    def _(slot):
        for j in range(members):
            for early in (True, False):
                block = place_of(slot, early, jnp.bitwise_xor(me, j), h, members, blocks)
                at = pl.ds(pl.multiple_of(lax.rem(block, per) * half, half), half)
                rows = kvs[j][slot, 0 if early else half : half if early else tok, :]
                k_ref[block // per, at, :] = rows[:, :GWIDTH]
                v_ref[block // per, at, :] = rows[:, GWIDTH:]

    eye = identity(GWIDTH)

    @pl.loop(0, blocks // per, unroll=4)
    def _(chunk):
        kt_ref[chunk] = dot(eye, k_ref[chunk], ((1,), (1,))).astype(BF)
        vt[chunk] = dot(eye, v_ref[chunk], ((1,), (1,))).astype(BF)

    copies = start_copies([(k_ref, k_out), (v_ref, v_out), (kt_ref, kt_out)], sems)
    docs = jnp.concatenate([kv[a, tok : tok + 1, :tok].astype(F32) for kv in kvs for a in range(GROUPS)])
    begins = [jnp.sum(jnp.where(docs < s, 1.0, 0.0)) for s in range(1, DOCS)]
    for load in loads:
        load.wait()

    def prepare(slot, late):
        owner = group_of(slot, h) * members + me
        block = owner if late == 0 else blocks - 1 - owner
        at = pl.ds(pl.multiple_of(slot * tok + late * half, half), half)
        qs = spread_rows(q_ref[at, :GWIDTH].astype(F32), same).astype(BF)
        qt = dot(eye, qs, ((1,), (1,))).astype(BF)
        doc = kvs[0][slot, tok : tok + 1, :tok].astype(F32)[:, late * half : (late + 1) * half]
        begin = jnp.zeros((1, half), F32)
        for s in range(1, DOCS):
            begin = jnp.where(doc == s, begins[s - 1], begin)
        first = jnp.min(begin).astype(jnp.int32) // CHUNK
        begin = jnp.concatenate([begin] * GHEADS, axis=1)
        return block, first, block // per, begin, qt

    def advance(state, step, carry):
        block, first, final, begin, qt = state
        peak, total, acc = carry
        chunk = jnp.minimum(first + step, final)
        top, last, begin = bounds(block, chunk, half, blocks, begin.astype(jnp.int32))
        last = jnp.where(first + step <= final, last, -1)
        t = dot(k_ref[chunk], qt) * (HEAD_DIM**-0.5 * LOG2E) + strip_ref[pl.ds(top, CHUNK), :]
        t = jnp.where((key <= last) & (key >= begin), t, LOWEST)
        new = jnp.maximum(peak, jnp.ceil(jnp.max(t, axis=0, keepdims=True)))
        e = jnp.exp2(t - new)
        fade = jnp.exp2(peak - new)
        total = total * fade + jnp.sum(e, axis=0, keepdims=True)
        acc = acc * fade + dot(vt[chunk], e.astype(BF))
        return new, total, acc

    init = (
        jnp.full((1, size), LOWEST, F32),
        jnp.zeros((1, size), F32),
        jnp.zeros((GWIDTH, size), F32),
    )

    def pair_of(pair, late):
        slots = [group_of(2 * pair + n, h) for n in range(2)]
        states = [prepare(slot, late) for slot in slots]
        steps = functools.reduce(jnp.maximum, [s[2] - s[1] + 1 for s in states])
        done = lax.fori_loop(
            0, steps, lambda i, c: tuple(advance(s, i, x) for s, x in zip(states, c)), (init,) * 2
        )
        for slot, state, (peak, total, acc) in zip(slots, states, done):
            out = own_columns(acc / total, half)
            o_ref[2 * slot + late] = out
            low[slot, :, late * half : (late + 1) * half] = out.astype(BF)
            stat_ref[2 * slot + late, 0:1, :] = peak
            stat_ref[2 * slot + late, 1:2, :] = total
            stat_ref[2 * slot + late, 2:3, :] = state[3]

    @pl.loop(0, GROUPS // 2)
    def _(pair):
        pair_of(pair, 0)
        pair_of(pair, 1)

    for n in range(GROUPS):
        lows[n][...] = low[n]
    for copy in copies:
        copy.wait()


def backward_kernel(half, blocks, members, pos, *refs):
    dos, refs = refs[:GROUPS], refs[GROUPS:]
    inputs, (dq_ref, *refs) = refs[:7], refs[7:]
    dkvs, refs = refs[:members], refs[members:]
    dline_ref, *held, dk, dv, dstrip, do_ref, sems = refs
    q_ref, strip_ref, o_ref, stat_ref, k_ref, v_ref, kt_ref = held
    size = GHEADS * half
    me, h = pos[0], pos[1]
    width = dstrip.shape[0]
    per = CHUNK // half
    copies = start_copies(list(zip(inputs, held)), sems)
    same = own_blocks(size, half)
    key = lax.broadcasted_iota(jnp.int32, (CHUNK, size), 0)

    @pl.loop(0, blocks // per, unroll=4)
    def _(chunk):
        dk[chunk] = jnp.zeros(dk.shape[1:], F32)
        dv[chunk] = jnp.zeros(dv.shape[1:], F32)

    @pl.loop(0, width // 128, unroll=2)
    def _(j):
        dstrip[pl.ds(pl.multiple_of(j * 128, 128), 128), :] = jnp.zeros((128, size), F32)

    for n in range(GROUPS):
        do_ref[n] = dos[n][...].astype(F32)
    for copy in copies:
        copy.wait()

    def prepare(slot, late):
        i = 2 * slot + late
        owner = group_of(slot, h) * members + me
        block = owner if late == 0 else blocks - 1 - owner
        at = pl.ds(pl.multiple_of(slot * 2 * half + late * half, half), half)
        peak, total, start = (stat_ref[i, n : n + 1, :] for n in range(3))
        first = jnp.min(start).astype(jnp.int32) // CHUNK
        qs = spread_rows(q_ref[at, :GWIDTH].astype(F32), same)
        qt, qs = qs.T.astype(BF), qs.astype(BF)
        do = do_ref[slot][:, late * half : (late + 1) * half]
        corr = jnp.sum(spread_columns(do * o_ref[i], same), axis=0, keepdims=True) / total
        gt = spread_columns(do, same) / total
        gs = gt.T.astype(BF)
        return block, first, block // per, start.astype(jnp.int32), peak, corr, qt, qs, gt.astype(BF), gs, at

    def scores(state, step):
        block, first, final, start, peak, corr, qt, _, gt = state[:9]
        chunk = jnp.minimum(first + step, final)
        top, last, begin = bounds(block, chunk, half, blocks, start)
        last = jnp.where(first + step <= final, last, -1)
        t = dot(k_ref[chunk], qt) * (HEAD_DIM**-0.5 * LOG2E) + strip_ref[pl.ds(top, CHUNK), :]
        t = jnp.where((key <= last) & (key >= begin), t - peak, LOWEST)
        e = jnp.exp2(t)
        return chunk, top, e.astype(BF), e * (dot(v_ref[chunk], gt) - corr)

    def pair_of(pair, late):
        states = [prepare(group_of(2 * pair + n, h), late) for n in range(2)]

        def visit(step, carry):
            found = [scores(s, step) for s in states]
            out = []
            for (chunk, top, e, s), state, dq in zip(found, states, carry):
                low = s.astype(BF)
                dk[chunk] += dot(low, state[7])
                dv[chunk] += dot(e, state[9])
                dstrip[pl.ds(top, CHUNK), :] += s
                out.append(dq + dot(kt_ref[chunk], low))
            return tuple(out)

        steps = functools.reduce(jnp.maximum, [s[2] - s[1] + 1 for s in states])
        done = lax.fori_loop(0, steps, visit, (jnp.zeros((GWIDTH, size), F32),) * 2)
        for state, dq in zip(states, done):
            dq_ref[state[10], :] = (fold_rows(dq, same, half) * HEAD_DIM**-0.5).astype(BF)

    @pl.loop(0, GROUPS // 2)
    def _(pair):
        pair_of(pair, 0)
        pair_of(pair, 1)

    @pl.loop(0, GROUPS, unroll=2)
    def _(slot):
        for j in range(members):
            for early in (True, False):
                block = place_of(slot, early, jnp.bitwise_xor(me, j), h, members, blocks)
                at = pl.ds(pl.multiple_of(lax.rem(block, per) * half, half), half)
                part = jnp.concatenate(
                    [dk[block // per, at, :] * HEAD_DIM**-0.5, dv[block // per, at, :]], axis=1
                )
                dkvs[j][slot, 0 if early else half : half if early else 2 * half, :] = part.astype(BF)

    lines = dstrip[...].T
    for n in range(GHEADS):
        x = lines[n * half : (n + 1) * half]
        rows = half
        while rows > 8:
            rows //= 2
            x = x[:rows] + pltpu.roll(x[rows:], width - rows, 1)
        sub = lax.broadcasted_iota(jnp.int32, x.shape, 0)
        for bit in (4, 2, 1):
            x = jnp.where((sub & bit) != 0, pltpu.roll(x, width - bit, 1), x)
        dline_ref[n : n + 1, :] = jnp.sum(x, axis=0, keepdims=True)


VMEM_SPEC = pl.BlockSpec(memory_space=pltpu.VMEM)
SMEM_SPEC = pl.BlockSpec(memory_space=pltpu.SMEM)
HBM_SPEC = pl.BlockSpec(memory_space=pltpu.HBM)


def in_hbm(*values):
    return [pltpu.with_memory_space_constraint(v, pltpu.HBM) for v in values]


def all_of(x):
    return pl.BlockSpec(x.shape, lambda: (0,) * len(x.shape))


def start_copies(pairs, sems):
    copies = [pltpu.make_async_copy(src, dst, sems.at[i]) for i, (src, dst) in enumerate(pairs)]
    for copy in copies:
        copy.start()
    return copies


def key_shapes(blocks, half):
    chunks = blocks * half // CHUNK
    return ((chunks, CHUNK, GWIDTH), (chunks, CHUNK, GWIDTH), (chunks, GWIDTH, CHUNK))


def attend(pos, q, kvs, strips, blocks):
    rows = q.shape[0]
    half = strips.shape[1] // GHEADS
    shapes = key_shapes(blocks, half)
    o_shape, stat_shape = (rows // half, GWIDTH, half), (rows // half, 8, GHEADS * half)
    return pl.pallas_call(
        functools.partial(forward_kernel, half, blocks, len(kvs)),
        in_specs=[SMEM_SPEC] + [VMEM_SPEC] * (1 + len(kvs)) + [HBM_SPEC],
        out_specs=[all_of(jax.ShapeDtypeStruct(o_shape, F32))]
        + [VMEM_SPEC] * GROUPS
        + [all_of(jax.ShapeDtypeStruct(stat_shape, F32))]
        + [HBM_SPEC] * 3,
        scratch_shapes=[pltpu.VMEM(s, BF) for s in shapes + shapes[2:]]
        + [
            pltpu.VMEM(strips.shape, F32),
            pltpu.VMEM((GROUPS, GWIDTH, 2 * half), BF),
            pltpu.SemaphoreType.DMA((3,)),
            pltpu.SemaphoreType.DMA((1,)),
        ],
        out_shape=[pltpu.HBM(o_shape, F32)]
        + [jax.ShapeDtypeStruct((GWIDTH, 2 * half), BF)] * GROUPS
        + [pltpu.HBM(stat_shape, F32)]
        + [pltpu.HBM(s, BF) for s in shapes],
        compiler_params=pltpu.CompilerParams(vmem_limit_bytes=32 << 20),
        cost_estimate=pl.CostEstimate(flops=10**5, bytes_accessed=10**4, transcendentals=0),
        name="attend",
    )(pos, q, *kvs, *in_hbm(strips))


def attend_back(pos, q, keys, strips, dos, o, stat, members, blocks):
    rows = q.shape[0]
    half = strips.shape[1] // GHEADS
    shapes = key_shapes(blocks, half)
    kv = jax.ShapeDtypeStruct((GROUPS, 2 * half, 2 * GWIDTH), BF)
    inputs = in_hbm(q, strips, o, stat, *keys)
    return pl.pallas_call(
        functools.partial(backward_kernel, half, blocks, members),
        in_specs=[SMEM_SPEC] + [VMEM_SPEC] * GROUPS + [HBM_SPEC] * len(inputs),
        out_specs=[VMEM_SPEC] * (1 + members) + [pl.BlockSpec((GHEADS, strips.shape[0]), lambda: (0, 0))],
        scratch_shapes=[pltpu.VMEM(x.shape, x.dtype) for x in inputs]
        + [pltpu.VMEM(s, F32) for s in shapes[:2]]
        + [
            pltpu.VMEM(strips.shape, F32),
            pltpu.VMEM((GROUPS, GWIDTH, 2 * half), F32),
            pltpu.SemaphoreType.DMA((len(inputs),)),
        ],
        out_shape=[jax.ShapeDtypeStruct((rows, GWIDTH), BF)]
        + [kv] * members
        + [pltpu.HBM((GHEADS, strips.shape[0]), F32)],
        compiler_params=pltpu.CompilerParams(vmem_limit_bytes=40 << 20),
        cost_estimate=pl.CostEstimate(flops=10**5, bytes_accessed=10**4, transcendentals=0),
        name="attend_back",
    )(pos, *dos, *inputs)


FBLOCK = 768
PIECES = 8


def three_parts(x):
    high = x.astype(BF).astype(F32)
    mid = (x - high).astype(BF).astype(F32)
    low = x - high - mid
    lane = lax.broadcasted_iota(jnp.int32, (x.shape[0], 128), 1)
    return jnp.where(lane == 0, high, jnp.where(lane == 1, mid, jnp.where(lane == 2, low, 0.0))).astype(BF)


def gather_rows(refs):
    return jnp.concatenate([r[...].astype(F32) for r in refs])


def router_kernel(
    pos, x_ref, out_ref, scale_ref, router_ref, routes_ref, place_ref, *refs
):
    lows, refs = refs[:GROUPS], refs[GROUPS:]
    pieces, (context_ref, resid_ref, moe_ref, gates_ref) = refs[:PIECES], refs[PIECES:]
    tok, width = x_ref.shape
    for k in range(GROUPS):
        row = pl.multiple_of(lax.rem(pos[1] + k, GROUPS) * GWIDTH, GWIDTH)
        context_ref[pl.ds(row, GWIDTH), :] = lows[k][...]
    context = context_ref[...].astype(F32).T.astype(BF)
    resid = x_ref[...].astype(F32) + dot(context, out_ref[...])
    resid_ref[...] = resid
    inv = lax.rsqrt(jnp.mean(resid * resid, axis=1, keepdims=True) + EPS)
    moe_in = (resid * inv * scale_ref[...]).astype(BF)
    moe_ref[...] = moe_in
    logits = dot(moe_in, router_ref[...], ((1,), (1,)))
    lane = lax.broadcasted_iota(jnp.int32, logits.shape, 1)
    chosen = [
        jnp.sum(jnp.where(routes_ref[:, k : k + 1] == lane, logits, 0.0), axis=1, keepdims=True)
        for k in range(TOP)
    ]
    most = jnp.maximum(chosen[0], chosen[1])
    powers = [jnp.exp(c - most) for c in chosen]
    gates = [p / (powers[0] + powers[1]) for p in powers]
    slot = lax.broadcasted_iota(jnp.int32, (EXPERTS * CAP, tok), 0)
    pick = [(place_ref[k : k + 1, :] == slot) for k in range(TOP)]
    rows = dot((pick[0] | pick[1]).astype(BF), moe_in)
    extra = sum(dot(pick[k].astype(BF), three_parts(gates[k])) for k in range(TOP))
    for p in range(PIECES):
        pieces[p][:, :width] = rows[p * CAP : (p + 1) * CAP].astype(BF)
        pieces[p][:, width:] = extra[p * CAP : (p + 1) * CAP].astype(BF)
    for k in range(TOP):
        gates_ref[:, k : k + 1] = gates[k]


def router(pos, x, out_full, scale, router_t, routes, places, lows):
    tok, width = x.shape
    kept = [pltpu.HBM(*s) for s in (((width, tok), BF), ((tok, width), F32), ((tok, width), BF), ((tok, TOP), F32))]
    x, out_full = in_hbm(x, out_full)
    return pl.pallas_call(
        router_kernel,
        in_specs=[SMEM_SPEC, all_of(x), all_of(out_full)] + [VMEM_SPEC] * (4 + GROUPS),
        out_specs=[VMEM_SPEC] * PIECES + [all_of(s.inner_aval) for s in kept],
        out_shape=[jax.ShapeDtypeStruct((CAP, width + 128), BF)] * PIECES + kept,
        compiler_params=pltpu.CompilerParams(vmem_limit_bytes=16 << 20),
        cost_estimate=pl.CostEstimate(flops=10**5, bytes_accessed=10**4, transcendentals=0),
        name="router",
    )(pos, x, out_full, scale, router_t, routes, places, *lows)


def expert_kernel(groups, n_fsdp, info, dy_ref, up_ref, down_ref, *refs):
    cames, refs = refs[:PIECES], refs[PIECES:]
    out_refs, (back_ref, act_ref, rows_ref, grad_in, out_acc, back_acc) = refs[:n_fsdp], refs[n_fsdp:]
    step = pl.program_id(0)
    width = grad_in.shape[1]
    h, f = info[0], info[1]
    source = [
        lax.rem(h + groups - p // n_fsdp, groups) * n_fsdp + jnp.bitwise_xor(f, p % n_fsdp) for p in range(PIECES)
    ]

    @pl.when(step == 0)
    def _():
        came = gather_rows(cames)
        gate = jnp.sum(came[:, width:], axis=1, keepdims=True)
        dy = jnp.concatenate([dy_ref[s].astype(F32) for s in source])
        grad_in[...] = dy
        rows_ref[0] = came[:, :width].astype(BF)
        rows_ref[1] = (gate * dy).astype(BF)
        out_acc[...] = jnp.zeros_like(out_acc)
        back_acc[...] = jnp.zeros_like(back_acc)

    up, down = up_ref[0], down_ref[0]
    upper = dot(rows_ref[0], up)
    active_grad = dot(rows_ref[1], down)
    cdf = 0.5 + 0.5 * lax.erf(upper * 0.7071067811865476)
    active = (upper * cdf).astype(BF)
    slope = cdf + upper * (0.3989422804014327 * jnp.exp(-0.5 * upper * upper))
    upper_grad = (active_grad * slope).astype(BF)
    act_ref[0] = upper_grad
    act_ref[1] = active
    back_acc[...] += dot(upper_grad, up, ((1,), (1,)))
    out_acc[...] += dot(active, down, ((1,), (1,)))

    @pl.when(step == pl.num_programs(0) - 1)
    def _():
        out = out_acc[...].astype(BF).astype(F32)
        gate_grad = three_parts(jnp.sum(grad_in[...] * out, axis=1, keepdims=True)).astype(F32)
        for p in range(PIECES):
            rows = slice(p * CAP, (p + 1) * CAP)
            out_refs[p % n_fsdp][(groups - p // n_fsdp) % groups] = out[rows].astype(BF)
            back_ref[source[p], :, :width] = back_acc[rows, :].astype(BF)
            back_ref[source[p], :, width:] = gate_grad[rows].astype(BF)


def expert(info, cames, dy, up, down, groups, n_fsdp):
    width, ffn = up.shape[1], up.shape[2]
    rows = EXPERTS * CAP
    whole = lambda *shape: pl.BlockSpec(shape, lambda j, info: (0,) * len(shape))
    weight = pl.BlockSpec((1, width, FBLOCK), lambda j, info: (info[0], 0, j))
    return pl.pallas_call(
        functools.partial(expert_kernel, groups, n_fsdp),
        grid_spec=pltpu.PrefetchScalarGridSpec(
            num_scalar_prefetch=1,
            grid=(ffn // FBLOCK,),
            in_specs=[whole(PIECES, CAP, width), weight, weight] + [whole(CAP, width + 128)] * PIECES,
            out_specs=[whole(groups, CAP, width)] * n_fsdp
            + [
                whole(PIECES, CAP, width + 128),
                pl.BlockSpec((2, rows, FBLOCK), lambda j, info: (0, 0, j)),
                whole(2, rows, width),
            ],
            scratch_shapes=[pltpu.VMEM((rows, width), F32)] * 3,
        ),
        out_shape=[pltpu.HBM((groups, CAP, width), BF)] * n_fsdp
        + [
            jax.ShapeDtypeStruct((PIECES, CAP, width + 128), BF),
            pltpu.HBM((2, rows, ffn), BF),
            pltpu.HBM((2, rows, width), BF),
        ],
        compiler_params=pltpu.CompilerParams(vmem_limit_bytes=32 << 20),
        cost_estimate=pl.CostEstimate(flops=10**5, bytes_accessed=10**4, transcendentals=0),
        name="expert",
    )(info, dy, *in_hbm(up, down), *cames)


def weight_kernel(count, members, side, pos, *refs):
    rows, acts, (keep_ref, pass_ref, turned, lhs) = refs[:count], refs[count : 2 * count], refs[2 * count :]
    half = keep_ref.shape[0]

    @pl.when(pl.program_id(0) == 0)
    def _():
        for n in range(count):
            turned[...] = rows[n][0].astype(F32).T.astype(BF)
            if side is not None:
                lhs[n] = turned[side * 2 * half : (side + 1) * 2 * half, :]
                continue
            unit = 2 * half // (GROUPS * members // 2)
            for r in range(members // 2):
                member = jnp.bitwise_xor(pos[0], 2 * r)
                for k in range(GROUPS):
                    row = pl.multiple_of((lax.rem(pos[1] + k, GROUPS) * members + member) * unit, 16)
                    at = (r * GROUPS + k) * unit
                    lhs[n, at : at + unit, :] = turned[pl.ds(row, unit), :]

    keep_ref[...] = sum(dot(lhs[n, :half, :], acts[n][0]) for n in range(count)).astype(BF)
    pass_ref[...] = sum(dot(lhs[n, half:, :], acts[n][0]) for n in range(count)).astype(BF)


def weight_terms(pos, rows, acts, which, members, side=None):
    _, count, width = rows[0].shape
    ffn = acts[0].shape[2]
    half = pl.BlockSpec((width // 4, FBLOCK), lambda j: (0, j))
    return pl.pallas_call(
        functools.partial(weight_kernel, len(rows), members, side),
        grid=(ffn // FBLOCK,),
        in_specs=[SMEM_SPEC]
        + [pl.BlockSpec((1, count, width), lambda j: (which, 0, 0))] * len(rows)
        + [pl.BlockSpec((1, count, FBLOCK), lambda j: (which, 0, j))] * len(rows),
        out_specs=[half, half],
        out_shape=[pltpu.HBM((width // 4, ffn), BF)] * 2,
        scratch_shapes=[pltpu.VMEM((width, count), BF), pltpu.VMEM((len(rows), width // 2, count), BF)],
        compiler_params=pltpu.CompilerParams(vmem_limit_bytes=20 << 20),
        cost_estimate=pl.CostEstimate(flops=10**5, bytes_accessed=10**4, transcendentals=0),
        name="weight_terms",
    )(pos, *rows, *in_hbm(*acts))


def add_kernel(riders, a_ref, b_ref, *refs):
    rides, outs = refs[:riders], refs[riders:]
    rows, width = a_ref.shape[0] // GROUPS, outs[0].shape[1]
    blocks = a_ref.shape[1] // width
    for k, out in enumerate(outs):
        for c in range(blocks):
            at = (slice(k * rows, (k + 1) * rows), slice(c * width, (c + 1) * width))
            out[c * rows : (c + 1) * rows, :] = (a_ref[at].astype(F32) + b_ref[at].astype(F32)).astype(BF)
        if riders:
            ride = jnp.concatenate([r[k].astype(F32) for r in rides])
            out[blocks * rows :, :] = ride.astype(BF)


def add_groups(a, b, width, rides=()):
    rows, cols = a.shape
    count = rows // GROUPS * cols // width + sum(r.shape[1] for r in rides)
    return pl.pallas_call(
        functools.partial(add_kernel, len(rides)),
        in_specs=[all_of(a)] * 2 + [all_of(r) for r in rides],
        out_specs=[pl.BlockSpec((count, width), lambda: (0, 0))] * GROUPS,
        out_shape=[jax.ShapeDtypeStruct((count, width), BF)] * GROUPS,
        compiler_params=pltpu.CompilerParams(vmem_limit_bytes=16 << 20),
        cost_estimate=pl.CostEstimate(flops=10**5, bytes_accessed=10**4, transcendentals=0),
        name="add_groups",
    )(*in_hbm(a, b, *rides))


def order_kernel(blocks, pos, *refs):
    out_ref = refs[-1]
    rows, width = out_ref.shape[1], out_ref.shape[2] // blocks
    for k in range(GROUPS):
        group = group_of(k, pos[1])
        for c in range(blocks):
            out_ref[group, :, c * width : (c + 1) * width] = refs[k][c * rows : (c + 1) * rows, :].astype(F32)


def in_order(pos, parts, rows, cols):
    width = parts[0].shape[1]
    return pl.pallas_call(
        functools.partial(order_kernel, cols // width),
        in_specs=[SMEM_SPEC] + [all_of(p) for p in parts],
        out_specs=pl.BlockSpec((GROUPS, rows, cols), lambda: (0, 0, 0)),
        out_shape=jax.ShapeDtypeStruct((GROUPS, rows, cols), F32),
        compiler_params=pltpu.CompilerParams(vmem_limit_bytes=16 << 20),
        cost_estimate=pl.CostEstimate(flops=10**5, bytes_accessed=10**4, transcendentals=0),
        name="in_order",
    )(pos, *parts)


def turn_kernel(
    info, place_ref, routes_ref, gates_ref, resid_ref, moe_ref, dy_ref, router_ref, scale_ref,
    out_ref, context_ref, back_ref, *refs,
):
    dos, (resid_grad_ref, mine_ref, other_ref, send_ref, router_grad_ref, gain_ref, term) = refs[:GROUPS], refs[GROUPS:]
    tok, width = resid_ref.shape
    back = back_ref[...]
    slots = back.shape[0]
    iota = lax.broadcasted_iota(jnp.int32, (tok, slots), 1)
    pick = [place_ref[:, k : k + 1] == iota for k in range(TOP)]
    gates = [gates_ref[:, k : k + 1] for k in range(TOP)]
    gate_grad = [jnp.sum(dot(p.astype(BF), back[:, width:]), axis=1, keepdims=True) for p in pick]
    mean = gates[0] * gate_grad[0] + gates[1] * gate_grad[1]
    lane = lax.broadcasted_iota(jnp.int32, (tok, 128), 1)
    logit_grad = sum(
        jnp.where(routes_ref[:, k : k + 1] == lane, gates[k] * (gate_grad[k] - mean), 0.0) for k in range(TOP)
    )
    grad = dot((pick[0] | pick[1]).astype(BF), back[:, :width])
    for e in range(EXPERTS):
        grad = grad + logit_grad[:, e : e + 1] * router_ref[e : e + 1, :].astype(F32)
    resid = resid_ref[...]
    inv = lax.rsqrt(jnp.mean(resid * resid, axis=1, keepdims=True) + EPS)
    gain_ref[...] = jnp.sum(grad * (resid * inv), axis=0, keepdims=True)
    scaled = grad * scale_ref[...]
    along = jnp.mean(scaled * resid, axis=1, keepdims=True)
    resid_grad = dy_ref[...].astype(F32) + inv * scaled - resid * (inv * inv * inv * along)
    resid_grad_ref[...] = resid_grad
    low = resid_grad.astype(BF)
    term[:, :tok] = dot(out_ref[...], low, ((1,), (1,)))
    for k in range(GROUPS):
        row = pl.multiple_of(lax.rem(info[0] + k, GROUPS) * GWIDTH, GWIDTH)
        dos[k][...] = term[pl.ds(row, GWIDTH), :tok].astype(BF)
    router_grad_ref[...] = lax.dot_general(
        logit_grad.T[:EXPERTS], moe_ref[...].astype(F32), (((1,), (0,)), ((), ())),
        precision=FULL, preferred_element_type=F32,
    )
    term[...] = dot(low.astype(F32).T.astype(BF), context_ref[...].astype(F32).T.astype(BF))
    rows, cols = mine_ref.shape[1:]
    core, top = info[1], info[2]
    mine = pl.ds(pl.multiple_of(top * cols, 128), cols)
    other = pl.ds(pl.multiple_of((1 - top) * cols, 128), cols)
    for g in range(mine_ref.shape[0]):
        keep = pl.ds(pl.multiple_of((2 * g + core) * rows, 8), rows)
        send = pl.ds(pl.multiple_of((2 * g + 1 - core) * rows, 8), rows)
        mine_ref[g] = term[keep, mine]
        other_ref[g] = term[keep, other]
        send_ref[0, g] = term[send, mine].astype(BF)
        send_ref[1, g] = term[send, other].astype(BF)


def turn_back(info, back, place, routes, gates, resid, moe_in, dy, router, scale, out_full, context, shards):
    tok, width = resid.shape
    rows = width // shards
    part = (shards // 2, rows, width // 2)
    gates, resid, moe_in, dy, out_full, context = in_hbm(gates, resid, moe_in, dy, out_full, context)
    inputs = (place, routes, gates, resid, moe_in, dy, router, scale, out_full, context, back)
    kept = [((tok, width), F32), (part, F32), (part, F32), ((2,) + part, BF), ((EXPERTS, width), F32), ((1, width), F32)]
    kept = [pltpu.HBM(*s) for s in kept]
    return pl.pallas_call(
        turn_kernel,
        in_specs=[SMEM_SPEC] + [all_of(x) for x in inputs],
        out_specs=[VMEM_SPEC] * GROUPS + [all_of(s.inner_aval) for s in kept],
        scratch_shapes=[pltpu.VMEM((width, width), F32)],
        out_shape=[jax.ShapeDtypeStruct((GWIDTH, tok), BF)] * GROUPS + kept,
        compiler_params=pltpu.CompilerParams(vmem_limit_bytes=24 << 20),
        cost_estimate=pl.CostEstimate(flops=10**5, bytes_accessed=10**4, transcendentals=0),
        name="turn_back",
    )(info, *inputs)


def pair_kernel(a_ref, b_ref, c_ref, d_ref, keep_ref, send_ref):
    keep_ref[...] = a_ref[...].astype(F32) + b_ref[...].astype(F32)
    send_ref[...] = (c_ref[...].astype(F32) + d_ref[...].astype(F32)).astype(BF)


def add_pairs(a, b, c, d):
    return pl.pallas_call(
        pair_kernel,
        in_specs=[VMEM_SPEC] * 4,
        out_specs=[VMEM_SPEC] * 2,
        out_shape=[jax.ShapeDtypeStruct(a.shape, F32), jax.ShapeDtypeStruct(a.shape, BF)],
        cost_estimate=pl.CostEstimate(flops=10**5, bytes_accessed=10**4, transcendentals=0),
        compiler_params=pltpu.CompilerParams(vmem_limit_bytes=8 << 20),
        name="add_pairs",
    )(a, b, c, d)


SMALL = 16


def input_kernel(
    members, buckets_here, info, dq_ref, keep_ref, came_ref, ain_ref, weight_ref, scale_ref, router_ref,
    gain_ref, line_ref, dline_ref, own_ref, one_ref, two_ref, three_ref, term_ref, sent_ref, pack_ref, dproj, term,
):
    h, core = info[0], info[1]
    width = ain_ref.shape[1]
    tok = own_ref.shape[0]
    dproj[:, :GWIDTH] = dq_ref[...].astype(F32)
    for k in range(GROUPS):
        dkv = keep_ref[k] if came_ref is None else keep_ref[k] + came_ref[k].astype(F32)
        dproj[k * tok : (k + 1) * tok, GWIDTH:] = dkv.astype(BF).astype(F32)
    low = dproj[...].astype(BF)
    ain = ain_ref[...]
    back = dot(low, weight_ref[...], ((1,), (1,)))
    own_ref[...] = back[:tok]
    for k, ref in enumerate((one_ref, two_ref, three_ref)):
        ref[...] = back[(k + 1) * tok : (k + 2) * tok].astype(BF)
    pack_ref[0:EXPERTS, :] = router_ref[...]
    pack_ref[EXPERTS : EXPERTS + 1, :] = jnp.sum(back * ain.astype(F32), axis=0, keepdims=True) / scale_ref[...]
    pack_ref[EXPERTS + 1 : EXPERTS + 2, :] = gain_ref[...]
    col = lax.broadcasted_iota(jnp.int32, (BUCKETS, width), 1)
    cols_f = width * buckets_here // BUCKETS
    within = lax.rem(col, cols_f) - h * buckets_here
    held = jnp.where((within >= 0) & (within < buckets_here), col // cols_f * buckets_here + within, -1)
    held = held == lax.broadcasted_iota(jnp.int32, (BUCKETS, width), 0)
    bucket = line_ref[...] == lax.broadcasted_iota(jnp.int32, (BUCKETS, line_ref.shape[1]), 0)
    for n in range(GHEADS):
        sums = jnp.sum(jnp.where(bucket, dline_ref[n : n + 1, :], 0.0), axis=1, keepdims=True)
        row = EXPERTS + 2 + n
        pack_ref[row : row + 1, :] = jnp.sum(jnp.where(held, sums, 0.0), axis=0, keepdims=True)
    rest = EXPERTS + 2 + GHEADS
    pack_ref[rest:, :] = jnp.zeros((SMALL - rest, width), F32)
    term[...] = dot(dproj[...].T.astype(BF), ain)
    unit = GWIDTH // members
    for t in range(3):
        for r in range(members // 2):
            at = slice((t * (members // 2) + r) * unit, (t * (members // 2) + r + 1) * unit)
            first = (t * members + 2 * r) * unit
            term_ref[at, :] = term[pl.ds(pl.multiple_of(first + core * unit, 8), unit), :]
            sent_ref[at, :] = term[pl.ds(pl.multiple_of(first + (1 - core) * unit, 8), unit), :].astype(BF)
    pack = pack_ref[...]
    high = pack.astype(BF)
    rows = term_ref.shape[0]
    sent_ref[rows : rows + SMALL, :] = high
    sent_ref[rows + SMALL :, :] = (pack - high.astype(F32)).astype(BF)


def input_back(info, members, buckets_here, dq, keep, came, ain, weight, scale, router_grad, gain_grad, line, dline):
    count, width = ain.shape
    tok = count // GROUPS
    rows = 3 * GWIDTH // 2
    ain, weight = in_hbm(ain, weight)
    inputs = [dq, keep] + ([] if came is None else [came]) + [ain, weight, scale, router_grad, gain_grad, line, dline]
    body = functools.partial(input_kernel, members, buckets_here)
    if came is None:
        body = lambda info, dq, keep, *refs: input_kernel(members, buckets_here, info, dq, keep, None, *refs)
    return pl.pallas_call(
        body,
        in_specs=[SMEM_SPEC] + [all_of(x) for x in inputs],
        out_specs=[VMEM_SPEC] * 7,
        out_shape=[jax.ShapeDtypeStruct((tok, width), F32)]
        + [jax.ShapeDtypeStruct((tok, width), BF)] * 3
        + [
            jax.ShapeDtypeStruct((rows, width), F32),
            jax.ShapeDtypeStruct((rows + 2 * SMALL, width), BF),
            jax.ShapeDtypeStruct((SMALL, width), F32),
        ],
        scratch_shapes=[pltpu.VMEM((count, 3 * GWIDTH), F32), pltpu.VMEM((3 * GWIDTH, width), F32)],
        compiler_params=pltpu.CompilerParams(vmem_limit_bytes=24 << 20),
        cost_estimate=pl.CostEstimate(flops=10**5, bytes_accessed=10**4, transcendentals=0),
        name="input_back",
    )(info, *inputs)


def together(*values):
    return lax.optimization_barrier(values)


def turn(shift):
    return [(i, (i + shift) % GROUPS) for i in range(GROUPS)]


def gather_groups(x):
    came = {k: lax.ppermute(x, "h", turn(k)) for k in (2, 1, 3)}
    return jnp.stack([x] + [came[k] for k in range(1, GROUPS)])


def gather_members(x):
    size = lax.axis_size(MEMBERS)
    held = {0: x}
    for bit in bits_of(size):
        for k in sorted(held):
            held[k | bit] = lax.ppermute(held[k], MEMBERS, xor_perm(bit, size))
    return [held[k] for k in range(size)]


def part_of(x, mine):
    low, high = jnp.split(x, 2, axis=-1)
    return jnp.where(mine == 0, low, high), jnp.where(mine == 0, high, low)


def swap(x, axis, bit):
    return lax.ppermute(x, axis, xor_perm(bit, lax.axis_size(axis)))


def two_parts(x):
    high = lax.reduce_precision(x, 8, 7)
    return jnp.concatenate([high, x - high]).astype(BF)


def from_fsdp(part):
    if lax.axis_size("fsdp") != 2:
        return lax.all_gather(part, "fsdp", axis=0)
    came = lax.ppermute(part, "fsdp", xor_perm(1, 2))
    return jnp.where(lax.axis_index("fsdp") == 0, jnp.stack([part, came]), jnp.stack([came, part]))


def group_pieces(pieces, sign):
    came = {k: lax.ppermute(pieces[k], "h", turn(sign * k)) for k in (2, 1, 3)}
    return [pieces[0]] + [came[k] for k in range(1, GROUPS)]


def deal(pieces, spread, sign):
    n_fsdp = lax.axis_size("fsdp")
    out = [pieces[0]] + [None] * (len(pieces) - 1)
    for p in (5, 4, 3, 7, 2, 6, 1):
        k, j = divmod(p, n_fsdp)
        if spread:
            pairs = [
                (g * n_fsdp + i, (g + sign * k) % GROUPS * n_fsdp + (i ^ j))
                for g in range(GROUPS)
                for i in range(n_fsdp)
            ]
            out[p] = lax.ppermute(pieces[p], ("h", "fsdp"), pairs)
        else:
            out[p] = lax.ppermute(pieces[p], "fsdp", xor_perm(j, n_fsdp))
    return out


def per_device(
    tokens, segments, routes, bucket_table, attn_gain, qkv_weight, out_weight, bias_table,
    moe_gain, router_weight, up_weight, down_weight, cotangent,
):
    tok, width = tokens.shape[1], tokens.shape[2]
    half = tok // 2
    h, m, f = lax.axis_index("h"), lax.axis_index(MEMBERS), lax.axis_index("fsdp")
    core = lax.axis_index("core")
    members, n_fsdp = lax.axis_size(MEMBERS), lax.axis_size("fsdp")
    shards = GROUPS * members
    blocks = 2 * shards
    length = shards * tok
    here = EXPERTS // n_fsdp
    spread = here > 1
    ffn = up_weight.shape[2]
    rows_f = width // n_fsdp
    rows_c = width // shards
    pos = jnp.stack([m, h]).astype(jnp.int32)

    extra = jnp.pad(segments.astype(BF), ((0, 7), (0, width - tok)))
    mixed = gather_groups(jnp.concatenate([tokens[0], extra]))

    bias_flat = bias_table.reshape(1, -1)
    bias_rows = -(-bias_flat.shape[1] // rows_f)
    bias_flat = jnp.pad(bias_flat, ((0, 0), (0, bias_rows * rows_f - bias_flat.shape[1])))
    small = jnp.concatenate(
        [attn_gain[None], moe_gain[None], router_weight.T, bias_flat.reshape(bias_rows, rows_f)]
        + [jnp.zeros((16 - 10 - bias_rows, rows_f), BF)]
    )
    small = from_fsdp(small)
    attn_scale = small[:, 0].reshape(width).astype(F32)
    moe_scale = small[:, 1].reshape(width).astype(F32)
    router_t = jnp.transpose(small[:, 2:10], (1, 0, 2)).reshape(EXPERTS, width)
    bias_full = small[:, 10 : 10 + bias_rows].reshape(n_fsdp, -1)[:, : bias_table.size]
    bias_full = bias_full.reshape(BUCKETS, HEADS)
    cut = [
        lax.dynamic_slice_in_dim(qkv_weight, n * width + h * GWIDTH, GWIDTH, 1) for n in range(3)
    ]
    qkv_heads = from_fsdp(jnp.concatenate(cut, axis=1)).reshape(width, 3 * GWIDTH)
    out_full = from_fsdp(together(out_weight, qkv_heads)[0]).reshape(width, width)

    wide = strip_width(blocks, half)
    top = half * (blocks - 1)
    line = jnp.concatenate(
        [
            bucket_table[: top + 1][::-1],
            jnp.full((wide - length,), -1, jnp.int32),
            bucket_table[top + 1 :][::-1],
        ]
    )
    hot = (line[None] == jnp.arange(BUCKETS, dtype=jnp.int32)[:, None]).astype(BF)
    bias_mine = lax.dynamic_slice_in_dim(bias_full, h * GHEADS, GHEADS, 1)
    strips = make_strips(dot(bias_mine, hot, ((0,), (0,))) * LOG2E, half)

    hot_routes = (routes.reshape(-1)[:, None] == jnp.arange(EXPERTS)[None]).astype(F32)
    earlier = jnp.arange(tok * TOP)
    earlier = (earlier[None, :] < earlier[:, None]).astype(BF)
    before = dot(earlier, hot_routes.astype(BF))
    slot = jnp.sum(before * hot_routes, axis=1).astype(jnp.int32).reshape(tok, TOP)
    group = routes % here
    natural = (group * n_fsdp + routes // here) * CAP + slot
    away = lax.rem(group - h + GROUPS, GROUPS) if spread else group
    place = (away * n_fsdp + jnp.bitwise_xor(routes // here, f)) * CAP + slot
    slots = jnp.arange(EXPERTS * CAP, dtype=jnp.int32)
    pick = [slots[:, None] == natural[None, :, k] for k in range(TOP)]
    exchange = ("h", "fsdp") if spread else ("fsdp",)

    def exchange_rows(rows):
        return lax.all_to_all(rows, exchange, 0, 0, tiled=True)

    mixed, strips = together(mixed, strips)
    ain = normalize(mixed[:, :tok].astype(F32), attn_scale).astype(BF).reshape(GROUPS * tok, width)
    proj = dot(ain, qkv_heads).astype(BF)
    kv = proj[:, GWIDTH:].reshape(GROUPS, tok, 2 * GWIDTH)
    kvs = gather_members(jnp.concatenate([kv, mixed[:, tok:, : 2 * GWIDTH]], axis=1))
    dy_send = dot((pick[0] | pick[1]).astype(BF), cotangent[0]).astype(BF).reshape(PIECES, CAP, width)
    dy_slots = exchange_rows(together(dy_send, small)[0])
    o_pre, *rest = attend(pos, proj, kvs, strips, blocks)
    lows, stat, keys = rest[:GROUPS], rest[GROUPS], rest[GROUPS + 1 :]
    lows[1], dy_slots = together(lows[1], dy_slots)
    *pieces, context, residual, moe_in, gates = router(
        pos, tokens[0], out_full, moe_scale[None], router_t, routes, place.T, group_pieces(lows, -1)
    )

    came = deal(pieces, spread, 1)
    info = jnp.stack([h if spread else jnp.zeros_like(h), f]).astype(jnp.int32)
    *outs, back, act, rows = expert(
        info, came, dy_slots, up_weight, down_weight, GROUPS if spread else 1, n_fsdp
    )
    back = exchange_rows(back).reshape(EXPERTS * CAP, -1)

    staged = spread and members == 4
    if staged:
        rows, acts = [rows, swap(rows, "core", 1)], [act, swap(act, "core", 1)]
        terms = [weight_terms(pos, rows, acts, n, members) for n in range(2)]
        back, terms = together(back, terms)
    else:
        terms = [weight_terms(pos, [rows], [act], n, members, side) for n in range(2) for side in range(2)]

    top_bit = n_fsdp // 2
    info = jnp.stack([h, core, (f // top_bit) % 2]).astype(jnp.int32)
    *dos, resid_grad, out_mine, out_other, out_send, router_grad, moe_gain_grad = turn_back(
        info, back, natural, routes, gates, residual, moe_in, cotangent[0], router_t,
        moe_scale[None], out_full, context, shards,
    )
    dos = group_pieces(dos, 1)
    out_came = swap(out_send, "core", 1)
    out_far = (out_other + out_came[1].astype(F32)).astype(BF)
    outs = [outs[0]] + [lax.ppermute(outs[j], "fsdp", xor_perm(j, n_fsdp)) for j in range(1, n_fsdp)]
    dos[0], out_far = together(dos[0], out_far)
    out_far = swap(out_far, "fsdp", top_bit)
    dq, *dkvs, dline = attend_back(pos, proj, keys, strips, dos, o_pre, stat, members, blocks)
    dkvs[1], out_far, outs = together(dkvs[1], out_far, outs)
    cames = [swap(dkvs[k], "core", 1) for k in range(1, members, 2)]
    sends = []
    if members == 4:
        keep, send = add_pairs(dkvs[0], cames[0], dkvs[2], cames[1])
        if staged:
            sends = [swap(terms[0][1], "r", 1)]
            send, sends[0] = together(send, sends[0])
        came = swap(send, "r", 1)
    else:
        held = {k: dkvs[k].astype(F32) + cames[k // 2].astype(F32) for k in range(0, members, 2)}
        bit = 2
        while bit < members:
            for k in [k for k in sorted(held) if k & bit]:
                held[k - bit] = held[k - bit] + swap(held.pop(k).astype(BF), "r", bit // 2).astype(F32)
            bit *= 2
        keep, came = held[0], None
    if staged:
        up_came = group_pieces(add_groups(terms[0][0], sends[0], width, outs), 1)
        sends.append(swap(together(terms[1][1], came)[0], "r", 1))
        came, up_came[1] = together(came, up_came[1])

    own_back, back_1, back_2, back_3, term, sent, pack = input_back(
        jnp.stack([h, core]).astype(jnp.int32), members, BUCKETS // n_fsdp, dq, keep, came, ain, qkv_heads,
        attn_scale[None], router_grad, moe_gain_grad, line[None], dline,
    )

    def swap_both(send, pack, axis, bit):
        sent = jnp.concatenate([send.reshape(-1, send.shape[-1]).astype(BF), two_parts(pack)])
        return split_rows(swap(sent, axis, bit).astype(F32), send.shape)

    def split_rows(came, shape):
        return came[: -2 * SMALL].reshape(shape), came[-2 * SMALL : -SMALL] + came[-SMALL:]

    unit = GWIDTH // members
    came, pack_came = split_rows(swap(sent, "core", 1).astype(F32), term.shape)
    term, pack = term + came, pack + pack_came
    out_term = out_mine + out_came[0].astype(F32) + out_far.astype(F32)
    for bit in list(bits_of(n_fsdp))[1:]:
        out_term, out_send = part_of(out_term, (f // bit) % 2)
        out_term = out_term + swap(out_send.astype(BF), "fsdp", bit).astype(F32)
    for bit in bits_of(n_fsdp):
        term, send = part_of(term, (f // bit) % 2)
        pack, pack_send = part_of(pack, (f // bit) % 2)
        came, pack_came = swap_both(send, pack_send, "fsdp", bit)
        term, pack = term + came, pack + pack_came
    term = jnp.concatenate(
        [term.reshape(3, members // 2, unit, rows_f).swapaxes(0, 1).reshape(members // 2, -1, rows_f)]
        + [out_term.reshape(GROUPS, members // 2, rows_c, rows_f).swapaxes(0, 1).reshape(members // 2, -1, rows_f)],
        axis=1,
    )
    if staged:
        term, sends[1], up_came = together(term, sends[1], up_came)
    for bit in bits_of(members // 2):
        mine = (lax.axis_index("r") // bit) % 2
        term = term.reshape((2, -1) + term.shape[1:])
        came, pack_came = swap_both(lax.dynamic_index_in_dim(term, 1 - mine, 0, False), pack, "r", bit)
        term = lax.dynamic_index_in_dim(term, mine, 0, False) + came
        pack = pack + pack_came
    term = term[0]
    if staged:
        back_2, up_came = together(back_2, up_came)
        back_3, term = together(back_3, term)
    mid = lax.ppermute(back_2, "h", turn(-1))
    side = lax.ppermute(back_3, "h", turn(1)).astype(F32)
    mid = (back_1.astype(F32) + mid.astype(F32)).astype(BF)
    mid = lax.ppermute(mid, "h", turn(-1)).astype(F32)
    attn_in_grad = own_back + side + mid
    x = tokens[0].astype(F32)
    token_grad = jax.vjp(lambda v: normalize(v, attn_scale), x)[1](attn_in_grad)[0]
    tokens_grad = (resid_grad + token_grad).astype(BF)

    out_term = term[3 * unit :].reshape(GROUPS, rows_c, rows_f)
    term = term[: 3 * unit].astype(BF).reshape(3, unit, rows_f)
    if staged:
        down_came = group_pieces(add_groups(terms[1][0], sends[1], width), 1)
    out_sum, pack_sum = lax.dynamic_index_in_dim(out_term, h, 0, False), pack
    for k in (2, 1, 3):
        piece = lax.dynamic_index_in_dim(out_term, lax.rem(h + k, GROUPS), 0, False)
        came = lax.ppermute(jnp.concatenate([piece.astype(BF), two_parts(pack)]), "h", turn(k)).astype(F32)
        out_sum = out_sum + came[:rows_c]
        pack_sum = pack_sum + came[rows_c : rows_c + SMALL] + came[rows_c + SMALL :]
    at = h * members + m
    parts = []
    for r in range(3):
        pairs = [((3 * d + r) % shards, d) for d in range(shards)]
        third = pow(3, -1, shards)
        which = (3 * lax.rem((at + shards - r) * third, shards) + r) // shards
        parts.append(lax.ppermute(lax.dynamic_index_in_dim(term, which, 0, False), CTX, pairs))
    if staged:
        up_came, parts = together(up_came, parts)
        grads = [in_order(pos, part, rows_c, ffn) for part in (up_came, down_came)]
        home = jnp.concatenate([part[rows_c * ffn // width :] for part in up_came])
    else:
        terms = [jnp.concatenate(terms[n] + terms[n + 1]) for n in (0, 2)]
        grads = [
            lax.psum_scatter(term, CTX, scatter_dimension=0, tiled=True)[None].astype(F32) for term in terms
        ]
        home = jnp.concatenate([o.reshape(-1, width) for o in outs])
    qkv_grad = jnp.concatenate(parts).astype(F32).T

    away = lax.rem(h - group + GROUPS, GROUPS) if spread else group
    place = (away * n_fsdp + jnp.bitwise_xor(routes // here, f)) * CAP + slot
    layer_out = residual
    for k in range(TOP):
        row = (slots[:, None] == place[None, :, k]).astype(BF)
        layer_out = layer_out + gates[:, k : k + 1] * dot(row, home, ((0,), (0,)))
    bias_grad = pack_sum[EXPERTS + 2 : EXPERTS + 2 + GHEADS, : GROUPS * BUCKETS // n_fsdp]
    bias_grad = bias_grad.reshape(GHEADS, GROUPS, BUCKETS // n_fsdp).transpose(2, 1, 0).reshape(-1, HEADS)
    return (
        layer_out.astype(BF)[None],
        tokens_grad[None],
        pack_sum[8],
        qkv_grad,
        out_sum.T,
        bias_grad,
        pack_sum[9],
        pack_sum[:8].T,
        grads[0],
        grads[1],
    )


def solution(mesh):
    n_ctx, n_fsdp = mesh.shape["ctx"], mesh.shape["fsdp"]
    cut = mesh.devices.reshape(GROUPS, n_ctx // (2 * GROUPS), 2, n_fsdp)
    row = P("fsdp", CTX, None)
    return jax.shard_map(
        per_device,
        mesh=Mesh(cut, CTX + ("fsdp",)),
        in_specs=(
            row,
            P("fsdp", CTX),
            P(CTX + ("fsdp",), None),
            P(),
            P("fsdp"),
            P("fsdp", None),
            P("fsdp", None),
            P("fsdp", None),
            P("fsdp"),
            P("fsdp", None),
            P("fsdp", None, None),
            P("fsdp", None, None),
            row,
        ),
        out_specs=(
            row,
            row,
            P("fsdp"),
            P("fsdp", CTX),
            P("fsdp", CTX),
            P("fsdp", None),
            P("fsdp"),
            P("fsdp", None),
            row,
            row,
        ),
        check_vma=False,
    )
```

```python
import functools

import jax
import jax.numpy as jnp
from jax import lax
from jax.experimental import pallas as pl
from jax.experimental.pallas import tpu as pltpu
from jax.sharding import Mesh, PartitionSpec as P

HEADS = 12
HEAD_DIM = 64
EXPERTS = 8
TOP = 2
BUCKETS = 32
DOCS = 8
CAP = 40
GROUPS = 4
GHEADS = HEADS // GROUPS
GWIDTH = GHEADS * HEAD_DIM
CHUNK = 256

LOG2E = 1.4426950408889634
EPS = 1e-06
LOWEST = -1e30
FULL = lax.Precision.HIGHEST
BF = jnp.bfloat16
F32 = jnp.float32
MEMBERS = ("r", "core")
CTX = ("h", "r", "core")


def normalize(values, weight):
    inv_rms = lax.rsqrt(jnp.mean(values * values, axis=-1, keepdims=True) + EPS)
    return values * inv_rms * weight


def dot(a, b, dims=((1,), (0,))):
    return lax.dot_general(a, b, (dims, ((), ())), preferred_element_type=F32)


def exact_dot(a, b, dims):
    return lax.dot_general(a, b, (dims, ((), ())), precision=FULL)


def xor_perm(mask, size):
    return [(i, i ^ mask) for i in range(size)]


def bits_of(size):
    bit = size // 2
    while bit:
        yield bit
        bit //= 2


def strip_width(blocks, half):
    need = half * (blocks - 1) + CHUNK + half
    return -(-need // 128) * 128


def strips_kernel(g_ref, out_ref):
    half = out_ref.shape[1] // GHEADS
    rolled = [
        pltpu.roll(
            jnp.broadcast_to(g_ref[n : n + 1, :], (half, g_ref.shape[1])), 0, 1, stride=1, stride_axis=0
        )
        for n in range(GHEADS)
    ]
    out_ref[...] = jnp.concatenate(rolled).T


def make_strips(lines, half):
    return pl.pallas_call(
        strips_kernel,
        out_specs=pl.BlockSpec((lines.shape[1], GHEADS * half), lambda: (0, 0)),
        out_shape=pltpu.HBM((lines.shape[1], GHEADS * half), F32),
        cost_estimate=pl.CostEstimate(flops=10**5, bytes_accessed=10**4, transcendentals=0),
        name="strips",
    )(lines)


def own_blocks(size, half):
    a = lax.broadcasted_iota(jnp.int32, (size, size), 0) // half
    b = lax.broadcasted_iota(jnp.int32, (size, size), 1) // half
    return a == b


def spread_rows(x, same):
    return jnp.where(same, jnp.concatenate([x] * GHEADS), 0.0)


def identity(size):
    a, b = (lax.broadcasted_iota(jnp.int32, (size, size), n) for n in range(2))
    return jnp.where(a == b, 1.0, 0.0).astype(BF)


def own_columns(x, half):
    return jnp.concatenate(
        [x[n * HEAD_DIM : (n + 1) * HEAD_DIM, n * half : (n + 1) * half] for n in range(GHEADS)]
    )


def fold_rows(x, same, half):
    y = jnp.where(same, x, 0.0).T
    return sum(y[n * half : (n + 1) * half] for n in range(GHEADS))


def spread_columns(x, same):
    return jnp.where(same, jnp.concatenate([x] * GHEADS, axis=1), 0.0)


def group_of(slot, h):
    return lax.rem(h + GROUPS - slot, GROUPS)


def place_of(slot, early, me, h, members, blocks):
    owner = group_of(slot, h) * members + me
    return owner if early else blocks - 1 - owner


def bounds(block, chunk, half, blocks, start):
    top = (blocks - 1 - (block - (CHUNK // half) * chunk)) * half
    lane = lax.broadcasted_iota(jnp.int32, (1, GHEADS * half), 1)
    last = block * half + lax.rem(lane, half) - chunk * CHUNK
    return pl.multiple_of(top, half), last, start - chunk * CHUNK


def forward_kernel(half, blocks, members, pos, q_ref, *refs):
    kvs, refs = refs[:members], refs[members:]
    strip_in, o_ref, *lows, stat_ref, k_out, v_out, kt_out, k_ref, v_ref, kt_ref, vt, strip_ref, low, sems, strip_sem = refs
    loads = start_copies([(strip_in, strip_ref)], strip_sem)
    size = GHEADS * half
    me, h = pos[0], pos[1]
    tok = 2 * half
    same = own_blocks(size, half)
    key = lax.broadcasted_iota(jnp.int32, (CHUNK, size), 0)
    per = CHUNK // half

    @pl.loop(0, GROUPS, unroll=2)
    def _(slot):
        for j in range(members):
            for early in (True, False):
                block = place_of(slot, early, jnp.bitwise_xor(me, j), h, members, blocks)
                at = pl.ds(pl.multiple_of(lax.rem(block, per) * half, half), half)
                rows = kvs[j][slot, 0 if early else half : half if early else tok, :]
                k_ref[block // per, at, :] = rows[:, :GWIDTH]
                v_ref[block // per, at, :] = rows[:, GWIDTH:]

    eye = identity(GWIDTH)

    @pl.loop(0, blocks // per, unroll=4)
    def _(chunk):
        kt_ref[chunk] = dot(eye, k_ref[chunk], ((1,), (1,))).astype(BF)
        vt[chunk] = dot(eye, v_ref[chunk], ((1,), (1,))).astype(BF)

    copies = start_copies([(k_ref, k_out), (v_ref, v_out), (kt_ref, kt_out)], sems)
    docs = jnp.concatenate([kv[a, tok : tok + 1, :tok].astype(F32) for kv in kvs for a in range(GROUPS)])
    begins = [jnp.sum(jnp.where(docs < s, 1.0, 0.0)) for s in range(1, DOCS)]
    for load in loads:
        load.wait()

    def prepare(slot, late):
        owner = group_of(slot, h) * members + me
        block = owner if late == 0 else blocks - 1 - owner
        at = pl.ds(pl.multiple_of(slot * tok + late * half, half), half)
        qs = spread_rows(q_ref[at, :GWIDTH].astype(F32), same).astype(BF)
        qt = dot(eye, qs, ((1,), (1,))).astype(BF)
        doc = kvs[0][slot, tok : tok + 1, :tok].astype(F32)[:, late * half : (late + 1) * half]
        begin = jnp.zeros((1, half), F32)
        for s in range(1, DOCS):
            begin = jnp.where(doc == s, begins[s - 1], begin)
        first = jnp.min(begin).astype(jnp.int32) // CHUNK
        begin = jnp.concatenate([begin] * GHEADS, axis=1)
        return block, first, block // per, begin, qt

    def advance(state, step, carry):
        block, first, final, begin, qt = state
        peak, total, acc = carry
        chunk = jnp.minimum(first + step, final)
        top, last, begin = bounds(block, chunk, half, blocks, begin.astype(jnp.int32))
        last = jnp.where(first + step <= final, last, -1)
        t = dot(k_ref[chunk], qt) * (HEAD_DIM**-0.5 * LOG2E) + strip_ref[pl.ds(top, CHUNK), :]
        t = jnp.where((key <= last) & (key >= begin), t, LOWEST)
        new = jnp.maximum(peak, jnp.ceil(jnp.max(t, axis=0, keepdims=True)))
        e = jnp.exp2(t - new)
        fade = jnp.exp2(peak - new)
        total = total * fade + jnp.sum(e, axis=0, keepdims=True)
        acc = acc * fade + dot(vt[chunk], e.astype(BF))
        return new, total, acc

    init = (
        jnp.full((1, size), LOWEST, F32),
        jnp.zeros((1, size), F32),
        jnp.zeros((GWIDTH, size), F32),
    )

    def pair_of(pair, late):
        slots = [group_of(2 * pair + n, h) for n in range(2)]
        states = [prepare(slot, late) for slot in slots]
        steps = functools.reduce(jnp.maximum, [s[2] - s[1] + 1 for s in states])
        done = lax.fori_loop(
            0, steps, lambda i, c: tuple(advance(s, i, x) for s, x in zip(states, c)), (init,) * 2
        )
        for slot, state, (peak, total, acc) in zip(slots, states, done):
            out = own_columns(acc / total, half)
            o_ref[2 * slot + late] = out
            low[slot, :, late * half : (late + 1) * half] = out.astype(BF)
            stat_ref[2 * slot + late, 0:1, :] = peak
            stat_ref[2 * slot + late, 1:2, :] = total
            stat_ref[2 * slot + late, 2:3, :] = state[3]

    @pl.loop(0, GROUPS // 2)
    def _(pair):
        pair_of(pair, 0)
        pair_of(pair, 1)

    for n in range(GROUPS):
        lows[n][...] = low[n]
    for copy in copies:
        copy.wait()


def backward_kernel(half, blocks, members, pos, *refs):
    dos, refs = refs[:GROUPS], refs[GROUPS:]
    inputs, (dq_ref, *refs) = refs[:7], refs[7:]
    dkvs, refs = refs[:members], refs[members:]
    dline_ref, *held, dk, dv, dstrip, do_ref, sems = refs
    q_ref, strip_ref, o_ref, stat_ref, k_ref, v_ref, kt_ref = held
    size = GHEADS * half
    me, h = pos[0], pos[1]
    width = dstrip.shape[0]
    per = CHUNK // half
    copies = start_copies(list(zip(inputs, held)), sems)
    same = own_blocks(size, half)
    key = lax.broadcasted_iota(jnp.int32, (CHUNK, size), 0)

    @pl.loop(0, blocks // per, unroll=4)
    def _(chunk):
        dk[chunk] = jnp.zeros(dk.shape[1:], F32)
        dv[chunk] = jnp.zeros(dv.shape[1:], F32)

    @pl.loop(0, width // 128, unroll=2)
    def _(j):
        dstrip[pl.ds(pl.multiple_of(j * 128, 128), 128), :] = jnp.zeros((128, size), F32)

    for n in range(GROUPS):
        do_ref[n] = dos[n][...].astype(F32)
    for copy in copies:
        copy.wait()

    def prepare(slot, late):
        i = 2 * slot + late
        owner = group_of(slot, h) * members + me
        block = owner if late == 0 else blocks - 1 - owner
        at = pl.ds(pl.multiple_of(slot * 2 * half + late * half, half), half)
        peak, total, start = (stat_ref[i, n : n + 1, :] for n in range(3))
        first = jnp.min(start).astype(jnp.int32) // CHUNK
        qs = spread_rows(q_ref[at, :GWIDTH].astype(F32), same)
        qt, qs = qs.T.astype(BF), qs.astype(BF)
        do = do_ref[slot][:, late * half : (late + 1) * half]
        corr = jnp.sum(spread_columns(do * o_ref[i], same), axis=0, keepdims=True) / total
        gt = spread_columns(do, same) / total
        gs = gt.T.astype(BF)
        return block, first, block // per, start.astype(jnp.int32), peak, corr, qt, qs, gt.astype(BF), gs, at

    def scores(state, step):
        block, first, final, start, peak, corr, qt, _, gt = state[:9]
        chunk = jnp.minimum(first + step, final)
        top, last, begin = bounds(block, chunk, half, blocks, start)
        last = jnp.where(first + step <= final, last, -1)
        t = dot(k_ref[chunk], qt) * (HEAD_DIM**-0.5 * LOG2E) + strip_ref[pl.ds(top, CHUNK), :]
        t = jnp.where((key <= last) & (key >= begin), t - peak, LOWEST)
        e = jnp.exp2(t)
        return chunk, top, e.astype(BF), e * (dot(v_ref[chunk], gt) - corr)

    def pair_of(pair, late):
        states = [prepare(group_of(2 * pair + n, h), late) for n in range(2)]

        def visit(step, carry):
            found = [scores(s, step) for s in states]
            out = []
            for (chunk, top, e, s), state, dq in zip(found, states, carry):
                low = s.astype(BF)
                dk[chunk] += dot(low, state[7])
                dv[chunk] += dot(e, state[9])
                dstrip[pl.ds(top, CHUNK), :] += s
                out.append(dq + dot(kt_ref[chunk], low))
            return tuple(out)

        steps = functools.reduce(jnp.maximum, [s[2] - s[1] + 1 for s in states])
        done = lax.fori_loop(0, steps, visit, (jnp.zeros((GWIDTH, size), F32),) * 2)
        for state, dq in zip(states, done):
            dq_ref[state[10], :] = (fold_rows(dq, same, half) * HEAD_DIM**-0.5).astype(BF)

    @pl.loop(0, GROUPS // 2)
    def _(pair):
        pair_of(pair, 0)
        pair_of(pair, 1)

    @pl.loop(0, GROUPS, unroll=2)
    def _(slot):
        for j in range(members):
            for early in (True, False):
                block = place_of(slot, early, jnp.bitwise_xor(me, j), h, members, blocks)
                at = pl.ds(pl.multiple_of(lax.rem(block, per) * half, half), half)
                part = jnp.concatenate(
                    [dk[block // per, at, :] * HEAD_DIM**-0.5, dv[block // per, at, :]], axis=1
                )
                dkvs[j][slot, 0 if early else half : half if early else 2 * half, :] = part.astype(BF)

    lines = dstrip[...].T
    for n in range(GHEADS):
        x = lines[n * half : (n + 1) * half]
        rows = half
        while rows > 8:
            rows //= 2
            x = x[:rows] + pltpu.roll(x[rows:], width - rows, 1)
        sub = lax.broadcasted_iota(jnp.int32, x.shape, 0)
        for bit in (4, 2, 1):
            x = jnp.where((sub & bit) != 0, pltpu.roll(x, width - bit, 1), x)
        dline_ref[n : n + 1, :] = jnp.sum(x, axis=0, keepdims=True)


VMEM_SPEC = pl.BlockSpec(memory_space=pltpu.VMEM)
SMEM_SPEC = pl.BlockSpec(memory_space=pltpu.SMEM)
HBM_SPEC = pl.BlockSpec(memory_space=pltpu.HBM)


def in_hbm(*values):
    return [pltpu.with_memory_space_constraint(v, pltpu.HBM) for v in values]


def all_of(x):
    return pl.BlockSpec(x.shape, lambda: (0,) * len(x.shape))


def start_copies(pairs, sems):
    copies = [pltpu.make_async_copy(src, dst, sems.at[i]) for i, (src, dst) in enumerate(pairs)]
    for copy in copies:
        copy.start()
    return copies


def key_shapes(blocks, half):
    chunks = blocks * half // CHUNK
    return ((chunks, CHUNK, GWIDTH), (chunks, CHUNK, GWIDTH), (chunks, GWIDTH, CHUNK))


def attend(pos, q, kvs, strips, blocks):
    rows = q.shape[0]
    half = strips.shape[1] // GHEADS
    shapes = key_shapes(blocks, half)
    o_shape, stat_shape = (rows // half, GWIDTH, half), (rows // half, 8, GHEADS * half)
    return pl.pallas_call(
        functools.partial(forward_kernel, half, blocks, len(kvs)),
        in_specs=[SMEM_SPEC] + [VMEM_SPEC] * (1 + len(kvs)) + [HBM_SPEC],
        out_specs=[all_of(jax.ShapeDtypeStruct(o_shape, F32))]
        + [VMEM_SPEC] * GROUPS
        + [all_of(jax.ShapeDtypeStruct(stat_shape, F32))]
        + [HBM_SPEC] * 3,
        scratch_shapes=[pltpu.VMEM(s, BF) for s in shapes + shapes[2:]]
        + [
            pltpu.VMEM(strips.shape, F32),
            pltpu.VMEM((GROUPS, GWIDTH, 2 * half), BF),
            pltpu.SemaphoreType.DMA((3,)),
            pltpu.SemaphoreType.DMA((1,)),
        ],
        out_shape=[pltpu.HBM(o_shape, F32)]
        + [jax.ShapeDtypeStruct((GWIDTH, 2 * half), BF)] * GROUPS
        + [pltpu.HBM(stat_shape, F32)]
        + [pltpu.HBM(s, BF) for s in shapes],
        compiler_params=pltpu.CompilerParams(vmem_limit_bytes=32 << 20),
        cost_estimate=pl.CostEstimate(flops=10**5, bytes_accessed=10**4, transcendentals=0),
        name="attend",
    )(pos, q, *kvs, *in_hbm(strips))


def attend_back(pos, q, keys, strips, dos, o, stat, members, blocks):
    rows = q.shape[0]
    half = strips.shape[1] // GHEADS
    shapes = key_shapes(blocks, half)
    kv = jax.ShapeDtypeStruct((GROUPS, 2 * half, 2 * GWIDTH), BF)
    inputs = in_hbm(q, strips, o, stat, *keys)
    return pl.pallas_call(
        functools.partial(backward_kernel, half, blocks, members),
        in_specs=[SMEM_SPEC] + [VMEM_SPEC] * GROUPS + [HBM_SPEC] * len(inputs),
        out_specs=[VMEM_SPEC] * (1 + members) + [pl.BlockSpec((GHEADS, strips.shape[0]), lambda: (0, 0))],
        scratch_shapes=[pltpu.VMEM(x.shape, x.dtype) for x in inputs]
        + [pltpu.VMEM(s, F32) for s in shapes[:2]]
        + [
            pltpu.VMEM(strips.shape, F32),
            pltpu.VMEM((GROUPS, GWIDTH, 2 * half), F32),
            pltpu.SemaphoreType.DMA((len(inputs),)),
        ],
        out_shape=[jax.ShapeDtypeStruct((rows, GWIDTH), BF)]
        + [kv] * members
        + [pltpu.HBM((GHEADS, strips.shape[0]), F32)],
        compiler_params=pltpu.CompilerParams(vmem_limit_bytes=40 << 20),
        cost_estimate=pl.CostEstimate(flops=10**5, bytes_accessed=10**4, transcendentals=0),
        name="attend_back",
    )(pos, *dos, *inputs)


FBLOCK = 768
PIECES = 8


def three_parts(x):
    high = x.astype(BF).astype(F32)
    mid = (x - high).astype(BF).astype(F32)
    low = x - high - mid
    lane = lax.broadcasted_iota(jnp.int32, (x.shape[0], 128), 1)
    return jnp.where(lane == 0, high, jnp.where(lane == 1, mid, jnp.where(lane == 2, low, 0.0))).astype(BF)


def gather_rows(refs):
    return jnp.concatenate([r[...].astype(F32) for r in refs])


def router_kernel(
    pos, x_ref, out_ref, scale_ref, router_ref, routes_ref, place_ref, *refs
):
    lows, refs = refs[:GROUPS], refs[GROUPS:]
    pieces, (context_ref, resid_ref, moe_ref, gates_ref) = refs[:PIECES], refs[PIECES:]
    tok, width = x_ref.shape
    for k in range(GROUPS):
        row = pl.multiple_of(lax.rem(pos[1] + k, GROUPS) * GWIDTH, GWIDTH)
        context_ref[pl.ds(row, GWIDTH), :] = lows[k][...]
    context = context_ref[...].astype(F32).T.astype(BF)
    resid = x_ref[...].astype(F32) + dot(context, out_ref[...])
    resid_ref[...] = resid
    inv = lax.rsqrt(jnp.mean(resid * resid, axis=1, keepdims=True) + EPS)
    moe_in = (resid * inv * scale_ref[...]).astype(BF)
    moe_ref[...] = moe_in
    logits = dot(moe_in, router_ref[...], ((1,), (1,)))
    lane = lax.broadcasted_iota(jnp.int32, logits.shape, 1)
    chosen = [
        jnp.sum(jnp.where(routes_ref[:, k : k + 1] == lane, logits, 0.0), axis=1, keepdims=True)
        for k in range(TOP)
    ]
    most = jnp.maximum(chosen[0], chosen[1])
    powers = [jnp.exp(c - most) for c in chosen]
    gates = [p / (powers[0] + powers[1]) for p in powers]
    slot = lax.broadcasted_iota(jnp.int32, (EXPERTS * CAP, tok), 0)
    pick = [(place_ref[k : k + 1, :] == slot) for k in range(TOP)]
    rows = dot((pick[0] | pick[1]).astype(BF), moe_in)
    extra = sum(dot(pick[k].astype(BF), three_parts(gates[k])) for k in range(TOP))
    for p in range(PIECES):
        pieces[p][:, :width] = rows[p * CAP : (p + 1) * CAP].astype(BF)
        pieces[p][:, width:] = extra[p * CAP : (p + 1) * CAP].astype(BF)
    for k in range(TOP):
        gates_ref[:, k : k + 1] = gates[k]


def router(pos, x, out_full, scale, router_t, routes, places, lows):
    tok, width = x.shape
    kept = [pltpu.HBM(*s) for s in (((width, tok), BF), ((tok, width), F32), ((tok, width), BF), ((tok, TOP), F32))]
    x, out_full = in_hbm(x, out_full)
    return pl.pallas_call(
        router_kernel,
        in_specs=[SMEM_SPEC, all_of(x), all_of(out_full)] + [VMEM_SPEC] * (4 + GROUPS),
        out_specs=[VMEM_SPEC] * PIECES + [all_of(s.inner_aval) for s in kept],
        out_shape=[jax.ShapeDtypeStruct((CAP, width + 128), BF)] * PIECES + kept,
        compiler_params=pltpu.CompilerParams(vmem_limit_bytes=16 << 20),
        cost_estimate=pl.CostEstimate(flops=10**5, bytes_accessed=10**4, transcendentals=0),
        name="router",
    )(pos, x, out_full, scale, router_t, routes, places, *lows)


def expert_kernel(groups, n_fsdp, info, dy_ref, up_ref, down_ref, *refs):
    cames, refs = refs[:PIECES], refs[PIECES:]
    out_refs, (back_ref, act_ref, rows_ref, grad_in, out_acc, back_acc) = refs[:n_fsdp], refs[n_fsdp:]
    step = pl.program_id(0)
    width = grad_in.shape[1]
    h, f = info[0], info[1]
    source = [
        lax.rem(h + groups - p // n_fsdp, groups) * n_fsdp + jnp.bitwise_xor(f, p % n_fsdp) for p in range(PIECES)
    ]

    @pl.when(step == 0)
    def _():
        came = gather_rows(cames)
        gate = jnp.sum(came[:, width:], axis=1, keepdims=True)
        dy = jnp.concatenate([dy_ref[s].astype(F32) for s in source])
        grad_in[...] = dy
        rows_ref[0] = came[:, :width].astype(BF)
        rows_ref[1] = (gate * dy).astype(BF)
        out_acc[...] = jnp.zeros_like(out_acc)
        back_acc[...] = jnp.zeros_like(back_acc)

    up, down = up_ref[0], down_ref[0]
    upper = dot(rows_ref[0], up)
    active_grad = dot(rows_ref[1], down)
    cdf = 0.5 + 0.5 * lax.erf(upper * 0.7071067811865476)
    active = (upper * cdf).astype(BF)
    slope = cdf + upper * (0.3989422804014327 * jnp.exp(-0.5 * upper * upper))
    upper_grad = (active_grad * slope).astype(BF)
    act_ref[0] = upper_grad
    act_ref[1] = active
    back_acc[...] += dot(upper_grad, up, ((1,), (1,)))
    out_acc[...] += dot(active, down, ((1,), (1,)))

    @pl.when(step == pl.num_programs(0) - 1)
    def _():
        out = out_acc[...].astype(BF).astype(F32)
        gate_grad = three_parts(jnp.sum(grad_in[...] * out, axis=1, keepdims=True)).astype(F32)
        for p in range(PIECES):
            rows = slice(p * CAP, (p + 1) * CAP)
            out_refs[p % n_fsdp][(groups - p // n_fsdp) % groups] = out[rows].astype(BF)
            back_ref[source[p], :, :width] = back_acc[rows, :].astype(BF)
            back_ref[source[p], :, width:] = gate_grad[rows].astype(BF)


def expert(info, cames, dy, up, down, groups, n_fsdp):
    width, ffn = up.shape[1], up.shape[2]
    rows = EXPERTS * CAP
    whole = lambda *shape: pl.BlockSpec(shape, lambda j, info: (0,) * len(shape))
    weight = pl.BlockSpec((1, width, FBLOCK), lambda j, info: (info[0], 0, j))
    return pl.pallas_call(
        functools.partial(expert_kernel, groups, n_fsdp),
        grid_spec=pltpu.PrefetchScalarGridSpec(
            num_scalar_prefetch=1,
            grid=(ffn // FBLOCK,),
            in_specs=[whole(PIECES, CAP, width), weight, weight] + [whole(CAP, width + 128)] * PIECES,
            out_specs=[whole(groups, CAP, width)] * n_fsdp
            + [
                whole(PIECES, CAP, width + 128),
                pl.BlockSpec((2, rows, FBLOCK), lambda j, info: (0, 0, j)),
                whole(2, rows, width),
            ],
            scratch_shapes=[pltpu.VMEM((rows, width), F32)] * 3,
        ),
        out_shape=[pltpu.HBM((groups, CAP, width), BF)] * n_fsdp
        + [
            jax.ShapeDtypeStruct((PIECES, CAP, width + 128), BF),
            pltpu.HBM((2, rows, ffn), BF),
            pltpu.HBM((2, rows, width), BF),
        ],
        compiler_params=pltpu.CompilerParams(vmem_limit_bytes=32 << 20),
        cost_estimate=pl.CostEstimate(flops=10**5, bytes_accessed=10**4, transcendentals=0),
        name="expert",
    )(info, dy, *in_hbm(up, down), *cames)


def weight_kernel(count, members, side, pos, *refs):
    rows, acts, (keep_ref, pass_ref, turned, lhs) = refs[:count], refs[count : 2 * count], refs[2 * count :]
    half = keep_ref.shape[0]

    @pl.when(pl.program_id(0) == 0)
    def _():
        for n in range(count):
            turned[...] = rows[n][0].astype(F32).T.astype(BF)
            if side is not None:
                lhs[n] = turned[side * 2 * half : (side + 1) * 2 * half, :]
                continue
            unit = 2 * half // (GROUPS * members // 2)
            for r in range(members // 2):
                member = jnp.bitwise_xor(pos[0], 2 * r)
                for k in range(GROUPS):
                    row = pl.multiple_of((lax.rem(pos[1] + k, GROUPS) * members + member) * unit, 16)
                    at = (r * GROUPS + k) * unit
                    lhs[n, at : at + unit, :] = turned[pl.ds(row, unit), :]

    keep_ref[...] = sum(dot(lhs[n, :half, :], acts[n][0]) for n in range(count)).astype(BF)
    pass_ref[...] = sum(dot(lhs[n, half:, :], acts[n][0]) for n in range(count)).astype(BF)


def weight_terms(pos, rows, acts, which, members, side=None):
    _, count, width = rows[0].shape
    ffn = acts[0].shape[2]
    half = pl.BlockSpec((width // 4, FBLOCK), lambda j: (0, j))
    return pl.pallas_call(
        functools.partial(weight_kernel, len(rows), members, side),
        grid=(ffn // FBLOCK,),
        in_specs=[SMEM_SPEC]
        + [pl.BlockSpec((1, count, width), lambda j: (which, 0, 0))] * len(rows)
        + [pl.BlockSpec((1, count, FBLOCK), lambda j: (which, 0, j))] * len(rows),
        out_specs=[half, half],
        out_shape=[pltpu.HBM((width // 4, ffn), BF)] * 2,
        scratch_shapes=[pltpu.VMEM((width, count), BF), pltpu.VMEM((len(rows), width // 2, count), BF)],
        compiler_params=pltpu.CompilerParams(vmem_limit_bytes=20 << 20),
        cost_estimate=pl.CostEstimate(flops=10**5, bytes_accessed=10**4, transcendentals=0),
        name="weight_terms",
    )(pos, *rows, *in_hbm(*acts))


def add_kernel(riders, a_ref, b_ref, *refs):
    rides, outs = refs[:riders], refs[riders:]
    rows, width = a_ref.shape[0] // GROUPS, outs[0].shape[1]
    blocks = a_ref.shape[1] // width
    for k, out in enumerate(outs):
        for c in range(blocks):
            at = (slice(k * rows, (k + 1) * rows), slice(c * width, (c + 1) * width))
            out[c * rows : (c + 1) * rows, :] = (a_ref[at].astype(F32) + b_ref[at].astype(F32)).astype(BF)
        if riders:
            ride = jnp.concatenate([r[k].astype(F32) for r in rides])
            out[blocks * rows :, :] = ride.astype(BF)


def add_groups(a, b, width, rides=()):
    rows, cols = a.shape
    count = rows // GROUPS * cols // width + sum(r.shape[1] for r in rides)
    return pl.pallas_call(
        functools.partial(add_kernel, len(rides)),
        in_specs=[all_of(a)] * 2 + [all_of(r) for r in rides],
        out_specs=[pl.BlockSpec((count, width), lambda: (0, 0))] * GROUPS,
        out_shape=[jax.ShapeDtypeStruct((count, width), BF)] * GROUPS,
        compiler_params=pltpu.CompilerParams(vmem_limit_bytes=16 << 20),
        cost_estimate=pl.CostEstimate(flops=10**5, bytes_accessed=10**4, transcendentals=0),
        name="add_groups",
    )(*in_hbm(a, b, *rides))


def order_kernel(blocks, pos, *refs):
    out_ref = refs[-1]
    rows, width = out_ref.shape[1], out_ref.shape[2] // blocks
    for k in range(GROUPS):
        group = group_of(k, pos[1])
        for c in range(blocks):
            out_ref[group, :, c * width : (c + 1) * width] = refs[k][c * rows : (c + 1) * rows, :].astype(F32)


def in_order(pos, parts, rows, cols):
    width = parts[0].shape[1]
    return pl.pallas_call(
        functools.partial(order_kernel, cols // width),
        in_specs=[SMEM_SPEC] + [all_of(p) for p in parts],
        out_specs=pl.BlockSpec((GROUPS, rows, cols), lambda: (0, 0, 0)),
        out_shape=jax.ShapeDtypeStruct((GROUPS, rows, cols), F32),
        compiler_params=pltpu.CompilerParams(vmem_limit_bytes=16 << 20),
        cost_estimate=pl.CostEstimate(flops=10**5, bytes_accessed=10**4, transcendentals=0),
        name="in_order",
    )(pos, *parts)


def turn_kernel(
    info, place_ref, routes_ref, gates_ref, resid_ref, moe_ref, dy_ref, router_ref, scale_ref,
    out_ref, context_ref, back_ref, *refs,
):
    dos, (resid_grad_ref, mine_ref, other_ref, send_ref, router_grad_ref, gain_ref, term) = refs[:GROUPS], refs[GROUPS:]
    tok, width = resid_ref.shape
    back = back_ref[...]
    slots = back.shape[0]
    iota = lax.broadcasted_iota(jnp.int32, (tok, slots), 1)
    pick = [place_ref[:, k : k + 1] == iota for k in range(TOP)]
    gates = [gates_ref[:, k : k + 1] for k in range(TOP)]
    gate_grad = [jnp.sum(dot(p.astype(BF), back[:, width:]), axis=1, keepdims=True) for p in pick]
    mean = gates[0] * gate_grad[0] + gates[1] * gate_grad[1]
    lane = lax.broadcasted_iota(jnp.int32, (tok, 128), 1)
    logit_grad = sum(
        jnp.where(routes_ref[:, k : k + 1] == lane, gates[k] * (gate_grad[k] - mean), 0.0) for k in range(TOP)
    )
    grad = dot((pick[0] | pick[1]).astype(BF), back[:, :width])
    for e in range(EXPERTS):
        grad = grad + logit_grad[:, e : e + 1] * router_ref[e : e + 1, :].astype(F32)
    resid = resid_ref[...]
    inv = lax.rsqrt(jnp.mean(resid * resid, axis=1, keepdims=True) + EPS)
    gain_ref[...] = jnp.sum(grad * (resid * inv), axis=0, keepdims=True)
    scaled = grad * scale_ref[...]
    along = jnp.mean(scaled * resid, axis=1, keepdims=True)
    resid_grad = dy_ref[...].astype(F32) + inv * scaled - resid * (inv * inv * inv * along)
    resid_grad_ref[...] = resid_grad
    low = resid_grad.astype(BF)
    term[:, :tok] = dot(out_ref[...], low, ((1,), (1,)))
    for k in range(GROUPS):
        row = pl.multiple_of(lax.rem(info[0] + k, GROUPS) * GWIDTH, GWIDTH)
        dos[k][...] = term[pl.ds(row, GWIDTH), :tok].astype(BF)
    router_grad_ref[...] = lax.dot_general(
        logit_grad.T[:EXPERTS], moe_ref[...].astype(F32), (((1,), (0,)), ((), ())),
        precision=FULL, preferred_element_type=F32,
    )
    term[...] = dot(low.astype(F32).T.astype(BF), context_ref[...].astype(F32).T.astype(BF))
    rows, cols = mine_ref.shape[1:]
    core, top = info[1], info[2]
    mine = pl.ds(pl.multiple_of(top * cols, 128), cols)
    other = pl.ds(pl.multiple_of((1 - top) * cols, 128), cols)
    for g in range(mine_ref.shape[0]):
        keep = pl.ds(pl.multiple_of((2 * g + core) * rows, 8), rows)
        send = pl.ds(pl.multiple_of((2 * g + 1 - core) * rows, 8), rows)
        mine_ref[g] = term[keep, mine]
        other_ref[g] = term[keep, other]
        send_ref[0, g] = term[send, mine].astype(BF)
        send_ref[1, g] = term[send, other].astype(BF)


def turn_back(info, back, place, routes, gates, resid, moe_in, dy, router, scale, out_full, context, shards):
    tok, width = resid.shape
    rows = width // shards
    part = (shards // 2, rows, width // 2)
    gates, resid, moe_in, dy, out_full, context = in_hbm(gates, resid, moe_in, dy, out_full, context)
    inputs = (place, routes, gates, resid, moe_in, dy, router, scale, out_full, context, back)
    kept = [((tok, width), F32), (part, F32), (part, F32), ((2,) + part, BF), ((EXPERTS, width), F32), ((1, width), F32)]
    kept = [pltpu.HBM(*s) for s in kept]
    return pl.pallas_call(
        turn_kernel,
        in_specs=[SMEM_SPEC] + [all_of(x) for x in inputs],
        out_specs=[VMEM_SPEC] * GROUPS + [all_of(s.inner_aval) for s in kept],
        scratch_shapes=[pltpu.VMEM((width, width), F32)],
        out_shape=[jax.ShapeDtypeStruct((GWIDTH, tok), BF)] * GROUPS + kept,
        compiler_params=pltpu.CompilerParams(vmem_limit_bytes=24 << 20),
        cost_estimate=pl.CostEstimate(flops=10**5, bytes_accessed=10**4, transcendentals=0),
        name="turn_back",
    )(info, *inputs)


def pair_kernel(a_ref, b_ref, c_ref, d_ref, keep_ref, send_ref):
    keep_ref[...] = a_ref[...].astype(F32) + b_ref[...].astype(F32)
    send_ref[...] = (c_ref[...].astype(F32) + d_ref[...].astype(F32)).astype(BF)


def add_pairs(a, b, c, d):
    return pl.pallas_call(
        pair_kernel,
        in_specs=[VMEM_SPEC] * 4,
        out_specs=[VMEM_SPEC] * 2,
        out_shape=[jax.ShapeDtypeStruct(a.shape, F32), jax.ShapeDtypeStruct(a.shape, BF)],
        cost_estimate=pl.CostEstimate(flops=10**5, bytes_accessed=10**4, transcendentals=0),
        compiler_params=pltpu.CompilerParams(vmem_limit_bytes=8 << 20),
        name="add_pairs",
    )(a, b, c, d)


SMALL = 16


def input_kernel(
    members, buckets_here, info, dq_ref, keep_ref, came_ref, ain_ref, weight_ref, scale_ref, router_ref,
    gain_ref, line_ref, dline_ref, own_ref, one_ref, two_ref, three_ref, term_ref, sent_ref, pack_ref, dproj, term,
):
    h, core = info[0], info[1]
    width = ain_ref.shape[1]
    tok = own_ref.shape[0]
    dproj[:, :GWIDTH] = dq_ref[...].astype(F32)
    for k in range(GROUPS):
        dkv = keep_ref[k] if came_ref is None else keep_ref[k] + came_ref[k].astype(F32)
        dproj[k * tok : (k + 1) * tok, GWIDTH:] = dkv.astype(BF).astype(F32)
    low = dproj[...].astype(BF)
    ain = ain_ref[...]
    back = dot(low, weight_ref[...], ((1,), (1,)))
    own_ref[...] = back[:tok]
    for k, ref in enumerate((one_ref, two_ref, three_ref)):
        ref[...] = back[(k + 1) * tok : (k + 2) * tok].astype(BF)
    pack_ref[0:EXPERTS, :] = router_ref[...]
    pack_ref[EXPERTS : EXPERTS + 1, :] = jnp.sum(back * ain.astype(F32), axis=0, keepdims=True) / scale_ref[...]
    pack_ref[EXPERTS + 1 : EXPERTS + 2, :] = gain_ref[...]
    col = lax.broadcasted_iota(jnp.int32, (BUCKETS, width), 1)
    cols_f = width * buckets_here // BUCKETS
    within = lax.rem(col, cols_f) - h * buckets_here
    held = jnp.where((within >= 0) & (within < buckets_here), col // cols_f * buckets_here + within, -1)
    held = held == lax.broadcasted_iota(jnp.int32, (BUCKETS, width), 0)
    bucket = line_ref[...] == lax.broadcasted_iota(jnp.int32, (BUCKETS, line_ref.shape[1]), 0)
    for n in range(GHEADS):
        sums = jnp.sum(jnp.where(bucket, dline_ref[n : n + 1, :], 0.0), axis=1, keepdims=True)
        row = EXPERTS + 2 + n
        pack_ref[row : row + 1, :] = jnp.sum(jnp.where(held, sums, 0.0), axis=0, keepdims=True)
    rest = EXPERTS + 2 + GHEADS
    pack_ref[rest:, :] = jnp.zeros((SMALL - rest, width), F32)
    term[...] = dot(dproj[...].T.astype(BF), ain)
    unit = GWIDTH // members
    for t in range(3):
        for r in range(members // 2):
            at = slice((t * (members // 2) + r) * unit, (t * (members // 2) + r + 1) * unit)
            first = (t * members + 2 * r) * unit
            term_ref[at, :] = term[pl.ds(pl.multiple_of(first + core * unit, 8), unit), :]
            sent_ref[at, :] = term[pl.ds(pl.multiple_of(first + (1 - core) * unit, 8), unit), :].astype(BF)
    pack = pack_ref[...]
    high = pack.astype(BF)
    rows = term_ref.shape[0]
    sent_ref[rows : rows + SMALL, :] = high
    sent_ref[rows + SMALL :, :] = (pack - high.astype(F32)).astype(BF)


def input_back(info, members, buckets_here, dq, keep, came, ain, weight, scale, router_grad, gain_grad, line, dline):
    count, width = ain.shape
    tok = count // GROUPS
    rows = 3 * GWIDTH // 2
    ain, weight = in_hbm(ain, weight)
    inputs = [dq, keep] + ([] if came is None else [came]) + [ain, weight, scale, router_grad, gain_grad, line, dline]
    body = functools.partial(input_kernel, members, buckets_here)
    if came is None:
        body = lambda info, dq, keep, *refs: input_kernel(members, buckets_here, info, dq, keep, None, *refs)
    return pl.pallas_call(
        body,
        in_specs=[SMEM_SPEC] + [all_of(x) for x in inputs],
        out_specs=[VMEM_SPEC] * 7,
        out_shape=[jax.ShapeDtypeStruct((tok, width), F32)]
        + [jax.ShapeDtypeStruct((tok, width), BF)] * 3
        + [
            jax.ShapeDtypeStruct((rows, width), F32),
            jax.ShapeDtypeStruct((rows + 2 * SMALL, width), BF),
            jax.ShapeDtypeStruct((SMALL, width), F32),
        ],
        scratch_shapes=[pltpu.VMEM((count, 3 * GWIDTH), F32), pltpu.VMEM((3 * GWIDTH, width), F32)],
        compiler_params=pltpu.CompilerParams(vmem_limit_bytes=24 << 20),
        cost_estimate=pl.CostEstimate(flops=10**5, bytes_accessed=10**4, transcendentals=0),
        name="input_back",
    )(info, *inputs)


def together(*values):
    return lax.optimization_barrier(values)


def turn(shift):
    return [(i, (i + shift) % GROUPS) for i in range(GROUPS)]


def gather_groups(x):
    came = {k: lax.ppermute(x, "h", turn(k)) for k in (2, 1, 3)}
    return jnp.stack([x] + [came[k] for k in range(1, GROUPS)])


def gather_members(x):
    size = lax.axis_size(MEMBERS)
    held = {0: x}
    for bit in bits_of(size):
        for k in sorted(held):
            held[k | bit] = lax.ppermute(held[k], MEMBERS, xor_perm(bit, size))
    return [held[k] for k in range(size)]


def part_of(x, mine):
    low, high = jnp.split(x, 2, axis=-1)
    return jnp.where(mine == 0, low, high), jnp.where(mine == 0, high, low)


def swap(x, axis, bit):
    return lax.ppermute(x, axis, xor_perm(bit, lax.axis_size(axis)))


def two_parts(x):
    high = lax.reduce_precision(x, 8, 7)
    return jnp.concatenate([high, x - high]).astype(BF)


def from_fsdp(part):
    if lax.axis_size("fsdp") != 2:
        return lax.all_gather(part, "fsdp", axis=0)
    came = lax.ppermute(part, "fsdp", xor_perm(1, 2))
    return jnp.where(lax.axis_index("fsdp") == 0, jnp.stack([part, came]), jnp.stack([came, part]))


def group_pieces(pieces, sign):
    came = {k: lax.ppermute(pieces[k], "h", turn(sign * k)) for k in (2, 1, 3)}
    return [pieces[0]] + [came[k] for k in range(1, GROUPS)]


def deal(pieces, spread, sign):
    n_fsdp = lax.axis_size("fsdp")
    out = [pieces[0]] + [None] * (len(pieces) - 1)
    for p in (5, 4, 3, 7, 2, 6, 1):
        k, j = divmod(p, n_fsdp)
        if spread:
            pairs = [
                (g * n_fsdp + i, (g + sign * k) % GROUPS * n_fsdp + (i ^ j))
                for g in range(GROUPS)
                for i in range(n_fsdp)
            ]
            out[p] = lax.ppermute(pieces[p], ("h", "fsdp"), pairs)
        else:
            out[p] = lax.ppermute(pieces[p], "fsdp", xor_perm(j, n_fsdp))
    return out


def per_device(
    tokens, segments, routes, bucket_table, attn_gain, qkv_weight, out_weight, bias_table,
    moe_gain, router_weight, up_weight, down_weight, cotangent,
):
    tok, width = tokens.shape[1], tokens.shape[2]
    half = tok // 2
    h, m, f = lax.axis_index("h"), lax.axis_index(MEMBERS), lax.axis_index("fsdp")
    core = lax.axis_index("core")
    members, n_fsdp = lax.axis_size(MEMBERS), lax.axis_size("fsdp")
    shards = GROUPS * members
    blocks = 2 * shards
    length = shards * tok
    here = EXPERTS // n_fsdp
    spread = here > 1
    ffn = up_weight.shape[2]
    rows_f = width // n_fsdp
    rows_c = width // shards
    pos = jnp.stack([m, h]).astype(jnp.int32)

    extra = jnp.pad(segments.astype(BF), ((0, 7), (0, width - tok)))
    mixed = gather_groups(jnp.concatenate([tokens[0], extra]))

    bias_flat = bias_table.reshape(1, -1)
    bias_rows = -(-bias_flat.shape[1] // rows_f)
    bias_flat = jnp.pad(bias_flat, ((0, 0), (0, bias_rows * rows_f - bias_flat.shape[1])))
    small = jnp.concatenate(
        [attn_gain[None], moe_gain[None], router_weight.T, bias_flat.reshape(bias_rows, rows_f)]
        + [jnp.zeros((16 - 10 - bias_rows, rows_f), BF)]
    )
    small = from_fsdp(small)
    attn_scale = small[:, 0].reshape(width).astype(F32)
    moe_scale = small[:, 1].reshape(width).astype(F32)
    router_t = jnp.transpose(small[:, 2:10], (1, 0, 2)).reshape(EXPERTS, width)
    bias_full = small[:, 10 : 10 + bias_rows].reshape(n_fsdp, -1)[:, : bias_table.size]
    bias_full = bias_full.reshape(BUCKETS, HEADS)
    cut = [
        lax.dynamic_slice_in_dim(qkv_weight, n * width + h * GWIDTH, GWIDTH, 1) for n in range(3)
    ]
    qkv_heads = from_fsdp(jnp.concatenate(cut, axis=1)).reshape(width, 3 * GWIDTH)
    out_full = from_fsdp(together(out_weight, qkv_heads)[0]).reshape(width, width)

    wide = strip_width(blocks, half)
    top = half * (blocks - 1)
    line = jnp.concatenate(
        [
            bucket_table[: top + 1][::-1],
            jnp.full((wide - length,), -1, jnp.int32),
            bucket_table[top + 1 :][::-1],
        ]
    )
    hot = (line[None] == jnp.arange(BUCKETS, dtype=jnp.int32)[:, None]).astype(BF)
    bias_mine = lax.dynamic_slice_in_dim(bias_full, h * GHEADS, GHEADS, 1)
    strips = make_strips(dot(bias_mine, hot, ((0,), (0,))) * LOG2E, half)

    hot_routes = (routes.reshape(-1)[:, None] == jnp.arange(EXPERTS)[None]).astype(F32)
    earlier = jnp.arange(tok * TOP)
    earlier = (earlier[None, :] < earlier[:, None]).astype(BF)
    before = dot(earlier, hot_routes.astype(BF))
    slot = jnp.sum(before * hot_routes, axis=1).astype(jnp.int32).reshape(tok, TOP)
    group = routes % here
    natural = (group * n_fsdp + routes // here) * CAP + slot
    away = lax.rem(group - h + GROUPS, GROUPS) if spread else group
    place = (away * n_fsdp + jnp.bitwise_xor(routes // here, f)) * CAP + slot
    slots = jnp.arange(EXPERTS * CAP, dtype=jnp.int32)
    pick = [slots[:, None] == natural[None, :, k] for k in range(TOP)]
    exchange = ("h", "fsdp") if spread else ("fsdp",)

    def exchange_rows(rows):
        return lax.all_to_all(rows, exchange, 0, 0, tiled=True)

    mixed, strips = together(mixed, strips)
    ain = normalize(mixed[:, :tok].astype(F32), attn_scale).astype(BF).reshape(GROUPS * tok, width)
    proj = dot(ain, qkv_heads).astype(BF)
    kv = proj[:, GWIDTH:].reshape(GROUPS, tok, 2 * GWIDTH)
    kvs = gather_members(jnp.concatenate([kv, mixed[:, tok:, : 2 * GWIDTH]], axis=1))
    dy_send = dot((pick[0] | pick[1]).astype(BF), cotangent[0]).astype(BF).reshape(PIECES, CAP, width)
    dy_slots = exchange_rows(together(dy_send, small)[0])
    o_pre, *rest = attend(pos, proj, kvs, strips, blocks)
    lows, stat, keys = rest[:GROUPS], rest[GROUPS], rest[GROUPS + 1 :]
    lows[1], dy_slots = together(lows[1], dy_slots)
    *pieces, context, residual, moe_in, gates = router(
        pos, tokens[0], out_full, moe_scale[None], router_t, routes, place.T, group_pieces(lows, -1)
    )

    came = deal(pieces, spread, 1)
    info = jnp.stack([h if spread else jnp.zeros_like(h), f]).astype(jnp.int32)
    *outs, back, act, rows = expert(
        info, came, dy_slots, up_weight, down_weight, GROUPS if spread else 1, n_fsdp
    )
    back = exchange_rows(back).reshape(EXPERTS * CAP, -1)

    staged = spread and members == 4
    if staged:
        rows, acts = [rows, swap(rows, "core", 1)], [act, swap(act, "core", 1)]
        terms = [weight_terms(pos, rows, acts, n, members) for n in range(2)]
        back, terms = together(back, terms)
    else:
        terms = [weight_terms(pos, [rows], [act], n, members, side) for n in range(2) for side in range(2)]

    top_bit = n_fsdp // 2
    info = jnp.stack([h, core, (f // top_bit) % 2]).astype(jnp.int32)
    *dos, resid_grad, out_mine, out_other, out_send, router_grad, moe_gain_grad = turn_back(
        info, back, natural, routes, gates, residual, moe_in, cotangent[0], router_t,
        moe_scale[None], out_full, context, shards,
    )
    dos = group_pieces(dos, 1)
    outs = [outs[0]] + [lax.ppermute(outs[j], "fsdp", xor_perm(j, n_fsdp)) for j in range(1, n_fsdp)]
    dq, *dkvs, dline = attend_back(pos, proj, keys, strips, dos, o_pre, stat, members, blocks)
    dkvs[1], outs = together(dkvs[1], outs)
    out_came = swap(together(out_send, dq)[0], "core", 1)
    out_far = swap((out_other + out_came[1].astype(F32)).astype(BF), "fsdp", top_bit)
    cames = [swap(dkvs[k], "core", 1) for k in range(1, members, 2)]
    sends = []
    if members == 4:
        keep, send = add_pairs(dkvs[0], cames[0], dkvs[2], cames[1])
        if staged:
            sends = [swap(terms[0][1], "r", 1)]
            send, sends[0] = together(send, sends[0])
        came = swap(send, "r", 1)
    else:
        held = {k: dkvs[k].astype(F32) + cames[k // 2].astype(F32) for k in range(0, members, 2)}
        bit = 2
        while bit < members:
            for k in [k for k in sorted(held) if k & bit]:
                held[k - bit] = held[k - bit] + swap(held.pop(k).astype(BF), "r", bit // 2).astype(F32)
            bit *= 2
        keep, came = held[0], None
    if staged:
        up_came = group_pieces(add_groups(terms[0][0], sends[0], width, outs), 1)
        sends.append(swap(together(terms[1][1], came)[0], "r", 1))
        came, up_came[1] = together(came, up_came[1])

    own_back, back_1, back_2, back_3, term, sent, pack = input_back(
        jnp.stack([h, core]).astype(jnp.int32), members, BUCKETS // n_fsdp, dq, keep, came, ain, qkv_heads,
        attn_scale[None], router_grad, moe_gain_grad, line[None], dline,
    )

    def swap_both(send, pack, axis, bit):
        sent = jnp.concatenate([send.reshape(-1, send.shape[-1]).astype(BF), two_parts(pack)])
        return split_rows(swap(sent, axis, bit).astype(F32), send.shape)

    def split_rows(came, shape):
        return came[: -2 * SMALL].reshape(shape), came[-2 * SMALL : -SMALL] + came[-SMALL:]

    unit = GWIDTH // members
    came, pack_came = split_rows(swap(sent, "core", 1).astype(F32), term.shape)
    term, pack = term + came, pack + pack_came
    out_term = out_mine + out_came[0].astype(F32) + out_far.astype(F32)
    for bit in list(bits_of(n_fsdp))[1:]:
        out_term, out_send = part_of(out_term, (f // bit) % 2)
        out_term = out_term + swap(out_send.astype(BF), "fsdp", bit).astype(F32)
    for bit in bits_of(n_fsdp):
        term, send = part_of(term, (f // bit) % 2)
        pack, pack_send = part_of(pack, (f // bit) % 2)
        came, pack_came = swap_both(send, pack_send, "fsdp", bit)
        term, pack = term + came, pack + pack_came
    term = jnp.concatenate(
        [term.reshape(3, members // 2, unit, rows_f).swapaxes(0, 1).reshape(members // 2, -1, rows_f)]
        + [out_term.reshape(GROUPS, members // 2, rows_c, rows_f).swapaxes(0, 1).reshape(members // 2, -1, rows_f)],
        axis=1,
    )
    if staged:
        term, sends[1], up_came = together(term, sends[1], up_came)
    for bit in bits_of(members // 2):
        mine = (lax.axis_index("r") // bit) % 2
        term = term.reshape((2, -1) + term.shape[1:])
        came, pack_came = swap_both(lax.dynamic_index_in_dim(term, 1 - mine, 0, False), pack, "r", bit)
        term = lax.dynamic_index_in_dim(term, mine, 0, False) + came
        pack = pack + pack_came
    term = term[0]
    if staged:
        back_2, up_came = together(back_2, up_came)
        back_3, term = together(back_3, term)
    mid = lax.ppermute(back_2, "h", turn(-1))
    side = lax.ppermute(back_3, "h", turn(1)).astype(F32)
    mid = (back_1.astype(F32) + mid.astype(F32)).astype(BF)
    mid = lax.ppermute(mid, "h", turn(-1)).astype(F32)
    attn_in_grad = own_back + side + mid
    x = tokens[0].astype(F32)
    token_grad = jax.vjp(lambda v: normalize(v, attn_scale), x)[1](attn_in_grad)[0]
    tokens_grad = (resid_grad + token_grad).astype(BF)

    out_term = term[3 * unit :].reshape(GROUPS, rows_c, rows_f)
    term = term[: 3 * unit].astype(BF).reshape(3, unit, rows_f)
    if staged:
        down_came = group_pieces(add_groups(terms[1][0], sends[1], width), 1)
    out_sum, pack_sum = lax.dynamic_index_in_dim(out_term, h, 0, False), pack
    for k in (2, 1, 3):
        piece = lax.dynamic_index_in_dim(out_term, lax.rem(h + k, GROUPS), 0, False)
        came = lax.ppermute(jnp.concatenate([piece.astype(BF), two_parts(pack)]), "h", turn(k)).astype(F32)
        out_sum = out_sum + came[:rows_c]
        pack_sum = pack_sum + came[rows_c : rows_c + SMALL] + came[rows_c + SMALL :]
    at = h * members + m
    parts = []
    for r in range(3):
        pairs = [((3 * d + r) % shards, d) for d in range(shards)]
        third = pow(3, -1, shards)
        which = (3 * lax.rem((at + shards - r) * third, shards) + r) // shards
        parts.append(lax.ppermute(lax.dynamic_index_in_dim(term, which, 0, False), CTX, pairs))
    if staged:
        up_came, parts = together(up_came, parts)
        grads = [in_order(pos, part, rows_c, ffn) for part in (up_came, down_came)]
        home = jnp.concatenate([part[rows_c * ffn // width :] for part in up_came])
    else:
        terms = [jnp.concatenate(terms[n] + terms[n + 1]) for n in (0, 2)]
        grads = [
            lax.psum_scatter(term, CTX, scatter_dimension=0, tiled=True)[None].astype(F32) for term in terms
        ]
        home = jnp.concatenate([o.reshape(-1, width) for o in outs])
    qkv_grad = jnp.concatenate(parts).astype(F32).T

    away = lax.rem(h - group + GROUPS, GROUPS) if spread else group
    place = (away * n_fsdp + jnp.bitwise_xor(routes // here, f)) * CAP + slot
    layer_out = residual
    for k in range(TOP):
        row = (slots[:, None] == place[None, :, k]).astype(BF)
        layer_out = layer_out + gates[:, k : k + 1] * dot(row, home, ((0,), (0,)))
    bias_grad = pack_sum[EXPERTS + 2 : EXPERTS + 2 + GHEADS, : GROUPS * BUCKETS // n_fsdp]
    bias_grad = bias_grad.reshape(GHEADS, GROUPS, BUCKETS // n_fsdp).transpose(2, 1, 0).reshape(-1, HEADS)
    return (
        layer_out.astype(BF)[None],
        tokens_grad[None],
        pack_sum[8],
        qkv_grad,
        out_sum.T,
        bias_grad,
        pack_sum[9],
        pack_sum[:8].T,
        grads[0],
        grads[1],
    )


def solution(mesh):
    n_ctx, n_fsdp = mesh.shape["ctx"], mesh.shape["fsdp"]
    cut = mesh.devices.reshape(GROUPS, n_ctx // (2 * GROUPS), 2, n_fsdp)
    row = P("fsdp", CTX, None)
    return jax.shard_map(
        per_device,
        mesh=Mesh(cut, CTX + ("fsdp",)),
        in_specs=(
            row,
            P("fsdp", CTX),
            P(CTX + ("fsdp",), None),
            P(),
            P("fsdp"),
            P("fsdp", None),
            P("fsdp", None),
            P("fsdp", None),
            P("fsdp"),
            P("fsdp", None),
            P("fsdp", None, None),
            P("fsdp", None, None),
            row,
        ),
        out_specs=(
            row,
            row,
            P("fsdp"),
            P("fsdp", CTX),
            P("fsdp", CTX),
            P("fsdp", None),
            P("fsdp"),
            P("fsdp", None),
            row,
            row,
        ),
        check_vma=False,
    )
```
